32 devices in a mesh: seq: 4 (over y, x), ctx: 8 (over z, core).
Axes of the slice: x: 2, y: 2, z: 4, core: 2. Of those that a mesh axis runs over, the one named last changes fastest.
Arguments:
- states: bfloat16 [4096, 1280], P(('seq', 'ctx')), may hold values from -0.15625 to 0.15625
- cotangent: bfloat16 [4096, 1280], P(('seq', 'ctx')), may hold values from -6 to 6
- attn_weights: float32 [1280, 5120], P(('seq', 'ctx')), may hold values from -0.15625 to 0.15625
- mlp_weights: float32 [1280, 15360], P(('seq', 'ctx')), may hold values from -0.15625 to 0.15625
- feature_gains: float32 [1280, 3], replicated, may hold values from 0.5 to 2
- unit_gains: float32 [5120, 2], replicated, may hold values from 0.5 to 2
- block_place: int32 [4, 8], P('seq'), may hold values from 0 to 7, each once within a row
Outputs:
- out_states: bfloat16 [4096, 1280], P(('seq', 'ctx'))
- grad_states: bfloat16 [4096, 1280], P(('seq', 'ctx'))
- grad_attn: float32 [1280, 5120], P(('seq', 'ctx'))
- grad_mlp: float32 [1280, 15360], P(('seq', 'ctx'))
- grad_feature_gains: float32 [1280, 3], P(('seq', 'ctx'))
- grad_unit_gains: float32 [5120, 2], P(('seq', 'ctx'))
The draws below stay inside these ranges and needn't reach their ends.
Inputs may be any that keep to these rules, and one draw needn't show every extreme that they name: Each row of block_place is a permutation of 0 to 7.
All inputs are finite; a program needn't handle non-finite values.
Results may differ from the reference program's by a relative error of at most 0.02.
The reference program's roundings to bfloat16 on the way count: a program that leaves them out, or rounds other values in their place, can miss the bound.
Values may be sent and summed in bfloat16 or wider, within the bound.
A program may use at most 384 MiB of HBM per device.

```python
import math
import jax
import jax.numpy as jnp
from jax import lax

D = 1280
HEADS = 20
HEAD_DIM = 64
FF = 5120
TOK_DEV = 128
SEQ_LEN = 1024
TOKENS = 4096
N_SEQ = 4
N_CTX = 8


def block_levels(rng, extent, pieces, least, largest):
    gain = 1.0
    for position, parts in pieces:
        steps = jax.random.uniform(jax.random.fold_in(jax.random.fold_in(rng, 6), position), (parts,), jnp.float32, least / len(pieces), largest / len(pieces))
        gain = gain * jnp.repeat(jnp.exp(steps), extent[position] // parts).reshape((-1,) + (1,) * (len(extent) - 1 - position))
    return gain


def centred(own_key, shape, scale, reach, shards=(), kind=jnp.bfloat16):
    entries = jax.random.normal(own_key, shape, jnp.float32) * scale
    if len(shards) > 0:
        entries = block_levels(own_key, shape, shards, -0.22, 0.18) * entries
    return jnp.clip(entries, min=-reach, max=reach).astype(kind)


def setup_inputs(seed: int = 0) -> dict:
    streams_of = jax.random.split(jax.random.key(seed), 8)
    return {
        "states": centred(streams_of[0], (TOKENS, D), D ** -0.5, 0.15625, ((0, 32),)),
        "cotangent": centred(streams_of[1], (TOKENS, D), 1.0, 6.0, ((0, 32),)),
        "attn_weights": centred(streams_of[2], (D, 4 * D), D ** -0.5, 0.15625, ((0, 32),), jnp.float32),
        "mlp_weights": centred(streams_of[3], (D, 3 * FF), D ** -0.5, 0.15625, ((0, 32),), jnp.float32),
        "feature_gains": jnp.clip(jnp.exp(jax.random.uniform(streams_of[4], (D, 3), jnp.float32, math.log(0.5), math.log(2.0))), 0.5, 2.0),
        "unit_gains": jnp.clip(jnp.exp(jax.random.uniform(streams_of[5], (FF, 2), jnp.float32, math.log(0.5), math.log(2.0))), 0.5, 2.0),
        "block_place": jax.vmap(lambda own: jax.random.permutation(own, N_CTX))(jax.random.split(streams_of[6], N_SEQ)).reshape((N_SEQ, N_CTX)).astype(jnp.int32),
    }


EPSILON = 1e-06
NEG_LARGE = -1e+30
PRECISE = lax.Precision.HIGHEST

@jax.custom_vjp
def low(v):
    return lax.optimization_barrier(v.astype(jnp.bfloat16)).astype(jnp.float32)

@jax.custom_vjp
def low_back(v):
    return v

def low_keep(v):
    return (low(v), None)

def low_pass(kept, grad):
    return (grad,)

def back_keep(v):
    return (v, None)

def back_low(kept, grad):
    return (low(grad),)
low.defvjp(low_keep, low_pass)
low_back.defvjp(back_keep, back_low)

def unit_rows(values_in):
    return values_in * lax.rsqrt(lax.optimization_barrier(jnp.sum(values_in * values_in, axis=-1, keepdims=True)) + EPSILON)

def product(left_mat, right_mat):
    return jnp.dot(left_mat, right_mat, precision=PRECISE, preferred_element_type=jnp.float32)

def attend(query_low, key_low, value_low, positions):
    qblock = min(512, SEQ_LEN)
    nblocks = SEQ_LEN // qblock
    score_scale = math.sqrt(HEAD_DIM)

    def one_block(inputs):
        query_rows, query_pos = inputs
        scores = low_back(score_scale * jnp.einsum('qhd,khd->hqk', query_rows, key_low, precision=PRECISE))
        allowed = positions[None, None, :] <= query_pos[None, :, None]
        masked = jnp.where(allowed, scores, NEG_LARGE)
        row_max = lax.optimization_barrier(jnp.max(masked, axis=-1, keepdims=True))
        powered = jnp.where(allowed, jnp.exp(masked - row_max), 0.0)
        weights = powered / lax.optimization_barrier(jnp.sum(powered, axis=-1, keepdims=True))
        return jnp.einsum('hqk,khd->qhd', low(weights), value_low, precision=PRECISE)
    blocks = lax.map(jax.checkpoint(one_block), (query_low.reshape(nblocks, qblock, HEADS, HEAD_DIM), positions.reshape(nblocks, qblock)))
    return blocks.reshape(SEQ_LEN, D)

def layer(states, attn_weights, mlp_weights, feature_gains, unit_gains, positions):
    attn_low = low(attn_weights)
    mlp_low = low(mlp_weights)
    projected = low_back(product(states, attn_low[:, :3 * D]))
    query_raw = projected[:, :D].reshape(SEQ_LEN, HEADS, HEAD_DIM)
    key_raw = projected[:, D:2 * D].reshape(SEQ_LEN, HEADS, HEAD_DIM)
    value_low = low(projected[:, 2 * D:]).reshape(SEQ_LEN, HEADS, HEAD_DIM)
    qk_gain = feature_gains[:, 0].reshape(HEADS, HEAD_DIM)
    query_low = low(unit_rows(query_raw) * qk_gain)
    key_low = low(unit_rows(key_raw) * qk_gain)
    attended = low(low_back(attend(query_low, key_low, value_low, positions)))
    branch_attn = low_back(product(attended, attn_low[:, 3 * D:]))
    mixed_one = unit_rows(states + feature_gains[:, 1] * (unit_rows(branch_attn) - states))
    up_gate = low_back(product(low(mixed_one), mlp_low[:, :2 * FF]))
    up_scaled = up_gate[:, :FF] * unit_gains[:, 0]
    gate_scaled = up_gate[:, FF:] * (unit_gains[:, 1] * math.sqrt(D))
    hidden = low(gate_scaled * jax.nn.sigmoid(gate_scaled) * up_scaled)
    branch_mlp = low_back(lax.dot_general(hidden, mlp_low[:, 2 * FF:], (((1,), (1,)), ((), ())), precision=PRECISE, preferred_element_type=jnp.float32))
    return unit_rows(mixed_one + feature_gains[:, 2] * (unit_rows(branch_mlp) - mixed_one))

def reference(states, cotangent, attn_weights, mlp_weights, feature_gains, unit_gains, block_place):
    seq_states = states.astype(jnp.float32).reshape(N_SEQ, SEQ_LEN, D)
    seq_cot = cotangent.astype(jnp.float32).reshape(N_SEQ, SEQ_LEN, D)
    offsets = jnp.arange(TOK_DEV, dtype=jnp.int32)

    def per_sequence(totals, inputs):
        seq_rows, seq_grad, places = inputs
        positions = (places.astype(jnp.int32)[:, None] * TOK_DEV + offsets[None, :]).reshape(SEQ_LEN)

        def forward(rows_in, attn_in, mlp_in, feat_in, unit_in):
            return layer(rows_in, attn_in, mlp_in, feat_in, unit_in, positions)
        result, pullback = jax.vjp(forward, seq_rows, attn_weights, mlp_weights, feature_gains, unit_gains)
        gradients = pullback(seq_grad)
        totals = tuple((summed + fresh for summed, fresh in zip(totals, gradients[1:])))
        return (totals, (result, gradients[0]))
    zero_totals = (jnp.zeros_like(attn_weights), jnp.zeros_like(mlp_weights), jnp.zeros_like(feature_gains), jnp.zeros_like(unit_gains))
    totals, (results, grad_rows) = lax.scan(per_sequence, zero_totals, (seq_states, seq_cot, block_place))
    out_states = results.reshape(TOKENS, D).astype(jnp.bfloat16)
    grad_states = grad_rows.reshape(TOKENS, D).astype(jnp.bfloat16)
    return (out_states, grad_states, totals[0], totals[1], totals[2], totals[3])
```

```python
import math

import jax
import jax.numpy as jnp
from jax import lax
from jax.sharding import PartitionSpec as P

D = 1280
HEADS = 20
HEAD_DIM = 64


EPSILON = 1e-06
NEG_LARGE = -1e30


def unit_rows(values_in):
    factor = lax.rsqrt(jnp.sum(values_in * values_in, axis=-1, keepdims=True) + EPSILON)
    return (values_in * factor, factor)


def unit_back(normed, factor, upstream):
    return factor * (upstream - normed * jnp.sum(upstream * normed, axis=-1, keepdims=True))


def contract_rows(left_mat, right_mat):
    return lax.dot_general(
        left_mat, right_mat, (((0,), (0,)), ((), ())), preferred_element_type=jnp.float32
    )


def contract_cols(left_mat, right_mat):
    return lax.dot_general(
        left_mat, right_mat, (((1,), (1,)), ((), ())), preferred_element_type=jnp.float32
    )


def shards_general(states, cotangent, attn_weights, mlp_weights, feature_gains, unit_gains, block_place):
    tok_rows = states.shape[0]
    model_width = states.shape[1]
    ff_width = unit_gains.shape[0]
    score_scale = math.sqrt(HEAD_DIM)
    gate_factor = unit_gains[:, 1] * math.sqrt(D)
    w_attn = lax.all_gather(attn_weights.astype(jnp.bfloat16), ("seq", "ctx"), axis=0, tiled=True)
    w_mlp = lax.all_gather(mlp_weights.astype(jnp.bfloat16), ("seq", "ctx"), axis=0, tiled=True)
    states_full = states.astype(jnp.float32)
    projected = jnp.dot(states, w_attn[:, : 3 * model_width], preferred_element_type=jnp.float32)
    head_shape = (tok_rows, HEADS, HEAD_DIM)
    qk_gain = feature_gains[:, 0].reshape(HEADS, HEAD_DIM)
    query_unit, query_factor = unit_rows(projected[:, :model_width].reshape(head_shape))
    key_unit, key_factor = unit_rows(
        projected[:, model_width : 2 * model_width].reshape(head_shape)
    )
    query_low = (query_unit * qk_gain).astype(jnp.bfloat16)
    key_low = (key_unit * qk_gain).astype(jnp.bfloat16).reshape(tok_rows, model_width)
    value_low = projected[:, 2 * model_width :].astype(jnp.bfloat16)
    keys_all, values_all = (
        lax.all_gather(key_low, "ctx", axis=0, tiled=True),
        lax.all_gather(value_low, "ctx", axis=0, tiled=True),
    )
    seq_len = keys_all.shape[0]
    ctx_lanes = jnp.arange(lax.axis_size("ctx"), dtype=jnp.int32)
    places = block_place[0]
    own_block = jnp.sum(jnp.where(ctx_lanes == lax.axis_index("ctx"), places, 0))
    query_pos = own_block * tok_rows + jnp.arange(tok_rows, dtype=jnp.int32)
    key_index = jnp.arange(seq_len, dtype=jnp.int32)
    key_owner = key_index // tok_rows
    key_pos = (
        jnp.sum(jnp.where(key_owner[:, None] == ctx_lanes[None, :], places[None, :], 0), axis=1)
        * tok_rows
        + key_index % tok_rows
    )
    kblock = min(512, seq_len)
    nblocks = seq_len // kblock
    key_blocks = keys_all.reshape(nblocks, kblock, HEADS, HEAD_DIM)
    value_blocks = values_all.reshape(nblocks, kblock, HEADS, HEAD_DIM)
    pos_blocks = key_pos.reshape(nblocks, kblock)

    def block_scores(key_rows, key_places):
        raw_scores = score_scale * jnp.einsum(
            "qhd,khd->hqk", query_low, key_rows, preferred_element_type=jnp.float32
        )
        allowed = key_places[None, None, :] <= query_pos[None, :, None]
        return (raw_scores, allowed)

    def max_step(running, inputs):
        running_max, running_sum = running
        key_rows, key_places = inputs
        raw_scores, allowed = block_scores(key_rows, key_places)
        masked = jnp.where(allowed, raw_scores, NEG_LARGE)
        new_max = jnp.maximum(running_max, jnp.max(masked, axis=-1))
        powered = jnp.where(allowed, jnp.exp(masked - new_max[..., None]), 0.0)
        running_sum = running_sum * jnp.exp(running_max - new_max) + jnp.sum(powered, axis=-1)
        return ((new_max, running_sum), None)

    start_max = jnp.full((HEADS, tok_rows), NEG_LARGE, jnp.float32)
    start_sum = jnp.zeros((HEADS, tok_rows), jnp.float32)
    (final_max, final_sum), _ = lax.scan(max_step, (start_max, start_sum), (key_blocks, pos_blocks))
    log_total = final_max + jnp.log(final_sum)

    def value_step(accumulated, inputs):
        key_rows, value_rows, key_places = inputs
        raw_scores, allowed = block_scores(key_rows, key_places)
        weights_low = jnp.where(allowed, jnp.exp(raw_scores - log_total[..., None]), 0.0).astype(
            jnp.bfloat16
        )
        accumulated = accumulated + jnp.einsum(
            "hqk,khd->qhd", weights_low, value_rows, preferred_element_type=jnp.float32
        )
        return (accumulated, None)

    attended, _ = lax.scan(
        value_step, jnp.zeros(head_shape, jnp.float32), (key_blocks, value_blocks, pos_blocks)
    )
    attended_low = attended.reshape(tok_rows, model_width).astype(jnp.bfloat16)
    branch_attn = jnp.dot(
        attended_low, w_attn[:, 3 * model_width :], preferred_element_type=jnp.float32
    )
    attn_unit, attn_factor = unit_rows(branch_attn)
    alpha_attn = feature_gains[:, 1]
    mixed_one, mix_factor = unit_rows(states_full + alpha_attn * (attn_unit - states_full))
    mixed_low = mixed_one.astype(jnp.bfloat16)
    up_gate = jnp.dot(mixed_low, w_mlp[:, : 2 * ff_width], preferred_element_type=jnp.float32)
    up_scaled = up_gate[:, :ff_width] * unit_gains[:, 0]
    gate_scaled = up_gate[:, ff_width:] * gate_factor
    sigmoid_gate = jax.nn.sigmoid(gate_scaled)
    activated = gate_scaled * sigmoid_gate
    hidden = (activated * up_scaled).astype(jnp.bfloat16)
    branch_mlp = contract_cols(hidden, w_mlp[:, 2 * ff_width :])
    mlp_unit, mlp_factor = unit_rows(branch_mlp)
    alpha_mlp = feature_gains[:, 2]
    out_full, out_factor = unit_rows(mixed_one + alpha_mlp * (mlp_unit - mixed_one))
    grad_mix_two = unit_back(out_full, out_factor, cotangent.astype(jnp.float32))
    grad_alpha_m = jnp.sum(grad_mix_two * (mlp_unit - mixed_one), axis=0)
    grad_branch_mlp = unit_back(mlp_unit, mlp_factor, grad_mix_two * alpha_mlp).astype(jnp.bfloat16)
    grad_hidden = jnp.dot(
        grad_branch_mlp, w_mlp[:, 2 * ff_width :], preferred_element_type=jnp.float32
    )
    grad_up_scaled = grad_hidden * activated
    grad_gate_scaled = (
        grad_hidden * up_scaled * sigmoid_gate * (1.0 + gate_scaled * (1.0 - sigmoid_gate))
    )
    grad_s_u = jnp.sum(grad_up_scaled * up_gate[:, :ff_width], axis=0)
    grad_s_v = jnp.sum(grad_gate_scaled * up_gate[:, ff_width:], axis=0) * math.sqrt(D)
    grad_up_gate = jnp.concatenate(
        [grad_up_scaled * unit_gains[:, 0], grad_gate_scaled * gate_factor], axis=1
    ).astype(jnp.bfloat16)
    grad_mixed_one = grad_mix_two * (1.0 - alpha_mlp) + contract_cols(
        grad_up_gate, w_mlp[:, : 2 * ff_width]
    )
    grad_mix_one = unit_back(mixed_one, mix_factor, grad_mixed_one)
    grad_alpha_a = jnp.sum(grad_mix_one * (attn_unit - states_full), axis=0)
    grad_branch_attn = unit_back(attn_unit, attn_factor, grad_mix_one * alpha_attn).astype(
        jnp.bfloat16
    )
    grad_attended = (
        contract_cols(grad_branch_attn, w_attn[:, 3 * model_width :])
        .astype(jnp.bfloat16)
        .reshape(head_shape)
    )
    row_dots = jnp.einsum("qhd,qhd->hq", grad_attended.astype(jnp.float32), attended)

    def grad_step(grad_query, inputs):
        key_rows, value_rows, key_places = inputs
        raw_scores, allowed = block_scores(key_rows, key_places)
        probabilities = jnp.where(allowed, jnp.exp(raw_scores - log_total[..., None]), 0.0)
        grad_prob = jnp.einsum(
            "qhd,khd->hqk", grad_attended, value_rows, preferred_element_type=jnp.float32
        )
        grad_scores = (probabilities * (grad_prob - row_dots[..., None])).astype(jnp.bfloat16)
        grad_query = grad_query + score_scale * jnp.einsum(
            "hqk,khd->qhd", grad_scores, key_rows, preferred_element_type=jnp.float32
        )
        key_terms = score_scale * jnp.einsum(
            "hqk,qhd->khd", grad_scores, query_low, preferred_element_type=jnp.float32
        )
        value_terms = jnp.einsum(
            "hqk,qhd->khd",
            probabilities.astype(jnp.bfloat16),
            grad_attended,
            preferred_element_type=jnp.float32,
        )
        return (grad_query, (key_terms, value_terms))

    grad_query_low, (key_terms, value_terms) = lax.scan(
        grad_step, jnp.zeros(head_shape, jnp.float32), (key_blocks, value_blocks, pos_blocks)
    )
    key_terms = key_terms.reshape(seq_len, model_width)
    value_terms = value_terms.reshape(seq_len, model_width)
    own_key_grad, own_value_grad = (
        lax.psum_scatter(
            key_terms.astype(jnp.bfloat16), "ctx", scatter_dimension=0, tiled=True
        ).astype(jnp.float32),
        lax.psum_scatter(
            value_terms.astype(jnp.bfloat16), "ctx", scatter_dimension=0, tiled=True
        ).astype(jnp.float32),
    )
    grad_key_low = own_key_grad.reshape(head_shape)
    grad_s_qk = jnp.sum(grad_query_low * query_unit + grad_key_low * key_unit, axis=0).reshape(
        model_width
    )
    grad_query_raw = unit_back(query_unit, query_factor, grad_query_low * qk_gain).reshape(
        tok_rows, model_width
    )
    grad_key_raw = unit_back(key_unit, key_factor, grad_key_low * qk_gain).reshape(
        tok_rows, model_width
    )
    grad_projected = jnp.concatenate([grad_query_raw, grad_key_raw, own_value_grad], axis=1).astype(
        jnp.bfloat16
    )
    grad_states = grad_mix_one * (1.0 - alpha_attn) + contract_cols(
        grad_projected, w_attn[:, : 3 * model_width]
    )
    feature_total = jnp.stack([grad_s_qk, grad_alpha_a, grad_alpha_m], axis=1)
    unit_fold = jnp.stack([grad_s_u, grad_s_v], axis=1).reshape(
        model_width, 2 * ff_width // model_width
    )
    attn_cols = 4 * model_width
    mlp_cols = 3 * ff_width
    attn_share = lax.psum_scatter(
        jnp.concatenate(
            [
                contract_rows(states, grad_projected),
                contract_rows(attended_low, grad_branch_attn),
                feature_total,
            ],
            axis=1,
        ),
        ("seq", "ctx"),
        scatter_dimension=0,
        tiled=True,
    )
    mlp_share = lax.psum_scatter(
        jnp.concatenate(
            [
                contract_rows(mixed_low, grad_up_gate),
                contract_rows(grad_branch_mlp, hidden),
                unit_fold,
            ],
            axis=1,
        ),
        ("seq", "ctx"),
        scatter_dimension=0,
        tiled=True,
    )
    grad_attn = attn_share[:, :attn_cols]
    grad_feature = attn_share[:, attn_cols:]
    grad_mlp = mlp_share[:, :mlp_cols]
    grad_unit = mlp_share[:, mlp_cols:].reshape(
        unit_gains.shape[0] // lax.axis_size(("seq", "ctx")), 2
    )
    return (
        out_full.astype(jnp.bfloat16),
        grad_states.astype(jnp.bfloat16),
        grad_attn,
        grad_mlp,
        grad_feature,
        grad_unit,
    )


CORES = 2
ALL = ("seq", "ctx")


def fits(n_seq, chips):
    return n_seq == 4 and chips == 4 and HEADS % chips == 0


def chip_groups(chips):
    return [[CORES * chip + core for chip in range(chips)] for core in range(CORES)]


def core_groups(chips):
    return [[CORES * chip + core for core in range(CORES)] for chip in range(chips)]


def copy_groups(n_seq, chips):
    return [
        [(seq * chips + chip) * CORES + core for seq in range(n_seq) for core in range(CORES)]
        for chip in range(chips)
    ]


def spread_weights(weights_low, parts, n_seq, chips):
    rows, columns = weights_low.shape
    share = columns // parts // chips
    by_chip = weights_low.reshape(rows, parts, chips, share).transpose(2, 0, 1, 3)
    by_chip = by_chip.reshape(chips, rows, parts * share)
    mine = lax.all_to_all(
        by_chip, "ctx", split_axis=0, concat_axis=0, tiled=True,
        axis_index_groups=chip_groups(chips),
    )
    full = lax.all_gather(mine, ALL, axis=0, axis_index_groups=copy_groups(n_seq, chips))
    full = full.reshape(n_seq, CORES, chips, rows, parts * share).transpose(0, 2, 1, 3, 4)
    return full.reshape(n_seq * CORES * chips * rows, parts * share)


def collect_grads(partial, parts, n_seq, chips):
    rows = partial.shape[0] // (n_seq * CORES * chips)
    share = partial.shape[1] // parts
    by_owner = partial.astype(jnp.bfloat16).reshape(n_seq, chips, CORES, rows, parts * share)
    by_owner = by_owner.transpose(0, 2, 1, 3, 4).reshape(n_seq * CORES * chips * rows, parts * share)
    mine = lax.psum_scatter(
        by_owner, ALL, scatter_dimension=0, tiled=True,
        axis_index_groups=copy_groups(n_seq, chips),
    ).reshape(chips, rows, parts * share)
    back = lax.all_to_all(
        mine, "ctx", split_axis=0, concat_axis=0, tiled=True,
        axis_index_groups=chip_groups(chips),
    )
    back = back.reshape(chips, rows, parts, share).transpose(1, 2, 0, 3)
    return back.reshape(rows, parts * chips * share).astype(jnp.float32)


def shards_split(states, cotangent, attn_weights, mlp_weights, feature_gains, unit_gains, block_place):
    tok_rows, model_width = states.shape
    ff_width = unit_gains.shape[0]
    n_seq, n_ctx = lax.axis_size("seq"), lax.axis_size("ctx")
    chips = n_ctx // CORES
    score_scale = math.sqrt(HEAD_DIM)
    chip = lax.axis_index("ctx") // CORES
    core = lax.axis_index("ctx") % CORES
    heads = HEADS // chips
    head_cols = heads * HEAD_DIM
    units = ff_width // chips
    group_rows = chips * tok_rows
    chip_grp, core_grp = chip_groups(chips), core_groups(chips)

    def gather_chips(own):
        return lax.all_gather(own, "ctx", axis=0, tiled=True, axis_index_groups=chip_grp)

    def sum_chips(partial):
        return lax.psum_scatter(
            partial.astype(jnp.bfloat16), "ctx", scatter_dimension=0, tiled=True,
            axis_index_groups=chip_grp,
        ).astype(jnp.float32)

    def to_tokens(by_heads):
        moved = lax.all_to_all(
            by_heads.reshape(chips, tok_rows, head_cols), "ctx", split_axis=0, concat_axis=0,
            tiled=True, axis_index_groups=chip_grp,
        )
        return moved.transpose(1, 0, 2).reshape(tok_rows, model_width)

    def to_heads(by_tokens):
        moved = lax.all_to_all(
            by_tokens.reshape(tok_rows, chips, head_cols).transpose(1, 0, 2), "ctx",
            split_axis=0, concat_axis=0, tiled=True, axis_index_groups=chip_grp,
        )
        return moved.reshape(group_rows, head_cols)

    attn_low = attn_weights.astype(jnp.bfloat16)
    w_qkv = spread_weights(attn_low[:, : 3 * model_width], 3, n_seq, chips)
    w_mlp = spread_weights(mlp_weights.astype(jnp.bfloat16), 3, n_seq, chips)
    w_out = lax.all_gather(attn_low[:, 3 * model_width :], ALL, axis=0, tiled=True)
    states_all = gather_chips(states)

    qk_gain = lax.dynamic_slice_in_dim(feature_gains[:, 0], chip * head_cols, head_cols)
    qk_gain = qk_gain.reshape(heads, HEAD_DIM)
    projected = jnp.dot(states_all, w_qkv, preferred_element_type=jnp.float32)
    head_shape = (group_rows, heads, HEAD_DIM)
    query_unit, query_factor = unit_rows(projected[:, :head_cols].reshape(head_shape))
    key_unit, key_factor = unit_rows(projected[:, head_cols : 2 * head_cols].reshape(head_shape))
    query_low = (query_unit * qk_gain).astype(jnp.bfloat16)
    key_low = (key_unit * qk_gain).astype(jnp.bfloat16)
    value_low = projected[:, 2 * head_cols :].astype(jnp.bfloat16).reshape(head_shape)
    both = lax.all_gather(
        jnp.stack([key_low, value_low]), "ctx", axis=1, tiled=True, axis_index_groups=core_grp
    )
    key_all, value_all = both[0], both[1]
    places = block_place[0].reshape(chips, CORES)
    offsets = jnp.arange(tok_rows, dtype=jnp.int32)
    own_places = jnp.sum(
        jnp.where(jnp.arange(CORES, dtype=jnp.int32)[None, :] == core, places, 0), axis=1
    )
    query_pos = (own_places[:, None] * tok_rows + offsets).reshape(group_rows)
    key_pos = (places.T[:, :, None] * tok_rows + offsets).reshape(CORES * group_rows)
    allowed = (key_pos[None, :] <= query_pos[:, None])[None]
    scores = score_scale * jnp.einsum(
        "qhd,khd->hqk", query_low, key_all, preferred_element_type=jnp.float32
    )
    masked = jnp.where(allowed, scores, NEG_LARGE)
    row_max = jnp.max(masked, axis=-1, keepdims=True)
    powered = jnp.where(allowed, jnp.exp(masked - row_max), 0.0)
    row_sum = jnp.sum(powered, axis=-1, keepdims=True)
    probabilities = powered / row_sum
    weights_low = probabilities.astype(jnp.bfloat16)
    attended = jnp.einsum("hqk,khd->qhd", weights_low, value_all, preferred_element_type=jnp.float32)
    attended_own = to_tokens(attended.reshape(group_rows, head_cols).astype(jnp.bfloat16))

    states_full = states.astype(jnp.float32)
    branch_attn = jnp.dot(attended_own, w_out, preferred_element_type=jnp.float32)
    attn_unit, attn_factor = unit_rows(branch_attn)
    alpha_attn = feature_gains[:, 1]
    mixed_one, mix_factor = unit_rows(states_full + alpha_attn * (attn_unit - states_full))

    gain_u = lax.dynamic_slice_in_dim(unit_gains[:, 0], chip * units, units)
    gain_v = lax.dynamic_slice_in_dim(unit_gains[:, 1], chip * units, units) * math.sqrt(D)
    mixed_all = gather_chips(mixed_one.astype(jnp.bfloat16))
    up_gate = jnp.dot(mixed_all, w_mlp[:, : 2 * units], preferred_element_type=jnp.float32)
    up_scaled = up_gate[:, :units] * gain_u
    gate_scaled = up_gate[:, units:] * gain_v
    sigmoid_gate = jax.nn.sigmoid(gate_scaled)
    activated = gate_scaled * sigmoid_gate
    hidden = (activated * up_scaled).astype(jnp.bfloat16)
    branch_mlp = sum_chips(contract_cols(hidden, w_mlp[:, 2 * units :]))
    mlp_unit, mlp_factor = unit_rows(branch_mlp)
    alpha_mlp = feature_gains[:, 2]
    out_full, out_factor = unit_rows(mixed_one + alpha_mlp * (mlp_unit - mixed_one))
    grad_mix_two = unit_back(out_full, out_factor, cotangent.astype(jnp.float32))
    grad_alpha_m = jnp.sum(grad_mix_two * (mlp_unit - mixed_one), axis=0)
    grad_branch_mlp = unit_back(mlp_unit, mlp_factor, grad_mix_two * alpha_mlp).astype(jnp.bfloat16)
    grad_branch_all = gather_chips(grad_branch_mlp)
    grad_hidden = jnp.dot(
        grad_branch_all, w_mlp[:, 2 * units :], preferred_element_type=jnp.float32
    )
    grad_up_scaled = grad_hidden * activated
    grad_gate_scaled = (
        grad_hidden * up_scaled * sigmoid_gate * (1.0 + gate_scaled * (1.0 - sigmoid_gate))
    )
    grad_s_u = jnp.sum(grad_up_scaled * up_gate[:, :units], axis=0)
    grad_s_v = jnp.sum(grad_gate_scaled * up_gate[:, units:], axis=0) * math.sqrt(D)
    grad_up_gate = jnp.concatenate(
        [grad_up_scaled * gain_u, grad_gate_scaled * gain_v], axis=1
    ).astype(jnp.bfloat16)
    grad_mixed_one = grad_mix_two * (1.0 - alpha_mlp) + sum_chips(
        contract_cols(grad_up_gate, w_mlp[:, : 2 * units])
    )
    grad_mlp = collect_grads(
        jnp.concatenate(
            [contract_rows(mixed_all, grad_up_gate), contract_rows(grad_branch_all, hidden)], axis=1
        ),
        3, n_seq, chips,
    )
    grad_mix_one = unit_back(mixed_one, mix_factor, grad_mixed_one)
    grad_alpha_a = jnp.sum(grad_mix_one * (attn_unit - states_full), axis=0)
    grad_branch_attn = unit_back(attn_unit, attn_factor, grad_mix_one * alpha_attn).astype(
        jnp.bfloat16
    )
    grad_out_proj = lax.psum_scatter(
        contract_rows(attended_own, grad_branch_attn).astype(jnp.bfloat16), ALL,
        scatter_dimension=0, tiled=True,
    ).astype(jnp.float32)
    grad_attended = to_heads(
        contract_cols(grad_branch_attn, w_out).astype(jnp.bfloat16)
    ).reshape(head_shape)
    row_dots = jnp.einsum("qhd,qhd->hq", grad_attended.astype(jnp.float32), attended)
    grad_prob = jnp.einsum(
        "qhd,khd->hqk", grad_attended, value_all, preferred_element_type=jnp.float32
    )
    grad_scores = (probabilities * (grad_prob - row_dots[..., None])).astype(jnp.bfloat16)
    grad_query_low = score_scale * jnp.einsum(
        "hqk,khd->qhd", grad_scores, key_all, preferred_element_type=jnp.float32
    )
    key_terms = score_scale * jnp.einsum(
        "hqk,qhd->khd", grad_scores, query_low, preferred_element_type=jnp.float32
    )
    value_terms = jnp.einsum(
        "hqk,qhd->khd", weights_low, grad_attended, preferred_element_type=jnp.float32
    )
    summed = lax.psum_scatter(
        jnp.stack([key_terms, value_terms]).astype(jnp.bfloat16), "ctx", scatter_dimension=1,
        tiled=True, axis_index_groups=core_grp,
    ).astype(jnp.float32)
    grad_key_low, grad_value = summed[0], summed[1]
    grad_s_qk = jnp.sum(grad_query_low * query_unit + grad_key_low * key_unit, axis=0)
    grad_query_raw = unit_back(query_unit, query_factor, grad_query_low * qk_gain)
    grad_key_raw = unit_back(key_unit, key_factor, grad_key_low * qk_gain)
    grad_projected = jnp.concatenate(
        [part.reshape(group_rows, head_cols) for part in (grad_query_raw, grad_key_raw, grad_value)],
        axis=1,
    ).astype(jnp.bfloat16)
    grad_states = grad_mix_one * (1.0 - alpha_attn) + sum_chips(
        contract_cols(grad_projected, w_qkv)
    )
    grad_qkv = collect_grads(contract_rows(states_all, grad_projected), 3, n_seq, chips)
    slot = lambda own, width: lax.dynamic_update_slice_in_dim(
        jnp.zeros((chips * width,), jnp.float32), own.reshape(width), chip * width, 0
    )
    small = jnp.concatenate(
        [slot(grad_s_qk, head_cols), grad_alpha_a, grad_alpha_m, slot(grad_s_u, units), slot(grad_s_v, units)]
    )
    small = lax.psum(small, ALL)
    rank = lax.axis_index(ALL)
    feature = small[: 3 * model_width].reshape(3, model_width).T
    unit = small[3 * model_width :].reshape(2, ff_width).T
    devices = n_seq * n_ctx
    grad_feature = lax.dynamic_slice_in_dim(feature, rank * (model_width // devices), model_width // devices)
    grad_unit = lax.dynamic_slice_in_dim(unit, rank * (ff_width // devices), ff_width // devices)
    return (
        out_full.astype(jnp.bfloat16),
        grad_states.astype(jnp.bfloat16),
        jnp.concatenate([grad_qkv, grad_out_proj], axis=1),
        grad_mlp,
        grad_feature,
        grad_unit,
    )


def solution(mesh):
    in_specs = (
        P(("seq", "ctx"), None),
        P(("seq", "ctx"), None),
        P(("seq", "ctx"), None),
        P(("seq", "ctx"), None),
        P(),
        P(),
        P("seq", None),
    )
    out_specs = (
        P(("seq", "ctx"), None),
        P(("seq", "ctx"), None),
        P(("seq", "ctx"), None),
        P(("seq", "ctx"), None),
        P(("seq", "ctx"), None),
        P(("seq", "ctx"), None),
    )
    chips = mesh.shape["ctx"] // CORES
    shards = shards_split if fits(mesh.shape["seq"], chips) else shards_general
    return jax.shard_map(shards, mesh=mesh, in_specs=in_specs, out_specs=out_specs, check_vma=False)
```

```python
import functools
import math

import jax
import jax.numpy as jnp
from jax import lax
from jax.experimental import pallas as pl
from jax.experimental.pallas import tpu as pltpu
from jax.sharding import PartitionSpec as P

D = 1280
HEADS = 20
HEAD_DIM = 64


EPSILON = 1e-06
NEG_LARGE = -1e30


def unit_rows(values_in):
    factor = lax.rsqrt(jnp.sum(values_in * values_in, axis=-1, keepdims=True) + EPSILON)
    return (values_in * factor, factor)


def unit_back(normed, factor, upstream):
    return factor * (upstream - normed * jnp.sum(upstream * normed, axis=-1, keepdims=True))


def contract_rows(left_mat, right_mat):
    return lax.dot_general(
        left_mat, right_mat, (((0,), (0,)), ((), ())), preferred_element_type=jnp.float32
    )


def contract_cols(left_mat, right_mat):
    return lax.dot_general(
        left_mat, right_mat, (((1,), (1,)), ((), ())), preferred_element_type=jnp.float32
    )


def shards_general(states, cotangent, attn_weights, mlp_weights, feature_gains, unit_gains, block_place):
    tok_rows = states.shape[0]
    model_width = states.shape[1]
    ff_width = unit_gains.shape[0]
    score_scale = math.sqrt(HEAD_DIM)
    gate_factor = unit_gains[:, 1] * math.sqrt(D)
    w_attn = lax.all_gather(attn_weights.astype(jnp.bfloat16), ("seq", "ctx"), axis=0, tiled=True)
    w_mlp = lax.all_gather(mlp_weights.astype(jnp.bfloat16), ("seq", "ctx"), axis=0, tiled=True)
    states_full = states.astype(jnp.float32)
    projected = jnp.dot(states, w_attn[:, : 3 * model_width], preferred_element_type=jnp.float32)
    head_shape = (tok_rows, HEADS, HEAD_DIM)
    qk_gain = feature_gains[:, 0].reshape(HEADS, HEAD_DIM)
    query_unit, query_factor = unit_rows(projected[:, :model_width].reshape(head_shape))
    key_unit, key_factor = unit_rows(
        projected[:, model_width : 2 * model_width].reshape(head_shape)
    )
    query_low = (query_unit * qk_gain).astype(jnp.bfloat16)
    key_low = (key_unit * qk_gain).astype(jnp.bfloat16).reshape(tok_rows, model_width)
    value_low = projected[:, 2 * model_width :].astype(jnp.bfloat16)
    keys_all, values_all = (
        lax.all_gather(key_low, "ctx", axis=0, tiled=True),
        lax.all_gather(value_low, "ctx", axis=0, tiled=True),
    )
    seq_len = keys_all.shape[0]
    ctx_lanes = jnp.arange(lax.axis_size("ctx"), dtype=jnp.int32)
    places = block_place[0]
    own_block = jnp.sum(jnp.where(ctx_lanes == lax.axis_index("ctx"), places, 0))
    query_pos = own_block * tok_rows + jnp.arange(tok_rows, dtype=jnp.int32)
    key_index = jnp.arange(seq_len, dtype=jnp.int32)
    key_owner = key_index // tok_rows
    key_pos = (
        jnp.sum(jnp.where(key_owner[:, None] == ctx_lanes[None, :], places[None, :], 0), axis=1)
        * tok_rows
        + key_index % tok_rows
    )
    kblock = min(512, seq_len)
    nblocks = seq_len // kblock
    key_blocks = keys_all.reshape(nblocks, kblock, HEADS, HEAD_DIM)
    value_blocks = values_all.reshape(nblocks, kblock, HEADS, HEAD_DIM)
    pos_blocks = key_pos.reshape(nblocks, kblock)

    def block_scores(key_rows, key_places):
        raw_scores = score_scale * jnp.einsum(
            "qhd,khd->hqk", query_low, key_rows, preferred_element_type=jnp.float32
        )
        allowed = key_places[None, None, :] <= query_pos[None, :, None]
        return (raw_scores, allowed)

    def max_step(running, inputs):
        running_max, running_sum = running
        key_rows, key_places = inputs
        raw_scores, allowed = block_scores(key_rows, key_places)
        masked = jnp.where(allowed, raw_scores, NEG_LARGE)
        new_max = jnp.maximum(running_max, jnp.max(masked, axis=-1))
        powered = jnp.where(allowed, jnp.exp(masked - new_max[..., None]), 0.0)
        running_sum = running_sum * jnp.exp(running_max - new_max) + jnp.sum(powered, axis=-1)
        return ((new_max, running_sum), None)

    start_max = jnp.full((HEADS, tok_rows), NEG_LARGE, jnp.float32)
    start_sum = jnp.zeros((HEADS, tok_rows), jnp.float32)
    (final_max, final_sum), _ = lax.scan(max_step, (start_max, start_sum), (key_blocks, pos_blocks))
    log_total = final_max + jnp.log(final_sum)

    def value_step(accumulated, inputs):
        key_rows, value_rows, key_places = inputs
        raw_scores, allowed = block_scores(key_rows, key_places)
        weights_low = jnp.where(allowed, jnp.exp(raw_scores - log_total[..., None]), 0.0).astype(
            jnp.bfloat16
        )
        accumulated = accumulated + jnp.einsum(
            "hqk,khd->qhd", weights_low, value_rows, preferred_element_type=jnp.float32
        )
        return (accumulated, None)

    attended, _ = lax.scan(
        value_step, jnp.zeros(head_shape, jnp.float32), (key_blocks, value_blocks, pos_blocks)
    )
    attended_low = attended.reshape(tok_rows, model_width).astype(jnp.bfloat16)
    branch_attn = jnp.dot(
        attended_low, w_attn[:, 3 * model_width :], preferred_element_type=jnp.float32
    )
    attn_unit, attn_factor = unit_rows(branch_attn)
    alpha_attn = feature_gains[:, 1]
    mixed_one, mix_factor = unit_rows(states_full + alpha_attn * (attn_unit - states_full))
    mixed_low = mixed_one.astype(jnp.bfloat16)
    up_gate = jnp.dot(mixed_low, w_mlp[:, : 2 * ff_width], preferred_element_type=jnp.float32)
    up_scaled = up_gate[:, :ff_width] * unit_gains[:, 0]
    gate_scaled = up_gate[:, ff_width:] * gate_factor
    sigmoid_gate = jax.nn.sigmoid(gate_scaled)
    activated = gate_scaled * sigmoid_gate
    hidden = (activated * up_scaled).astype(jnp.bfloat16)
    branch_mlp = contract_cols(hidden, w_mlp[:, 2 * ff_width :])
    mlp_unit, mlp_factor = unit_rows(branch_mlp)
    alpha_mlp = feature_gains[:, 2]
    out_full, out_factor = unit_rows(mixed_one + alpha_mlp * (mlp_unit - mixed_one))
    grad_mix_two = unit_back(out_full, out_factor, cotangent.astype(jnp.float32))
    grad_alpha_m = jnp.sum(grad_mix_two * (mlp_unit - mixed_one), axis=0)
    grad_branch_mlp = unit_back(mlp_unit, mlp_factor, grad_mix_two * alpha_mlp).astype(jnp.bfloat16)
    grad_hidden = jnp.dot(
        grad_branch_mlp, w_mlp[:, 2 * ff_width :], preferred_element_type=jnp.float32
    )
    grad_up_scaled = grad_hidden * activated
    grad_gate_scaled = (
        grad_hidden * up_scaled * sigmoid_gate * (1.0 + gate_scaled * (1.0 - sigmoid_gate))
    )
    grad_s_u = jnp.sum(grad_up_scaled * up_gate[:, :ff_width], axis=0)
    grad_s_v = jnp.sum(grad_gate_scaled * up_gate[:, ff_width:], axis=0) * math.sqrt(D)
    grad_up_gate = jnp.concatenate(
        [grad_up_scaled * unit_gains[:, 0], grad_gate_scaled * gate_factor], axis=1
    ).astype(jnp.bfloat16)
    grad_mixed_one = grad_mix_two * (1.0 - alpha_mlp) + contract_cols(
        grad_up_gate, w_mlp[:, : 2 * ff_width]
    )
    grad_mix_one = unit_back(mixed_one, mix_factor, grad_mixed_one)
    grad_alpha_a = jnp.sum(grad_mix_one * (attn_unit - states_full), axis=0)
    grad_branch_attn = unit_back(attn_unit, attn_factor, grad_mix_one * alpha_attn).astype(
        jnp.bfloat16
    )
    grad_attended = (
        contract_cols(grad_branch_attn, w_attn[:, 3 * model_width :])
        .astype(jnp.bfloat16)
        .reshape(head_shape)
    )
    row_dots = jnp.einsum("qhd,qhd->hq", grad_attended.astype(jnp.float32), attended)

    def grad_step(grad_query, inputs):
        key_rows, value_rows, key_places = inputs
        raw_scores, allowed = block_scores(key_rows, key_places)
        probabilities = jnp.where(allowed, jnp.exp(raw_scores - log_total[..., None]), 0.0)
        grad_prob = jnp.einsum(
            "qhd,khd->hqk", grad_attended, value_rows, preferred_element_type=jnp.float32
        )
        grad_scores = (probabilities * (grad_prob - row_dots[..., None])).astype(jnp.bfloat16)
        grad_query = grad_query + score_scale * jnp.einsum(
            "hqk,khd->qhd", grad_scores, key_rows, preferred_element_type=jnp.float32
        )
        key_terms = score_scale * jnp.einsum(
            "hqk,qhd->khd", grad_scores, query_low, preferred_element_type=jnp.float32
        )
        value_terms = jnp.einsum(
            "hqk,qhd->khd",
            probabilities.astype(jnp.bfloat16),
            grad_attended,
            preferred_element_type=jnp.float32,
        )
        return (grad_query, (key_terms, value_terms))

    grad_query_low, (key_terms, value_terms) = lax.scan(
        grad_step, jnp.zeros(head_shape, jnp.float32), (key_blocks, value_blocks, pos_blocks)
    )
    key_terms = key_terms.reshape(seq_len, model_width)
    value_terms = value_terms.reshape(seq_len, model_width)
    own_key_grad, own_value_grad = (
        lax.psum_scatter(
            key_terms.astype(jnp.bfloat16), "ctx", scatter_dimension=0, tiled=True
        ).astype(jnp.float32),
        lax.psum_scatter(
            value_terms.astype(jnp.bfloat16), "ctx", scatter_dimension=0, tiled=True
        ).astype(jnp.float32),
    )
    grad_key_low = own_key_grad.reshape(head_shape)
    grad_s_qk = jnp.sum(grad_query_low * query_unit + grad_key_low * key_unit, axis=0).reshape(
        model_width
    )
    grad_query_raw = unit_back(query_unit, query_factor, grad_query_low * qk_gain).reshape(
        tok_rows, model_width
    )
    grad_key_raw = unit_back(key_unit, key_factor, grad_key_low * qk_gain).reshape(
        tok_rows, model_width
    )
    grad_projected = jnp.concatenate([grad_query_raw, grad_key_raw, own_value_grad], axis=1).astype(
        jnp.bfloat16
    )
    grad_states = grad_mix_one * (1.0 - alpha_attn) + contract_cols(
        grad_projected, w_attn[:, : 3 * model_width]
    )
    feature_total = jnp.stack([grad_s_qk, grad_alpha_a, grad_alpha_m], axis=1)
    unit_fold = jnp.stack([grad_s_u, grad_s_v], axis=1).reshape(
        model_width, 2 * ff_width // model_width
    )
    attn_cols = 4 * model_width
    mlp_cols = 3 * ff_width
    attn_share = lax.psum_scatter(
        jnp.concatenate(
            [
                contract_rows(states, grad_projected),
                contract_rows(attended_low, grad_branch_attn),
                feature_total,
            ],
            axis=1,
        ),
        ("seq", "ctx"),
        scatter_dimension=0,
        tiled=True,
    )
    mlp_share = lax.psum_scatter(
        jnp.concatenate(
            [
                contract_rows(mixed_low, grad_up_gate),
                contract_rows(grad_branch_mlp, hidden),
                unit_fold,
            ],
            axis=1,
        ),
        ("seq", "ctx"),
        scatter_dimension=0,
        tiled=True,
    )
    grad_attn = attn_share[:, :attn_cols]
    grad_feature = attn_share[:, attn_cols:]
    grad_mlp = mlp_share[:, :mlp_cols]
    grad_unit = mlp_share[:, mlp_cols:].reshape(
        unit_gains.shape[0] // lax.axis_size(("seq", "ctx")), 2
    )
    return (
        out_full.astype(jnp.bfloat16),
        grad_states.astype(jnp.bfloat16),
        grad_attn,
        grad_mlp,
        grad_feature,
        grad_unit,
    )


CORES = 2
ALL = ("seq", "ctx")


def fits(n_seq, chips):
    return n_seq == 4 and chips == 4 and HEADS % chips == 0


def chip_groups(chips):
    return [[CORES * chip + core for chip in range(chips)] for core in range(CORES)]


def core_groups(chips):
    return [[CORES * chip + core for core in range(CORES)] for chip in range(chips)]


def copy_groups(n_seq, chips):
    return [
        [(seq * chips + chip) * CORES + core for seq in range(n_seq) for core in range(CORES)]
        for chip in range(chips)
    ]


def spread_weights(weights_low, parts, n_seq, chips):
    rows, columns = weights_low.shape
    share = columns // parts // chips
    by_chip = weights_low.reshape(rows, parts, chips, share).transpose(2, 0, 1, 3)
    by_chip = by_chip.reshape(chips, rows, parts * share)
    mine = lax.all_to_all(
        by_chip, "ctx", split_axis=0, concat_axis=0, tiled=True,
        axis_index_groups=chip_groups(chips),
    )
    full = lax.all_gather(mine, ALL, axis=0, axis_index_groups=copy_groups(n_seq, chips))
    full = full.reshape(n_seq, CORES, chips, rows, parts * share).transpose(0, 2, 1, 3, 4)
    return full.reshape(n_seq * CORES * chips * rows, parts * share)


def collect_grads(partial, parts, n_seq, chips):
    rows = partial.shape[0] // (n_seq * CORES * chips)
    share = partial.shape[1] // parts
    by_owner = partial.astype(jnp.bfloat16).reshape(n_seq, chips, CORES, rows, parts * share)
    by_owner = by_owner.transpose(0, 2, 1, 3, 4).reshape(n_seq * CORES * chips * rows, parts * share)
    mine = lax.psum_scatter(
        by_owner, ALL, scatter_dimension=0, tiled=True,
        axis_index_groups=copy_groups(n_seq, chips),
    ).reshape(chips, rows, parts * share)
    back = lax.all_to_all(
        mine, "ctx", split_axis=0, concat_axis=0, tiled=True,
        axis_index_groups=chip_groups(chips),
    )
    back = back.reshape(chips, rows, parts, share).transpose(1, 2, 0, 3)
    return back.reshape(rows, parts * chips * share).astype(jnp.float32)


MESH = pl.DeviceIdType.MESH
VMEM = pltpu.VMEM
CHIPS = 4
STEPS = (1, 2, 3)
LIMIT = 60 * 1024 * 1024


def place_of():
    seq = lax.axis_index("seq")
    ctx = lax.axis_index("ctx")
    return seq, ctx // CORES, ctx % CORES


def chip_peer(step):
    seq, chip, core = place_of()
    other = lax.rem(chip + step, CHIPS)
    return (seq, other * CORES + core), other


def seq_peer(step):
    seq, chip, core = place_of()
    other = seq ^ step
    return (other, chip * CORES + core), other


def twin():
    seq, chip, core = place_of()
    return (seq, chip * CORES + 1 - core)


def meet():
    devices = [chip_peer(step)[0] for step in STEPS] + [seq_peer(step)[0] for step in STEPS] + [twin()]
    gate = pltpu.get_barrier_semaphore()
    for device in devices:
        pl.semaphore_signal(gate, inc=1, device_id=device, device_id_type=MESH)
    pl.semaphore_wait(gate, len(devices))


def remote(src, dst, send, recv, device):
    return pltpu.make_async_remote_copy(
        src_ref=src, dst_ref=dst, send_sem=send, recv_sem=recv, device_id=device,
        device_id_type=MESH,
    )


def begin(copy):
    copy.start()
    return copy


def rows_at(index, count):
    return pl.ds(pl.multiple_of(index * count, count), count)


def gather_line(src, dst_of, send, recv):
    return [
        begin(remote(src, dst_of, send.at[step], recv.at[step], chip_peer(step)[0])) for step in STEPS
    ]


def dot(left, right):
    return jnp.dot(left, right, preferred_element_type=jnp.float32)


def dot_nt(left, right):
    return lax.dot_general(
        left, right, (((1,), (1,)), ((), ())), preferred_element_type=jnp.float32
    )


def dot_tn(left, right):
    return lax.dot_general(
        left, right, (((0,), (0,)), ((), ())), preferred_element_type=jnp.float32
    )


def dma(*shape):
    return pltpu.SemaphoreType.DMA(shape)


def in_vmem():
    return pl.BlockSpec(memory_space=pltpu.VMEM)


def in_hbm():
    return pl.BlockSpec(memory_space=pl.ANY)


def attend_kernel(
    states, qkv_src, mlp_src, qk_gain, query_pos, key_pos,
    states_all, w_qkv, w_part, raw_out, query_out, both, att_out, inv_out, attx,
    stage_q, low_q, stage_m, low_m, raw, att_low,
    local_sem, x_send, x_recv, q_send, q_recv, mt_send, mt_recv, wz_send, wz_recv,
    ws_send, ws_recv, wt_send, wt_recv, m_send, m_recv, kv_send, kv_recv, a_send, a_recv,
):
    seq, chip, core = place_of()
    rows = qkv_src.shape[2]
    half_cols = qkv_src.shape[3]
    part_cols = half_cols // 3
    tok_rows = states.shape[0]
    heads = qk_gain.shape[0]
    head_cols = heads * HEAD_DIM
    group_rows = tok_rows * CHIPS
    chip_rows = CORES * rows
    seq_rows = CHIPS * chip_rows
    half_units = w_part.shape[2]
    ff_width = mlp_src.shape[1] // 3
    meet()
    block = rows_at(chip, tok_rows)
    mine = rows_at(core, rows)
    swaps = [
        begin(remote(qkv_src.at[at, 1 - core], stage_q.at[at, mine], q_send.at[at], q_recv.at[at], twin()))
        for at in range(CHIPS)
    ]
    keeps = [
        begin(pltpu.make_async_copy(qkv_src.at[at, core], stage_q.at[at, mine], local_sem.at[at]))
        for at in range(CHIPS)
    ]
    states_all[block, :] = states[...]
    m_swaps, m_keeps = [], []
    for part in range(3):
        for at in range(CHIPS):
            start = part * ff_width + at * CORES * half_units
            theirs = pl.ds(pl.multiple_of(start + (1 - core) * half_units, 128), half_units)
            ours = pl.ds(pl.multiple_of(start + core * half_units, 128), half_units)
            there = stage_m.at[part, at, mine]
            m_swaps.append(begin(remote(mlp_src.at[:, theirs], there, mt_send.at[part, at], mt_recv.at[part, at], twin())))
            m_keeps.append(begin(pltpu.make_async_copy(mlp_src.at[:, ours], there, local_sem.at[CHIPS + part * CHIPS + at])))
    for copy in keeps:
        copy.wait()
    for copy in swaps:
        copy.wait()
    low_q[...] = stage_q[...].astype(jnp.bfloat16)
    my_rows = rows_at(seq * CHIPS + chip, chip_rows)
    line = []
    for step in STEPS:
        device, other = chip_peer(step)
        line.append(begin(remote(low_q.at[other], w_qkv.at[core, my_rows], wz_send.at[step], wz_recv.at[step], device)))
    w_qkv[core, my_rows, :] = low_q[chip]
    for copy in m_keeps:
        copy.wait()
    for copy in m_swaps:
        copy.wait()
    low_m[...] = stage_m[...].astype(jnp.bfloat16)
    for copy in line:
        copy.wait_recv()
    sends = gather_line(states, states_all.at[block], x_send, x_recv)
    seq_part = w_qkv.at[core, rows_at(seq, seq_rows)]
    across = [
        begin(remote(seq_part, seq_part, ws_send.at[step], ws_recv.at[step], seq_peer(step)[0]))
        for step in STEPS
    ]
    for copy in across:
        copy.wait_recv()
    swap = begin(remote(w_qkv.at[core], w_qkv.at[core], wt_send.at[0], wt_recv.at[0], twin()))
    swap.wait()
    for copy in sends:
        copy.wait_recv()
    m_line = []
    for part in range(3):
        for step in STEPS:
            device, other = chip_peer(step)
            there = w_part.at[part, rows_at(chip, chip_rows)]
            m_line.append(begin(remote(low_m.at[part, other], there, m_send.at[part, step], m_recv.at[part, step], device)))
        w_part[part, rows_at(chip, chip_rows), :] = low_m[part, chip]

    for half in range(CORES):
        value = dot(states_all[...], w_qkv[half])
        for which in range(3):
            start = which * head_cols + half * part_cols
            raw[:, start : start + part_cols] = value[:, which * part_cols : (which + 1) * part_cols]
    for head in range(heads):
        gain = qk_gain[head]
        for which in range(2):
            start = which * head_cols + head * HEAD_DIM
            value = raw[:, start : start + HEAD_DIM]
            factor = lax.rsqrt(jnp.sum(value * value, axis=-1, keepdims=True) + EPSILON)
            low = (value * factor * gain).astype(jnp.bfloat16)
            raw_out[which, head] = value
            if which == 0:
                query_out[head] = low * math.sqrt(HEAD_DIM)
            else:
                both[core, 0, head] = low
        start = 2 * head_cols + head * HEAD_DIM
        both[core, 1, head] = raw[:, start : start + HEAD_DIM].astype(jnp.bfloat16)
    swap = begin(remote(both.at[core], both.at[core], kv_send.at[0], kv_recv.at[0], twin()))
    swap.wait()

    tile = min(128, group_rows)
    tiles = group_rows // tile

    def one_tile(index, carry):
        head = index // tiles
        at = rows_at(lax.rem(index, tiles), tile)
        query = query_out[head, at, :]
        allowed = key_pos[...] <= query_pos[at, :]
        scores = jnp.concatenate([dot_nt(query, both[half, 0, head]) for half in range(CORES)], axis=1)
        powered = jnp.exp(jnp.where(allowed, scores, NEG_LARGE))
        inverse = 1.0 / jnp.sum(powered, axis=-1, keepdims=True)
        weights = (powered * inverse).astype(jnp.bfloat16)
        att_out[head, at, :] = sum(
            dot(weights[:, half * group_rows : (half + 1) * group_rows], both[half, 1, head])
            for half in range(CORES)
        )
        inv_out[head, at, :] = inverse
        return carry

    lax.fori_loop(0, heads * tiles, one_tile, 0)
    for head in range(heads):
        att_low[:, head * HEAD_DIM : (head + 1) * HEAD_DIM] = att_out[head].astype(jnp.bfloat16)
    out = []
    for step in STEPS:
        device, other = chip_peer(step)
        out.append(begin(remote(att_low.at[rows_at(other, tok_rows)], attx.at[chip], a_send.at[step], a_recv.at[step], device)))
    attx[chip] = att_low[block, :]
    for copy in out + m_line:
        copy.wait()
    for copy in sends + line + across:
        copy.wait_send()


def attend_call(states, qkv_src, mlp_src, qk_gain, query_pos, key_pos):
    tok_rows, model_width = states.shape
    chips, _, rows, half_cols = qkv_src.shape
    heads = qk_gain.shape[0]
    group_rows = chips * tok_rows
    half_units = mlp_src.shape[1] // 3 // chips // CORES
    f32, low = jnp.float32, jnp.bfloat16
    shape = jax.ShapeDtypeStruct
    return pl.pallas_call(
        attend_kernel,
        out_shape=[
            shape((group_rows, model_width), low),
            shape((CORES, model_width, half_cols), low),
            shape((3, chips * CORES * rows, half_units), low),
            shape((2, heads, group_rows, HEAD_DIM), f32),
            shape((heads, group_rows, HEAD_DIM), low),
            shape((CORES, 2, heads, group_rows, HEAD_DIM), low),
            shape((heads, group_rows, HEAD_DIM), f32),
            shape((heads, group_rows, 1), f32),
            shape((chips, tok_rows, heads * HEAD_DIM), low),
        ],
        in_specs=[in_vmem(), in_hbm(), in_hbm(), in_vmem(), in_vmem(), in_vmem()],
        out_specs=[in_vmem()] * 9,
        scratch_shapes=[
            VMEM((chips, CORES * rows, half_cols), f32),
            VMEM((chips, CORES * rows, half_cols), low),
            VMEM((3, chips, CORES * rows, half_units), f32),
            VMEM((3, chips, CORES * rows, half_units), low),
            VMEM((group_rows, 3 * heads * HEAD_DIM), f32),
            VMEM((group_rows, heads * HEAD_DIM), low),
            dma(16), dma(4), dma(4), dma(4), dma(4), dma(3, 4), dma(3, 4), dma(4), dma(4),
            dma(4), dma(4), dma(1), dma(1), dma(3, 4), dma(3, 4), dma(1), dma(1), dma(4), dma(4),
        ],
        compiler_params=pltpu.CompilerParams(
            collective_id=1, has_side_effects=True, vmem_limit_bytes=LIMIT
        ),
        name="attend",
    )(states, qkv_src, mlp_src, qk_gain, query_pos, key_pos)


def unit_of(value):
    factor = lax.rsqrt(jnp.sum(value * value, axis=-1, keepdims=True) + EPSILON)
    return value * factor, factor


def mlp_kernel(
    attx, states, cotangent, w_out, alpha_attn, alpha_mlp, gain_u, gain_v, w_part,
    out, grad_attx, grad_w_out, grad_direct, dot_a, dot_m, dot_u, dot_v, grad_half,
    weights, mixed_one, attn_unit, factors, mixed_low, mixed_all, up, gate, hidden, part,
    sums, grad_two, branch_low, branch_all, grad_u, grad_v, wide, turned, arrived,
    local_sem, ws_send, ws_recv, wt_send, wt_recv, x_send, x_recv, r_send, r_recv,
    g_send, g_recv, b_send, b_recv, d_send, d_recv,
):
    seq, chip, core = place_of()
    tok_rows, model_width = states.shape
    chip_heads = attx.shape[2]
    seq_rows = w_part.shape[1]
    half_units = w_part.shape[2]
    group_rows = CHIPS * tok_rows
    block = rows_at(chip, tok_rows)
    meet()
    seq_at = rows_at(seq, seq_rows)

    def spread(which):
        return [
            begin(remote(w_part.at[which], weights.at[which, core, seq_at], ws_send.at[which, step], ws_recv.at[which, step], seq_peer(step)[0]))
            for step in STEPS
        ]

    across = spread(0) + spread(1)
    keeps = [
        begin(pltpu.make_async_copy(w_part.at[which], weights.at[which, core, seq_at], local_sem.at[which]))
        for which in range(3)
    ]
    branch = sum(dot(attx[at], w_out[at]) for at in range(CHIPS))
    unit, factor = unit_of(branch)
    attn_unit[...] = unit
    factors[0] = factor
    base = states[...].astype(jnp.float32)
    value, factor = unit_of(base + alpha_attn[...] * (unit - base))
    mixed_one[...] = value
    factors[1] = factor
    mixed_low[...] = value.astype(jnp.bfloat16)
    line = gather_line(mixed_low, mixed_all.at[block], x_send, x_recv)
    mixed_all[block, :] = mixed_low[...]
    for copy in keeps:
        copy.wait()
    for copy in across:
        copy.wait_recv()
    swaps = [
        begin(remote(weights.at[which, core], weights.at[which, core], wt_send.at[which], wt_recv.at[which], twin()))
        for which in range(2)
    ]
    across += spread(2)
    for copy in line:
        copy.wait_recv()
    for copy in swaps:
        copy.wait_recv()
    for half in range(CORES):
        up[half] = dot(mixed_all[...], weights[0, half])
        gate[half] = dot(mixed_all[...], weights[1, half])
    slab = min(64, group_rows)
    slabs = group_rows // slab

    def activate(index, carry):
        half = index // slabs
        at = rows_at(lax.rem(index, slabs), slab)
        gated = gate[half, at, :] * gain_v[half]
        scaled = up[half, at, :] * gain_u[half]
        hidden[half, at, :] = (gated * jax.nn.sigmoid(gated) * scaled).astype(jnp.bfloat16)
        return carry

    lax.fori_loop(0, CORES * slabs, activate, 0)
    for copy in across[-3:]:
        copy.wait_recv()
    swap = begin(remote(weights.at[2, core], weights.at[2, core], wt_send.at[2], wt_recv.at[2], twin()))
    swaps.append(swap)
    swap.wait_recv()
    tile = model_width // 5

    def down(index, carry):
        at = rows_at(index, tile)
        part[0, :, at] = sum(dot_nt(hidden[half], weights[2, half, at, :]) for half in range(CORES)).astype(jnp.bfloat16)
        return carry

    lax.fori_loop(0, model_width // tile, down, 0)

    def reduce_line(which, send, recv):
        sent = []
        for step in STEPS:
            device, other = chip_peer(step)
            sent.append(begin(remote(part.at[which, rows_at(other, tok_rows)], sums.at[which, step], send.at[step], recv.at[step], device)))
        return sent

    def reduced(which):
        total = part[which, block, :].astype(jnp.float32)
        for step in STEPS:
            total = total + sums[which, step].astype(jnp.float32)
        return total

    sent = reduce_line(0, r_send, r_recv)
    for copy in sent:
        copy.wait_recv()
    mlp_unit, mlp_factor = unit_of(reduced(0))
    value, factor = unit_of(mixed_one[...] + alpha_mlp[...] * (mlp_unit - mixed_one[...]))
    out[...] = value.astype(jnp.bfloat16)
    above = cotangent[...].astype(jnp.float32)
    grad = factor * (above - value * jnp.sum(above * value, axis=-1, keepdims=True))
    grad_two[...] = grad
    dot_m[...] = jnp.sum(grad * (mlp_unit - mixed_one[...]), axis=0, keepdims=True)
    grad = grad * alpha_mlp[...]
    grad = mlp_factor * (grad - mlp_unit * jnp.sum(grad * mlp_unit, axis=-1, keepdims=True))
    branch_low[...] = grad.astype(jnp.bfloat16)
    back = gather_line(branch_low, branch_all.at[block], g_send, g_recv)
    branch_all[block, :] = branch_low[...]
    turned[0] = mixed_all[...].T
    for copy in back:
        copy.wait_recv()
    for half in range(CORES):
        wide[half] = dot(branch_all[...], weights[2, half])
    dot_u[...] = jnp.zeros_like(dot_u)
    dot_v[...] = jnp.zeros_like(dot_v)

    def deactivate(index, carry):
        half = index // slabs
        at = rows_at(lax.rem(index, slabs), slab)
        gated = gate[half, at, :] * gain_v[half]
        scaled = up[half, at, :] * gain_u[half]
        upstream = wide[half, at, :]
        sig = jax.nn.sigmoid(gated)
        to_up = upstream * (gated * sig)
        to_gate = upstream * scaled * sig * (1.0 + gated * (1.0 - sig))
        dot_u[half] += jnp.sum(to_up * up[half, at, :], axis=0, keepdims=True)
        dot_v[half] += jnp.sum(to_gate * gate[half, at, :], axis=0, keepdims=True)
        grad_u[half, at, :] = (to_up * gain_u[half]).astype(jnp.bfloat16)
        grad_v[half, at, :] = (to_gate * gain_v[half]).astype(jnp.bfloat16)
        return carry

    lax.fori_loop(0, CORES * slabs, deactivate, 0)

    def back_down(index, carry):
        at = rows_at(index, tile)
        part[1, :, at] = sum(
            dot_nt(grad_u[half], weights[0, half, at, :]) + dot_nt(grad_v[half], weights[1, half, at, :])
            for half in range(CORES)
        ).astype(jnp.bfloat16)
        return carry

    lax.fori_loop(0, model_width // tile, back_down, 0)
    for copy in swaps:
        copy.wait_send()
    sent += reduce_line(1, b_send, b_recv)
    turned[1] = branch_all[...].T
    pairs = ((0, grad_u), (1, grad_v), (2, hidden))
    swaps = []
    for which, right in pairs:
        left = 1 if which == 2 else 0

        def weight_grad(index, carry, which=which, right=right, left=left):
            half = index // 5
            at = rows_at(lax.rem(index, 5), tile)
            weights[which, half, at, :] = dot(turned[left, at, :], right[half]).astype(jnp.bfloat16)
            return carry

        lax.fori_loop(0, CORES * 5, weight_grad, 0)
        swaps.append(begin(remote(weights.at[which, 1 - core], arrived.at[which], d_send.at[which], d_recv.at[which], twin())))
    for copy in sent[3:]:
        copy.wait_recv()
    grad = grad_two[...] * (1.0 - alpha_mlp[...]) + reduced(1)
    value = mixed_one[...]
    grad = factors[1] * (grad - value * jnp.sum(grad * value, axis=-1, keepdims=True))
    unit = attn_unit[...]
    dot_a[...] = jnp.sum(grad * (unit - states[...].astype(jnp.float32)), axis=0, keepdims=True)
    grad_direct[...] = grad * (1.0 - alpha_attn[...])
    grad = grad * alpha_attn[...]
    grad = factors[0] * (grad - unit * jnp.sum(grad * unit, axis=-1, keepdims=True))
    low = grad.astype(jnp.bfloat16)
    for at in range(CHIPS):
        grad_attx[at] = dot_nt(low, w_out[at]).astype(jnp.bfloat16)
        grad_w_out[at] = dot_tn(attx[at], low).astype(jnp.bfloat16)
    for which in range(3):
        swaps[which].wait_recv()
        grad_half[which] = (
            weights[which, core].astype(jnp.float32) + arrived[which].astype(jnp.float32)
        ).astype(jnp.bfloat16)
    for copy in across + line + sent + back + swaps:
        copy.wait_send()


def mlp_call(attx, states, cotangent, w_out, alpha_attn, alpha_mlp, gain_u, gain_v, w_part):
    tok_rows, model_width = states.shape
    chips, _, chip_heads = attx.shape
    half_units = w_part.shape[2]
    group_rows = chips * tok_rows
    f32, low = jnp.float32, jnp.bfloat16
    shape = jax.ShapeDtypeStruct
    tokens, group = (tok_rows, model_width), (group_rows, model_width)
    wide = (CORES, group_rows, half_units)
    matrix = (model_width, half_units)
    return pl.pallas_call(
        mlp_kernel,
        out_shape=[
            shape(tokens, low),
            shape(attx.shape, low),
            shape((chips, chip_heads, model_width), low),
            shape(tokens, f32),
            shape((1, model_width), f32),
            shape((1, model_width), f32),
            shape((CORES, 1, half_units), f32),
            shape((CORES, 1, half_units), f32),
            shape((3,) + matrix, low),
        ],
        in_specs=[in_vmem()] * 8 + [in_hbm()],
        out_specs=[in_vmem()] * 9,
        scratch_shapes=[
            VMEM((3, CORES) + matrix, low),
            VMEM(tokens, f32),
            VMEM(tokens, f32),
            VMEM((2, tok_rows, 1), f32),
            VMEM(tokens, low),
            VMEM(group, low),
            VMEM(wide, f32),
            VMEM(wide, f32),
            VMEM(wide, low),
            VMEM((2,) + group, low),
            VMEM((2, chips) + tokens, low),
            VMEM(tokens, f32),
            VMEM(tokens, low),
            VMEM(group, low),
            VMEM(wide, low),
            VMEM(wide, low),
            VMEM(wide, f32),
            VMEM((2, model_width, group_rows), low),
            VMEM((3,) + matrix, low),
            dma(3), dma(3, 4), dma(3, 4), dma(3), dma(3), dma(4), dma(4), dma(4), dma(4),
            dma(4), dma(4), dma(4), dma(4), dma(3), dma(3),
        ],
        compiler_params=pltpu.CompilerParams(
            collective_id=2, has_side_effects=True, vmem_limit_bytes=LIMIT
        ),
        name="mlp",
    )(attx, states, cotangent, w_out, alpha_attn, alpha_mlp, gain_u, gain_v, w_part)


def shards_split(states, cotangent, attn_weights, mlp_weights, feature_gains, unit_gains, block_place):
    tok_rows, model_width = states.shape
    ff_width = unit_gains.shape[0]
    n_seq, n_ctx = lax.axis_size("seq"), lax.axis_size("ctx")
    chips = n_ctx // CORES
    score_scale = math.sqrt(HEAD_DIM)
    chip = lax.axis_index("ctx") // CORES
    core = lax.axis_index("ctx") % CORES
    heads = HEADS // chips
    head_cols = heads * HEAD_DIM
    units = ff_width // chips
    group_rows = chips * tok_rows
    chip_grp, core_grp = chip_groups(chips), core_groups(chips)

    def gather_chips(own):
        return lax.all_gather(own, "ctx", axis=0, tiled=True, axis_index_groups=chip_grp)

    def sum_chips(partial):
        return lax.psum_scatter(
            partial.astype(jnp.bfloat16), "ctx", scatter_dimension=0, tiled=True,
            axis_index_groups=chip_grp,
        ).astype(jnp.float32)

    def to_tokens(by_heads):
        moved = lax.all_to_all(
            by_heads.reshape(chips, tok_rows, head_cols), "ctx", split_axis=0, concat_axis=0,
            tiled=True, axis_index_groups=chip_grp,
        )
        return moved.transpose(1, 0, 2).reshape(tok_rows, model_width)

    def to_heads(by_tokens):
        moved = lax.all_to_all(
            by_tokens.reshape(tok_rows, chips, head_cols).transpose(1, 0, 2), "ctx",
            split_axis=0, concat_axis=0, tiled=True, axis_index_groups=chip_grp,
        )
        return moved.reshape(group_rows, head_cols)

    rows = attn_weights.shape[0]
    qkv_src = attn_weights[:, : 3 * model_width].reshape(rows, 3, chips, CORES, head_cols // CORES)
    qkv_src = qkv_src.transpose(2, 3, 0, 1, 4).reshape(chips, CORES, rows, -1)
    w_out = lax.all_gather(
        attn_weights[:, 3 * model_width :].astype(jnp.bfloat16), ALL, axis=0, tiled=True
    )
    qk_gain = lax.dynamic_slice_in_dim(feature_gains[:, 0], chip * head_cols, head_cols)
    qk_gain = qk_gain.reshape(heads, HEAD_DIM)
    places = block_place[0].reshape(chips, CORES)
    offsets = jnp.arange(tok_rows, dtype=jnp.int32)
    own_places = jnp.sum(
        jnp.where(jnp.arange(CORES, dtype=jnp.int32)[None, :] == core, places, 0), axis=1
    )
    query_pos = (own_places[:, None] * tok_rows + offsets).reshape(group_rows)
    key_pos = (places.T[:, :, None] * tok_rows + offsets).reshape(CORES * group_rows)
    head_shape = (group_rows, heads, HEAD_DIM)
    states_all, w_halves, w_part, raw, query_h, both_h, att_h, inverse, attx = attend_call(
        states, qkv_src, mlp_weights, qk_gain.reshape(heads, 1, HEAD_DIM),
        query_pos.reshape(group_rows, 1), key_pos.reshape(1, CORES * group_rows),
    )
    w_qkv = w_halves.reshape(CORES, model_width, 3, head_cols // CORES).transpose(1, 2, 0, 3)
    w_qkv = w_qkv.reshape(model_width, 3 * head_cols)
    attended_own = attx.transpose(1, 0, 2).reshape(tok_rows, model_width)
    attended = att_h.transpose(1, 0, 2)
    query_low = query_h.transpose(1, 0, 2) / 8
    key_all = both_h[:, 0].transpose(0, 2, 1, 3).reshape(CORES * group_rows, heads, HEAD_DIM)
    value_all = both_h[:, 1].transpose(0, 2, 1, 3).reshape(CORES * group_rows, heads, HEAD_DIM)
    query_unit, query_factor = unit_rows(raw[0].transpose(1, 0, 2))
    key_unit, key_factor = unit_rows(raw[1].transpose(1, 0, 2))
    allowed = (key_pos[None, :] <= query_pos[:, None])[None]
    scores = score_scale * jnp.einsum(
        "qhd,khd->hqk", query_low, key_all, preferred_element_type=jnp.float32
    )
    probabilities = jnp.where(allowed, jnp.exp(scores) * inverse, 0.0)
    weights_low = probabilities.astype(jnp.bfloat16)
    w_out_parts = w_out.reshape(chips, head_cols, model_width)
    gain_u = lax.dynamic_slice_in_dim(unit_gains[:, 0], chip * units, units)
    gain_v = lax.dynamic_slice_in_dim(unit_gains[:, 1], chip * units, units) * math.sqrt(D)
    (
        out_low, grad_attx, grad_w_out, grad_direct, grad_alpha_a, grad_alpha_m, grad_s_u, grad_s_v, grad_half
    ) = mlp_call(
        attx, states, cotangent, w_out_parts, feature_gains[:, 1].reshape(1, model_width),
        feature_gains[:, 2].reshape(1, model_width), gain_u.reshape(CORES, 1, units // CORES),
        gain_v.reshape(CORES, 1, units // CORES), w_part,
    )
    grad_s_v = grad_s_v * math.sqrt(D)
    grad_out_proj = lax.psum_scatter(
        grad_w_out.reshape(model_width, model_width), ALL, scatter_dimension=0, tiled=True
    ).astype(jnp.float32)
    halves = lax.psum_scatter(
        grad_half.reshape(3, n_seq, -1, units // CORES), "seq", scatter_dimension=1, tiled=True
    )
    halves = halves.reshape(3, chips, -1, units // CORES).transpose(1, 0, 2, 3)
    moved = lax.all_to_all(
        halves, "ctx", split_axis=0, concat_axis=0, tiled=True, axis_index_groups=chip_grp
    )
    moved = lax.all_gather(moved, "ctx", axis=0, axis_index_groups=core_grp)
    moved = moved.reshape(CORES, chips, 3, CORES, rows, units // CORES)
    moved = lax.dynamic_index_in_dim(moved, core, 3, keepdims=False)
    grad_mlp = moved.transpose(3, 2, 1, 0, 4).reshape(rows, 3 * ff_width).astype(jnp.float32)
    grad_attended = lax.all_to_all(
        grad_attx, "ctx", split_axis=0, concat_axis=0, tiled=True, axis_index_groups=chip_grp
    ).reshape(head_shape)
    row_dots = jnp.einsum("qhd,qhd->hq", grad_attended.astype(jnp.float32), attended)
    grad_prob = jnp.einsum(
        "qhd,khd->hqk", grad_attended, value_all, preferred_element_type=jnp.float32
    )
    grad_scores = (probabilities * (grad_prob - row_dots[..., None])).astype(jnp.bfloat16)
    grad_query_low = score_scale * jnp.einsum(
        "hqk,khd->qhd", grad_scores, key_all, preferred_element_type=jnp.float32
    )
    key_terms = score_scale * jnp.einsum(
        "hqk,qhd->khd", grad_scores, query_low, preferred_element_type=jnp.float32
    )
    value_terms = jnp.einsum(
        "hqk,qhd->khd", weights_low, grad_attended, preferred_element_type=jnp.float32
    )
    summed = lax.psum_scatter(
        jnp.stack([key_terms, value_terms]).astype(jnp.bfloat16), "ctx", scatter_dimension=1,
        tiled=True, axis_index_groups=core_grp,
    ).astype(jnp.float32)
    grad_key_low, grad_value = summed[0], summed[1]
    grad_s_qk = jnp.sum(grad_query_low * query_unit + grad_key_low * key_unit, axis=0)
    grad_query_raw = unit_back(query_unit, query_factor, grad_query_low * qk_gain)
    grad_key_raw = unit_back(key_unit, key_factor, grad_key_low * qk_gain)
    grad_projected = jnp.concatenate(
        [part.reshape(group_rows, head_cols) for part in (grad_query_raw, grad_key_raw, grad_value)],
        axis=1,
    ).astype(jnp.bfloat16)
    grad_states = grad_direct + sum_chips(
        contract_cols(grad_projected, w_qkv)
    )
    grad_qkv = collect_grads(contract_rows(states_all, grad_projected), 3, n_seq, chips)
    slot = lambda own, width: lax.dynamic_update_slice_in_dim(
        jnp.zeros((chips * width,), jnp.float32), own.reshape(width), chip * width, 0
    )
    small = jnp.concatenate(
        [slot(grad_s_qk, head_cols), grad_alpha_a.reshape(-1), grad_alpha_m.reshape(-1), slot(grad_s_u, units), slot(grad_s_v, units)]
    )
    small = lax.psum(small, ALL)
    rank = lax.axis_index(ALL)
    feature = small[: 3 * model_width].reshape(3, model_width).T
    unit = small[3 * model_width :].reshape(2, ff_width).T
    devices = n_seq * n_ctx
    grad_feature = lax.dynamic_slice_in_dim(feature, rank * (model_width // devices), model_width // devices)
    grad_unit = lax.dynamic_slice_in_dim(unit, rank * (ff_width // devices), ff_width // devices)
    return (
        out_low,
        grad_states.astype(jnp.bfloat16),
        jnp.concatenate([grad_qkv, grad_out_proj], axis=1),
        grad_mlp,
        grad_feature,
        grad_unit,
    )


def solution(mesh):
    in_specs = (
        P(("seq", "ctx"), None),
        P(("seq", "ctx"), None),
        P(("seq", "ctx"), None),
        P(("seq", "ctx"), None),
        P(),
        P(),
        P("seq", None),
    )
    out_specs = (
        P(("seq", "ctx"), None),
        P(("seq", "ctx"), None),
        P(("seq", "ctx"), None),
        P(("seq", "ctx"), None),
        P(("seq", "ctx"), None),
        P(("seq", "ctx"), None),
    )
    chips = mesh.shape["ctx"] // CORES
    shards = shards_split if fits(mesh.shape["seq"], chips) else shards_general
    return jax.shard_map(shards, mesh=mesh, in_specs=in_specs, out_specs=out_specs, check_vma=False)
```

```python
import functools
import math

import jax
import jax.numpy as jnp
from jax import lax
from jax.experimental import pallas as pl
from jax.experimental.pallas import tpu as pltpu
from jax.sharding import PartitionSpec as P

D = 1280
HEADS = 20
HEAD_DIM = 64


EPSILON = 1e-06
NEG_LARGE = -1e30


def unit_rows(values_in):
    factor = lax.rsqrt(jnp.sum(values_in * values_in, axis=-1, keepdims=True) + EPSILON)
    return (values_in * factor, factor)


def unit_back(normed, factor, upstream):
    return factor * (upstream - normed * jnp.sum(upstream * normed, axis=-1, keepdims=True))


def contract_rows(left_mat, right_mat):
    return lax.dot_general(
        left_mat, right_mat, (((0,), (0,)), ((), ())), preferred_element_type=jnp.float32
    )


def contract_cols(left_mat, right_mat):
    return lax.dot_general(
        left_mat, right_mat, (((1,), (1,)), ((), ())), preferred_element_type=jnp.float32
    )


def shards_general(states, cotangent, attn_weights, mlp_weights, feature_gains, unit_gains, block_place):
    tok_rows = states.shape[0]
    model_width = states.shape[1]
    ff_width = unit_gains.shape[0]
    score_scale = math.sqrt(HEAD_DIM)
    gate_factor = unit_gains[:, 1] * math.sqrt(D)
    w_attn = lax.all_gather(attn_weights.astype(jnp.bfloat16), ("seq", "ctx"), axis=0, tiled=True)
    w_mlp = lax.all_gather(mlp_weights.astype(jnp.bfloat16), ("seq", "ctx"), axis=0, tiled=True)
    states_full = states.astype(jnp.float32)
    projected = jnp.dot(states, w_attn[:, : 3 * model_width], preferred_element_type=jnp.float32)
    head_shape = (tok_rows, HEADS, HEAD_DIM)
    qk_gain = feature_gains[:, 0].reshape(HEADS, HEAD_DIM)
    query_unit, query_factor = unit_rows(projected[:, :model_width].reshape(head_shape))
    key_unit, key_factor = unit_rows(
        projected[:, model_width : 2 * model_width].reshape(head_shape)
    )
    query_low = (query_unit * qk_gain).astype(jnp.bfloat16)
    key_low = (key_unit * qk_gain).astype(jnp.bfloat16).reshape(tok_rows, model_width)
    value_low = projected[:, 2 * model_width :].astype(jnp.bfloat16)
    keys_all, values_all = (
        lax.all_gather(key_low, "ctx", axis=0, tiled=True),
        lax.all_gather(value_low, "ctx", axis=0, tiled=True),
    )
    seq_len = keys_all.shape[0]
    ctx_lanes = jnp.arange(lax.axis_size("ctx"), dtype=jnp.int32)
    places = block_place[0]
    own_block = jnp.sum(jnp.where(ctx_lanes == lax.axis_index("ctx"), places, 0))
    query_pos = own_block * tok_rows + jnp.arange(tok_rows, dtype=jnp.int32)
    key_index = jnp.arange(seq_len, dtype=jnp.int32)
    key_owner = key_index // tok_rows
    key_pos = (
        jnp.sum(jnp.where(key_owner[:, None] == ctx_lanes[None, :], places[None, :], 0), axis=1)
        * tok_rows
        + key_index % tok_rows
    )
    kblock = min(512, seq_len)
    nblocks = seq_len // kblock
    key_blocks = keys_all.reshape(nblocks, kblock, HEADS, HEAD_DIM)
    value_blocks = values_all.reshape(nblocks, kblock, HEADS, HEAD_DIM)
    pos_blocks = key_pos.reshape(nblocks, kblock)

    def block_scores(key_rows, key_places):
        raw_scores = score_scale * jnp.einsum(
            "qhd,khd->hqk", query_low, key_rows, preferred_element_type=jnp.float32
        )
        allowed = key_places[None, None, :] <= query_pos[None, :, None]
        return (raw_scores, allowed)

    def max_step(running, inputs):
        running_max, running_sum = running
        key_rows, key_places = inputs
        raw_scores, allowed = block_scores(key_rows, key_places)
        masked = jnp.where(allowed, raw_scores, NEG_LARGE)
        new_max = jnp.maximum(running_max, jnp.max(masked, axis=-1))
        powered = jnp.where(allowed, jnp.exp(masked - new_max[..., None]), 0.0)
        running_sum = running_sum * jnp.exp(running_max - new_max) + jnp.sum(powered, axis=-1)
        return ((new_max, running_sum), None)

    start_max = jnp.full((HEADS, tok_rows), NEG_LARGE, jnp.float32)
    start_sum = jnp.zeros((HEADS, tok_rows), jnp.float32)
    (final_max, final_sum), _ = lax.scan(max_step, (start_max, start_sum), (key_blocks, pos_blocks))
    log_total = final_max + jnp.log(final_sum)

    def value_step(accumulated, inputs):
        key_rows, value_rows, key_places = inputs
        raw_scores, allowed = block_scores(key_rows, key_places)
        weights_low = jnp.where(allowed, jnp.exp(raw_scores - log_total[..., None]), 0.0).astype(
            jnp.bfloat16
        )
        accumulated = accumulated + jnp.einsum(
            "hqk,khd->qhd", weights_low, value_rows, preferred_element_type=jnp.float32
        )
        return (accumulated, None)

    attended, _ = lax.scan(
        value_step, jnp.zeros(head_shape, jnp.float32), (key_blocks, value_blocks, pos_blocks)
    )
    attended_low = attended.reshape(tok_rows, model_width).astype(jnp.bfloat16)
    branch_attn = jnp.dot(
        attended_low, w_attn[:, 3 * model_width :], preferred_element_type=jnp.float32
    )
    attn_unit, attn_factor = unit_rows(branch_attn)
    alpha_attn = feature_gains[:, 1]
    mixed_one, mix_factor = unit_rows(states_full + alpha_attn * (attn_unit - states_full))
    mixed_low = mixed_one.astype(jnp.bfloat16)
    up_gate = jnp.dot(mixed_low, w_mlp[:, : 2 * ff_width], preferred_element_type=jnp.float32)
    up_scaled = up_gate[:, :ff_width] * unit_gains[:, 0]
    gate_scaled = up_gate[:, ff_width:] * gate_factor
    sigmoid_gate = jax.nn.sigmoid(gate_scaled)
    activated = gate_scaled * sigmoid_gate
    hidden = (activated * up_scaled).astype(jnp.bfloat16)
    branch_mlp = contract_cols(hidden, w_mlp[:, 2 * ff_width :])
    mlp_unit, mlp_factor = unit_rows(branch_mlp)
    alpha_mlp = feature_gains[:, 2]
    out_full, out_factor = unit_rows(mixed_one + alpha_mlp * (mlp_unit - mixed_one))
    grad_mix_two = unit_back(out_full, out_factor, cotangent.astype(jnp.float32))
    grad_alpha_m = jnp.sum(grad_mix_two * (mlp_unit - mixed_one), axis=0)
    grad_branch_mlp = unit_back(mlp_unit, mlp_factor, grad_mix_two * alpha_mlp).astype(jnp.bfloat16)
    grad_hidden = jnp.dot(
        grad_branch_mlp, w_mlp[:, 2 * ff_width :], preferred_element_type=jnp.float32
    )
    grad_up_scaled = grad_hidden * activated
    grad_gate_scaled = (
        grad_hidden * up_scaled * sigmoid_gate * (1.0 + gate_scaled * (1.0 - sigmoid_gate))
    )
    grad_s_u = jnp.sum(grad_up_scaled * up_gate[:, :ff_width], axis=0)
    grad_s_v = jnp.sum(grad_gate_scaled * up_gate[:, ff_width:], axis=0) * math.sqrt(D)
    grad_up_gate = jnp.concatenate(
        [grad_up_scaled * unit_gains[:, 0], grad_gate_scaled * gate_factor], axis=1
    ).astype(jnp.bfloat16)
    grad_mixed_one = grad_mix_two * (1.0 - alpha_mlp) + contract_cols(
        grad_up_gate, w_mlp[:, : 2 * ff_width]
    )
    grad_mix_one = unit_back(mixed_one, mix_factor, grad_mixed_one)
    grad_alpha_a = jnp.sum(grad_mix_one * (attn_unit - states_full), axis=0)
    grad_branch_attn = unit_back(attn_unit, attn_factor, grad_mix_one * alpha_attn).astype(
        jnp.bfloat16
    )
    grad_attended = (
        contract_cols(grad_branch_attn, w_attn[:, 3 * model_width :])
        .astype(jnp.bfloat16)
        .reshape(head_shape)
    )
    row_dots = jnp.einsum("qhd,qhd->hq", grad_attended.astype(jnp.float32), attended)

    def grad_step(grad_query, inputs):
        key_rows, value_rows, key_places = inputs
        raw_scores, allowed = block_scores(key_rows, key_places)
        probabilities = jnp.where(allowed, jnp.exp(raw_scores - log_total[..., None]), 0.0)
        grad_prob = jnp.einsum(
            "qhd,khd->hqk", grad_attended, value_rows, preferred_element_type=jnp.float32
        )
        grad_scores = (probabilities * (grad_prob - row_dots[..., None])).astype(jnp.bfloat16)
        grad_query = grad_query + score_scale * jnp.einsum(
            "hqk,khd->qhd", grad_scores, key_rows, preferred_element_type=jnp.float32
        )
        key_terms = score_scale * jnp.einsum(
            "hqk,qhd->khd", grad_scores, query_low, preferred_element_type=jnp.float32
        )
        value_terms = jnp.einsum(
            "hqk,qhd->khd",
            probabilities.astype(jnp.bfloat16),
            grad_attended,
            preferred_element_type=jnp.float32,
        )
        return (grad_query, (key_terms, value_terms))

    grad_query_low, (key_terms, value_terms) = lax.scan(
        grad_step, jnp.zeros(head_shape, jnp.float32), (key_blocks, value_blocks, pos_blocks)
    )
    key_terms = key_terms.reshape(seq_len, model_width)
    value_terms = value_terms.reshape(seq_len, model_width)
    own_key_grad, own_value_grad = (
        lax.psum_scatter(
            key_terms.astype(jnp.bfloat16), "ctx", scatter_dimension=0, tiled=True
        ).astype(jnp.float32),
        lax.psum_scatter(
            value_terms.astype(jnp.bfloat16), "ctx", scatter_dimension=0, tiled=True
        ).astype(jnp.float32),
    )
    grad_key_low = own_key_grad.reshape(head_shape)
    grad_s_qk = jnp.sum(grad_query_low * query_unit + grad_key_low * key_unit, axis=0).reshape(
        model_width
    )
    grad_query_raw = unit_back(query_unit, query_factor, grad_query_low * qk_gain).reshape(
        tok_rows, model_width
    )
    grad_key_raw = unit_back(key_unit, key_factor, grad_key_low * qk_gain).reshape(
        tok_rows, model_width
    )
    grad_projected = jnp.concatenate([grad_query_raw, grad_key_raw, own_value_grad], axis=1).astype(
        jnp.bfloat16
    )
    grad_states = grad_mix_one * (1.0 - alpha_attn) + contract_cols(
        grad_projected, w_attn[:, : 3 * model_width]
    )
    feature_total = jnp.stack([grad_s_qk, grad_alpha_a, grad_alpha_m], axis=1)
    unit_fold = jnp.stack([grad_s_u, grad_s_v], axis=1).reshape(
        model_width, 2 * ff_width // model_width
    )
    attn_cols = 4 * model_width
    mlp_cols = 3 * ff_width
    attn_share = lax.psum_scatter(
        jnp.concatenate(
            [
                contract_rows(states, grad_projected),
                contract_rows(attended_low, grad_branch_attn),
                feature_total,
            ],
            axis=1,
        ),
        ("seq", "ctx"),
        scatter_dimension=0,
        tiled=True,
    )
    mlp_share = lax.psum_scatter(
        jnp.concatenate(
            [
                contract_rows(mixed_low, grad_up_gate),
                contract_rows(grad_branch_mlp, hidden),
                unit_fold,
            ],
            axis=1,
        ),
        ("seq", "ctx"),
        scatter_dimension=0,
        tiled=True,
    )
    grad_attn = attn_share[:, :attn_cols]
    grad_feature = attn_share[:, attn_cols:]
    grad_mlp = mlp_share[:, :mlp_cols]
    grad_unit = mlp_share[:, mlp_cols:].reshape(
        unit_gains.shape[0] // lax.axis_size(("seq", "ctx")), 2
    )
    return (
        out_full.astype(jnp.bfloat16),
        grad_states.astype(jnp.bfloat16),
        grad_attn,
        grad_mlp,
        grad_feature,
        grad_unit,
    )


CORES = 2
ALL = ("seq", "ctx")


def fits(n_seq, chips):
    return n_seq == 4 and chips == 4 and HEADS % chips == 0


MESH = pl.DeviceIdType.MESH
VMEM = pltpu.VMEM
CHIPS = 4
STEPS = (1, 2, 3)
LIMIT = 60 * 1024 * 1024


def place_of():
    seq = lax.axis_index("seq")
    ctx = lax.axis_index("ctx")
    return seq, ctx // CORES, ctx % CORES


def chip_peer(step):
    seq, chip, core = place_of()
    other = lax.rem(chip + step, CHIPS)
    return (seq, other * CORES + core), other


def seq_peer(step):
    seq, chip, core = place_of()
    other = seq ^ step
    return (other, chip * CORES + core), other


def twin():
    seq, chip, core = place_of()
    return (seq, chip * CORES + 1 - core)


def meet():
    devices = [chip_peer(step)[0] for step in STEPS] + [seq_peer(step)[0] for step in STEPS] + [twin()]
    gate = pltpu.get_barrier_semaphore()
    for device in devices:
        pl.semaphore_signal(gate, inc=1, device_id=device, device_id_type=MESH)
    pl.semaphore_wait(gate, len(devices))


def remote(src, dst, send, recv, device):
    return pltpu.make_async_remote_copy(
        src_ref=src, dst_ref=dst, send_sem=send, recv_sem=recv, device_id=device,
        device_id_type=MESH,
    )


def begin(copy):
    copy.start()
    return copy


def rows_at(index, count):
    return pl.ds(pl.multiple_of(index * count, count), count)


def gather_line(src, dst_of, send, recv):
    return [
        begin(remote(src, dst_of, send.at[step], recv.at[step], chip_peer(step)[0])) for step in STEPS
    ]


def dot(left, right):
    return jnp.dot(left, right, preferred_element_type=jnp.float32)


def dot_nt(left, right):
    return lax.dot_general(
        left, right, (((1,), (1,)), ((), ())), preferred_element_type=jnp.float32
    )


def dot_tn(left, right):
    return lax.dot_general(
        left, right, (((0,), (0,)), ((), ())), preferred_element_type=jnp.float32
    )


def dma(*shape):
    return pltpu.SemaphoreType.DMA(shape)


def in_vmem():
    return pl.BlockSpec(memory_space=pltpu.VMEM)


def in_hbm():
    return pl.BlockSpec(memory_space=pl.ANY)


def attend_kernel(
    states, qkv_src, mlp_src, qk_gain, query_pos, key_pos,
    states_all, w_qkv, w_part, raw_out, query_out, both, att_out, inv_out, attx,
    stage_q, low_q, stage_m, low_m, raw, att_low,
    local_sem, x_send, x_recv, q_send, q_recv, mt_send, mt_recv, wz_send, wz_recv,
    ws_send, ws_recv, wt_send, wt_recv, m_send, m_recv, kv_send, kv_recv, a_send, a_recv,
):
    seq, chip, core = place_of()
    rows = qkv_src.shape[2]
    half_cols = qkv_src.shape[3]
    part_cols = half_cols // 3
    tok_rows = states.shape[0]
    heads = qk_gain.shape[0]
    head_cols = heads * HEAD_DIM
    group_rows = tok_rows * CHIPS
    chip_rows = CORES * rows
    seq_rows = CHIPS * chip_rows
    half_units = w_part.shape[2]
    ff_width = mlp_src.shape[1] // 3
    meet()
    block = rows_at(chip, tok_rows)
    mine = rows_at(core, rows)
    swaps = [
        begin(remote(qkv_src.at[at, 1 - core], stage_q.at[at, mine], q_send.at[at], q_recv.at[at], twin()))
        for at in range(CHIPS)
    ]
    keeps = [
        begin(pltpu.make_async_copy(qkv_src.at[at, core], stage_q.at[at, mine], local_sem.at[at]))
        for at in range(CHIPS)
    ]
    states_all[block, :] = states[...]
    m_swaps, m_keeps = [], []
    for part in range(3):
        for at in range(CHIPS):
            start = part * ff_width + at * CORES * half_units
            theirs = pl.ds(pl.multiple_of(start + (1 - core) * half_units, 128), half_units)
            ours = pl.ds(pl.multiple_of(start + core * half_units, 128), half_units)
            there = stage_m.at[part, at, mine]
            m_swaps.append(begin(remote(mlp_src.at[:, theirs], there, mt_send.at[part, at], mt_recv.at[part, at], twin())))
            m_keeps.append(begin(pltpu.make_async_copy(mlp_src.at[:, ours], there, local_sem.at[CHIPS + part * CHIPS + at])))
    for copy in keeps:
        copy.wait()
    for copy in swaps:
        copy.wait()
    low_q[...] = stage_q[...].astype(jnp.bfloat16)
    my_rows = rows_at(seq * CHIPS + chip, chip_rows)
    line = []
    for step in STEPS:
        device, other = chip_peer(step)
        line.append(begin(remote(low_q.at[other], w_qkv.at[core, my_rows], wz_send.at[step], wz_recv.at[step], device)))
    w_qkv[core, my_rows, :] = low_q[chip]
    for copy in m_keeps:
        copy.wait()
    for copy in m_swaps:
        copy.wait()
    low_m[...] = stage_m[...].astype(jnp.bfloat16)
    for copy in line:
        copy.wait_recv()
    sends = gather_line(states, states_all.at[block], x_send, x_recv)
    seq_part = w_qkv.at[core, rows_at(seq, seq_rows)]
    across = [
        begin(remote(seq_part, seq_part, ws_send.at[step], ws_recv.at[step], seq_peer(step)[0]))
        for step in STEPS
    ]
    for copy in across:
        copy.wait_recv()
    swap = begin(remote(w_qkv.at[core], w_qkv.at[core], wt_send.at[0], wt_recv.at[0], twin()))
    swap.wait()
    for copy in sends:
        copy.wait_recv()
    m_line = []
    for part in range(3):
        for step in STEPS:
            device, other = chip_peer(step)
            there = w_part.at[part, rows_at(chip, chip_rows)]
            m_line.append(begin(remote(low_m.at[part, other], there, m_send.at[part, step], m_recv.at[part, step], device)))
        w_part[part, rows_at(chip, chip_rows), :] = low_m[part, chip]

    for half in range(CORES):
        value = dot(states_all[...], w_qkv[half])
        for which in range(3):
            start = which * head_cols + half * part_cols
            raw[:, start : start + part_cols] = value[:, which * part_cols : (which + 1) * part_cols]
    for head in range(heads):
        gain = qk_gain[head]
        for which in range(2):
            start = which * head_cols + head * HEAD_DIM
            value = raw[:, start : start + HEAD_DIM]
            factor = lax.rsqrt(jnp.sum(value * value, axis=-1, keepdims=True) + EPSILON)
            low = (value * factor * gain).astype(jnp.bfloat16)
            raw_out[which, head] = value
            if which == 0:
                query_out[head] = low * math.sqrt(HEAD_DIM)
            else:
                both[core, 0, head] = low
        start = 2 * head_cols + head * HEAD_DIM
        both[core, 1, head] = raw[:, start : start + HEAD_DIM].astype(jnp.bfloat16)
    swap = begin(remote(both.at[core], both.at[core], kv_send.at[0], kv_recv.at[0], twin()))
    swap.wait()

    tile = min(128, group_rows)
    tiles = group_rows // tile

    def one_tile(index, carry):
        head = index // tiles
        at = rows_at(lax.rem(index, tiles), tile)
        query = query_out[head, at, :]
        allowed = key_pos[...] <= query_pos[at, :]
        scores = jnp.concatenate([dot_nt(query, both[half, 0, head]) for half in range(CORES)], axis=1)
        powered = jnp.exp(jnp.where(allowed, scores, NEG_LARGE))
        inverse = 1.0 / jnp.sum(powered, axis=-1, keepdims=True)
        weights = (powered * inverse).astype(jnp.bfloat16)
        att_out[head, at, :] = sum(
            dot(weights[:, half * group_rows : (half + 1) * group_rows], both[half, 1, head])
            for half in range(CORES)
        )
        inv_out[head, at, :] = inverse
        return carry

    lax.fori_loop(0, heads * tiles, one_tile, 0)
    for head in range(heads):
        att_low[:, head * HEAD_DIM : (head + 1) * HEAD_DIM] = att_out[head].astype(jnp.bfloat16)
    out = []
    for step in STEPS:
        device, other = chip_peer(step)
        out.append(begin(remote(att_low.at[rows_at(other, tok_rows)], attx.at[chip], a_send.at[step], a_recv.at[step], device)))
    attx[chip] = att_low[block, :]
    for copy in out + m_line:
        copy.wait()
    for copy in sends + line + across:
        copy.wait_send()


def attend_call(states, qkv_src, mlp_src, qk_gain, query_pos, key_pos):
    tok_rows, model_width = states.shape
    chips, _, rows, half_cols = qkv_src.shape
    heads = qk_gain.shape[0]
    group_rows = chips * tok_rows
    half_units = mlp_src.shape[1] // 3 // chips // CORES
    f32, low = jnp.float32, jnp.bfloat16
    shape = jax.ShapeDtypeStruct
    return pl.pallas_call(
        attend_kernel,
        out_shape=[
            shape((group_rows, model_width), low),
            shape((CORES, model_width, half_cols), low),
            shape((3, chips * CORES * rows, half_units), low),
            shape((2, heads, group_rows, HEAD_DIM), f32),
            shape((heads, group_rows, HEAD_DIM), low),
            shape((CORES, 2, heads, group_rows, HEAD_DIM), low),
            shape((heads, group_rows, HEAD_DIM), f32),
            shape((heads, group_rows, 1), f32),
            shape((chips, tok_rows, heads * HEAD_DIM), low),
        ],
        in_specs=[in_vmem(), in_hbm(), in_hbm(), in_vmem(), in_vmem(), in_vmem()],
        out_specs=[in_vmem()] * 9,
        scratch_shapes=[
            VMEM((chips, CORES * rows, half_cols), f32),
            VMEM((chips, CORES * rows, half_cols), low),
            VMEM((3, chips, CORES * rows, half_units), f32),
            VMEM((3, chips, CORES * rows, half_units), low),
            VMEM((group_rows, 3 * heads * HEAD_DIM), f32),
            VMEM((group_rows, heads * HEAD_DIM), low),
            dma(16), dma(4), dma(4), dma(4), dma(4), dma(3, 4), dma(3, 4), dma(4), dma(4),
            dma(4), dma(4), dma(1), dma(1), dma(3, 4), dma(3, 4), dma(1), dma(1), dma(4), dma(4),
        ],
        compiler_params=pltpu.CompilerParams(
            collective_id=1, has_side_effects=True, vmem_limit_bytes=LIMIT
        ),
        name="attend",
    )(states, qkv_src, mlp_src, qk_gain, query_pos, key_pos)


def unit_of(value):
    factor = lax.rsqrt(jnp.sum(value * value, axis=-1, keepdims=True) + EPSILON)
    return value * factor, factor


def mlp_kernel(
    attx, states, cotangent, w_out, alpha_attn, alpha_mlp, gain_u, gain_v, w_part,
    out, grad_attx, grad_w_out, grad_direct, dot_a, dot_m, dot_u, dot_v, grad_half,
    weights, mixed_one, attn_unit, factors, mixed_low, mixed_all, up, gate, hidden, part,
    sums, grad_two, branch_low, branch_all, grad_u, grad_v, wide, turned, arrived,
    local_sem, ws_send, ws_recv, wt_send, wt_recv, x_send, x_recv, r_send, r_recv,
    g_send, g_recv, b_send, b_recv, d_send, d_recv,
):
    seq, chip, core = place_of()
    tok_rows, model_width = states.shape
    chip_heads = attx.shape[2]
    seq_rows = w_part.shape[1]
    half_units = w_part.shape[2]
    group_rows = CHIPS * tok_rows
    block = rows_at(chip, tok_rows)
    meet()
    seq_at = rows_at(seq, seq_rows)

    def spread(which):
        return [
            begin(remote(w_part.at[which], weights.at[which, core, seq_at], ws_send.at[which, step], ws_recv.at[which, step], seq_peer(step)[0]))
            for step in STEPS
        ]

    across = spread(0) + spread(1)
    keeps = [
        begin(pltpu.make_async_copy(w_part.at[which], weights.at[which, core, seq_at], local_sem.at[which]))
        for which in range(3)
    ]
    branch = sum(dot(attx[at], w_out[at]) for at in range(CHIPS))
    unit, factor = unit_of(branch)
    attn_unit[...] = unit
    factors[0] = factor
    base = states[...].astype(jnp.float32)
    value, factor = unit_of(base + alpha_attn[...] * (unit - base))
    mixed_one[...] = value
    factors[1] = factor
    mixed_low[...] = value.astype(jnp.bfloat16)
    line = gather_line(mixed_low, mixed_all.at[block], x_send, x_recv)
    mixed_all[block, :] = mixed_low[...]
    for copy in keeps:
        copy.wait()
    for copy in across:
        copy.wait_recv()
    swaps = [
        begin(remote(weights.at[which, core], weights.at[which, core], wt_send.at[which], wt_recv.at[which], twin()))
        for which in range(2)
    ]
    across += spread(2)
    for copy in line:
        copy.wait_recv()
    for copy in swaps:
        copy.wait_recv()
    for half in range(CORES):
        up[half] = dot(mixed_all[...], weights[0, half])
        gate[half] = dot(mixed_all[...], weights[1, half])
    slab = min(64, group_rows)
    slabs = group_rows // slab

    def activate(index, carry):
        half = index // slabs
        at = rows_at(lax.rem(index, slabs), slab)
        gated = gate[half, at, :] * gain_v[half]
        scaled = up[half, at, :] * gain_u[half]
        hidden[half, at, :] = (gated * jax.nn.sigmoid(gated) * scaled).astype(jnp.bfloat16)
        return carry

    lax.fori_loop(0, CORES * slabs, activate, 0)
    for copy in across[-3:]:
        copy.wait_recv()
    swap = begin(remote(weights.at[2, core], weights.at[2, core], wt_send.at[2], wt_recv.at[2], twin()))
    swaps.append(swap)
    swap.wait_recv()
    tile = model_width // 5

    def down(index, carry):
        at = rows_at(index, tile)
        part[0, :, at] = sum(dot_nt(hidden[half], weights[2, half, at, :]) for half in range(CORES)).astype(jnp.bfloat16)
        return carry

    lax.fori_loop(0, model_width // tile, down, 0)

    def reduce_line(which, send, recv):
        sent = []
        for step in STEPS:
            device, other = chip_peer(step)
            sent.append(begin(remote(part.at[which, rows_at(other, tok_rows)], sums.at[which, step], send.at[step], recv.at[step], device)))
        return sent

    def reduced(which):
        total = part[which, block, :].astype(jnp.float32)
        for step in STEPS:
            total = total + sums[which, step].astype(jnp.float32)
        return total

    sent = reduce_line(0, r_send, r_recv)
    for copy in sent:
        copy.wait_recv()
    mlp_unit, mlp_factor = unit_of(reduced(0))
    value, factor = unit_of(mixed_one[...] + alpha_mlp[...] * (mlp_unit - mixed_one[...]))
    out[...] = value.astype(jnp.bfloat16)
    above = cotangent[...].astype(jnp.float32)
    grad = factor * (above - value * jnp.sum(above * value, axis=-1, keepdims=True))
    grad_two[...] = grad
    dot_m[...] = jnp.sum(grad * (mlp_unit - mixed_one[...]), axis=0, keepdims=True)
    grad = grad * alpha_mlp[...]
    grad = mlp_factor * (grad - mlp_unit * jnp.sum(grad * mlp_unit, axis=-1, keepdims=True))
    branch_low[...] = grad.astype(jnp.bfloat16)
    back = gather_line(branch_low, branch_all.at[block], g_send, g_recv)
    branch_all[block, :] = branch_low[...]
    turned[0] = mixed_all[...].T
    for copy in back:
        copy.wait_recv()
    for half in range(CORES):
        wide[half] = dot(branch_all[...], weights[2, half])
    dot_u[...] = jnp.zeros_like(dot_u)
    dot_v[...] = jnp.zeros_like(dot_v)

    def deactivate(index, carry):
        half = index // slabs
        at = rows_at(lax.rem(index, slabs), slab)
        gated = gate[half, at, :] * gain_v[half]
        scaled = up[half, at, :] * gain_u[half]
        upstream = wide[half, at, :]
        sig = jax.nn.sigmoid(gated)
        to_up = upstream * (gated * sig)
        to_gate = upstream * scaled * sig * (1.0 + gated * (1.0 - sig))
        dot_u[half] += jnp.sum(to_up * up[half, at, :], axis=0, keepdims=True)
        dot_v[half] += jnp.sum(to_gate * gate[half, at, :], axis=0, keepdims=True)
        grad_u[half, at, :] = (to_up * gain_u[half]).astype(jnp.bfloat16)
        grad_v[half, at, :] = (to_gate * gain_v[half]).astype(jnp.bfloat16)
        return carry

    lax.fori_loop(0, CORES * slabs, deactivate, 0)

    def back_down(index, carry):
        at = rows_at(index, tile)
        part[1, :, at] = sum(
            dot_nt(grad_u[half], weights[0, half, at, :]) + dot_nt(grad_v[half], weights[1, half, at, :])
            for half in range(CORES)
        ).astype(jnp.bfloat16)
        return carry

    lax.fori_loop(0, model_width // tile, back_down, 0)
    for copy in swaps:
        copy.wait_send()
    sent += reduce_line(1, b_send, b_recv)
    turned[1] = branch_all[...].T
    pairs = ((0, grad_u), (1, grad_v), (2, hidden))
    swaps = []
    for which, right in pairs:
        left = 1 if which == 2 else 0

        def weight_grad(index, carry, which=which, right=right, left=left):
            half = index // 5
            at = rows_at(lax.rem(index, 5), tile)
            weights[which, half, at, :] = dot(turned[left, at, :], right[half]).astype(jnp.bfloat16)
            return carry

        lax.fori_loop(0, CORES * 5, weight_grad, 0)
        swaps.append(begin(remote(weights.at[which, 1 - core], arrived.at[which], d_send.at[which], d_recv.at[which], twin())))
    for copy in sent[3:]:
        copy.wait_recv()
    grad = grad_two[...] * (1.0 - alpha_mlp[...]) + reduced(1)
    value = mixed_one[...]
    grad = factors[1] * (grad - value * jnp.sum(grad * value, axis=-1, keepdims=True))
    unit = attn_unit[...]
    dot_a[...] = jnp.sum(grad * (unit - states[...].astype(jnp.float32)), axis=0, keepdims=True)
    grad_direct[...] = grad * (1.0 - alpha_attn[...])
    grad = grad * alpha_attn[...]
    grad = factors[0] * (grad - unit * jnp.sum(grad * unit, axis=-1, keepdims=True))
    low = grad.astype(jnp.bfloat16)
    for at in range(CHIPS):
        grad_attx[at] = dot_nt(low, w_out[at]).astype(jnp.bfloat16)
        grad_w_out[at] = dot_tn(attx[at], low).astype(jnp.bfloat16)
    for which in range(3):
        swaps[which].wait_recv()
        grad_half[which] = (
            weights[which, core].astype(jnp.float32) + arrived[which].astype(jnp.float32)
        ).astype(jnp.bfloat16)
    for copy in across + line + sent + back + swaps:
        copy.wait_send()


def mlp_call(attx, states, cotangent, w_out, alpha_attn, alpha_mlp, gain_u, gain_v, w_part):
    tok_rows, model_width = states.shape
    chips, _, chip_heads = attx.shape
    half_units = w_part.shape[2]
    group_rows = chips * tok_rows
    f32, low = jnp.float32, jnp.bfloat16
    shape = jax.ShapeDtypeStruct
    tokens, group = (tok_rows, model_width), (group_rows, model_width)
    wide = (CORES, group_rows, half_units)
    matrix = (model_width, half_units)
    return pl.pallas_call(
        mlp_kernel,
        out_shape=[
            shape(tokens, low),
            shape(attx.shape, low),
            shape((chips, chip_heads, model_width), low),
            shape(tokens, f32),
            shape((1, model_width), f32),
            shape((1, model_width), f32),
            shape((CORES, 1, half_units), f32),
            shape((CORES, 1, half_units), f32),
            shape((3,) + matrix, low),
        ],
        in_specs=[in_vmem()] * 8 + [in_hbm()],
        out_specs=[in_vmem()] * 9,
        scratch_shapes=[
            VMEM((3, CORES) + matrix, low),
            VMEM(tokens, f32),
            VMEM(tokens, f32),
            VMEM((2, tok_rows, 1), f32),
            VMEM(tokens, low),
            VMEM(group, low),
            VMEM(wide, f32),
            VMEM(wide, f32),
            VMEM(wide, low),
            VMEM((2,) + group, low),
            VMEM((2, chips) + tokens, low),
            VMEM(tokens, f32),
            VMEM(tokens, low),
            VMEM(group, low),
            VMEM(wide, low),
            VMEM(wide, low),
            VMEM(wide, f32),
            VMEM((2, model_width, group_rows), low),
            VMEM((3,) + matrix, low),
            dma(3), dma(3, 4), dma(3, 4), dma(3), dma(3), dma(4), dma(4), dma(4), dma(4),
            dma(4), dma(4), dma(4), dma(4), dma(3), dma(3),
        ],
        compiler_params=pltpu.CompilerParams(
            collective_id=2, has_side_effects=True, vmem_limit_bytes=LIMIT
        ),
        name="mlp",
    )(attx, states, cotangent, w_out, alpha_attn, alpha_mlp, gain_u, gain_v, w_part)


def back_kernel(
    grad_attx, grad_half, grad_w_out, small_in, raw, query, both, att, inverse, states_all,
    w_qkv, qk_gain, query_pos, key_pos, grad_direct,
    grad_states, out_mlp, out_qkv, out_proj, small_out,
    att_low, heads_low, to_keys, swap_low, swap_kv, grad_heads, grad_sides, part, sums, turned,
    grad_q, half_q, seq_q, line_q, wide_q, half_o, pair_o, seq_got, seq_low, line_got, wide,
    wide_o, small, small_pair, small_seq, dots,
    local_sem, a_send, a_recv, s_send, s_recv, o_send, o_recv, kv_send, kv_recv, r_send, r_recv,
    qt_send, qt_recv, qs_send, qs_recv, qz_send, qz_recv, z_send, z_recv, f_send, f_recv,
    p_send, p_recv, t_send, t_recv,
):
    seq, chip, core = place_of()
    tok_rows, model_width = grad_direct.shape
    heads = qk_gain.shape[0]
    head_cols = heads * HEAD_DIM
    group_rows = CHIPS * tok_rows
    half_units = grad_half.shape[2]
    seq_rows = seq_got.shape[2]
    chip_rows = seq_rows // CHIPS
    rows = chip_rows // CORES
    part_cols = head_cols // CORES
    ff_width = out_mlp.shape[1] // 3
    scale = math.sqrt(HEAD_DIM)
    block = rows_at(chip, tok_rows)
    f32, low = jnp.float32, jnp.bfloat16
    meet()
    waits = []
    line = []
    for step in STEPS:
        device, other = chip_peer(step)
        line.append(begin(remote(grad_attx.at[other], att_low.at[block], a_send.at[step], a_recv.at[step], device)))
    att_low[block, :] = grad_attx[chip]
    half_at = pl.ds(pl.multiple_of(core * half_units, 128), half_units)
    other_at = pl.ds(pl.multiple_of((1 - core) * half_units, 128), half_units)
    pair = begin(remote(grad_w_out.at[:, :, other_at], pair_o, o_send.at[0], o_recv.at[0], twin()))
    across = []
    for which in range(3):
        for step in STEPS:
            device, other = seq_peer(step)
            across.append(begin(remote(grad_half.at[which, rows_at(other, seq_rows)], seq_got.at[which, step - 1], s_send.at[which, step], s_recv.at[which, step], device)))
    keeps = [
        begin(pltpu.make_async_copy(grad_half.at[which, rows_at(seq, seq_rows)], seq_low.at[which], local_sem.at[which]))
        for which in range(3)
    ]
    to_keys[...] = jnp.zeros_like(to_keys)
    dots[...] = jnp.zeros_like(dots)
    turned[...] = states_all[...].T
    pair.wait_recv()
    for at in range(4):
        half_o[at] = (grad_w_out[at, :, half_at].astype(f32) + pair_o[at].astype(f32)).astype(low)
    for step in STEPS:
        device, other = seq_peer(step)
        across.append(begin(remote(half_o.at[other], seq_got.at[3, step - 1], s_send.at[3, step], s_recv.at[3, step], device)))
    for copy in line:
        copy.wait_recv()
    for head in range(heads):
        heads_low[head] = att_low[:, head * HEAD_DIM : (head + 1) * HEAD_DIM]

    tile = min(128, group_rows)
    tiles = group_rows // tile

    def raw_back(which, head, at, upstream):
        value = raw[which, head, at, :]
        unit, factor = unit_of(value)
        dots[head] += jnp.sum(upstream * unit, axis=0, keepdims=True)
        upstream = upstream * qk_gain[head]
        upstream = factor * (upstream - unit * jnp.sum(upstream * unit, axis=-1, keepdims=True))
        grad_heads[which, head, at, :] = upstream.astype(low)

    def one_tile(index, carry):
        head = index // tiles
        at = rows_at(lax.rem(index, tiles), tile)
        rows_q = query[head, at, :]
        grad_att = heads_low[head, at, :]
        allowed = key_pos[...] <= query_pos[at, :]
        scores = jnp.concatenate([dot_nt(rows_q, both[half, 0, head]) for half in range(CORES)], axis=1)
        probs = jnp.exp(jnp.where(allowed, scores, NEG_LARGE)) * inverse[head, at, :]
        grad_prob = jnp.concatenate([dot_nt(grad_att, both[half, 1, head]) for half in range(CORES)], axis=1)
        row_dot = jnp.sum(grad_att.astype(f32) * att[head, at, :], axis=-1, keepdims=True)
        grad_scores = (probs * (grad_prob - row_dot)).astype(low)
        weights = probs.astype(low)
        total = jnp.zeros((tile, HEAD_DIM), f32)
        for half in range(CORES):
            cols = slice(half * group_rows, (half + 1) * group_rows)
            total = total + dot(grad_scores[:, cols], both[half, 0, head])
            to_keys[half, 0, head] += dot_tn(grad_scores[:, cols], rows_q)
            to_keys[half, 1, head] += dot_tn(weights[:, cols], grad_att)
        raw_back(0, head, at, total * scale)
        return carry

    lax.fori_loop(0, heads * tiles, one_tile, 0)
    swap_low[...] = to_keys[1 - core].astype(low)
    swap = begin(remote(swap_low, swap_kv, kv_send.at[0], kv_recv.at[0], twin()))
    swap.wait()

    def one_key(index, carry):
        head = index // tiles
        at = rows_at(lax.rem(index, tiles), tile)
        mine = to_keys[core, 0, head, at, :] + swap_kv[0, head, at, :].astype(f32)
        raw_back(1, head, at, mine)
        value = to_keys[core, 1, head, at, :] + swap_kv[1, head, at, :].astype(f32)
        grad_heads[2, head, at, :] = value.astype(low)
        return carry

    lax.fori_loop(0, heads * tiles, one_key, 0)
    for which in range(3):
        full = jnp.concatenate([grad_heads[which, head] for head in range(heads)], axis=1)
        for half in range(CORES):
            grad_sides[half, :, which * part_cols : (which + 1) * part_cols] = full[:, half * part_cols : (half + 1) * part_cols]
    wide_tile = model_width // 5

    def down(index, carry):
        at = rows_at(index, wide_tile)
        part[:, at] = sum(dot_nt(grad_sides[half], w_qkv[half, at, :]) for half in range(CORES)).astype(low)
        return carry

    lax.fori_loop(0, 5, down, 0)
    reduce = []
    for step in STEPS:
        device, other = chip_peer(step)
        reduce.append(begin(remote(part.at[rows_at(other, tok_rows)], sums.at[step - 1], r_send.at[step], r_recv.at[step], device)))

    def weight_grad(index, carry):
        half = index // 5
        at = rows_at(lax.rem(index, 5), wide_tile)
        grad_q[half, at, :] = dot(turned[at, :], grad_sides[half]).astype(low)
        return carry

    lax.fori_loop(0, CORES * 5, weight_grad, 0)
    swap_q = begin(remote(grad_q.at[1 - core], half_q, qt_send.at[0], qt_recv.at[0], twin()))
    small[...] = small_in[...]
    small[4:5, :head_cols] = jnp.concatenate([dots[head] for head in range(heads)], axis=1)
    swap_s = begin(remote(small, small_pair, t_send.at[0], t_recv.at[0], twin()))
    swap_q.wait()
    half_q[...] = (grad_q[core].astype(f32) + half_q[...].astype(f32)).astype(low)
    across_q = []
    for step in STEPS:
        device, other = seq_peer(step)
        across_q.append(begin(remote(half_q.at[rows_at(other, seq_rows)], seq_q.at[step - 1], qs_send.at[step], qs_recv.at[step], device)))
    swap_s.wait()
    small[...] = small[...] + small_pair[...]
    spread_s = [
        begin(remote(small, small_seq.at[step - 1], t_send.at[step], t_recv.at[step], seq_peer(step)[0]))
        for step in STEPS
    ]
    for copy in keeps:
        copy.wait()
    seq_low[3] = half_o[seq]
    onward = []
    for which in range(4):
        for copy in across[3 * which : 3 * which + 3]:
            copy.wait_recv()
        total = seq_low[which].astype(f32)
        for step in STEPS:
            total = total + seq_got[which, step - 1].astype(f32)
        seq_low[which] = total.astype(low)
        for step in STEPS:
            device, other = chip_peer(step)
            onward.append(begin(remote(seq_low.at[which, rows_at(other, chip_rows)], line_got.at[which, chip], z_send.at[which, step], z_recv.at[which, step], device)))
        line_got[which, chip] = seq_low[which, rows_at(chip, chip_rows), :]
    for copy in across_q:
        copy.wait_recv()
    total = half_q[rows_at(seq, seq_rows), :].astype(f32)
    for step in STEPS:
        total = total + seq_q[step - 1].astype(f32)
    grad_q[0, :seq_rows, :] = total.astype(low)
    onward_q = []
    for step in STEPS:
        device, other = chip_peer(step)
        onward_q.append(begin(remote(grad_q.at[0, rows_at(other, chip_rows)], line_q.at[chip], qz_send.at[step], qz_recv.at[step], device)))
    line_q[chip] = grad_q[0, rows_at(chip, chip_rows), :]
    for copy in spread_s:
        copy.wait()
    small_pair[...] = small[...] + small_seq[0] + small_seq[1] + small_seq[2]
    small_out[chip] = small_pair[...]
    ends = gather_line(small_pair, small_out.at[chip], p_send, p_recv)
    for copy in reduce:
        copy.wait_recv()
    total = part[block, :].astype(f32) + grad_direct[...]
    for step in STEPS:
        total = total + sums[step - 1].astype(f32)
    grad_states[...] = total.astype(low)

    mine = rows_at(core, rows)
    theirs = rows_at(1 - core, rows)
    last, lasts = [], []
    for which in range(3):
        for copy in onward[3 * which : 3 * which + 3]:
            copy.wait_recv()
        for at in range(CHIPS):
            wide[which, at] = line_got[which, at].astype(f32)
            start = which * ff_width + at * CORES * half_units + core * half_units
            there = out_mlp.at[:, pl.ds(pl.multiple_of(start, 128), half_units)]
            last.append(begin(remote(wide.at[which, at, theirs], there, f_send.at[which, at], f_recv.at[which, at], twin())))
            lasts.append(begin(pltpu.make_async_copy(wide.at[which, at, mine], there, local_sem.at[3 + which * CHIPS + at])))
    for copy in onward[9:]:
        copy.wait_recv()
    total = line_got[3, 0].astype(f32)
    for at in range(1, CHIPS):
        total = total + line_got[3, at].astype(f32)
    wide_o[...] = total
    there = out_proj.at[:, half_at]
    last.append(begin(remote(wide_o.at[theirs], there, f_send.at[3, 0], f_recv.at[3, 0], twin())))
    lasts.append(begin(pltpu.make_async_copy(wide_o.at[mine], there, local_sem.at[15])))
    for copy in onward_q:
        copy.wait_recv()
    wide_q[...] = line_q[...].astype(f32)
    there = out_qkv.at[core]
    last.append(begin(remote(wide_q.at[:, theirs], there, f_send.at[3, 1], f_recv.at[3, 1], twin())))
    lasts.append(begin(pltpu.make_async_copy(wide_q.at[:, mine], there, local_sem.at[16])))
    for copy in ends + last + lasts:
        copy.wait()
    for copy in line + [pair] + across + reduce + across_q + onward + onward_q:
        copy.wait_send()


def back_call(
    grad_attx, grad_half, grad_w_out, small_in, raw, query, both, att, inverse, states_all,
    w_qkv, qk_gain, query_pos, key_pos, grad_direct, rows,
):
    tok_rows, model_width = grad_direct.shape
    chips = grad_attx.shape[0]
    heads = qk_gain.shape[0]
    head_cols = heads * HEAD_DIM
    group_rows = chips * tok_rows
    half_units = grad_half.shape[2]
    half_cols = w_qkv.shape[2]
    chip_rows = CORES * rows
    seq_rows = chips * chip_rows
    f32, low = jnp.float32, jnp.bfloat16
    shape = jax.ShapeDtypeStruct
    per_head = (heads, group_rows, HEAD_DIM)
    return pl.pallas_call(
        back_kernel,
        out_shape=[
            shape((tok_rows, model_width), low),
            shape((rows, 3 * chips * CORES * half_units), f32),
            shape((CORES, chips, rows, half_cols), f32),
            shape((rows, CORES * half_units), f32),
            shape((chips,) + small_in.shape, f32),
        ],
        in_specs=[in_vmem(), in_hbm()] + [in_vmem()] * 13,
        out_specs=[in_vmem(), in_hbm(), in_hbm(), in_hbm(), in_vmem()],
        scratch_shapes=[
            VMEM((group_rows, head_cols), low),
            VMEM(per_head, low),
            VMEM((CORES, 2) + per_head, f32),
            VMEM((2,) + per_head, low),
            VMEM((2,) + per_head, low),
            VMEM((3,) + per_head, low),
            VMEM((CORES, group_rows, half_cols), low),
            VMEM((group_rows, model_width), low),
            VMEM((3, tok_rows, model_width), low),
            VMEM((model_width, group_rows), low),
            VMEM((CORES, model_width, half_cols), low),
            VMEM((model_width, half_cols), low),
            VMEM((3, seq_rows, half_cols), low),
            VMEM((chips, chip_rows, half_cols), low),
            VMEM((chips, chip_rows, half_cols), f32),
            VMEM((4, seq_rows, half_units), low),
            VMEM((4, seq_rows, half_units), low),
            VMEM((4, 3, seq_rows, half_units), low),
            VMEM((4, seq_rows, half_units), low),
            VMEM((4, chips, chip_rows, half_units), low),
            VMEM((3, chips, chip_rows, half_units), f32),
            VMEM((chip_rows, half_units), f32),
            VMEM(small_in.shape, f32),
            VMEM(small_in.shape, f32),
            VMEM((3,) + small_in.shape, f32),
            VMEM((heads, 1, HEAD_DIM), f32),
            dma(17), dma(4), dma(4), dma(4, 4), dma(4, 4), dma(1), dma(1), dma(1), dma(1),
            dma(4), dma(4), dma(1), dma(1), dma(4), dma(4), dma(4), dma(4), dma(4, 4), dma(4, 4),
            dma(4, 4), dma(4, 4), dma(4), dma(4), dma(4), dma(4),
        ],
        compiler_params=pltpu.CompilerParams(
            collective_id=3, has_side_effects=True, vmem_limit_bytes=LIMIT
        ),
        name="back",
    )(
        grad_attx, grad_half, grad_w_out, small_in, raw, query, both, att, inverse, states_all,
        w_qkv, qk_gain, query_pos, key_pos, grad_direct,
    )


def shards_split(states, cotangent, attn_weights, mlp_weights, feature_gains, unit_gains, block_place):
    tok_rows, model_width = states.shape
    ff_width = unit_gains.shape[0]
    n_seq, n_ctx = lax.axis_size("seq"), lax.axis_size("ctx")
    chips = n_ctx // CORES
    chip = lax.axis_index("ctx") // CORES
    core = lax.axis_index("ctx") % CORES
    heads = HEADS // chips
    head_cols = heads * HEAD_DIM
    units = ff_width // chips
    group_rows = chips * tok_rows
    rows = attn_weights.shape[0]
    qkv_src = attn_weights[:, : 3 * model_width].reshape(rows, 3, chips, CORES, head_cols // CORES)
    qkv_src = qkv_src.transpose(2, 3, 0, 1, 4).reshape(chips, CORES, rows, -1)
    w_out = lax.all_gather(
        attn_weights[:, 3 * model_width :].astype(jnp.bfloat16), ALL, axis=0, tiled=True
    )
    qk_gain = lax.dynamic_slice_in_dim(feature_gains[:, 0], chip * head_cols, head_cols)
    qk_gain = qk_gain.reshape(heads, 1, HEAD_DIM)
    places = block_place[0].reshape(chips, CORES)
    offsets = jnp.arange(tok_rows, dtype=jnp.int32)
    own_places = jnp.sum(
        jnp.where(jnp.arange(CORES, dtype=jnp.int32)[None, :] == core, places, 0), axis=1
    )
    query_pos = (own_places[:, None] * tok_rows + offsets).reshape(group_rows, 1)
    key_pos = (places.T[:, :, None] * tok_rows + offsets).reshape(1, CORES * group_rows)
    states_all, w_qkv, w_part, raw, query, both, att, inverse, attx = attend_call(
        states, qkv_src, mlp_weights, qk_gain, query_pos, key_pos
    )
    gain_u = lax.dynamic_slice_in_dim(unit_gains[:, 0], chip * units, units)
    gain_v = lax.dynamic_slice_in_dim(unit_gains[:, 1], chip * units, units) * math.sqrt(D)
    (
        out_low, grad_attx, grad_w_out, grad_direct, grad_alpha_a, grad_alpha_m, grad_s_u, grad_s_v, grad_half
    ) = mlp_call(
        attx, states, cotangent, w_out.reshape(chips, head_cols, model_width),
        feature_gains[:, 1].reshape(1, model_width), feature_gains[:, 2].reshape(1, model_width),
        gain_u.reshape(CORES, 1, units // CORES), gain_v.reshape(CORES, 1, units // CORES), w_part,
    )
    small = jnp.concatenate(
        [
            grad_alpha_a, grad_alpha_m, grad_s_u.reshape(1, units),
            grad_s_v.reshape(1, units) * math.sqrt(D), jnp.zeros((4, units), jnp.float32),
        ]
    )
    grad_states, grad_mlp, grad_qkv, grad_proj, small = back_call(
        grad_attx, grad_half, grad_w_out, small, raw, query, both, att, inverse, states_all,
        w_qkv, qk_gain, query_pos, key_pos, grad_direct, rows,
    )
    grad_qkv = grad_qkv.reshape(CORES, chips, rows, 3, head_cols // CORES)
    grad_qkv = grad_qkv.transpose(2, 3, 1, 0, 4).reshape(rows, 3 * model_width)
    feature = jnp.stack(
        [small[:, 4, :head_cols].reshape(-1), jnp.sum(small[:, 0], axis=0), jnp.sum(small[:, 1], axis=0)],
        axis=1,
    )
    unit = jnp.stack([small[:, 2].reshape(-1), small[:, 3].reshape(-1)], axis=1)
    rank = lax.axis_index(ALL)
    unit_rows_own = ff_width // (n_seq * n_ctx)
    return (
        out_low,
        grad_states,
        jnp.concatenate([grad_qkv, grad_proj], axis=1),
        grad_mlp,
        lax.dynamic_slice_in_dim(feature, rank * rows, rows),
        lax.dynamic_slice_in_dim(unit, rank * unit_rows_own, unit_rows_own),
    )


def solution(mesh):
    in_specs = (
        P(("seq", "ctx"), None),
        P(("seq", "ctx"), None),
        P(("seq", "ctx"), None),
        P(("seq", "ctx"), None),
        P(),
        P(),
        P("seq", None),
    )
    out_specs = (
        P(("seq", "ctx"), None),
        P(("seq", "ctx"), None),
        P(("seq", "ctx"), None),
        P(("seq", "ctx"), None),
        P(("seq", "ctx"), None),
        P(("seq", "ctx"), None),
    )
    chips = mesh.shape["ctx"] // CORES
    shards = shards_split if fits(mesh.shape["seq"], chips) else shards_general
    return jax.shard_map(shards, mesh=mesh, in_specs=in_specs, out_specs=out_specs, check_vma=False)
```

```python
import functools
import math

import jax
import jax.numpy as jnp
from jax import lax
from jax.experimental import pallas as pl
from jax.experimental.pallas import tpu as pltpu
from jax.sharding import PartitionSpec as P

D = 1280
HEADS = 20
HEAD_DIM = 64


EPSILON = 1e-06
NEG_LARGE = -1e30


def unit_rows(values_in):
    factor = lax.rsqrt(jnp.sum(values_in * values_in, axis=-1, keepdims=True) + EPSILON)
    return (values_in * factor, factor)


def unit_back(normed, factor, upstream):
    return factor * (upstream - normed * jnp.sum(upstream * normed, axis=-1, keepdims=True))


def contract_rows(left_mat, right_mat):
    return lax.dot_general(
        left_mat, right_mat, (((0,), (0,)), ((), ())), preferred_element_type=jnp.float32
    )


def contract_cols(left_mat, right_mat):
    return lax.dot_general(
        left_mat, right_mat, (((1,), (1,)), ((), ())), preferred_element_type=jnp.float32
    )


def shards_general(states, cotangent, attn_weights, mlp_weights, feature_gains, unit_gains, block_place):
    tok_rows = states.shape[0]
    model_width = states.shape[1]
    ff_width = unit_gains.shape[0]
    score_scale = math.sqrt(HEAD_DIM)
    gate_factor = unit_gains[:, 1] * math.sqrt(D)
    w_attn = lax.all_gather(attn_weights.astype(jnp.bfloat16), ("seq", "ctx"), axis=0, tiled=True)
    w_mlp = lax.all_gather(mlp_weights.astype(jnp.bfloat16), ("seq", "ctx"), axis=0, tiled=True)
    states_full = states.astype(jnp.float32)
    projected = jnp.dot(states, w_attn[:, : 3 * model_width], preferred_element_type=jnp.float32)
    head_shape = (tok_rows, HEADS, HEAD_DIM)
    qk_gain = feature_gains[:, 0].reshape(HEADS, HEAD_DIM)
    query_unit, query_factor = unit_rows(projected[:, :model_width].reshape(head_shape))
    key_unit, key_factor = unit_rows(
        projected[:, model_width : 2 * model_width].reshape(head_shape)
    )
    query_low = (query_unit * qk_gain).astype(jnp.bfloat16)
    key_low = (key_unit * qk_gain).astype(jnp.bfloat16).reshape(tok_rows, model_width)
    value_low = projected[:, 2 * model_width :].astype(jnp.bfloat16)
    keys_all, values_all = (
        lax.all_gather(key_low, "ctx", axis=0, tiled=True),
        lax.all_gather(value_low, "ctx", axis=0, tiled=True),
    )
    seq_len = keys_all.shape[0]
    ctx_lanes = jnp.arange(lax.axis_size("ctx"), dtype=jnp.int32)
    places = block_place[0]
    own_block = jnp.sum(jnp.where(ctx_lanes == lax.axis_index("ctx"), places, 0))
    query_pos = own_block * tok_rows + jnp.arange(tok_rows, dtype=jnp.int32)
    key_index = jnp.arange(seq_len, dtype=jnp.int32)
    key_owner = key_index // tok_rows
    key_pos = (
        jnp.sum(jnp.where(key_owner[:, None] == ctx_lanes[None, :], places[None, :], 0), axis=1)
        * tok_rows
        + key_index % tok_rows
    )
    kblock = min(512, seq_len)
    nblocks = seq_len // kblock
    key_blocks = keys_all.reshape(nblocks, kblock, HEADS, HEAD_DIM)
    value_blocks = values_all.reshape(nblocks, kblock, HEADS, HEAD_DIM)
    pos_blocks = key_pos.reshape(nblocks, kblock)

    def block_scores(key_rows, key_places):
        raw_scores = score_scale * jnp.einsum(
            "qhd,khd->hqk", query_low, key_rows, preferred_element_type=jnp.float32
        )
        allowed = key_places[None, None, :] <= query_pos[None, :, None]
        return (raw_scores, allowed)

    def max_step(running, inputs):
        running_max, running_sum = running
        key_rows, key_places = inputs
        raw_scores, allowed = block_scores(key_rows, key_places)
        masked = jnp.where(allowed, raw_scores, NEG_LARGE)
        new_max = jnp.maximum(running_max, jnp.max(masked, axis=-1))
        powered = jnp.where(allowed, jnp.exp(masked - new_max[..., None]), 0.0)
        running_sum = running_sum * jnp.exp(running_max - new_max) + jnp.sum(powered, axis=-1)
        return ((new_max, running_sum), None)

    start_max = jnp.full((HEADS, tok_rows), NEG_LARGE, jnp.float32)
    start_sum = jnp.zeros((HEADS, tok_rows), jnp.float32)
    (final_max, final_sum), _ = lax.scan(max_step, (start_max, start_sum), (key_blocks, pos_blocks))
    log_total = final_max + jnp.log(final_sum)

    def value_step(accumulated, inputs):
        key_rows, value_rows, key_places = inputs
        raw_scores, allowed = block_scores(key_rows, key_places)
        weights_low = jnp.where(allowed, jnp.exp(raw_scores - log_total[..., None]), 0.0).astype(
            jnp.bfloat16
        )
        accumulated = accumulated + jnp.einsum(
            "hqk,khd->qhd", weights_low, value_rows, preferred_element_type=jnp.float32
        )
        return (accumulated, None)

    attended, _ = lax.scan(
        value_step, jnp.zeros(head_shape, jnp.float32), (key_blocks, value_blocks, pos_blocks)
    )
    attended_low = attended.reshape(tok_rows, model_width).astype(jnp.bfloat16)
    branch_attn = jnp.dot(
        attended_low, w_attn[:, 3 * model_width :], preferred_element_type=jnp.float32
    )
    attn_unit, attn_factor = unit_rows(branch_attn)
    alpha_attn = feature_gains[:, 1]
    mixed_one, mix_factor = unit_rows(states_full + alpha_attn * (attn_unit - states_full))
    mixed_low = mixed_one.astype(jnp.bfloat16)
    up_gate = jnp.dot(mixed_low, w_mlp[:, : 2 * ff_width], preferred_element_type=jnp.float32)
    up_scaled = up_gate[:, :ff_width] * unit_gains[:, 0]
    gate_scaled = up_gate[:, ff_width:] * gate_factor
    sigmoid_gate = jax.nn.sigmoid(gate_scaled)
    activated = gate_scaled * sigmoid_gate
    hidden = (activated * up_scaled).astype(jnp.bfloat16)
    branch_mlp = contract_cols(hidden, w_mlp[:, 2 * ff_width :])
    mlp_unit, mlp_factor = unit_rows(branch_mlp)
    alpha_mlp = feature_gains[:, 2]
    out_full, out_factor = unit_rows(mixed_one + alpha_mlp * (mlp_unit - mixed_one))
    grad_mix_two = unit_back(out_full, out_factor, cotangent.astype(jnp.float32))
    grad_alpha_m = jnp.sum(grad_mix_two * (mlp_unit - mixed_one), axis=0)
    grad_branch_mlp = unit_back(mlp_unit, mlp_factor, grad_mix_two * alpha_mlp).astype(jnp.bfloat16)
    grad_hidden = jnp.dot(
        grad_branch_mlp, w_mlp[:, 2 * ff_width :], preferred_element_type=jnp.float32
    )
    grad_up_scaled = grad_hidden * activated
    grad_gate_scaled = (
        grad_hidden * up_scaled * sigmoid_gate * (1.0 + gate_scaled * (1.0 - sigmoid_gate))
    )
    grad_s_u = jnp.sum(grad_up_scaled * up_gate[:, :ff_width], axis=0)
    grad_s_v = jnp.sum(grad_gate_scaled * up_gate[:, ff_width:], axis=0) * math.sqrt(D)
    grad_up_gate = jnp.concatenate(
        [grad_up_scaled * unit_gains[:, 0], grad_gate_scaled * gate_factor], axis=1
    ).astype(jnp.bfloat16)
    grad_mixed_one = grad_mix_two * (1.0 - alpha_mlp) + contract_cols(
        grad_up_gate, w_mlp[:, : 2 * ff_width]
    )
    grad_mix_one = unit_back(mixed_one, mix_factor, grad_mixed_one)
    grad_alpha_a = jnp.sum(grad_mix_one * (attn_unit - states_full), axis=0)
    grad_branch_attn = unit_back(attn_unit, attn_factor, grad_mix_one * alpha_attn).astype(
        jnp.bfloat16
    )
    grad_attended = (
        contract_cols(grad_branch_attn, w_attn[:, 3 * model_width :])
        .astype(jnp.bfloat16)
        .reshape(head_shape)
    )
    row_dots = jnp.einsum("qhd,qhd->hq", grad_attended.astype(jnp.float32), attended)

    def grad_step(grad_query, inputs):
        key_rows, value_rows, key_places = inputs
        raw_scores, allowed = block_scores(key_rows, key_places)
        probabilities = jnp.where(allowed, jnp.exp(raw_scores - log_total[..., None]), 0.0)
        grad_prob = jnp.einsum(
            "qhd,khd->hqk", grad_attended, value_rows, preferred_element_type=jnp.float32
        )
        grad_scores = (probabilities * (grad_prob - row_dots[..., None])).astype(jnp.bfloat16)
        grad_query = grad_query + score_scale * jnp.einsum(
            "hqk,khd->qhd", grad_scores, key_rows, preferred_element_type=jnp.float32
        )
        key_terms = score_scale * jnp.einsum(
            "hqk,qhd->khd", grad_scores, query_low, preferred_element_type=jnp.float32
        )
        value_terms = jnp.einsum(
            "hqk,qhd->khd",
            probabilities.astype(jnp.bfloat16),
            grad_attended,
            preferred_element_type=jnp.float32,
        )
        return (grad_query, (key_terms, value_terms))

    grad_query_low, (key_terms, value_terms) = lax.scan(
        grad_step, jnp.zeros(head_shape, jnp.float32), (key_blocks, value_blocks, pos_blocks)
    )
    key_terms = key_terms.reshape(seq_len, model_width)
    value_terms = value_terms.reshape(seq_len, model_width)
    own_key_grad, own_value_grad = (
        lax.psum_scatter(
            key_terms.astype(jnp.bfloat16), "ctx", scatter_dimension=0, tiled=True
        ).astype(jnp.float32),
        lax.psum_scatter(
            value_terms.astype(jnp.bfloat16), "ctx", scatter_dimension=0, tiled=True
        ).astype(jnp.float32),
    )
    grad_key_low = own_key_grad.reshape(head_shape)
    grad_s_qk = jnp.sum(grad_query_low * query_unit + grad_key_low * key_unit, axis=0).reshape(
        model_width
    )
    grad_query_raw = unit_back(query_unit, query_factor, grad_query_low * qk_gain).reshape(
        tok_rows, model_width
    )
    grad_key_raw = unit_back(key_unit, key_factor, grad_key_low * qk_gain).reshape(
        tok_rows, model_width
    )
    grad_projected = jnp.concatenate([grad_query_raw, grad_key_raw, own_value_grad], axis=1).astype(
        jnp.bfloat16
    )
    grad_states = grad_mix_one * (1.0 - alpha_attn) + contract_cols(
        grad_projected, w_attn[:, : 3 * model_width]
    )
    feature_total = jnp.stack([grad_s_qk, grad_alpha_a, grad_alpha_m], axis=1)
    unit_fold = jnp.stack([grad_s_u, grad_s_v], axis=1).reshape(
        model_width, 2 * ff_width // model_width
    )
    attn_cols = 4 * model_width
    mlp_cols = 3 * ff_width
    attn_share = lax.psum_scatter(
        jnp.concatenate(
            [
                contract_rows(states, grad_projected),
                contract_rows(attended_low, grad_branch_attn),
                feature_total,
            ],
            axis=1,
        ),
        ("seq", "ctx"),
        scatter_dimension=0,
        tiled=True,
    )
    mlp_share = lax.psum_scatter(
        jnp.concatenate(
            [
                contract_rows(mixed_low, grad_up_gate),
                contract_rows(grad_branch_mlp, hidden),
                unit_fold,
            ],
            axis=1,
        ),
        ("seq", "ctx"),
        scatter_dimension=0,
        tiled=True,
    )
    grad_attn = attn_share[:, :attn_cols]
    grad_feature = attn_share[:, attn_cols:]
    grad_mlp = mlp_share[:, :mlp_cols]
    grad_unit = mlp_share[:, mlp_cols:].reshape(
        unit_gains.shape[0] // lax.axis_size(("seq", "ctx")), 2
    )
    return (
        out_full.astype(jnp.bfloat16),
        grad_states.astype(jnp.bfloat16),
        grad_attn,
        grad_mlp,
        grad_feature,
        grad_unit,
    )


CORES = 2
ALL = ("seq", "ctx")


def fits(n_seq, chips):
    return n_seq == 4 and chips == 4 and HEADS % chips == 0


MESH = pl.DeviceIdType.MESH
VMEM = pltpu.VMEM
CHIPS = 4
STEPS = (1, 2, 3)
LIMIT = 60 * 1024 * 1024


def place_of():
    seq = lax.axis_index("seq")
    ctx = lax.axis_index("ctx")
    return seq, ctx // CORES, ctx % CORES


def chip_peer(step):
    seq, chip, core = place_of()
    other = lax.rem(chip + step, CHIPS)
    return (seq, other * CORES + core), other


def seq_peer(step):
    seq, chip, core = place_of()
    other = seq ^ step
    return (other, chip * CORES + core), other


def twin():
    seq, chip, core = place_of()
    return (seq, chip * CORES + 1 - core)


def meet():
    devices = [chip_peer(step)[0] for step in STEPS] + [seq_peer(step)[0] for step in STEPS] + [twin()]
    gate = pltpu.get_barrier_semaphore()
    for device in devices:
        pl.semaphore_signal(gate, inc=1, device_id=device, device_id_type=MESH)
    pl.semaphore_wait(gate, len(devices))


def remote(src, dst, send, recv, device):
    return pltpu.make_async_remote_copy(
        src_ref=src, dst_ref=dst, send_sem=send, recv_sem=recv, device_id=device,
        device_id_type=MESH,
    )


def begin(copy):
    copy.start()
    return copy


def rows_at(index, count):
    return pl.ds(pl.multiple_of(index * count, count), count)


def device_on(chip):
    seq, _, core = place_of()
    return (seq, chip * CORES + core)


def when(condition, action):
    pl.when(condition)(action)


PIECES = 2


def piece_at(block, piece, count):
    step = count // PIECES
    return pl.ds(pl.multiple_of(block * count + piece * step, step), step)


def gather_copy(src, everything, count, block, side, hop, piece, send, recv):
    chip = place_of()[1]
    there = everything.at[piece_at(block, piece, count)]
    near = chip + 1 if side == 0 else chip - 1
    here = there if src is None else src.at[piece_at(0, piece, count)]
    return remote(here, there, send.at[side, hop, piece], recv.at[side, hop, piece], device_on(near))


def gather_start(src, everything, count, send, recv):
    chip = place_of()[1]
    for piece in range(PIECES):
        for side in range(2):
            copy = gather_copy(src, everything, count, chip, side, 0, piece, send, recv)
            when(chip < CHIPS - 1 if side == 0 else chip > 0, copy.start)


def gather_hop(everything, count, hop, send, recv):
    chip = place_of()[1]
    for piece in range(PIECES):
        for side in range(2):
            block = chip - hop if side == 0 else chip + hop

            def pass_on(side=side, piece=piece, block=block):
                gather_copy(None, everything, count, block, side, hop - 1, piece, send, recv).wait_recv()
                if hop < CHIPS - 1:
                    copy = gather_copy(None, everything, count, block, side, hop, piece, send, recv)
                    when(chip < CHIPS - 1 if side == 0 else chip > 0, copy.start)

            when(block >= 0 if side == 0 else block < CHIPS, pass_on)


def gather_drain(everything, count, send, recv):
    chip = place_of()[1]
    for hop in range(CHIPS - 1):
        for piece in range(PIECES):
            for side in range(2):
                copy = gather_copy(None, everything, count, chip, side, hop, piece, send, recv)
                block = chip - hop if side == 0 else chip + hop
                sent = (block >= 0) & (chip < CHIPS - 1) if side == 0 else (block < CHIPS) & (chip > 0)
                when(sent, copy.wait_send)


def inside_line():
    chip = place_of()[1]
    return (chip > 0) & (chip < CHIPS - 1)


def spans_line(other):
    return abs(place_of()[1] - other) == CHIPS - 1


def reduce_start(part, count, sums, via, send, recv):
    chip = place_of()[1]
    near = jnp.where(chip == 0, 1, CHIPS - 2)
    first = remote(part.at[rows_at(CHIPS - 1 - chip, count)], via, send.at[0], recv.at[0], device_on(near))

    def ahead():
        first.start()
        first.wait_send()

    when(jnp.logical_not(inside_line()), ahead)
    for step in STEPS:
        device, other = chip_peer(step)
        copy = remote(part.at[rows_at(other, count)], sums.at[step - 1], send.at[step], recv.at[step], device)
        if step == 2:
            when(jnp.logical_not(inside_line()), copy.start)
        else:
            when(jnp.logical_not(spans_line(other)), copy.start)


def reduce_relay(part, count, sums, via, mixed, send, recv):
    chip = place_of()[1]
    other = lax.rem(chip + 2, CHIPS)
    copy = remote(mixed, sums.at[1], send.at[2], recv.at[2], device_on(other))

    def pass_on():
        remote(mixed, via, send.at[0], recv.at[0], device_on(other)).wait_recv()
        mixed[...] = (
            part[rows_at(other, count), :].astype(jnp.float32) + via[...].astype(jnp.float32)
        ).astype(mixed.dtype)
        copy.start()

    when(inside_line(), pass_on)


def reduce_wait(part, count, sums, total, send, recv):
    chip = place_of()[1]
    total[...] = part[rows_at(chip, count), :].astype(jnp.float32)
    for step in (1, 3, 2):
        source = lax.rem(chip + CHIPS - step, CHIPS)

        def add(step=step, source=source):
            here = sums.at[step - 1]
            remote(here, here, send.at[step], recv.at[step], device_on(source)).wait_recv()
            total[...] += sums[step - 1].astype(jnp.float32)

        when(jnp.logical_not(spans_line(source)), add)


def reduce_drain(part, count, sums, send, recv):
    rows = part.at[rows_at(0, count)]
    for step in STEPS:
        device, other = chip_peer(step)
        copy = remote(rows, sums.at[step - 1], send.at[step], recv.at[step], device)
        when(jnp.logical_not(spans_line(other)), copy.wait_send)


def to_line(src, there, send, recv):
    return [
        begin(remote(src, there, send.at[step], recv.at[step], chip_peer(step)[0])) for step in STEPS
    ]


def dot(left, right):
    return jnp.dot(left, right, preferred_element_type=jnp.float32)


def dot_nt(left, right):
    return lax.dot_general(
        left, right, (((1,), (1,)), ((), ())), preferred_element_type=jnp.float32
    )


def dot_tn(left, right):
    return lax.dot_general(
        left, right, (((0,), (0,)), ((), ())), preferred_element_type=jnp.float32
    )


def dma(*shape):
    return pltpu.SemaphoreType.DMA(shape)


def line_dma():
    return dma(2, CHIPS, PIECES)


def in_vmem():
    return pl.BlockSpec(memory_space=pltpu.VMEM)


def in_hbm():
    return pl.BlockSpec(memory_space=pl.ANY)


def attend_kernel(
    states, qkv_src, mlp_src, qk_gain, query_pos, key_pos,
    states_all, w_qkv, w_up, w_gate, low_down, raw_out, query_out, both, att_out, inv_out, attx,
    stage_q, low_q, stage_m, low_m, raw, att_low,
    local_sem, x_send, x_recv, q_send, q_recv, mt_send, mt_recv, wz_send, wz_recv,
    ws_send, ws_recv, wt_send, wt_recv, m_send, m_recv, ms_send, ms_recv, kv_send, kv_recv, a_send, a_recv,
):
    seq, chip, core = place_of()
    rows = qkv_src.shape[2]
    half_cols = qkv_src.shape[3]
    part_cols = half_cols // 3
    tok_rows = states.shape[0]
    heads = qk_gain.shape[0]
    head_cols = heads * HEAD_DIM
    group_rows = tok_rows * CHIPS
    chip_rows = CORES * rows
    seq_rows = CHIPS * chip_rows
    half_units = w_up.shape[1]
    ff_width = mlp_src.shape[1] // 3
    meet()
    block = rows_at(chip, tok_rows)
    mine = rows_at(core, rows)
    swaps = [
        begin(remote(qkv_src.at[at, 1 - core], stage_q.at[at, mine], q_send.at[at], q_recv.at[at], twin()))
        for at in range(CHIPS)
    ]
    keeps = [
        begin(pltpu.make_async_copy(qkv_src.at[at, core], stage_q.at[at, mine], local_sem.at[at]))
        for at in range(CHIPS)
    ]
    states_all[block, :] = states[...]
    m_swaps, m_keeps = [], []
    for part in range(3):
        for at in range(CHIPS):
            start = part * ff_width + at * CORES * half_units
            theirs = pl.ds(pl.multiple_of(start + (1 - core) * half_units, 128), half_units)
            ours = pl.ds(pl.multiple_of(start + core * half_units, 128), half_units)
            there = stage_m.at[part, at, mine]
            m_swaps.append(begin(remote(mlp_src.at[:, theirs], there, mt_send.at[part, at], mt_recv.at[part, at], twin())))
            m_keeps.append(begin(pltpu.make_async_copy(mlp_src.at[:, ours], there, local_sem.at[CHIPS + part * CHIPS + at])))
    for copy in keeps:
        copy.wait()
    for copy in swaps:
        copy.wait()
    low_q[...] = stage_q[...].astype(jnp.bfloat16)
    my_rows = rows_at(seq * CHIPS + chip, chip_rows)
    line = []
    for step in STEPS:
        device, other = chip_peer(step)
        line.append(begin(remote(low_q.at[other], w_qkv.at[core, my_rows], wz_send.at[step], wz_recv.at[step], device)))
    w_qkv[core, my_rows, :] = low_q[chip]
    for copy in m_keeps:
        copy.wait()
    for copy in m_swaps:
        copy.wait()
    low_m[...] = stage_m[:2].astype(jnp.bfloat16)
    low_down[...] = stage_m[2].astype(jnp.bfloat16)
    for copy in line:
        copy.wait_recv()
    gather_start(states, states_all, tok_rows, x_send, x_recv)
    seq_at = rows_at(seq, seq_rows)
    seq_part = w_qkv.at[core, seq_at]
    across = [
        begin(remote(seq_part, seq_part, ws_send.at[step], ws_recv.at[step], seq_peer(step)[0]))
        for step in STEPS
    ]
    gather_hop(states_all, tok_rows, 1, x_send, x_recv)
    for copy in across:
        copy.wait_recv()
    swap = begin(remote(w_qkv.at[core], w_qkv.at[core], wt_send.at[0], wt_recv.at[0], twin()))
    gather_hop(states_all, tok_rows, 2, x_send, x_recv)
    gather_hop(states_all, tok_rows, 3, x_send, x_recv)
    here = rows_at(chip, chip_rows)

    def to_chips(part, there):
        return [
            begin(remote(low_m.at[part, chip_peer(step)[1]], there, m_send.at[part, step], m_recv.at[part, step], chip_peer(step)[0]))
            for step in STEPS
        ]

    mine_up = w_up.at[seq_at]
    m_line = to_chips(0, w_up.at[my_rows])
    w_up[my_rows, :] = low_m[0, chip]
    w_gate[here, :] = low_m[1, chip]
    swap.wait()

    for half in range(CORES):
        value = dot(states_all[...], w_qkv[half])
        for which in range(3):
            start = which * head_cols + half * part_cols
            raw[:, start : start + part_cols] = value[:, which * part_cols : (which + 1) * part_cols]
    for head in range(heads):
        gain = qk_gain[head]
        for which in range(2):
            start = which * head_cols + head * HEAD_DIM
            value = raw[:, start : start + HEAD_DIM]
            factor = lax.rsqrt(jnp.sum(value * value, axis=-1, keepdims=True) + EPSILON)
            low = (value * factor * gain).astype(jnp.bfloat16)
            raw_out[which, head] = value
            if which == 0:
                query_out[head] = low * math.sqrt(HEAD_DIM)
            else:
                both[core, 0, head] = low
        start = 2 * head_cols + head * HEAD_DIM
        both[core, 1, head] = raw[:, start : start + HEAD_DIM].astype(jnp.bfloat16)
    swap = begin(remote(both.at[core], both.at[core], kv_send.at[0], kv_recv.at[0], twin()))
    for copy in m_line:
        copy.wait_recv()
    m_line += to_chips(1, w_gate.at[here])
    up_across = [
        begin(remote(mine_up, mine_up, ms_send.at[step], ms_recv.at[step], seq_peer(step)[0]))
        for step in STEPS
    ]
    swap.wait()

    tile = min(128, group_rows)
    tiles = group_rows // tile

    def one_tile(index, carry):
        head = index // tiles
        at = rows_at(lax.rem(index, tiles), tile)
        query = query_out[head, at, :]
        allowed = key_pos[...] <= query_pos[at, :]
        scores = jnp.concatenate([dot_nt(query, both[half, 0, head]) for half in range(CORES)], axis=1)
        powered = jnp.exp(jnp.where(allowed, scores, NEG_LARGE))
        inverse = 1.0 / jnp.sum(powered, axis=-1, keepdims=True)
        weights = (powered * inverse).astype(jnp.bfloat16)
        att_out[head, at, :] = sum(
            dot(weights[:, half * group_rows : (half + 1) * group_rows], both[half, 1, head])
            for half in range(CORES)
        )
        inv_out[head, at, :] = inverse
        return carry

    lax.fori_loop(0, heads * tiles, one_tile, 0)
    for head in range(heads):
        att_low[:, head * HEAD_DIM : (head + 1) * HEAD_DIM] = att_out[head].astype(jnp.bfloat16)
    out = []
    for step in STEPS:
        device, other = chip_peer(step)
        out.append(begin(remote(att_low.at[rows_at(other, tok_rows)], attx.at[chip], a_send.at[step], a_recv.at[step], device)))
    attx[chip] = att_low[block, :]
    for copy in m_line[3:]:
        copy.wait_recv()
    for copy in out + up_across:
        copy.wait()
    gather_drain(states_all, tok_rows, x_send, x_recv)
    for copy in m_line + line + across:
        copy.wait_send()


def attend_call(states, qkv_src, mlp_src, qk_gain, query_pos, key_pos):
    tok_rows, model_width = states.shape
    chips, _, rows, half_cols = qkv_src.shape
    heads = qk_gain.shape[0]
    group_rows = chips * tok_rows
    half_units = mlp_src.shape[1] // 3 // chips // CORES
    f32, low = jnp.float32, jnp.bfloat16
    shape = jax.ShapeDtypeStruct
    return pl.pallas_call(
        attend_kernel,
        out_shape=[
            shape((group_rows, model_width), low),
            shape((CORES, model_width, half_cols), low),
            shape((model_width, half_units), low),
            shape((chips * CORES * rows, half_units), low),
            shape((chips, CORES * rows, half_units), low),
            shape((2, heads, group_rows, HEAD_DIM), f32),
            shape((heads, group_rows, HEAD_DIM), low),
            shape((CORES, 2, heads, group_rows, HEAD_DIM), low),
            shape((heads, group_rows, HEAD_DIM), f32),
            shape((heads, group_rows, 1), f32),
            shape((chips, tok_rows, heads * HEAD_DIM), low),
        ],
        in_specs=[in_vmem(), in_hbm(), in_hbm(), in_vmem(), in_vmem(), in_vmem()],
        out_specs=[in_vmem()] * 11,
        scratch_shapes=[
            VMEM((chips, CORES * rows, half_cols), f32),
            VMEM((chips, CORES * rows, half_cols), low),
            VMEM((3, chips, CORES * rows, half_units), f32),
            VMEM((2, chips, CORES * rows, half_units), low),
            VMEM((group_rows, 3 * heads * HEAD_DIM), f32),
            VMEM((group_rows, heads * HEAD_DIM), low),
            dma(16), line_dma(), line_dma(), dma(4), dma(4), dma(3, 4), dma(3, 4), dma(4), dma(4),
            dma(4), dma(4), dma(1), dma(1), dma(2, 4), dma(2, 4), dma(4), dma(4), dma(1), dma(1), dma(4), dma(4),
        ],
        compiler_params=pltpu.CompilerParams(
            collective_id=1, has_side_effects=True, vmem_limit_bytes=LIMIT
        ),
        name="attend",
    )(states, qkv_src, mlp_src, qk_gain, query_pos, key_pos)


def unit_of(value):
    factor = lax.rsqrt(jnp.sum(value * value, axis=-1, keepdims=True) + EPSILON)
    return value * factor, factor


def mlp_kernel(
    attx, states, cotangent, w_out, alpha_attn, alpha_mlp, gain_u, gain_v, w_up, w_gate, low_down,
    out, grad_attx, grad_w_out, grad_direct, dot_a, dot_m, dot_u, dot_v, grad_half, grad_down,
    weights, mixed_one, attn_unit, factors, mixed_low, mixed_all, up, gate, hidden, part,
    sums, via, passed, total, grad_two, branch_low, branch_all, grad_u, grad_v, wide, turned, arrived,
    w_down, down_half, down_got,
    local_sem, ws_send, ws_recv, wt_send, wt_recv, x_send, x_recv, r_send, r_recv,
    g_send, g_recv, b_send, b_recv, d_send, d_recv, wz_send, wz_recv, ds_send, ds_recv,
):
    seq, chip, core = place_of()
    tok_rows, model_width = states.shape
    chip_heads = attx.shape[2]
    seq_rows, half_units = w_gate.shape
    chip_rows = low_down.shape[1]
    group_rows = CHIPS * tok_rows
    block = rows_at(chip, tok_rows)
    meet()
    seq_at = rows_at(seq, seq_rows)
    here = rows_at(chip, chip_rows)
    swaps = [begin(remote(w_up, weights.at[0, core], wt_send.at[0], wt_recv.at[0], twin()))]
    to_chips = [
        begin(remote(low_down.at[chip_peer(step)[1]], w_down.at[here], wz_send.at[step], wz_recv.at[step], chip_peer(step)[0]))
        for step in STEPS
    ]

    def spread(which, src):
        return [
            begin(remote(src, weights.at[which, core, seq_at], ws_send.at[which, step], ws_recv.at[which, step], seq_peer(step)[0]))
            for step in STEPS
        ]

    across = spread(1, w_gate)
    keeps = [
        begin(pltpu.make_async_copy(w_up, weights.at[0, core], local_sem.at[0])),
        begin(pltpu.make_async_copy(w_gate, weights.at[1, core, seq_at], local_sem.at[1])),
    ]
    w_down[here, :] = low_down[chip]
    branch = sum(dot(attx[at], w_out[at]) for at in range(CHIPS))
    unit, factor = unit_of(branch)
    attn_unit[...] = unit
    factors[0] = factor
    base = states[...].astype(jnp.float32)
    value, factor = unit_of(base + alpha_attn[...] * (unit - base))
    mixed_one[...] = value
    factors[1] = factor
    mixed_low[...] = value.astype(jnp.bfloat16)
    gather_start(mixed_low, mixed_all, tok_rows, x_send, x_recv)
    mixed_all[block, :] = mixed_low[...]
    for copy in keeps:
        copy.wait()
    for copy in to_chips:
        copy.wait_recv()
    gather_hop(mixed_all, tok_rows, 1, x_send, x_recv)
    for copy in across:
        copy.wait_recv()
    across += spread(2, w_down)
    weights[2, core, seq_at, :] = w_down[...]
    swaps.append(begin(remote(weights.at[1, core], weights.at[1, core], wt_send.at[1], wt_recv.at[1], twin())))
    gather_hop(mixed_all, tok_rows, 2, x_send, x_recv)
    gather_hop(mixed_all, tok_rows, 3, x_send, x_recv)
    for copy in swaps:
        copy.wait_recv()
    for half in range(CORES):
        up[half] = dot(mixed_all[...], weights[0, half])
        gate[half] = dot(mixed_all[...], weights[1, half])
    slab = min(64, group_rows)
    slabs = group_rows // slab

    def activate(index, carry):
        half = index // slabs
        at = rows_at(lax.rem(index, slabs), slab)
        gated = gate[half, at, :] * gain_v[half]
        scaled = up[half, at, :] * gain_u[half]
        hidden[half, at, :] = (gated * jax.nn.sigmoid(gated) * scaled).astype(jnp.bfloat16)
        return carry

    lax.fori_loop(0, CORES * slabs, activate, 0)
    for copy in across[-3:]:
        copy.wait_recv()
    swap = begin(remote(weights.at[2, core], weights.at[2, core], wt_send.at[2], wt_recv.at[2], twin()))
    swaps.append(swap)
    swap.wait_recv()
    tile = model_width // 5

    def down(index, carry):
        at = rows_at(index, tile)
        part[0, :, at] = sum(dot_nt(hidden[half], weights[2, half, at, :]) for half in range(CORES)).astype(jnp.bfloat16)
        return carry

    lax.fori_loop(0, model_width // tile, down, 0)

    reduce_start(part.at[0], tok_rows, sums.at[0], via.at[0], r_send, r_recv)
    reduce_relay(part.at[0], tok_rows, sums.at[0], via.at[0], passed.at[0], r_send, r_recv)
    reduce_wait(part.at[0], tok_rows, sums.at[0], total, r_send, r_recv)
    mlp_unit, mlp_factor = unit_of(total[...])
    value, factor = unit_of(mixed_one[...] + alpha_mlp[...] * (mlp_unit - mixed_one[...]))
    out[...] = value.astype(jnp.bfloat16)
    above = cotangent[...].astype(jnp.float32)
    grad = factor * (above - value * jnp.sum(above * value, axis=-1, keepdims=True))
    grad_two[...] = grad
    dot_m[...] = jnp.sum(grad * (mlp_unit - mixed_one[...]), axis=0, keepdims=True)
    grad = grad * alpha_mlp[...]
    grad = mlp_factor * (grad - mlp_unit * jnp.sum(grad * mlp_unit, axis=-1, keepdims=True))
    branch_low[...] = grad.astype(jnp.bfloat16)
    gather_start(branch_low, branch_all, tok_rows, g_send, g_recv)
    branch_all[block, :] = branch_low[...]
    gather_hop(branch_all, tok_rows, 1, g_send, g_recv)
    gather_hop(branch_all, tok_rows, 2, g_send, g_recv)
    turned[0] = mixed_all[...].T
    gather_hop(branch_all, tok_rows, 3, g_send, g_recv)
    for half in range(CORES):
        wide[half] = dot(branch_all[...], weights[2, half])
    dot_u[...] = jnp.zeros_like(dot_u)
    dot_v[...] = jnp.zeros_like(dot_v)

    def deactivate(index, carry):
        half = index // slabs
        at = rows_at(lax.rem(index, slabs), slab)
        gated = gate[half, at, :] * gain_v[half]
        scaled = up[half, at, :] * gain_u[half]
        upstream = wide[half, at, :]
        sig = jax.nn.sigmoid(gated)
        to_up = upstream * (gated * sig)
        to_gate = upstream * scaled * sig * (1.0 + gated * (1.0 - sig))
        dot_u[half] += jnp.sum(to_up * up[half, at, :], axis=0, keepdims=True)
        dot_v[half] += jnp.sum(to_gate * gate[half, at, :], axis=0, keepdims=True)
        grad_u[half, at, :] = (to_up * gain_u[half]).astype(jnp.bfloat16)
        grad_v[half, at, :] = (to_gate * gain_v[half]).astype(jnp.bfloat16)
        return carry

    lax.fori_loop(0, CORES * slabs, deactivate, 0)

    def back_down(index, carry):
        at = rows_at(index, tile)
        part[1, :, at] = sum(
            dot_nt(grad_u[half], weights[0, half, at, :]) + dot_nt(grad_v[half], weights[1, half, at, :])
            for half in range(CORES)
        ).astype(jnp.bfloat16)
        return carry

    lax.fori_loop(0, model_width // tile, back_down, 0)
    for copy in swaps:
        copy.wait_send()
    reduce_start(part.at[1], tok_rows, sums.at[1], via.at[1], b_send, b_recv)
    turned[1] = branch_all[...].T
    swaps = {}

    def weight_grads(which, left, right):
        def one(index, carry):
            half = index // 5
            at = rows_at(lax.rem(index, 5), tile)
            weights[which, half, at, :] = dot(turned[left, at, :], right[half]).astype(jnp.bfloat16)
            return carry

        lax.fori_loop(0, CORES * 5, one, 0)
        swaps[which] = begin(remote(weights.at[which, 1 - core], arrived.at[which], d_send.at[which], d_recv.at[which], twin()))

    def both_cores(which):
        swaps[which].wait_recv()
        return (weights[which, core].astype(jnp.float32) + arrived[which].astype(jnp.float32)).astype(jnp.bfloat16)

    weight_grads(2, 1, hidden)
    reduce_relay(part.at[1], tok_rows, sums.at[1], via.at[1], passed.at[1], b_send, b_recv)
    down_half[...] = both_cores(2)
    down_across = [
        begin(remote(down_half.at[rows_at(seq_peer(step)[1], seq_rows)], down_got.at[step - 1], ds_send.at[step], ds_recv.at[step], seq_peer(step)[0]))
        for step in STEPS
    ]
    weight_grads(0, 0, grad_u)
    weight_grads(1, 0, grad_v)
    reduce_wait(part.at[1], tok_rows, sums.at[1], total, b_send, b_recv)
    grad = grad_two[...] * (1.0 - alpha_mlp[...]) + total[...]
    value = mixed_one[...]
    grad = factors[1] * (grad - value * jnp.sum(grad * value, axis=-1, keepdims=True))
    unit = attn_unit[...]
    dot_a[...] = jnp.sum(grad * (unit - states[...].astype(jnp.float32)), axis=0, keepdims=True)
    grad_direct[...] = grad * (1.0 - alpha_attn[...])
    grad = grad * alpha_attn[...]
    grad = factors[0] * (grad - unit * jnp.sum(grad * unit, axis=-1, keepdims=True))
    low = grad.astype(jnp.bfloat16)
    for at in range(CHIPS):
        grad_attx[at] = dot_nt(low, w_out[at]).astype(jnp.bfloat16)
        grad_w_out[at] = dot_tn(attx[at], low).astype(jnp.bfloat16)
    for which in range(2):
        grad_half[which] = both_cores(which)
    whole = down_half[seq_at, :].astype(jnp.float32)
    for step in STEPS:
        down_across[step - 1].wait_recv()
        whole = whole + down_got[step - 1].astype(jnp.float32)
    grad_down[...] = whole.astype(jnp.bfloat16)
    gather_drain(mixed_all, tok_rows, x_send, x_recv)
    gather_drain(branch_all, tok_rows, g_send, g_recv)
    reduce_drain(part.at[0], tok_rows, sums.at[0], r_send, r_recv)
    reduce_drain(part.at[1], tok_rows, sums.at[1], b_send, b_recv)
    for copy in across + to_chips + down_across + [swaps[which] for which in range(3)]:
        copy.wait_send()


def mlp_call(attx, states, cotangent, w_out, alpha_attn, alpha_mlp, gain_u, gain_v, w_up, w_gate, low_down):
    tok_rows, model_width = states.shape
    chips, _, chip_heads = attx.shape
    seq_rows, half_units = w_gate.shape
    group_rows = chips * tok_rows
    f32, low = jnp.float32, jnp.bfloat16
    shape = jax.ShapeDtypeStruct
    tokens, group = (tok_rows, model_width), (group_rows, model_width)
    wide = (CORES, group_rows, half_units)
    matrix = (model_width, half_units)
    return pl.pallas_call(
        mlp_kernel,
        out_shape=[
            shape(tokens, low),
            shape(attx.shape, low),
            shape((chips, chip_heads, model_width), low),
            shape(tokens, f32),
            shape((1, model_width), f32),
            shape((1, model_width), f32),
            shape((CORES, 1, half_units), f32),
            shape((CORES, 1, half_units), f32),
            shape((2,) + matrix, low),
            shape((seq_rows, half_units), low),
        ],
        in_specs=[in_vmem()] * 8 + [in_hbm(), in_vmem(), in_vmem()],
        out_specs=[in_vmem()] * 10,
        scratch_shapes=[
            VMEM((3, CORES) + matrix, low),
            VMEM(tokens, f32),
            VMEM(tokens, f32),
            VMEM((2, tok_rows, 1), f32),
            VMEM(tokens, low),
            VMEM(group, low),
            VMEM(wide, f32),
            VMEM(wide, f32),
            VMEM(wide, low),
            VMEM((2,) + group, low),
            VMEM((2, 3) + tokens, low),
            VMEM((2,) + tokens, low),
            VMEM((2,) + tokens, low),
            VMEM(tokens, f32),
            VMEM(tokens, f32),
            VMEM(tokens, low),
            VMEM(group, low),
            VMEM(wide, low),
            VMEM(wide, low),
            VMEM(wide, f32),
            VMEM((2, model_width, group_rows), low),
            VMEM((3,) + matrix, low),
            VMEM((seq_rows, half_units), low),
            VMEM(matrix, low),
            VMEM((3, seq_rows, half_units), low),
            dma(2), dma(3, 4), dma(3, 4), dma(3), dma(3), line_dma(), line_dma(), dma(4), dma(4),
            line_dma(), line_dma(), dma(4), dma(4), dma(3), dma(3), dma(4), dma(4), dma(4), dma(4),
        ],
        compiler_params=pltpu.CompilerParams(
            collective_id=2, has_side_effects=True, vmem_limit_bytes=LIMIT
        ),
        name="mlp",
    )(
        attx, states, cotangent, w_out, alpha_attn, alpha_mlp, gain_u, gain_v, w_up, w_gate, low_down
    )


def back_kernel(
    grad_attx, grad_half, grad_down, grad_w_out, small_in, raw, query, both, att, inverse, states_all,
    w_qkv, qk_gain, query_pos, key_pos, grad_direct,
    grad_states, out_mlp, out_qkv, out_proj, small_out,
    att_low, heads_low, to_keys, swap_low, swap_kv, grad_heads, grad_sides, part, sums, via, passed, total, turned,
    grad_q, half_q, seq_q, line_q, wide_q, half_o, pair_o, seq_got, seq_low, line_got, wide,
    wide_o, small, small_pair, small_seq, dots,
    local_sem, a_send, a_recv, s_send, s_recv, o_send, o_recv, kv_send, kv_recv, r_send, r_recv,
    qt_send, qt_recv, qs_send, qs_recv, qz_send, qz_recv, z_send, z_recv, f_send, f_recv,
    p_send, p_recv, t_send, t_recv,
):
    seq, chip, core = place_of()
    tok_rows, model_width = grad_direct.shape
    heads = qk_gain.shape[0]
    head_cols = heads * HEAD_DIM
    group_rows = CHIPS * tok_rows
    half_units = grad_half.shape[2]
    seq_rows = seq_got.shape[2]
    chip_rows = seq_rows // CHIPS
    rows = chip_rows // CORES
    part_cols = head_cols // CORES
    ff_width = out_mlp.shape[1] // 3
    scale = math.sqrt(HEAD_DIM)
    block = rows_at(chip, tok_rows)
    f32, low = jnp.float32, jnp.bfloat16
    meet()
    waits = []
    line = []
    for step in STEPS:
        device, other = chip_peer(step)
        line.append(begin(remote(grad_attx.at[other], att_low.at[block], a_send.at[step], a_recv.at[step], device)))
    att_low[block, :] = grad_attx[chip]
    half_at = pl.ds(pl.multiple_of(core * half_units, 128), half_units)
    other_at = pl.ds(pl.multiple_of((1 - core) * half_units, 128), half_units)
    pair = begin(remote(grad_w_out.at[:, :, other_at], pair_o, o_send.at[0], o_recv.at[0], twin()))
    across = []
    onward = {}

    def to_chips(which, src):
        onward[which] = [
            begin(remote(src.at[rows_at(chip_peer(step)[1], chip_rows)], line_got.at[which, chip], z_send.at[which, step], z_recv.at[which, step], chip_peer(step)[0]))
            for step in STEPS
        ]
        line_got[which, chip] = src[rows_at(chip, chip_rows), :]

    to_chips(2, grad_down)
    for which in range(2):
        for step in STEPS:
            device, other = seq_peer(step)
            across.append(begin(remote(grad_half.at[which, rows_at(other, seq_rows)], seq_got.at[which, step - 1], s_send.at[which, step], s_recv.at[which, step], device)))
    keeps = [
        begin(pltpu.make_async_copy(grad_half.at[which, rows_at(seq, seq_rows)], seq_low.at[which], local_sem.at[which]))
        for which in range(2)
    ]
    to_keys[...] = jnp.zeros_like(to_keys)
    dots[...] = jnp.zeros_like(dots)
    turned[...] = states_all[...].T
    pair.wait_recv()
    for at in range(4):
        half_o[at] = (grad_w_out[at, :, half_at].astype(f32) + pair_o[at].astype(f32)).astype(low)
    for step in STEPS:
        device, other = seq_peer(step)
        across.append(begin(remote(half_o.at[other], seq_got.at[2, step - 1], s_send.at[2, step], s_recv.at[2, step], device)))
    for copy in line:
        copy.wait_recv()
    for head in range(heads):
        heads_low[head] = att_low[:, head * HEAD_DIM : (head + 1) * HEAD_DIM]

    tile = min(128, group_rows)
    tiles = group_rows // tile

    def raw_back(which, head, at, upstream):
        value = raw[which, head, at, :]
        unit, factor = unit_of(value)
        dots[head] += jnp.sum(upstream * unit, axis=0, keepdims=True)
        upstream = upstream * qk_gain[head]
        upstream = factor * (upstream - unit * jnp.sum(upstream * unit, axis=-1, keepdims=True))
        grad_heads[which, head, at, :] = upstream.astype(low)

    def one_tile(index, carry):
        head = index // tiles
        at = rows_at(lax.rem(index, tiles), tile)
        rows_q = query[head, at, :]
        grad_att = heads_low[head, at, :]
        allowed = key_pos[...] <= query_pos[at, :]
        scores = jnp.concatenate([dot_nt(rows_q, both[half, 0, head]) for half in range(CORES)], axis=1)
        probs = jnp.exp(jnp.where(allowed, scores, NEG_LARGE)) * inverse[head, at, :]
        grad_prob = jnp.concatenate([dot_nt(grad_att, both[half, 1, head]) for half in range(CORES)], axis=1)
        row_dot = jnp.sum(grad_att.astype(f32) * att[head, at, :], axis=-1, keepdims=True)
        grad_scores = (probs * (grad_prob - row_dot)).astype(low)
        weights = probs.astype(low)
        total = jnp.zeros((tile, HEAD_DIM), f32)
        for half in range(CORES):
            cols = slice(half * group_rows, (half + 1) * group_rows)
            total = total + dot(grad_scores[:, cols], both[half, 0, head])
            to_keys[half, 0, head] += dot_tn(grad_scores[:, cols], rows_q)
            to_keys[half, 1, head] += dot_tn(weights[:, cols], grad_att)
        raw_back(0, head, at, total * scale)
        return carry

    lax.fori_loop(0, heads * tiles, one_tile, 0)
    swap_low[...] = to_keys[1 - core].astype(low)
    swap = begin(remote(swap_low, swap_kv, kv_send.at[0], kv_recv.at[0], twin()))
    swap.wait()

    def one_key(index, carry):
        head = index // tiles
        at = rows_at(lax.rem(index, tiles), tile)
        mine = to_keys[core, 0, head, at, :] + swap_kv[0, head, at, :].astype(f32)
        raw_back(1, head, at, mine)
        value = to_keys[core, 1, head, at, :] + swap_kv[1, head, at, :].astype(f32)
        grad_heads[2, head, at, :] = value.astype(low)
        return carry

    lax.fori_loop(0, heads * tiles, one_key, 0)
    for which in range(3):
        full = jnp.concatenate([grad_heads[which, head] for head in range(heads)], axis=1)
        for half in range(CORES):
            grad_sides[half, :, which * part_cols : (which + 1) * part_cols] = full[:, half * part_cols : (half + 1) * part_cols]
    wide_tile = model_width // 5

    def down(index, carry):
        at = rows_at(index, wide_tile)
        part[:, at] = sum(dot_nt(grad_sides[half], w_qkv[half, at, :]) for half in range(CORES)).astype(low)
        return carry

    lax.fori_loop(0, 5, down, 0)
    reduce_start(part, tok_rows, sums, via, r_send, r_recv)

    def weight_grad(index, carry):
        half = index // 5
        at = rows_at(lax.rem(index, 5), wide_tile)
        grad_q[half, at, :] = dot(turned[at, :], grad_sides[half]).astype(low)
        return carry

    lax.fori_loop(0, CORES * 5, weight_grad, 0)
    swap_q = begin(remote(grad_q.at[1 - core], half_q, qt_send.at[0], qt_recv.at[0], twin()))
    reduce_relay(part, tok_rows, sums, via, passed, r_send, r_recv)
    small[...] = small_in[...]
    small[4:5, :head_cols] = jnp.concatenate([dots[head] for head in range(heads)], axis=1)
    swap_s = begin(remote(small, small_pair, t_send.at[0], t_recv.at[0], twin()))
    swap_q.wait()
    half_q[...] = (grad_q[core].astype(f32) + half_q[...].astype(f32)).astype(low)
    across_q = []
    for step in STEPS:
        device, other = seq_peer(step)
        across_q.append(begin(remote(half_q.at[rows_at(other, seq_rows)], seq_q.at[step - 1], qs_send.at[step], qs_recv.at[step], device)))
    swap_s.wait()
    small[...] = small[...] + small_pair[...]
    spread_s = [
        begin(remote(small, small_seq.at[step - 1], t_send.at[step], t_recv.at[step], seq_peer(step)[0]))
        for step in STEPS
    ]
    for copy in keeps:
        copy.wait()
    seq_low[2] = half_o[seq]
    for at, which in enumerate((0, 1, 3)):
        for copy in across[3 * at : 3 * at + 3]:
            copy.wait_recv()
        whole = seq_low[at].astype(f32)
        for step in STEPS:
            whole = whole + seq_got[at, step - 1].astype(f32)
        seq_low[at] = whole.astype(low)
        to_chips(which, seq_low.at[at])
    for copy in across_q:
        copy.wait_recv()
    whole = half_q[rows_at(seq, seq_rows), :].astype(f32)
    for step in STEPS:
        whole = whole + seq_q[step - 1].astype(f32)
    grad_q[0, :seq_rows, :] = whole.astype(low)
    onward_q = []
    for step in STEPS:
        device, other = chip_peer(step)
        onward_q.append(begin(remote(grad_q.at[0, rows_at(other, chip_rows)], line_q.at[chip], qz_send.at[step], qz_recv.at[step], device)))
    line_q[chip] = grad_q[0, rows_at(chip, chip_rows), :]
    for copy in spread_s:
        copy.wait()
    small_pair[...] = small[...] + small_seq[0] + small_seq[1] + small_seq[2]
    small_out[chip] = small_pair[...]
    ends = to_line(small_pair, small_out.at[chip], p_send, p_recv)
    reduce_wait(part, tok_rows, sums, total, r_send, r_recv)
    grad_states[...] = (total[...] + grad_direct[...]).astype(low)

    mine = rows_at(core, rows)
    theirs = rows_at(1 - core, rows)
    last, lasts = [], []
    for which in (2, 0, 1):
        for copy in onward[which]:
            copy.wait_recv()
        for at in range(CHIPS):
            wide[which, at] = line_got[which, at].astype(f32)
            start = which * ff_width + at * CORES * half_units + core * half_units
            there = out_mlp.at[:, pl.ds(pl.multiple_of(start, 128), half_units)]
            last.append(begin(remote(wide.at[which, at, theirs], there, f_send.at[which, at], f_recv.at[which, at], twin())))
            lasts.append(begin(pltpu.make_async_copy(wide.at[which, at, mine], there, local_sem.at[3 + which * CHIPS + at])))
    for copy in onward[3]:
        copy.wait_recv()
    whole = line_got[3, 0].astype(f32)
    for at in range(1, CHIPS):
        whole = whole + line_got[3, at].astype(f32)
    wide_o[...] = whole
    there = out_proj.at[:, half_at]
    last.append(begin(remote(wide_o.at[theirs], there, f_send.at[3, 0], f_recv.at[3, 0], twin())))
    lasts.append(begin(pltpu.make_async_copy(wide_o.at[mine], there, local_sem.at[15])))
    for copy in onward_q:
        copy.wait_recv()
    wide_q[...] = line_q[...].astype(f32)
    there = out_qkv.at[core]
    last.append(begin(remote(wide_q.at[:, theirs], there, f_send.at[3, 1], f_recv.at[3, 1], twin())))
    lasts.append(begin(pltpu.make_async_copy(wide_q.at[:, mine], there, local_sem.at[16])))
    for copy in ends + last + lasts:
        copy.wait()
    reduce_drain(part, tok_rows, sums, r_send, r_recv)
    for copy in line + [pair] + across + across_q + onward_q + sum(onward.values(), []):
        copy.wait_send()


def back_call(
    grad_attx, grad_half, grad_down, grad_w_out, small_in, raw, query, both, att, inverse, states_all,
    w_qkv, qk_gain, query_pos, key_pos, grad_direct, rows,
):
    tok_rows, model_width = grad_direct.shape
    chips = grad_attx.shape[0]
    heads = qk_gain.shape[0]
    head_cols = heads * HEAD_DIM
    group_rows = chips * tok_rows
    half_units = grad_half.shape[2]
    half_cols = w_qkv.shape[2]
    chip_rows = CORES * rows
    seq_rows = chips * chip_rows
    f32, low = jnp.float32, jnp.bfloat16
    shape = jax.ShapeDtypeStruct
    per_head = (heads, group_rows, HEAD_DIM)
    return pl.pallas_call(
        back_kernel,
        out_shape=[
            shape((tok_rows, model_width), low),
            shape((rows, 3 * chips * CORES * half_units), f32),
            shape((CORES, chips, rows, half_cols), f32),
            shape((rows, CORES * half_units), f32),
            shape((chips,) + small_in.shape, f32),
        ],
        in_specs=[in_vmem(), in_hbm()] + [in_vmem()] * 14,
        out_specs=[in_vmem(), in_hbm(), in_hbm(), in_hbm(), in_vmem()],
        scratch_shapes=[
            VMEM((group_rows, head_cols), low),
            VMEM(per_head, low),
            VMEM((CORES, 2) + per_head, f32),
            VMEM((2,) + per_head, low),
            VMEM((2,) + per_head, low),
            VMEM((3,) + per_head, low),
            VMEM((CORES, group_rows, half_cols), low),
            VMEM((group_rows, model_width), low),
            VMEM((3, tok_rows, model_width), low),
            VMEM((tok_rows, model_width), low),
            VMEM((tok_rows, model_width), low),
            VMEM((tok_rows, model_width), f32),
            VMEM((model_width, group_rows), low),
            VMEM((CORES, model_width, half_cols), low),
            VMEM((model_width, half_cols), low),
            VMEM((3, seq_rows, half_cols), low),
            VMEM((chips, chip_rows, half_cols), low),
            VMEM((chips, chip_rows, half_cols), f32),
            VMEM((4, seq_rows, half_units), low),
            VMEM((4, seq_rows, half_units), low),
            VMEM((3, 3, seq_rows, half_units), low),
            VMEM((3, seq_rows, half_units), low),
            VMEM((4, chips, chip_rows, half_units), low),
            VMEM((3, chips, chip_rows, half_units), f32),
            VMEM((chip_rows, half_units), f32),
            VMEM(small_in.shape, f32),
            VMEM(small_in.shape, f32),
            VMEM((3,) + small_in.shape, f32),
            VMEM((heads, 1, HEAD_DIM), f32),
            dma(17), dma(4), dma(4), dma(4, 4), dma(4, 4), dma(1), dma(1), dma(1), dma(1),
            dma(4), dma(4), dma(1), dma(1), dma(4), dma(4), dma(4), dma(4), dma(4, 4), dma(4, 4),
            dma(4, 4), dma(4, 4), dma(4), dma(4), dma(4), dma(4),
        ],
        compiler_params=pltpu.CompilerParams(
            collective_id=3, has_side_effects=True, vmem_limit_bytes=LIMIT
        ),
        name="back",
    )(
        grad_attx, grad_half, grad_down, grad_w_out, small_in, raw, query, both, att, inverse, states_all,
        w_qkv, qk_gain, query_pos, key_pos, grad_direct,
    )


def shards_split(states, cotangent, attn_weights, mlp_weights, feature_gains, unit_gains, block_place):
    tok_rows, model_width = states.shape
    ff_width = unit_gains.shape[0]
    n_seq, n_ctx = lax.axis_size("seq"), lax.axis_size("ctx")
    chips = n_ctx // CORES
    chip = lax.axis_index("ctx") // CORES
    core = lax.axis_index("ctx") % CORES
    heads = HEADS // chips
    head_cols = heads * HEAD_DIM
    units = ff_width // chips
    group_rows = chips * tok_rows
    rows = attn_weights.shape[0]
    qkv_src = attn_weights[:, : 3 * model_width].reshape(rows, 3, chips, CORES, head_cols // CORES)
    qkv_src = qkv_src.transpose(2, 3, 0, 1, 4).reshape(chips, CORES, rows, -1)
    w_out = lax.all_gather(
        attn_weights[:, 3 * model_width :].astype(jnp.bfloat16), ALL, axis=0, tiled=True
    )
    qk_gain = lax.dynamic_slice_in_dim(feature_gains[:, 0], chip * head_cols, head_cols)
    qk_gain = qk_gain.reshape(heads, 1, HEAD_DIM)
    places = block_place[0].reshape(chips, CORES)
    offsets = jnp.arange(tok_rows, dtype=jnp.int32)
    own_places = jnp.sum(
        jnp.where(jnp.arange(CORES, dtype=jnp.int32)[None, :] == core, places, 0), axis=1
    )
    query_pos = (own_places[:, None] * tok_rows + offsets).reshape(group_rows, 1)
    key_pos = (places.T[:, :, None] * tok_rows + offsets).reshape(1, CORES * group_rows)
    states_all, w_qkv, w_up, w_gate, low_down, raw, query, both, att, inverse, attx = attend_call(
        states, qkv_src, mlp_weights, qk_gain, query_pos, key_pos
    )
    gain_u = lax.dynamic_slice_in_dim(unit_gains[:, 0], chip * units, units)
    gain_v = lax.dynamic_slice_in_dim(unit_gains[:, 1], chip * units, units) * math.sqrt(D)
    (
        out_low, grad_attx, grad_w_out, grad_direct, grad_alpha_a, grad_alpha_m, grad_s_u, grad_s_v, grad_half, grad_down
    ) = mlp_call(
        attx, states, cotangent, w_out.reshape(chips, head_cols, model_width),
        feature_gains[:, 1].reshape(1, model_width), feature_gains[:, 2].reshape(1, model_width),
        gain_u.reshape(CORES, 1, units // CORES), gain_v.reshape(CORES, 1, units // CORES), w_up, w_gate, low_down,
    )
    small = jnp.concatenate(
        [
            grad_alpha_a, grad_alpha_m, grad_s_u.reshape(1, units),
            grad_s_v.reshape(1, units) * math.sqrt(D), jnp.zeros((4, units), jnp.float32),
        ]
    )
    grad_states, grad_mlp, grad_qkv, grad_proj, small = back_call(
        grad_attx, grad_half, grad_down, grad_w_out, small, raw, query, both, att, inverse, states_all,
        w_qkv, qk_gain, query_pos, key_pos, grad_direct, rows,
    )
    grad_qkv = grad_qkv.reshape(CORES, chips, rows, 3, head_cols // CORES)
    grad_qkv = grad_qkv.transpose(2, 3, 1, 0, 4).reshape(rows, 3 * model_width)
    feature = jnp.stack(
        [small[:, 4, :head_cols].reshape(-1), jnp.sum(small[:, 0], axis=0), jnp.sum(small[:, 1], axis=0)],
        axis=1,
    )
    unit = jnp.stack([small[:, 2].reshape(-1), small[:, 3].reshape(-1)], axis=1)
    rank = lax.axis_index(ALL)
    unit_rows_own = ff_width // (n_seq * n_ctx)
    return (
        out_low,
        grad_states,
        jnp.concatenate([grad_qkv, grad_proj], axis=1),
        grad_mlp,
        lax.dynamic_slice_in_dim(feature, rank * rows, rows),
        lax.dynamic_slice_in_dim(unit, rank * unit_rows_own, unit_rows_own),
    )


def solution(mesh):
    in_specs = (
        P(("seq", "ctx"), None),
        P(("seq", "ctx"), None),
        P(("seq", "ctx"), None),
        P(("seq", "ctx"), None),
        P(),
        P(),
        P("seq", None),
    )
    out_specs = (
        P(("seq", "ctx"), None),
        P(("seq", "ctx"), None),
        P(("seq", "ctx"), None),
        P(("seq", "ctx"), None),
        P(("seq", "ctx"), None),
        P(("seq", "ctx"), None),
    )
    chips = mesh.shape["ctx"] // CORES
    shards = shards_split if fits(mesh.shape["seq"], chips) else shards_general
    return jax.shard_map(shards, mesh=mesh, in_specs=in_specs, out_specs=out_specs, check_vma=False)
```

```python
import functools
import math

import jax
import jax.numpy as jnp
from jax import lax
from jax.experimental import pallas as pl
from jax.experimental.pallas import tpu as pltpu
from jax.sharding import PartitionSpec as P

D = 1280
HEADS = 20
HEAD_DIM = 64


EPSILON = 1e-06
NEG_LARGE = -1e30


def unit_rows(values_in):
    factor = lax.rsqrt(jnp.sum(values_in * values_in, axis=-1, keepdims=True) + EPSILON)
    return (values_in * factor, factor)


def unit_back(normed, factor, upstream):
    return factor * (upstream - normed * jnp.sum(upstream * normed, axis=-1, keepdims=True))


def contract_rows(left_mat, right_mat):
    return lax.dot_general(
        left_mat, right_mat, (((0,), (0,)), ((), ())), preferred_element_type=jnp.float32
    )


def contract_cols(left_mat, right_mat):
    return lax.dot_general(
        left_mat, right_mat, (((1,), (1,)), ((), ())), preferred_element_type=jnp.float32
    )


def shards_general(states, cotangent, attn_weights, mlp_weights, feature_gains, unit_gains, block_place):
    tok_rows = states.shape[0]
    model_width = states.shape[1]
    ff_width = unit_gains.shape[0]
    score_scale = math.sqrt(HEAD_DIM)
    gate_factor = unit_gains[:, 1] * math.sqrt(D)
    w_attn = lax.all_gather(attn_weights.astype(jnp.bfloat16), ("seq", "ctx"), axis=0, tiled=True)
    w_mlp = lax.all_gather(mlp_weights.astype(jnp.bfloat16), ("seq", "ctx"), axis=0, tiled=True)
    states_full = states.astype(jnp.float32)
    projected = jnp.dot(states, w_attn[:, : 3 * model_width], preferred_element_type=jnp.float32)
    head_shape = (tok_rows, HEADS, HEAD_DIM)
    qk_gain = feature_gains[:, 0].reshape(HEADS, HEAD_DIM)
    query_unit, query_factor = unit_rows(projected[:, :model_width].reshape(head_shape))
    key_unit, key_factor = unit_rows(
        projected[:, model_width : 2 * model_width].reshape(head_shape)
    )
    query_low = (query_unit * qk_gain).astype(jnp.bfloat16)
    key_low = (key_unit * qk_gain).astype(jnp.bfloat16).reshape(tok_rows, model_width)
    value_low = projected[:, 2 * model_width :].astype(jnp.bfloat16)
    keys_all, values_all = (
        lax.all_gather(key_low, "ctx", axis=0, tiled=True),
        lax.all_gather(value_low, "ctx", axis=0, tiled=True),
    )
    seq_len = keys_all.shape[0]
    ctx_lanes = jnp.arange(lax.axis_size("ctx"), dtype=jnp.int32)
    places = block_place[0]
    own_block = jnp.sum(jnp.where(ctx_lanes == lax.axis_index("ctx"), places, 0))
    query_pos = own_block * tok_rows + jnp.arange(tok_rows, dtype=jnp.int32)
    key_index = jnp.arange(seq_len, dtype=jnp.int32)
    key_owner = key_index // tok_rows
    key_pos = (
        jnp.sum(jnp.where(key_owner[:, None] == ctx_lanes[None, :], places[None, :], 0), axis=1)
        * tok_rows
        + key_index % tok_rows
    )
    kblock = min(512, seq_len)
    nblocks = seq_len // kblock
    key_blocks = keys_all.reshape(nblocks, kblock, HEADS, HEAD_DIM)
    value_blocks = values_all.reshape(nblocks, kblock, HEADS, HEAD_DIM)
    pos_blocks = key_pos.reshape(nblocks, kblock)

    def block_scores(key_rows, key_places):
        raw_scores = score_scale * jnp.einsum(
            "qhd,khd->hqk", query_low, key_rows, preferred_element_type=jnp.float32
        )
        allowed = key_places[None, None, :] <= query_pos[None, :, None]
        return (raw_scores, allowed)

    def max_step(running, inputs):
        running_max, running_sum = running
        key_rows, key_places = inputs
        raw_scores, allowed = block_scores(key_rows, key_places)
        masked = jnp.where(allowed, raw_scores, NEG_LARGE)
        new_max = jnp.maximum(running_max, jnp.max(masked, axis=-1))
        powered = jnp.where(allowed, jnp.exp(masked - new_max[..., None]), 0.0)
        running_sum = running_sum * jnp.exp(running_max - new_max) + jnp.sum(powered, axis=-1)
        return ((new_max, running_sum), None)

    start_max = jnp.full((HEADS, tok_rows), NEG_LARGE, jnp.float32)
    start_sum = jnp.zeros((HEADS, tok_rows), jnp.float32)
    (final_max, final_sum), _ = lax.scan(max_step, (start_max, start_sum), (key_blocks, pos_blocks))
    log_total = final_max + jnp.log(final_sum)

    def value_step(accumulated, inputs):
        key_rows, value_rows, key_places = inputs
        raw_scores, allowed = block_scores(key_rows, key_places)
        weights_low = jnp.where(allowed, jnp.exp(raw_scores - log_total[..., None]), 0.0).astype(
            jnp.bfloat16
        )
        accumulated = accumulated + jnp.einsum(
            "hqk,khd->qhd", weights_low, value_rows, preferred_element_type=jnp.float32
        )
        return (accumulated, None)

    attended, _ = lax.scan(
        value_step, jnp.zeros(head_shape, jnp.float32), (key_blocks, value_blocks, pos_blocks)
    )
    attended_low = attended.reshape(tok_rows, model_width).astype(jnp.bfloat16)
    branch_attn = jnp.dot(
        attended_low, w_attn[:, 3 * model_width :], preferred_element_type=jnp.float32
    )
    attn_unit, attn_factor = unit_rows(branch_attn)
    alpha_attn = feature_gains[:, 1]
    mixed_one, mix_factor = unit_rows(states_full + alpha_attn * (attn_unit - states_full))
    mixed_low = mixed_one.astype(jnp.bfloat16)
    up_gate = jnp.dot(mixed_low, w_mlp[:, : 2 * ff_width], preferred_element_type=jnp.float32)
    up_scaled = up_gate[:, :ff_width] * unit_gains[:, 0]
    gate_scaled = up_gate[:, ff_width:] * gate_factor
    sigmoid_gate = jax.nn.sigmoid(gate_scaled)
    activated = gate_scaled * sigmoid_gate
    hidden = (activated * up_scaled).astype(jnp.bfloat16)
    branch_mlp = contract_cols(hidden, w_mlp[:, 2 * ff_width :])
    mlp_unit, mlp_factor = unit_rows(branch_mlp)
    alpha_mlp = feature_gains[:, 2]
    out_full, out_factor = unit_rows(mixed_one + alpha_mlp * (mlp_unit - mixed_one))
    grad_mix_two = unit_back(out_full, out_factor, cotangent.astype(jnp.float32))
    grad_alpha_m = jnp.sum(grad_mix_two * (mlp_unit - mixed_one), axis=0)
    grad_branch_mlp = unit_back(mlp_unit, mlp_factor, grad_mix_two * alpha_mlp).astype(jnp.bfloat16)
    grad_hidden = jnp.dot(
        grad_branch_mlp, w_mlp[:, 2 * ff_width :], preferred_element_type=jnp.float32
    )
    grad_up_scaled = grad_hidden * activated
    grad_gate_scaled = (
        grad_hidden * up_scaled * sigmoid_gate * (1.0 + gate_scaled * (1.0 - sigmoid_gate))
    )
    grad_s_u = jnp.sum(grad_up_scaled * up_gate[:, :ff_width], axis=0)
    grad_s_v = jnp.sum(grad_gate_scaled * up_gate[:, ff_width:], axis=0) * math.sqrt(D)
    grad_up_gate = jnp.concatenate(
        [grad_up_scaled * unit_gains[:, 0], grad_gate_scaled * gate_factor], axis=1
    ).astype(jnp.bfloat16)
    grad_mixed_one = grad_mix_two * (1.0 - alpha_mlp) + contract_cols(
        grad_up_gate, w_mlp[:, : 2 * ff_width]
    )
    grad_mix_one = unit_back(mixed_one, mix_factor, grad_mixed_one)
    grad_alpha_a = jnp.sum(grad_mix_one * (attn_unit - states_full), axis=0)
    grad_branch_attn = unit_back(attn_unit, attn_factor, grad_mix_one * alpha_attn).astype(
        jnp.bfloat16
    )
    grad_attended = (
        contract_cols(grad_branch_attn, w_attn[:, 3 * model_width :])
        .astype(jnp.bfloat16)
        .reshape(head_shape)
    )
    row_dots = jnp.einsum("qhd,qhd->hq", grad_attended.astype(jnp.float32), attended)

    def grad_step(grad_query, inputs):
        key_rows, value_rows, key_places = inputs
        raw_scores, allowed = block_scores(key_rows, key_places)
        probabilities = jnp.where(allowed, jnp.exp(raw_scores - log_total[..., None]), 0.0)
        grad_prob = jnp.einsum(
            "qhd,khd->hqk", grad_attended, value_rows, preferred_element_type=jnp.float32
        )
        grad_scores = (probabilities * (grad_prob - row_dots[..., None])).astype(jnp.bfloat16)
        grad_query = grad_query + score_scale * jnp.einsum(
            "hqk,khd->qhd", grad_scores, key_rows, preferred_element_type=jnp.float32
        )
        key_terms = score_scale * jnp.einsum(
            "hqk,qhd->khd", grad_scores, query_low, preferred_element_type=jnp.float32
        )
        value_terms = jnp.einsum(
            "hqk,qhd->khd",
            probabilities.astype(jnp.bfloat16),
            grad_attended,
            preferred_element_type=jnp.float32,
        )
        return (grad_query, (key_terms, value_terms))

    grad_query_low, (key_terms, value_terms) = lax.scan(
        grad_step, jnp.zeros(head_shape, jnp.float32), (key_blocks, value_blocks, pos_blocks)
    )
    key_terms = key_terms.reshape(seq_len, model_width)
    value_terms = value_terms.reshape(seq_len, model_width)
    own_key_grad, own_value_grad = (
        lax.psum_scatter(
            key_terms.astype(jnp.bfloat16), "ctx", scatter_dimension=0, tiled=True
        ).astype(jnp.float32),
        lax.psum_scatter(
            value_terms.astype(jnp.bfloat16), "ctx", scatter_dimension=0, tiled=True
        ).astype(jnp.float32),
    )
    grad_key_low = own_key_grad.reshape(head_shape)
    grad_s_qk = jnp.sum(grad_query_low * query_unit + grad_key_low * key_unit, axis=0).reshape(
        model_width
    )
    grad_query_raw = unit_back(query_unit, query_factor, grad_query_low * qk_gain).reshape(
        tok_rows, model_width
    )
    grad_key_raw = unit_back(key_unit, key_factor, grad_key_low * qk_gain).reshape(
        tok_rows, model_width
    )
    grad_projected = jnp.concatenate([grad_query_raw, grad_key_raw, own_value_grad], axis=1).astype(
        jnp.bfloat16
    )
    grad_states = grad_mix_one * (1.0 - alpha_attn) + contract_cols(
        grad_projected, w_attn[:, : 3 * model_width]
    )
    feature_total = jnp.stack([grad_s_qk, grad_alpha_a, grad_alpha_m], axis=1)
    unit_fold = jnp.stack([grad_s_u, grad_s_v], axis=1).reshape(
        model_width, 2 * ff_width // model_width
    )
    attn_cols = 4 * model_width
    mlp_cols = 3 * ff_width
    attn_share = lax.psum_scatter(
        jnp.concatenate(
            [
                contract_rows(states, grad_projected),
                contract_rows(attended_low, grad_branch_attn),
                feature_total,
            ],
            axis=1,
        ),
        ("seq", "ctx"),
        scatter_dimension=0,
        tiled=True,
    )
    mlp_share = lax.psum_scatter(
        jnp.concatenate(
            [
                contract_rows(mixed_low, grad_up_gate),
                contract_rows(grad_branch_mlp, hidden),
                unit_fold,
            ],
            axis=1,
        ),
        ("seq", "ctx"),
        scatter_dimension=0,
        tiled=True,
    )
    grad_attn = attn_share[:, :attn_cols]
    grad_feature = attn_share[:, attn_cols:]
    grad_mlp = mlp_share[:, :mlp_cols]
    grad_unit = mlp_share[:, mlp_cols:].reshape(
        unit_gains.shape[0] // lax.axis_size(("seq", "ctx")), 2
    )
    return (
        out_full.astype(jnp.bfloat16),
        grad_states.astype(jnp.bfloat16),
        grad_attn,
        grad_mlp,
        grad_feature,
        grad_unit,
    )


CORES = 2
ALL = ("seq", "ctx")


def fits(n_seq, chips):
    return n_seq == 4 and chips == 4 and HEADS % chips == 0


MESH = pl.DeviceIdType.MESH
VMEM = pltpu.VMEM
CHIPS = 4
STEPS = (1, 2, 3)
LIMIT = 60 * 1024 * 1024


def place_of():
    seq = lax.axis_index("seq")
    ctx = lax.axis_index("ctx")
    return seq, ctx // CORES, ctx % CORES


def chip_peer(step):
    seq, chip, core = place_of()
    other = lax.rem(chip + step, CHIPS)
    return (seq, other * CORES + core), other


def seq_peer(step):
    seq, chip, core = place_of()
    other = seq ^ step
    return (other, chip * CORES + core), other


def twin():
    seq, chip, core = place_of()
    return (seq, chip * CORES + 1 - core)


def meet():
    devices = [chip_peer(step)[0] for step in STEPS] + [seq_peer(step)[0] for step in STEPS] + [twin()]
    gate = pltpu.get_barrier_semaphore()
    for device in devices:
        pl.semaphore_signal(gate, inc=1, device_id=device, device_id_type=MESH)
    pl.semaphore_wait(gate, len(devices))


def remote(src, dst, send, recv, device):
    return pltpu.make_async_remote_copy(
        src_ref=src, dst_ref=dst, send_sem=send, recv_sem=recv, device_id=device,
        device_id_type=MESH,
    )


def begin(copy):
    copy.start()
    return copy


def rows_at(index, count):
    return pl.ds(pl.multiple_of(index * count, count), count)


def device_on(chip):
    seq, _, core = place_of()
    return (seq, chip * CORES + core)


def when(condition, action):
    pl.when(condition)(action)


PIECES = 2


def piece_at(block, piece, count):
    step = count // PIECES
    return pl.ds(pl.multiple_of(block * count + piece * step, step), step)


def gather_copy(src, everything, count, block, side, hop, piece, send, recv):
    chip = place_of()[1]
    there = everything.at[piece_at(block, piece, count)]
    near = chip + 1 if side == 0 else chip - 1
    here = there if src is None else src.at[piece_at(0, piece, count)]
    return remote(here, there, send.at[side, hop, piece], recv.at[side, hop, piece], device_on(near))


def gather_start(src, everything, count, send, recv):
    chip = place_of()[1]
    for piece in range(PIECES):
        for side in range(2):
            copy = gather_copy(src, everything, count, chip, side, 0, piece, send, recv)
            when(chip < CHIPS - 1 if side == 0 else chip > 0, copy.start)


def gather_hop(everything, count, hop, send, recv):
    chip = place_of()[1]
    for piece in range(PIECES):
        for side in range(2):
            block = chip - hop if side == 0 else chip + hop

            def pass_on(side=side, piece=piece, block=block):
                gather_copy(None, everything, count, block, side, hop - 1, piece, send, recv).wait_recv()
                if hop < CHIPS - 1:
                    copy = gather_copy(None, everything, count, block, side, hop, piece, send, recv)
                    when(chip < CHIPS - 1 if side == 0 else chip > 0, copy.start)

            when(block >= 0 if side == 0 else block < CHIPS, pass_on)


def gather_drain(everything, count, send, recv):
    chip = place_of()[1]
    for hop in range(CHIPS - 1):
        for piece in range(PIECES):
            for side in range(2):
                copy = gather_copy(None, everything, count, chip, side, hop, piece, send, recv)
                block = chip - hop if side == 0 else chip + hop
                sent = (block >= 0) & (chip < CHIPS - 1) if side == 0 else (block < CHIPS) & (chip > 0)
                when(sent, copy.wait_send)


def inside_line():
    chip = place_of()[1]
    return (chip > 0) & (chip < CHIPS - 1)


def spans_line(other):
    return abs(place_of()[1] - other) == CHIPS - 1


def reduce_start(part, count, sums, via, send, recv):
    chip = place_of()[1]
    near = jnp.where(chip == 0, 1, CHIPS - 2)
    first = remote(part.at[rows_at(CHIPS - 1 - chip, count)], via, send.at[0], recv.at[0], device_on(near))

    def ahead():
        first.start()
        first.wait_send()

    when(jnp.logical_not(inside_line()), ahead)
    for step in STEPS:
        device, other = chip_peer(step)
        copy = remote(part.at[rows_at(other, count)], sums.at[step - 1], send.at[step], recv.at[step], device)
        if step == 2:
            when(jnp.logical_not(inside_line()), copy.start)
        else:
            when(jnp.logical_not(spans_line(other)), copy.start)


def reduce_relay(part, count, sums, via, mixed, send, recv):
    chip = place_of()[1]
    other = lax.rem(chip + 2, CHIPS)
    copy = remote(mixed, sums.at[1], send.at[2], recv.at[2], device_on(other))

    def pass_on():
        remote(mixed, via, send.at[0], recv.at[0], device_on(other)).wait_recv()
        mixed[...] = (
            part[rows_at(other, count), :].astype(jnp.float32) + via[...].astype(jnp.float32)
        ).astype(mixed.dtype)
        copy.start()

    when(inside_line(), pass_on)


def reduce_wait(part, count, sums, total, send, recv):
    chip = place_of()[1]
    total[...] = part[rows_at(chip, count), :].astype(jnp.float32)
    for step in (1, 3, 2):
        source = lax.rem(chip + CHIPS - step, CHIPS)

        def add(step=step, source=source):
            here = sums.at[step - 1]
            remote(here, here, send.at[step], recv.at[step], device_on(source)).wait_recv()
            total[...] += sums[step - 1].astype(jnp.float32)

        when(jnp.logical_not(spans_line(source)), add)


def reduce_drain(part, count, sums, send, recv):
    rows = part.at[rows_at(0, count)]
    for step in STEPS:
        device, other = chip_peer(step)
        copy = remote(rows, sums.at[step - 1], send.at[step], recv.at[step], device)
        when(jnp.logical_not(spans_line(other)), copy.wait_send)


def to_line(src, there, send, recv):
    return [
        begin(remote(src, there, send.at[step], recv.at[step], chip_peer(step)[0])) for step in STEPS
    ]


def dot(left, right):
    return jnp.dot(left, right, preferred_element_type=jnp.float32)


def dot_nt(left, right):
    return lax.dot_general(
        left, right, (((1,), (1,)), ((), ())), preferred_element_type=jnp.float32
    )


def dot_tn(left, right):
    return lax.dot_general(
        left, right, (((0,), (0,)), ((), ())), preferred_element_type=jnp.float32
    )


def dma(*shape):
    return pltpu.SemaphoreType.DMA(shape)


def line_dma():
    return dma(2, CHIPS, PIECES)


def in_vmem():
    return pl.BlockSpec(memory_space=pltpu.VMEM)


def in_hbm():
    return pl.BlockSpec(memory_space=pl.ANY)


def key_positions(places, key_pos, tok_rows):
    lanes = lax.broadcasted_iota(jnp.int32, (1, tok_rows), 1)
    for at_core in range(CORES):
        for at_chip in range(CHIPS):
            start = (at_core * CHIPS + at_chip) * tok_rows
            key_pos[:, start : start + tok_rows] = places[0, CORES * at_chip + at_core] * tok_rows + lanes


def kept_pairs(places, key_pos, block, core, tok_rows):
    down = lax.broadcasted_iota(jnp.int32, (tok_rows, 1), 0)
    return key_pos[...] <= places[0, CORES * block + core] * tok_rows + down


def attend_kernel(
    states, attn_src, mlp_src, qk_gain, places,
    states_all, w_qkv, w_out, w_up, w_gate, low_down, raw_out, query_out, both, att_out, inv_out, attx,
    src_q, stage_q, low_q, stage_o, low_o, stage_m, low_m, raw, att_low, key_pos,
    local_sem, x_send, x_recv, q_send, q_recv, mt_send, mt_recv, wz_send, wz_recv,
    ws_send, ws_recv, wt_send, wt_recv, oz_send, oz_recv, os_send, os_recv, m_send, m_recv,
    ms_send, ms_recv, kv_send, kv_recv, a_send, a_recv,
):
    seq, chip, core = place_of()
    rows = attn_src.shape[0]
    tok_rows, model_width = states.shape
    heads = qk_gain.shape[0]
    head_cols = heads * HEAD_DIM
    part_cols = head_cols // CORES
    group_rows = tok_rows * CHIPS
    chip_rows = CORES * rows
    seq_rows = CHIPS * chip_rows
    half_units = w_up.shape[1]
    half_width = model_width // CORES
    ff_width = mlp_src.shape[1] // 3
    low = jnp.bfloat16
    for at in range(CHIPS):
        for half in range(CORES):
            for which in range(3):
                start = which * model_width + at * head_cols + half * part_cols
                src_q[at, half, :, which * part_cols : (which + 1) * part_cols] = attn_src[:, start : start + part_cols]
    meet()
    block = rows_at(chip, tok_rows)
    mine = rows_at(core, rows)
    half_at = pl.ds(pl.multiple_of(3 * model_width + core * half_width, 128), half_width)
    other_at = pl.ds(pl.multiple_of(3 * model_width + (1 - core) * half_width, 128), half_width)
    swap_o = begin(remote(attn_src.at[:, other_at], stage_o.at[mine], q_send.at[1], q_recv.at[1], twin()))
    swap_q = begin(remote(src_q.at[:, 1 - core], stage_q.at[:, mine], q_send.at[0], q_recv.at[0], twin()))
    stage_o[mine, :] = attn_src[:, half_at]
    stage_q[:, mine, :] = src_q[:, core]
    m_swaps, m_keeps = [], []
    for part in range(3):
        for at in range(CHIPS):
            start = part * ff_width + at * CORES * half_units
            theirs = pl.ds(pl.multiple_of(start + (1 - core) * half_units, 128), half_units)
            ours = pl.ds(pl.multiple_of(start + core * half_units, 128), half_units)
            there = stage_m.at[part, at, mine]
            m_swaps.append(begin(remote(mlp_src.at[:, theirs], there, mt_send.at[part, at], mt_recv.at[part, at], twin())))
            m_keeps.append(begin(pltpu.make_async_copy(mlp_src.at[:, ours], there, local_sem.at[part * CHIPS + at])))
    my_rows = rows_at(seq * CHIPS + chip, chip_rows)
    seq_at = rows_at(seq, seq_rows)
    swap_o.wait()
    low_o[...] = stage_o[...].astype(low)
    o_line = to_line(low_o, w_out.at[core, my_rows], oz_send, oz_recv)
    w_out[core, my_rows, :] = low_o[...]
    swap_q.wait()
    low_q[...] = stage_q[...].astype(low)
    line = []
    for step in STEPS:
        device, other = chip_peer(step)
        line.append(begin(remote(low_q.at[other], w_qkv.at[core, my_rows], wz_send.at[step], wz_recv.at[step], device)))
    w_qkv[core, my_rows, :] = low_q[chip]
    states_all[block, :] = states[...]
    key_positions(places, key_pos, tok_rows)
    for copy in line:
        copy.wait_recv()
    gather_start(states, states_all, tok_rows, x_send, x_recv)

    def across(part, send, recv):
        return [begin(remote(part, part, send.at[step], recv.at[step], seq_peer(step)[0])) for step in STEPS]

    q_across = across(w_qkv.at[core, seq_at], ws_send, ws_recv)
    for copy in m_keeps:
        copy.wait()
    for copy in m_swaps:
        copy.wait()
    low_m[...] = stage_m[:2].astype(low)
    low_down[...] = stage_m[2].astype(low)
    gather_hop(states_all, tok_rows, 1, x_send, x_recv)
    for copy in o_line + q_across:
        copy.wait_recv()
    swap = begin(remote(w_qkv.at[core], w_qkv.at[core], wt_send.at[0], wt_recv.at[0], twin()))
    o_across = across(w_out.at[core, seq_at], os_send, os_recv)
    gather_hop(states_all, tok_rows, 2, x_send, x_recv)
    gather_hop(states_all, tok_rows, 3, x_send, x_recv)
    here = rows_at(chip, chip_rows)

    def to_chips(part, there):
        return [
            begin(remote(low_m.at[part, chip_peer(step)[1]], there, m_send.at[part, step], m_recv.at[part, step], chip_peer(step)[0]))
            for step in STEPS
        ]

    m_line = to_chips(0, w_up.at[my_rows])
    w_up[my_rows, :] = low_m[0, chip]
    w_gate[here, :] = low_m[1, chip]
    swap.wait()

    for half in range(CORES):
        value = dot(states_all[...], w_qkv[half])
        for which in range(3):
            start = which * head_cols + half * part_cols
            raw[:, start : start + part_cols] = value[:, which * part_cols : (which + 1) * part_cols]
    for head in reversed(range(3 * heads)):
        which, head = head // heads, head % heads
        start = which * head_cols + head * HEAD_DIM
        value = raw[:, start : start + HEAD_DIM]
        if which == 2:
            both[core, 1, head] = value.astype(low)
            continue
        factor = lax.rsqrt(jnp.sum(value * value, axis=-1, keepdims=True) + EPSILON)
        scaled = (value * factor * qk_gain[head]).astype(low)
        raw_out[which, head] = value
        if which == 1:
            both[core, 0, head] = scaled
            if head == 0:
                swap = begin(remote(both.at[core], both.at[core], kv_send.at[0], kv_recv.at[0], twin()))
        else:
            query_out[head] = scaled * math.sqrt(HEAD_DIM)
    for copy in m_line + o_across:
        copy.wait_recv()
    m_line += to_chips(1, w_gate.at[here])
    swap_o = begin(remote(w_out.at[core], w_out.at[core], wt_send.at[1], wt_recv.at[1], twin()))
    up_across = across(w_up.at[seq_at], ms_send, ms_recv)
    swap.wait()

    def one_block(index, carry):
        step = lax.rem(index + 1, CHIPS)
        device, other = chip_peer(step)
        at = rows_at(other, tok_rows)
        allowed = kept_pairs(places, key_pos, other, core, tok_rows)

        def one_head(head, carry):
            query = query_out[head, at, :]
            scores = jnp.concatenate([dot_nt(query, both[half, 0, head]) for half in range(CORES)], axis=1)
            powered = jnp.exp(jnp.where(allowed, scores, NEG_LARGE))
            inverse = 1.0 / jnp.sum(powered, axis=-1, keepdims=True)
            weights = (powered * inverse).astype(low)
            att_out[head, at, :] = sum(
                dot(weights[:, half * group_rows : (half + 1) * group_rows], both[half, 1, head])
                for half in range(CORES)
            )
            inv_out[head, at, :] = inverse
            return carry

        lax.fori_loop(0, heads, one_head, 0)
        for head in range(heads):
            att_low[at, head * HEAD_DIM : (head + 1) * HEAD_DIM] = att_out[head, at, :].astype(low)
        when(step != 0, remote(att_low.at[at], attx.at[chip], a_send.at[step], a_recv.at[step], device).start)
        return carry

    lax.fori_loop(0, CHIPS, one_block, 0)
    attx[chip] = att_low[block, :]
    for step in STEPS:
        remote(att_low.at[block], attx.at[chip], a_send.at[step], a_recv.at[step], chip_peer(step)[0]).wait()
    for copy in m_line[3:] + up_across:
        copy.wait_recv()
    swap_o.wait()
    gather_drain(states_all, tok_rows, x_send, x_recv)
    for copy in m_line + line + o_line + q_across + o_across + up_across:
        copy.wait_send()


def in_smem():
    return pl.BlockSpec(memory_space=pltpu.SMEM)


def attend_call(states, attn_src, mlp_src, qk_gain, places):
    tok_rows, model_width = states.shape
    rows = attn_src.shape[0]
    heads = qk_gain.shape[0]
    chips, chip_rows = CHIPS, CORES * rows
    group_rows = chips * tok_rows
    half_units = mlp_src.shape[1] // 3 // chips // CORES
    half_width, half_cols = model_width // CORES, 3 * heads * HEAD_DIM // CORES
    f32, low = jnp.float32, jnp.bfloat16
    shape = jax.ShapeDtypeStruct
    return pl.pallas_call(
        attend_kernel,
        out_shape=[
            shape((group_rows, model_width), low),
            shape((CORES, model_width, half_cols), low),
            shape((CORES, model_width, half_width), low),
            shape((model_width, half_units), low),
            shape((chips * chip_rows, half_units), low),
            shape((chips, chip_rows, half_units), low),
            shape((2, heads, group_rows, HEAD_DIM), f32),
            shape((heads, group_rows, HEAD_DIM), low),
            shape((CORES, 2, heads, group_rows, HEAD_DIM), low),
            shape((heads, group_rows, HEAD_DIM), f32),
            shape((heads, group_rows, 1), f32),
            shape((chips, tok_rows, heads * HEAD_DIM), low),
        ],
        in_specs=[in_vmem(), in_vmem(), in_hbm(), in_vmem(), in_smem()],
        out_specs=[in_vmem()] * 12,
        scratch_shapes=[
            VMEM((chips, CORES, rows, half_cols), f32),
            VMEM((chips, chip_rows, half_cols), f32),
            VMEM((chips, chip_rows, half_cols), low),
            VMEM((chip_rows, half_width), f32),
            VMEM((chip_rows, half_width), low),
            VMEM((3, chips, chip_rows, half_units), f32),
            VMEM((2, chips, chip_rows, half_units), low),
            VMEM((group_rows, 3 * heads * HEAD_DIM), f32),
            VMEM((group_rows, heads * HEAD_DIM), low),
            VMEM((1, CORES * group_rows), jnp.int32),
            dma(12), line_dma(), line_dma(), dma(2), dma(2), dma(3, 4), dma(3, 4), dma(4), dma(4),
            dma(4), dma(4), dma(2), dma(2), dma(4), dma(4), dma(4), dma(4), dma(2, 4), dma(2, 4),
            dma(4), dma(4), dma(1), dma(1), dma(4), dma(4),
        ],
        compiler_params=pltpu.CompilerParams(
            collective_id=1, has_side_effects=True, vmem_limit_bytes=LIMIT
        ),
        name="attend",
    )(states, attn_src, mlp_src, qk_gain, places)


def unit_of(value):
    factor = lax.rsqrt(jnp.sum(value * value, axis=-1, keepdims=True) + EPSILON)
    return value * factor, factor


def mlp_kernel(
    attx, states, cotangent, w_out, alpha_attn, alpha_mlp, gain_u, gain_v, w_up, w_gate, low_down,
    out, grad_attx, grad_w_out, grad_direct, small, grad_half, grad_down,
    weights, mixed_one, attn_unit, factors, mixed_low, mixed_all, up, gate, hidden, part,
    sums, via, passed, total, grad_two, branch_low, branch_all, grad_u, grad_v, wide, turned, arrived,
    w_down, down_half, down_got, dot_u, dot_v,
    local_sem, ws_send, ws_recv, wt_send, wt_recv, x_send, x_recv, r_send, r_recv,
    g_send, g_recv, b_send, b_recv, d_send, d_recv, wz_send, wz_recv, ds_send, ds_recv,
):
    seq, chip, core = place_of()
    tok_rows, model_width = states.shape
    chip_heads = attx.shape[2]
    seq_rows, half_units = w_gate.shape
    chip_rows = low_down.shape[1]
    half_width = w_out.shape[2]
    group_rows = CHIPS * tok_rows
    block = rows_at(chip, tok_rows)
    meet()
    seq_at = rows_at(seq, seq_rows)
    here = rows_at(chip, chip_rows)
    swaps = [begin(remote(w_up, weights.at[0, core], wt_send.at[0], wt_recv.at[0], twin()))]
    to_chips = [
        begin(remote(low_down.at[chip_peer(step)[1]], w_down.at[here], wz_send.at[step], wz_recv.at[step], chip_peer(step)[0]))
        for step in STEPS
    ]

    def spread(which, src):
        return [
            begin(remote(src, weights.at[which, core, seq_at], ws_send.at[which, step], ws_recv.at[which, step], seq_peer(step)[0]))
            for step in STEPS
        ]

    across = spread(1, w_gate)
    keeps = [
        begin(pltpu.make_async_copy(w_up, weights.at[0, core], local_sem.at[0])),
        begin(pltpu.make_async_copy(w_gate, weights.at[1, core, seq_at], local_sem.at[1])),
    ]
    w_down[here, :] = low_down[chip]
    part_at = [slice(at * chip_heads, (at + 1) * chip_heads) for at in range(CHIPS)]
    half_at = [slice(half * half_width, (half + 1) * half_width) for half in range(CORES)]
    branch = jnp.concatenate(
        [sum(dot(attx[at], w_out[half, part_at[at], :]) for at in range(CHIPS)) for half in range(CORES)],
        axis=1,
    )
    unit, factor = unit_of(branch)
    attn_unit[...] = unit
    factors[0] = factor
    base = states[...].astype(jnp.float32)
    value, factor = unit_of(base + alpha_attn[...] * (unit - base))
    mixed_one[...] = value
    factors[1] = factor
    mixed_low[...] = value.astype(jnp.bfloat16)
    gather_start(mixed_low, mixed_all, tok_rows, x_send, x_recv)
    mixed_all[block, :] = mixed_low[...]
    for copy in keeps:
        copy.wait()
    for copy in to_chips:
        copy.wait_recv()
    gather_hop(mixed_all, tok_rows, 1, x_send, x_recv)
    for copy in across:
        copy.wait_recv()
    across += spread(2, w_down)
    weights[2, core, seq_at, :] = w_down[...]
    swaps.append(begin(remote(weights.at[1, core], weights.at[1, core], wt_send.at[1], wt_recv.at[1], twin())))
    gather_hop(mixed_all, tok_rows, 2, x_send, x_recv)
    gather_hop(mixed_all, tok_rows, 3, x_send, x_recv)
    for copy in swaps:
        copy.wait_recv()
    for half in range(CORES):
        up[half] = dot(mixed_all[...], weights[0, half])
        gate[half] = dot(mixed_all[...], weights[1, half])
    slab = min(64, group_rows)
    slabs = group_rows // slab

    def activate(index, carry):
        half = index // slabs
        at = rows_at(lax.rem(index, slabs), slab)
        gated = gate[half, at, :] * gain_v[half]
        scaled = up[half, at, :] * gain_u[half]
        hidden[half, at, :] = (gated * jax.nn.sigmoid(gated) * scaled).astype(jnp.bfloat16)
        return carry

    lax.fori_loop(0, CORES * slabs, activate, 0)
    for copy in across[-3:]:
        copy.wait_recv()
    swap = begin(remote(weights.at[2, core], weights.at[2, core], wt_send.at[2], wt_recv.at[2], twin()))
    swaps.append(swap)
    swap.wait_recv()
    tile = model_width // 5

    def down(index, carry):
        at = rows_at(index, tile)
        part[0, :, at] = sum(dot_nt(hidden[half], weights[2, half, at, :]) for half in range(CORES)).astype(jnp.bfloat16)
        return carry

    lax.fori_loop(0, model_width // tile, down, 0)

    reduce_start(part.at[0], tok_rows, sums.at[0], via.at[0], r_send, r_recv)
    reduce_relay(part.at[0], tok_rows, sums.at[0], via.at[0], passed.at[0], r_send, r_recv)
    reduce_wait(part.at[0], tok_rows, sums.at[0], total, r_send, r_recv)
    mlp_unit, mlp_factor = unit_of(total[...])
    value, factor = unit_of(mixed_one[...] + alpha_mlp[...] * (mlp_unit - mixed_one[...]))
    out[...] = value.astype(jnp.bfloat16)
    above = cotangent[...].astype(jnp.float32)
    grad = factor * (above - value * jnp.sum(above * value, axis=-1, keepdims=True))
    grad_two[...] = grad
    small[...] = jnp.zeros_like(small)
    small[1:2, :] = jnp.sum(grad * (mlp_unit - mixed_one[...]), axis=0, keepdims=True)
    grad = grad * alpha_mlp[...]
    grad = mlp_factor * (grad - mlp_unit * jnp.sum(grad * mlp_unit, axis=-1, keepdims=True))
    branch_low[...] = grad.astype(jnp.bfloat16)
    gather_start(branch_low, branch_all, tok_rows, g_send, g_recv)
    branch_all[block, :] = branch_low[...]
    gather_hop(branch_all, tok_rows, 1, g_send, g_recv)
    gather_hop(branch_all, tok_rows, 2, g_send, g_recv)
    turned[0] = mixed_all[...].T
    gather_hop(branch_all, tok_rows, 3, g_send, g_recv)
    for half in range(CORES):
        wide[half] = dot(branch_all[...], weights[2, half])
    dot_u[...] = jnp.zeros_like(dot_u)
    dot_v[...] = jnp.zeros_like(dot_v)

    def deactivate(index, carry):
        half = index // slabs
        at = rows_at(lax.rem(index, slabs), slab)
        gated = gate[half, at, :] * gain_v[half]
        scaled = up[half, at, :] * gain_u[half]
        upstream = wide[half, at, :]
        sig = jax.nn.sigmoid(gated)
        to_up = upstream * (gated * sig)
        to_gate = upstream * scaled * sig * (1.0 + gated * (1.0 - sig))
        dot_u[half] += jnp.sum(to_up * up[half, at, :], axis=0, keepdims=True)
        dot_v[half] += jnp.sum(to_gate * gate[half, at, :], axis=0, keepdims=True)
        grad_u[half, at, :] = (to_up * gain_u[half]).astype(jnp.bfloat16)
        grad_v[half, at, :] = (to_gate * gain_v[half]).astype(jnp.bfloat16)
        return carry

    lax.fori_loop(0, CORES * slabs, deactivate, 0)

    def back_down(index, carry):
        at = rows_at(index, tile)
        part[1, :, at] = sum(
            dot_nt(grad_u[half], weights[0, half, at, :]) + dot_nt(grad_v[half], weights[1, half, at, :])
            for half in range(CORES)
        ).astype(jnp.bfloat16)
        return carry

    lax.fori_loop(0, model_width // tile, back_down, 0)
    for copy in swaps:
        copy.wait_send()
    reduce_start(part.at[1], tok_rows, sums.at[1], via.at[1], b_send, b_recv)
    turned[1] = branch_all[...].T
    swaps = {}

    def weight_grads(which, left, right):
        def one(index, carry):
            half = index // 5
            at = rows_at(lax.rem(index, 5), tile)
            weights[which, half, at, :] = dot(turned[left, at, :], right[half]).astype(jnp.bfloat16)
            return carry

        lax.fori_loop(0, CORES * 5, one, 0)
        swaps[which] = begin(remote(weights.at[which, 1 - core], arrived.at[which], d_send.at[which], d_recv.at[which], twin()))

    def both_cores(which):
        swaps[which].wait_recv()
        return (weights[which, core].astype(jnp.float32) + arrived[which].astype(jnp.float32)).astype(jnp.bfloat16)

    weight_grads(2, 1, hidden)
    reduce_relay(part.at[1], tok_rows, sums.at[1], via.at[1], passed.at[1], b_send, b_recv)
    down_half[...] = both_cores(2)
    down_across = [
        begin(remote(down_half.at[rows_at(seq_peer(step)[1], seq_rows)], down_got.at[step - 1], ds_send.at[step], ds_recv.at[step], seq_peer(step)[0]))
        for step in STEPS
    ]
    weight_grads(0, 0, grad_u)
    weight_grads(1, 0, grad_v)
    reduce_wait(part.at[1], tok_rows, sums.at[1], total, b_send, b_recv)
    grad = grad_two[...] * (1.0 - alpha_mlp[...]) + total[...]
    value = mixed_one[...]
    grad = factors[1] * (grad - value * jnp.sum(grad * value, axis=-1, keepdims=True))
    unit = attn_unit[...]
    small[0:1, :] = jnp.sum(grad * (unit - states[...].astype(jnp.float32)), axis=0, keepdims=True)
    grad_direct[...] = grad * (1.0 - alpha_attn[...])
    grad = grad * alpha_attn[...]
    grad = factors[0] * (grad - unit * jnp.sum(grad * unit, axis=-1, keepdims=True))
    low = grad.astype(jnp.bfloat16)
    for at in range(CHIPS):
        grad_attx[at] = sum(
            dot_nt(low[:, half_at[half]], w_out[half, part_at[at], :]) for half in range(CORES)
        ).astype(jnp.bfloat16)
        for half in range(CORES):
            grad_w_out[half, at] = dot_tn(attx[at], low[:, half_at[half]]).astype(jnp.bfloat16)
    for half in range(CORES):
        unit_at = slice(half * half_units, (half + 1) * half_units)
        small[2:3, unit_at] = dot_u[half]
        small[3:4, unit_at] = dot_v[half] * math.sqrt(D)
    for which in range(2):
        grad_half[which] = both_cores(which)
    whole = down_half[seq_at, :].astype(jnp.float32)
    for step in STEPS:
        down_across[step - 1].wait_recv()
        whole = whole + down_got[step - 1].astype(jnp.float32)
    grad_down[...] = whole.astype(jnp.bfloat16)
    gather_drain(mixed_all, tok_rows, x_send, x_recv)
    gather_drain(branch_all, tok_rows, g_send, g_recv)
    reduce_drain(part.at[0], tok_rows, sums.at[0], r_send, r_recv)
    reduce_drain(part.at[1], tok_rows, sums.at[1], b_send, b_recv)
    for copy in across + to_chips + down_across + [swaps[which] for which in range(3)]:
        copy.wait_send()


def mlp_call(attx, states, cotangent, w_out, alpha_attn, alpha_mlp, gain_u, gain_v, w_up, w_gate, low_down):
    tok_rows, model_width = states.shape
    chips, _, chip_heads = attx.shape
    seq_rows, half_units = w_gate.shape
    group_rows = chips * tok_rows
    f32, low = jnp.float32, jnp.bfloat16
    shape = jax.ShapeDtypeStruct
    tokens, group = (tok_rows, model_width), (group_rows, model_width)
    wide = (CORES, group_rows, half_units)
    matrix = (model_width, half_units)
    return pl.pallas_call(
        mlp_kernel,
        out_shape=[
            shape(tokens, low),
            shape(attx.shape, low),
            shape((CORES, chips, chip_heads, model_width // CORES), low),
            shape(tokens, f32),
            shape((8, max(model_width, CORES * half_units)), f32),
            shape((2,) + matrix, low),
            shape((seq_rows, half_units), low),
        ],
        in_specs=[in_vmem()] * 8 + [in_hbm(), in_vmem(), in_vmem()],
        out_specs=[in_vmem()] * 7,
        scratch_shapes=[
            VMEM((3, CORES) + matrix, low),
            VMEM(tokens, f32),
            VMEM(tokens, f32),
            VMEM((2, tok_rows, 1), f32),
            VMEM(tokens, low),
            VMEM(group, low),
            VMEM(wide, f32),
            VMEM(wide, f32),
            VMEM(wide, low),
            VMEM((2,) + group, low),
            VMEM((2, 3) + tokens, low),
            VMEM((2,) + tokens, low),
            VMEM((2,) + tokens, low),
            VMEM(tokens, f32),
            VMEM(tokens, f32),
            VMEM(tokens, low),
            VMEM(group, low),
            VMEM(wide, low),
            VMEM(wide, low),
            VMEM(wide, f32),
            VMEM((2, model_width, group_rows), low),
            VMEM((3,) + matrix, low),
            VMEM((seq_rows, half_units), low),
            VMEM(matrix, low),
            VMEM((3, seq_rows, half_units), low),
            VMEM((CORES, 1, half_units), f32),
            VMEM((CORES, 1, half_units), f32),
            dma(2), dma(3, 4), dma(3, 4), dma(3), dma(3), line_dma(), line_dma(), dma(4), dma(4),
            line_dma(), line_dma(), dma(4), dma(4), dma(3), dma(3), dma(4), dma(4), dma(4), dma(4),
        ],
        compiler_params=pltpu.CompilerParams(
            collective_id=2, has_side_effects=True, vmem_limit_bytes=LIMIT
        ),
        name="mlp",
    )(
        attx, states, cotangent, w_out, alpha_attn, alpha_mlp, gain_u, gain_v, w_up, w_gate, low_down
    )


def back_kernel(
    grad_attx, grad_half, grad_down, grad_w_out, small_in, raw, query, both, att, inverse, states_all,
    w_qkv, qk_gain, places, grad_direct,
    grad_states, out_mlp, out_attn, feature, unit,
    att_low, heads_low, to_keys, swap_low, swap_kv, grad_heads, grad_sides, part, sums, via, passed, total, turned,
    grad_q, half_q, seq_q, line_q, wide_q, half_o, pair_o, seq_got, seq_low, line_got, wide,
    wide_o, small, small_pair, small_seq, dots, small_all, flat_q, sides_q, key_pos,
    local_sem, a_send, a_recv, s_send, s_recv, o_send, o_recv, kv_send, kv_recv, r_send, r_recv,
    qt_send, qt_recv, qs_send, qs_recv, qz_send, qz_recv, z_send, z_recv, f_send, f_recv,
    p_send, p_recv, t_send, t_recv,
):
    seq, chip, core = place_of()
    tok_rows, model_width = grad_direct.shape
    heads = qk_gain.shape[0]
    head_cols = heads * HEAD_DIM
    group_rows = CHIPS * tok_rows
    half_units = grad_half.shape[2]
    seq_rows = seq_got.shape[2]
    chip_rows = seq_rows // CHIPS
    rows = chip_rows // CORES
    part_cols = head_cols // CORES
    ff_width = out_mlp.shape[1] // 3
    scale = math.sqrt(HEAD_DIM)
    block = rows_at(chip, tok_rows)
    f32, low = jnp.float32, jnp.bfloat16
    meet()
    waits = []
    line = []
    for step in STEPS:
        device, other = chip_peer(step)
        line.append(begin(remote(grad_attx.at[other], att_low.at[block], a_send.at[step], a_recv.at[step], device)))
    att_low[block, :] = grad_attx[chip]
    key_positions(places, key_pos, tok_rows)
    pair = begin(remote(grad_w_out.at[1 - core], pair_o, o_send.at[0], o_recv.at[0], twin()))
    across = []
    onward = {}

    def to_chips(which, src):
        onward[which] = [
            begin(remote(src.at[rows_at(chip_peer(step)[1], chip_rows)], line_got.at[which, chip], z_send.at[which, step], z_recv.at[which, step], chip_peer(step)[0]))
            for step in STEPS
        ]
        line_got[which, chip] = src[rows_at(chip, chip_rows), :]

    to_chips(2, grad_down)
    for which in range(2):
        for step in STEPS:
            device, other = seq_peer(step)
            across.append(begin(remote(grad_half.at[which, rows_at(other, seq_rows)], seq_got.at[which, step - 1], s_send.at[which, step], s_recv.at[which, step], device)))
    keeps = [
        begin(pltpu.make_async_copy(grad_half.at[which, rows_at(seq, seq_rows)], seq_low.at[which], local_sem.at[which]))
        for which in range(2)
    ]
    to_keys[...] = jnp.zeros_like(to_keys)
    dots[...] = jnp.zeros_like(dots)
    turned[...] = states_all[...].T
    pair.wait_recv()
    for at in range(4):
        half_o[at] = (grad_w_out[core, at].astype(f32) + pair_o[at].astype(f32)).astype(low)
    for step in STEPS:
        device, other = seq_peer(step)
        across.append(begin(remote(half_o.at[other], seq_got.at[2, step - 1], s_send.at[2, step], s_recv.at[2, step], device)))
    tile = tok_rows
    tiles = CHIPS

    def raw_back(which, head, at, upstream):
        value = raw[which, head, at, :]
        unit, factor = unit_of(value)
        dots[head] += jnp.sum(upstream * unit, axis=0, keepdims=True)
        upstream = upstream * qk_gain[head]
        upstream = factor * (upstream - unit * jnp.sum(upstream * unit, axis=-1, keepdims=True))
        grad_heads[which, head, at, :] = upstream.astype(low)

    def one_block(step, carry):
        other = lax.rem(chip + CHIPS - step, CHIPS)
        at = rows_at(other, tok_rows)
        copy = remote(grad_attx.at[0], att_low.at[at], a_send.at[step], a_recv.at[step], device_on(other))
        when(step > 0, copy.wait_recv)
        for head in range(heads):
            heads_low[head, at, :] = att_low[at, head * HEAD_DIM : (head + 1) * HEAD_DIM]
        allowed = kept_pairs(places, key_pos, other, core, tok_rows)

        def one_head(head, carry):
            rows_q = query[head, at, :]
            grad_att = heads_low[head, at, :]
            scores = jnp.concatenate([dot_nt(rows_q, both[half, 0, head]) for half in range(CORES)], axis=1)
            probs = jnp.exp(jnp.where(allowed, scores, NEG_LARGE)) * inverse[head, at, :]
            grad_prob = jnp.concatenate([dot_nt(grad_att, both[half, 1, head]) for half in range(CORES)], axis=1)
            row_dot = jnp.sum(grad_att.astype(f32) * att[head, at, :], axis=-1, keepdims=True)
            grad_scores = (probs * (grad_prob - row_dot)).astype(low)
            weights = probs.astype(low)
            to_query = jnp.zeros((tok_rows, HEAD_DIM), f32)
            for half in range(CORES):
                cols = slice(half * group_rows, (half + 1) * group_rows)
                to_query = to_query + dot(grad_scores[:, cols], both[half, 0, head])
                to_keys[half, 0, head] += dot_tn(grad_scores[:, cols], rows_q)
                to_keys[half, 1, head] += dot_tn(weights[:, cols], grad_att)
            raw_back(0, head, at, to_query * scale)
            return carry

        lax.fori_loop(0, heads, one_head, 0)
        return carry

    lax.fori_loop(0, CHIPS, one_block, 0)
    swap_low[...] = to_keys[1 - core].astype(low)
    swap = begin(remote(swap_low, swap_kv, kv_send.at[0], kv_recv.at[0], twin()))
    swap.wait()

    def one_key(index, carry):
        head = index // tiles
        at = rows_at(lax.rem(index, tiles), tile)
        mine = to_keys[core, 0, head, at, :] + swap_kv[0, head, at, :].astype(f32)
        raw_back(1, head, at, mine)
        value = to_keys[core, 1, head, at, :] + swap_kv[1, head, at, :].astype(f32)
        grad_heads[2, head, at, :] = value.astype(low)
        return carry

    lax.fori_loop(0, heads * tiles, one_key, 0)
    for which in range(3):
        full = jnp.concatenate([grad_heads[which, head] for head in range(heads)], axis=1)
        for half in range(CORES):
            grad_sides[half, :, which * part_cols : (which + 1) * part_cols] = full[:, half * part_cols : (half + 1) * part_cols]
    wide_tile = model_width // 5

    def down(index, carry):
        at = rows_at(index, wide_tile)
        part[:, at] = sum(dot_nt(grad_sides[half], w_qkv[half, at, :]) for half in range(CORES)).astype(low)
        return carry

    lax.fori_loop(0, 5, down, 0)
    reduce_start(part, tok_rows, sums, via, r_send, r_recv)

    def weight_grad(index, carry):
        half = index // 5
        at = rows_at(lax.rem(index, 5), wide_tile)
        grad_q[half, at, :] = dot(turned[at, :], grad_sides[half]).astype(low)
        return carry

    lax.fori_loop(0, CORES * 5, weight_grad, 0)
    swap_q = begin(remote(grad_q.at[1 - core], half_q, qt_send.at[0], qt_recv.at[0], twin()))
    reduce_relay(part, tok_rows, sums, via, passed, r_send, r_recv)
    small[...] = small_in[...]
    small[4:5, :head_cols] = jnp.concatenate([dots[head] for head in range(heads)], axis=1)
    swap_s = begin(remote(small, small_pair, t_send.at[0], t_recv.at[0], twin()))
    swap_q.wait()
    half_q[...] = (grad_q[core].astype(f32) + half_q[...].astype(f32)).astype(low)
    across_q = []
    for step in STEPS:
        device, other = seq_peer(step)
        across_q.append(begin(remote(half_q.at[rows_at(other, seq_rows)], seq_q.at[step - 1], qs_send.at[step], qs_recv.at[step], device)))
    swap_s.wait()
    small[...] = small[...] + small_pair[...]
    spread_s = [
        begin(remote(small, small_seq.at[step - 1], t_send.at[step], t_recv.at[step], seq_peer(step)[0]))
        for step in STEPS
    ]
    for copy in keeps:
        copy.wait()
    seq_low[2] = half_o[seq]
    for at, which in enumerate((0, 1, 3)):
        for copy in across[3 * at : 3 * at + 3]:
            copy.wait_recv()
        whole = seq_low[at].astype(f32)
        for step in STEPS:
            whole = whole + seq_got[at, step - 1].astype(f32)
        seq_low[at] = whole.astype(low)
        to_chips(which, seq_low.at[at])
    for copy in across_q:
        copy.wait_recv()
    whole = half_q[rows_at(seq, seq_rows), :].astype(f32)
    for step in STEPS:
        whole = whole + seq_q[step - 1].astype(f32)
    grad_q[0, :seq_rows, :] = whole.astype(low)
    onward_q = []
    for step in STEPS:
        device, other = chip_peer(step)
        onward_q.append(begin(remote(grad_q.at[0, rows_at(other, chip_rows)], line_q.at[chip], qz_send.at[step], qz_recv.at[step], device)))
    line_q[chip] = grad_q[0, rows_at(chip, chip_rows), :]
    for copy in spread_s:
        copy.wait()
    small_pair[...] = small[...] + small_seq[0] + small_seq[1] + small_seq[2]
    small_all[chip] = small_pair[...]
    ends = to_line(small_pair, small_all.at[chip], p_send, p_recv)
    reduce_wait(part, tok_rows, sums, total, r_send, r_recv)
    grad_states[...] = (total[...] + grad_direct[...]).astype(low)

    mine = rows_at(core, rows)
    theirs = rows_at(1 - core, rows)
    last, lasts = [], []
    for which in (2, 0, 1):
        for copy in onward[which]:
            copy.wait_recv()
        for at in range(CHIPS):
            wide[which, at] = line_got[which, at].astype(f32)
            start = which * ff_width + at * CORES * half_units + core * half_units
            there = out_mlp.at[:, pl.ds(pl.multiple_of(start, 128), half_units)]
            last.append(begin(remote(wide.at[which, at, theirs], there, f_send.at[which, at], f_recv.at[which, at], twin())))
            lasts.append(begin(pltpu.make_async_copy(wide.at[which, at, mine], there, local_sem.at[3 + which * CHIPS + at])))
    for copy in onward[3]:
        copy.wait_recv()
    whole = line_got[3, 0].astype(f32)
    for at in range(1, CHIPS):
        whole = whole + line_got[3, at].astype(f32)
    wide_o[...] = whole
    start = 3 * model_width + core * half_units
    there = out_attn.at[:, pl.ds(pl.multiple_of(start, 128), half_units)]
    last.append(begin(remote(wide_o.at[theirs], there, f_send.at[3, 0], f_recv.at[3, 0], twin())))
    lasts.append(begin(pltpu.make_async_copy(wide_o.at[mine], there, local_sem.at[15])))
    for copy in onward_q:
        copy.wait_recv()
    wide_q[...] = line_q[...].astype(f32)
    sides_q[core] = wide_q[:, mine, :]
    swap_q = begin(remote(wide_q.at[:, theirs], sides_q.at[core], f_send.at[3, 1], f_recv.at[3, 1], twin()))
    for copy in ends:
        copy.wait()
    alphas = small_all[0] + small_all[1] + small_all[2] + small_all[3]
    feature[1:3, :] = alphas[0:2, :]
    for at in range(CHIPS):
        feature[0:1, at * head_cols : (at + 1) * head_cols] = small_all[at, 4:5, :head_cols]
        width = CORES * half_units
        unit[:, at * width : (at + 1) * width] = small_all[at, 2:4, :width]
    swap_q.wait()
    for at in range(CHIPS):
        for half in range(CORES):
            for which in range(3):
                start = which * model_width + at * head_cols + half * part_cols
                flat_q[:, start : start + part_cols] = sides_q[half, at, :, which * part_cols : (which + 1) * part_cols]
    lasts.append(begin(pltpu.make_async_copy(flat_q, out_attn.at[:, pl.ds(0, 3 * model_width)], local_sem.at[16])))
    for copy in last + lasts:
        copy.wait()
    reduce_drain(part, tok_rows, sums, r_send, r_recv)
    for copy in line + [pair] + across + across_q + onward_q + sum(onward.values(), []):
        copy.wait_send()


def back_call(
    grad_attx, grad_half, grad_down, grad_w_out, small_in, raw, query, both, att, inverse, states_all,
    w_qkv, qk_gain, places, grad_direct, rows,
):
    tok_rows, model_width = grad_direct.shape
    chips = grad_attx.shape[0]
    heads = qk_gain.shape[0]
    head_cols = heads * HEAD_DIM
    group_rows = chips * tok_rows
    half_units = grad_half.shape[2]
    half_cols = w_qkv.shape[2]
    chip_rows = CORES * rows
    seq_rows = chips * chip_rows
    f32, low = jnp.float32, jnp.bfloat16
    shape = jax.ShapeDtypeStruct
    per_head = (heads, group_rows, HEAD_DIM)
    return pl.pallas_call(
        back_kernel,
        out_shape=[
            shape((tok_rows, model_width), low),
            shape((rows, 3 * chips * CORES * half_units), f32),
            shape((rows, 4 * model_width), f32),
            shape((3, model_width), f32),
            shape((2, chips * CORES * half_units), f32),
        ],
        in_specs=[in_vmem(), in_hbm()] + [in_vmem()] * 11 + [in_smem(), in_vmem()],
        out_specs=[in_vmem(), in_hbm(), in_hbm(), in_vmem(), in_vmem()],
        scratch_shapes=[
            VMEM((group_rows, head_cols), low),
            VMEM(per_head, low),
            VMEM((CORES, 2) + per_head, f32),
            VMEM((2,) + per_head, low),
            VMEM((2,) + per_head, low),
            VMEM((3,) + per_head, low),
            VMEM((CORES, group_rows, half_cols), low),
            VMEM((group_rows, model_width), low),
            VMEM((3, tok_rows, model_width), low),
            VMEM((tok_rows, model_width), low),
            VMEM((tok_rows, model_width), low),
            VMEM((tok_rows, model_width), f32),
            VMEM((model_width, group_rows), low),
            VMEM((CORES, model_width, half_cols), low),
            VMEM((model_width, half_cols), low),
            VMEM((3, seq_rows, half_cols), low),
            VMEM((chips, chip_rows, half_cols), low),
            VMEM((chips, chip_rows, half_cols), f32),
            VMEM((4, seq_rows, half_units), low),
            VMEM((4, seq_rows, half_units), low),
            VMEM((3, 3, seq_rows, half_units), low),
            VMEM((3, seq_rows, half_units), low),
            VMEM((4, chips, chip_rows, half_units), low),
            VMEM((3, chips, chip_rows, half_units), f32),
            VMEM((chip_rows, half_units), f32),
            VMEM(small_in.shape, f32),
            VMEM(small_in.shape, f32),
            VMEM((3,) + small_in.shape, f32),
            VMEM((heads, 1, HEAD_DIM), f32),
            VMEM((chips,) + small_in.shape, f32),
            VMEM((rows, 3 * model_width), f32),
            VMEM((CORES, chips, rows, half_cols), f32),
            VMEM((1, CORES * group_rows), jnp.int32),
            dma(17), dma(4), dma(4), dma(4, 4), dma(4, 4), dma(1), dma(1), dma(1), dma(1),
            dma(4), dma(4), dma(1), dma(1), dma(4), dma(4), dma(4), dma(4), dma(4, 4), dma(4, 4),
            dma(4, 4), dma(4, 4), dma(4), dma(4), dma(4), dma(4),
        ],
        compiler_params=pltpu.CompilerParams(
            collective_id=3, has_side_effects=True, vmem_limit_bytes=LIMIT
        ),
        name="back",
    )(
        grad_attx, grad_half, grad_down, grad_w_out, small_in, raw, query, both, att, inverse, states_all,
        w_qkv, qk_gain, places, grad_direct,
    )


def shards_split(states, cotangent, attn_weights, mlp_weights, feature_gains, unit_gains, block_place):
    tok_rows, model_width = states.shape
    ff_width = unit_gains.shape[0]
    n_seq, n_ctx = lax.axis_size("seq"), lax.axis_size("ctx")
    chips = n_ctx // CORES
    chip = lax.axis_index("ctx") // CORES
    heads = HEADS // chips
    head_cols = heads * HEAD_DIM
    units = ff_width // chips
    rows = attn_weights.shape[0]
    qk_gain = lax.dynamic_slice_in_dim(feature_gains[:, 0], chip * head_cols, head_cols)
    qk_gain = qk_gain.reshape(heads, 1, HEAD_DIM)
    states_all, w_qkv, w_out, w_up, w_gate, low_down, raw, query, both, att, inverse, attx = attend_call(
        states, attn_weights, mlp_weights, qk_gain, block_place
    )
    gain_u = lax.dynamic_slice_in_dim(unit_gains[:, 0], chip * units, units)
    gain_v = lax.dynamic_slice_in_dim(unit_gains[:, 1], chip * units, units) * math.sqrt(D)
    out_low, grad_attx, grad_w_out, grad_direct, small, grad_half, grad_down = mlp_call(
        attx, states, cotangent, w_out, feature_gains[:, 1].reshape(1, model_width),
        feature_gains[:, 2].reshape(1, model_width), gain_u.reshape(CORES, 1, units // CORES),
        gain_v.reshape(CORES, 1, units // CORES), w_up, w_gate, low_down,
    )
    grad_states, grad_mlp, grad_attn, feature, unit = back_call(
        grad_attx, grad_half, grad_down, grad_w_out, small, raw, query, both, att, inverse, states_all,
        w_qkv, qk_gain, block_place, grad_direct, rows,
    )
    rank = lax.axis_index(ALL)
    unit_rows_own = ff_width // (n_seq * n_ctx)
    return (
        out_low,
        grad_states,
        grad_attn,
        grad_mlp,
        lax.dynamic_slice_in_dim(feature, rank * rows, rows, axis=1).T,
        lax.dynamic_slice_in_dim(unit, rank * unit_rows_own, unit_rows_own, axis=1).T,
    )


def solution(mesh):
    in_specs = (
        P(("seq", "ctx"), None),
        P(("seq", "ctx"), None),
        P(("seq", "ctx"), None),
        P(("seq", "ctx"), None),
        P(),
        P(),
        P("seq", None),
    )
    out_specs = (
        P(("seq", "ctx"), None),
        P(("seq", "ctx"), None),
        P(("seq", "ctx"), None),
        P(("seq", "ctx"), None),
        P(("seq", "ctx"), None),
        P(("seq", "ctx"), None),
    )
    chips = mesh.shape["ctx"] // CORES
    shards = shards_split if fits(mesh.shape["seq"], chips) else shards_general
    return jax.shard_map(shards, mesh=mesh, in_specs=in_specs, out_specs=out_specs, check_vma=False)
```

```python
import functools
import math

import jax
import jax.numpy as jnp
from jax import lax
from jax.experimental import pallas as pl
from jax.experimental.pallas import tpu as pltpu
from jax.sharding import PartitionSpec as P

D = 1280
HEADS = 20
HEAD_DIM = 64


EPSILON = 1e-06
NEG_LARGE = -1e30


def unit_rows(values_in):
    factor = lax.rsqrt(jnp.sum(values_in * values_in, axis=-1, keepdims=True) + EPSILON)
    return (values_in * factor, factor)


def unit_back(normed, factor, upstream):
    return factor * (upstream - normed * jnp.sum(upstream * normed, axis=-1, keepdims=True))


def contract_rows(left_mat, right_mat):
    return lax.dot_general(
        left_mat, right_mat, (((0,), (0,)), ((), ())), preferred_element_type=jnp.float32
    )


def contract_cols(left_mat, right_mat):
    return lax.dot_general(
        left_mat, right_mat, (((1,), (1,)), ((), ())), preferred_element_type=jnp.float32
    )


def shards_general(states, cotangent, attn_weights, mlp_weights, feature_gains, unit_gains, block_place):
    tok_rows = states.shape[0]
    model_width = states.shape[1]
    ff_width = unit_gains.shape[0]
    score_scale = math.sqrt(HEAD_DIM)
    gate_factor = unit_gains[:, 1] * math.sqrt(D)
    w_attn = lax.all_gather(attn_weights.astype(jnp.bfloat16), ("seq", "ctx"), axis=0, tiled=True)
    w_mlp = lax.all_gather(mlp_weights.astype(jnp.bfloat16), ("seq", "ctx"), axis=0, tiled=True)
    states_full = states.astype(jnp.float32)
    projected = jnp.dot(states, w_attn[:, : 3 * model_width], preferred_element_type=jnp.float32)
    head_shape = (tok_rows, HEADS, HEAD_DIM)
    qk_gain = feature_gains[:, 0].reshape(HEADS, HEAD_DIM)
    query_unit, query_factor = unit_rows(projected[:, :model_width].reshape(head_shape))
    key_unit, key_factor = unit_rows(
        projected[:, model_width : 2 * model_width].reshape(head_shape)
    )
    query_low = (query_unit * qk_gain).astype(jnp.bfloat16)
    key_low = (key_unit * qk_gain).astype(jnp.bfloat16).reshape(tok_rows, model_width)
    value_low = projected[:, 2 * model_width :].astype(jnp.bfloat16)
    keys_all, values_all = (
        lax.all_gather(key_low, "ctx", axis=0, tiled=True),
        lax.all_gather(value_low, "ctx", axis=0, tiled=True),
    )
    seq_len = keys_all.shape[0]
    ctx_lanes = jnp.arange(lax.axis_size("ctx"), dtype=jnp.int32)
    places = block_place[0]
    own_block = jnp.sum(jnp.where(ctx_lanes == lax.axis_index("ctx"), places, 0))
    query_pos = own_block * tok_rows + jnp.arange(tok_rows, dtype=jnp.int32)
    key_index = jnp.arange(seq_len, dtype=jnp.int32)
    key_owner = key_index // tok_rows
    key_pos = (
        jnp.sum(jnp.where(key_owner[:, None] == ctx_lanes[None, :], places[None, :], 0), axis=1)
        * tok_rows
        + key_index % tok_rows
    )
    kblock = min(512, seq_len)
    nblocks = seq_len // kblock
    key_blocks = keys_all.reshape(nblocks, kblock, HEADS, HEAD_DIM)
    value_blocks = values_all.reshape(nblocks, kblock, HEADS, HEAD_DIM)
    pos_blocks = key_pos.reshape(nblocks, kblock)

    def block_scores(key_rows, key_places):
        raw_scores = score_scale * jnp.einsum(
            "qhd,khd->hqk", query_low, key_rows, preferred_element_type=jnp.float32
        )
        allowed = key_places[None, None, :] <= query_pos[None, :, None]
        return (raw_scores, allowed)

    def max_step(running, inputs):
        running_max, running_sum = running
        key_rows, key_places = inputs
        raw_scores, allowed = block_scores(key_rows, key_places)
        masked = jnp.where(allowed, raw_scores, NEG_LARGE)
        new_max = jnp.maximum(running_max, jnp.max(masked, axis=-1))
        powered = jnp.where(allowed, jnp.exp(masked - new_max[..., None]), 0.0)
        running_sum = running_sum * jnp.exp(running_max - new_max) + jnp.sum(powered, axis=-1)
        return ((new_max, running_sum), None)

    start_max = jnp.full((HEADS, tok_rows), NEG_LARGE, jnp.float32)
    start_sum = jnp.zeros((HEADS, tok_rows), jnp.float32)
    (final_max, final_sum), _ = lax.scan(max_step, (start_max, start_sum), (key_blocks, pos_blocks))
    log_total = final_max + jnp.log(final_sum)

    def value_step(accumulated, inputs):
        key_rows, value_rows, key_places = inputs
        raw_scores, allowed = block_scores(key_rows, key_places)
        weights_low = jnp.where(allowed, jnp.exp(raw_scores - log_total[..., None]), 0.0).astype(
            jnp.bfloat16
        )
        accumulated = accumulated + jnp.einsum(
            "hqk,khd->qhd", weights_low, value_rows, preferred_element_type=jnp.float32
        )
        return (accumulated, None)

    attended, _ = lax.scan(
        value_step, jnp.zeros(head_shape, jnp.float32), (key_blocks, value_blocks, pos_blocks)
    )
    attended_low = attended.reshape(tok_rows, model_width).astype(jnp.bfloat16)
    branch_attn = jnp.dot(
        attended_low, w_attn[:, 3 * model_width :], preferred_element_type=jnp.float32
    )
    attn_unit, attn_factor = unit_rows(branch_attn)
    alpha_attn = feature_gains[:, 1]
    mixed_one, mix_factor = unit_rows(states_full + alpha_attn * (attn_unit - states_full))
    mixed_low = mixed_one.astype(jnp.bfloat16)
    up_gate = jnp.dot(mixed_low, w_mlp[:, : 2 * ff_width], preferred_element_type=jnp.float32)
    up_scaled = up_gate[:, :ff_width] * unit_gains[:, 0]
    gate_scaled = up_gate[:, ff_width:] * gate_factor
    sigmoid_gate = jax.nn.sigmoid(gate_scaled)
    activated = gate_scaled * sigmoid_gate
    hidden = (activated * up_scaled).astype(jnp.bfloat16)
    branch_mlp = contract_cols(hidden, w_mlp[:, 2 * ff_width :])
    mlp_unit, mlp_factor = unit_rows(branch_mlp)
    alpha_mlp = feature_gains[:, 2]
    out_full, out_factor = unit_rows(mixed_one + alpha_mlp * (mlp_unit - mixed_one))
    grad_mix_two = unit_back(out_full, out_factor, cotangent.astype(jnp.float32))
    grad_alpha_m = jnp.sum(grad_mix_two * (mlp_unit - mixed_one), axis=0)
    grad_branch_mlp = unit_back(mlp_unit, mlp_factor, grad_mix_two * alpha_mlp).astype(jnp.bfloat16)
    grad_hidden = jnp.dot(
        grad_branch_mlp, w_mlp[:, 2 * ff_width :], preferred_element_type=jnp.float32
    )
    grad_up_scaled = grad_hidden * activated
    grad_gate_scaled = (
        grad_hidden * up_scaled * sigmoid_gate * (1.0 + gate_scaled * (1.0 - sigmoid_gate))
    )
    grad_s_u = jnp.sum(grad_up_scaled * up_gate[:, :ff_width], axis=0)
    grad_s_v = jnp.sum(grad_gate_scaled * up_gate[:, ff_width:], axis=0) * math.sqrt(D)
    grad_up_gate = jnp.concatenate(
        [grad_up_scaled * unit_gains[:, 0], grad_gate_scaled * gate_factor], axis=1
    ).astype(jnp.bfloat16)
    grad_mixed_one = grad_mix_two * (1.0 - alpha_mlp) + contract_cols(
        grad_up_gate, w_mlp[:, : 2 * ff_width]
    )
    grad_mix_one = unit_back(mixed_one, mix_factor, grad_mixed_one)
    grad_alpha_a = jnp.sum(grad_mix_one * (attn_unit - states_full), axis=0)
    grad_branch_attn = unit_back(attn_unit, attn_factor, grad_mix_one * alpha_attn).astype(
        jnp.bfloat16
    )
    grad_attended = (
        contract_cols(grad_branch_attn, w_attn[:, 3 * model_width :])
        .astype(jnp.bfloat16)
        .reshape(head_shape)
    )
    row_dots = jnp.einsum("qhd,qhd->hq", grad_attended.astype(jnp.float32), attended)

    def grad_step(grad_query, inputs):
        key_rows, value_rows, key_places = inputs
        raw_scores, allowed = block_scores(key_rows, key_places)
        probabilities = jnp.where(allowed, jnp.exp(raw_scores - log_total[..., None]), 0.0)
        grad_prob = jnp.einsum(
            "qhd,khd->hqk", grad_attended, value_rows, preferred_element_type=jnp.float32
        )
        grad_scores = (probabilities * (grad_prob - row_dots[..., None])).astype(jnp.bfloat16)
        grad_query = grad_query + score_scale * jnp.einsum(
            "hqk,khd->qhd", grad_scores, key_rows, preferred_element_type=jnp.float32
        )
        key_terms = score_scale * jnp.einsum(
            "hqk,qhd->khd", grad_scores, query_low, preferred_element_type=jnp.float32
        )
        value_terms = jnp.einsum(
            "hqk,qhd->khd",
            probabilities.astype(jnp.bfloat16),
            grad_attended,
            preferred_element_type=jnp.float32,
        )
        return (grad_query, (key_terms, value_terms))

    grad_query_low, (key_terms, value_terms) = lax.scan(
        grad_step, jnp.zeros(head_shape, jnp.float32), (key_blocks, value_blocks, pos_blocks)
    )
    key_terms = key_terms.reshape(seq_len, model_width)
    value_terms = value_terms.reshape(seq_len, model_width)
    own_key_grad, own_value_grad = (
        lax.psum_scatter(
            key_terms.astype(jnp.bfloat16), "ctx", scatter_dimension=0, tiled=True
        ).astype(jnp.float32),
        lax.psum_scatter(
            value_terms.astype(jnp.bfloat16), "ctx", scatter_dimension=0, tiled=True
        ).astype(jnp.float32),
    )
    grad_key_low = own_key_grad.reshape(head_shape)
    grad_s_qk = jnp.sum(grad_query_low * query_unit + grad_key_low * key_unit, axis=0).reshape(
        model_width
    )
    grad_query_raw = unit_back(query_unit, query_factor, grad_query_low * qk_gain).reshape(
        tok_rows, model_width
    )
    grad_key_raw = unit_back(key_unit, key_factor, grad_key_low * qk_gain).reshape(
        tok_rows, model_width
    )
    grad_projected = jnp.concatenate([grad_query_raw, grad_key_raw, own_value_grad], axis=1).astype(
        jnp.bfloat16
    )
    grad_states = grad_mix_one * (1.0 - alpha_attn) + contract_cols(
        grad_projected, w_attn[:, : 3 * model_width]
    )
    feature_total = jnp.stack([grad_s_qk, grad_alpha_a, grad_alpha_m], axis=1)
    unit_fold = jnp.stack([grad_s_u, grad_s_v], axis=1).reshape(
        model_width, 2 * ff_width // model_width
    )
    attn_cols = 4 * model_width
    mlp_cols = 3 * ff_width
    attn_share = lax.psum_scatter(
        jnp.concatenate(
            [
                contract_rows(states, grad_projected),
                contract_rows(attended_low, grad_branch_attn),
                feature_total,
            ],
            axis=1,
        ),
        ("seq", "ctx"),
        scatter_dimension=0,
        tiled=True,
    )
    mlp_share = lax.psum_scatter(
        jnp.concatenate(
            [
                contract_rows(mixed_low, grad_up_gate),
                contract_rows(grad_branch_mlp, hidden),
                unit_fold,
            ],
            axis=1,
        ),
        ("seq", "ctx"),
        scatter_dimension=0,
        tiled=True,
    )
    grad_attn = attn_share[:, :attn_cols]
    grad_feature = attn_share[:, attn_cols:]
    grad_mlp = mlp_share[:, :mlp_cols]
    grad_unit = mlp_share[:, mlp_cols:].reshape(
        unit_gains.shape[0] // lax.axis_size(("seq", "ctx")), 2
    )
    return (
        out_full.astype(jnp.bfloat16),
        grad_states.astype(jnp.bfloat16),
        grad_attn,
        grad_mlp,
        grad_feature,
        grad_unit,
    )


CORES = 2
ALL = ("seq", "ctx")


def fits(n_seq, chips):
    return n_seq == 4 and chips == 4 and HEADS % chips == 0


MESH = pl.DeviceIdType.MESH
VMEM = pltpu.VMEM
CHIPS = 4
STEPS = (1, 2, 3)
LIMIT = 60 * 1024 * 1024


def place_of():
    seq = lax.axis_index("seq")
    ctx = lax.axis_index("ctx")
    return seq, ctx // CORES, ctx % CORES


def chip_peer(step):
    seq, chip, core = place_of()
    other = lax.rem(chip + step, CHIPS)
    return (seq, other * CORES + core), other


def seq_peer(step):
    seq, chip, core = place_of()
    other = seq ^ step
    return (other, chip * CORES + core), other


def twin():
    seq, chip, core = place_of()
    return (seq, chip * CORES + 1 - core)


def meet():
    devices = [chip_peer(step)[0] for step in STEPS] + [seq_peer(step)[0] for step in STEPS] + [twin()]
    gate = pltpu.get_barrier_semaphore()
    for device in devices:
        pl.semaphore_signal(gate, inc=1, device_id=device, device_id_type=MESH)
    pl.semaphore_wait(gate, len(devices))


def remote(src, dst, send, recv, device):
    return pltpu.make_async_remote_copy(
        src_ref=src, dst_ref=dst, send_sem=send, recv_sem=recv, device_id=device,
        device_id_type=MESH,
    )


def begin(copy):
    copy.start()
    return copy


def rows_at(index, count):
    return pl.ds(pl.multiple_of(index * count, count), count)


def device_on(chip):
    seq, _, core = place_of()
    return (seq, chip * CORES + core)


def when(condition, action):
    pl.when(condition)(action)


PIECES = 2


def piece_at(block, piece, count):
    step = count // PIECES
    return pl.ds(pl.multiple_of(block * count + piece * step, step), step)


def gather_copy(src, everything, count, block, side, hop, piece, send, recv):
    chip = place_of()[1]
    there = everything.at[piece_at(block, piece, count)]
    near = chip + 1 if side == 0 else chip - 1
    here = there if src is None else src.at[piece_at(0, piece, count)]
    return remote(here, there, send.at[side, hop, piece], recv.at[side, hop, piece], device_on(near))


def gather_start(src, everything, count, send, recv):
    chip = place_of()[1]
    for piece in range(PIECES):
        for side in range(2):
            copy = gather_copy(src, everything, count, chip, side, 0, piece, send, recv)
            when(chip < CHIPS - 1 if side == 0 else chip > 0, copy.start)


def gather_hop(everything, count, hop, send, recv):
    chip = place_of()[1]
    for piece in range(PIECES):
        for side in range(2):
            block = chip - hop if side == 0 else chip + hop

            def pass_on(side=side, piece=piece, block=block):
                gather_copy(None, everything, count, block, side, hop - 1, piece, send, recv).wait_recv()
                if hop < CHIPS - 1:
                    copy = gather_copy(None, everything, count, block, side, hop, piece, send, recv)
                    when(chip < CHIPS - 1 if side == 0 else chip > 0, copy.start)

            when(block >= 0 if side == 0 else block < CHIPS, pass_on)


def gather_drain(everything, count, send, recv):
    chip = place_of()[1]
    for hop in range(CHIPS - 1):
        for piece in range(PIECES):
            for side in range(2):
                copy = gather_copy(None, everything, count, chip, side, hop, piece, send, recv)
                block = chip - hop if side == 0 else chip + hop
                sent = (block >= 0) & (chip < CHIPS - 1) if side == 0 else (block < CHIPS) & (chip > 0)
                when(sent, copy.wait_send)


def inside_line():
    chip = place_of()[1]
    return (chip > 0) & (chip < CHIPS - 1)


def spans_line(other):
    return abs(place_of()[1] - other) == CHIPS - 1


def reduce_start(part, count, sums, via, send, recv):
    chip = place_of()[1]
    near = jnp.where(chip == 0, 1, CHIPS - 2)
    first = remote(part.at[rows_at(CHIPS - 1 - chip, count)], via, send.at[0], recv.at[0], device_on(near))

    def ahead():
        first.start()
        first.wait_send()

    when(jnp.logical_not(inside_line()), ahead)
    for step in STEPS:
        device, other = chip_peer(step)
        copy = remote(part.at[rows_at(other, count)], sums.at[step - 1], send.at[step], recv.at[step], device)
        if step == 2:
            when(jnp.logical_not(inside_line()), copy.start)
        else:
            when(jnp.logical_not(spans_line(other)), copy.start)


def reduce_relay(part, count, sums, via, mixed, send, recv):
    chip = place_of()[1]
    other = lax.rem(chip + 2, CHIPS)
    copy = remote(mixed, sums.at[1], send.at[2], recv.at[2], device_on(other))

    def pass_on():
        remote(mixed, via, send.at[0], recv.at[0], device_on(other)).wait_recv()
        mixed[...] = (
            part[rows_at(other, count), :].astype(jnp.float32) + via[...].astype(jnp.float32)
        ).astype(mixed.dtype)
        copy.start()

    when(inside_line(), pass_on)


def reduce_wait(part, count, sums, total, send, recv):
    chip = place_of()[1]
    total[...] = part[rows_at(chip, count), :].astype(jnp.float32)
    for step in (1, 3, 2):
        source = lax.rem(chip + CHIPS - step, CHIPS)

        def add(step=step, source=source):
            here = sums.at[step - 1]
            remote(here, here, send.at[step], recv.at[step], device_on(source)).wait_recv()
            total[...] += sums[step - 1].astype(jnp.float32)

        when(jnp.logical_not(spans_line(source)), add)


def reduce_drain(part, count, sums, send, recv):
    rows = part.at[rows_at(0, count)]
    for step in STEPS:
        device, other = chip_peer(step)
        copy = remote(rows, sums.at[step - 1], send.at[step], recv.at[step], device)
        when(jnp.logical_not(spans_line(other)), copy.wait_send)


def side_peer(side):
    return seq_peer(side + 1)


def seq_rows_at(block, side, count):
    half = count // 2
    return pl.ds(pl.multiple_of(block * count + side * half, half), half)


def spread_start(src, dst, count, send, recv):
    seq = place_of()[0]
    return [
        begin(remote(src, dst.at[rows_at(seq, count)], send.at[side], recv.at[side], side_peer(side)[0]))
        for side in range(2)
    ]


def spread_relay(dst, count, send, recv):
    copies = []
    for side in range(2):
        block = side_peer(side)[1]
        whole = dst.at[rows_at(block, count)]
        remote(whole, whole, send.at[side], recv.at[side], side_peer(side)[0]).wait_recv()
        part = dst.at[seq_rows_at(block, side, count)]
        copies.append(begin(remote(part, part, send.at[2 + side], recv.at[2 + side], side_peer(1 - side)[0])))
    return copies


def fold_start(src, got, count, send, recv):
    seq = place_of()[0]
    copies = []
    for side in range(2):
        device, other = side_peer(side)
        for at, block in enumerate((other, seq ^ 3)):
            here = src.at[seq_rows_at(block, side, count)]
            copies.append(begin(remote(here, got.at[side, at], send.at[side, at], recv.at[side, at], device)))
    return copies


def fold_relay(src, got, held, last, count, copies, send, recv):
    more = []
    for side in range(2):
        device, other = side_peer(1 - side)
        copies[2 * side + 1].wait_recv()
        rows = seq_rows_at(other, side, count)
        held[side] = (src[rows, :].astype(jnp.float32) + got[side, 1].astype(jnp.float32)).astype(held.dtype)
        more.append(begin(remote(held.at[side], last.at[side], send.at[2, side], recv.at[2, side], device)))
    return more


def fold_end(src, got, last, out, count, copies, more):
    seq = place_of()[0]
    half = count // 2
    for side in range(2):
        copies[2 * side].wait_recv()
        more[side].wait_recv()
        rows = seq_rows_at(seq, side, count)
        out[side * half : (side + 1) * half, :] = (
            src[rows, :].astype(jnp.float32) + got[side, 0].astype(jnp.float32) + last[side].astype(jnp.float32)
        ).astype(out.dtype)


def to_line(src, there, send, recv):
    return [
        begin(remote(src, there, send.at[step], recv.at[step], chip_peer(step)[0])) for step in STEPS
    ]


def dot(left, right):
    return jnp.dot(left, right, preferred_element_type=jnp.float32)


def dot_nt(left, right):
    return lax.dot_general(
        left, right, (((1,), (1,)), ((), ())), preferred_element_type=jnp.float32
    )


def dot_tn(left, right):
    return lax.dot_general(
        left, right, (((0,), (0,)), ((), ())), preferred_element_type=jnp.float32
    )


def dma(*shape):
    return pltpu.SemaphoreType.DMA(shape)


def line_dma():
    return dma(2, CHIPS, PIECES)


def in_vmem():
    return pl.BlockSpec(memory_space=pltpu.VMEM)


def in_hbm():
    return pl.BlockSpec(memory_space=pl.ANY)


def key_positions(places, key_pos, tok_rows):
    lanes = lax.broadcasted_iota(jnp.int32, (1, tok_rows), 1)
    for at_core in range(CORES):
        for at_chip in range(CHIPS):
            start = (at_core * CHIPS + at_chip) * tok_rows
            key_pos[:, start : start + tok_rows] = places[0, CORES * at_chip + at_core] * tok_rows + lanes


def kept_pairs(places, key_pos, block, core, tok_rows):
    down = lax.broadcasted_iota(jnp.int32, (tok_rows, 1), 0)
    return key_pos[...] <= places[0, CORES * block + core] * tok_rows + down


def attend_kernel(
    states, attn_src, mlp_src, qk_gain, places,
    to_states, to_qkv, to_out, w_up, w_gate, low_down, to_raw, to_query, to_both, to_att, to_inv, attx,
    states_all, w_qkv, w_out, raw_out, query_out, both, att_out, inv_out, src_q, stage_q, low_q, stage_o, low_o, stage_m, low_m, raw, att_low, key_pos,
    local_sem, keep_sem, att_sem, x_send, x_recv, q_send, q_recv, mt_send, mt_recv, wz_send, wz_recv,
    ws_send, ws_recv, wt_send, wt_recv, oz_send, oz_recv, os_send, os_recv, m_send, m_recv,
    ms_send, ms_recv, kv_send, kv_recv, a_send, a_recv,
):
    seq, chip, core = place_of()
    rows = attn_src.shape[0]
    tok_rows, model_width = states.shape
    heads = qk_gain.shape[0]
    head_cols = heads * HEAD_DIM
    part_cols = head_cols // CORES
    group_rows = tok_rows * CHIPS
    chip_rows = CORES * rows
    seq_rows = CHIPS * chip_rows
    half_units = w_up.shape[1]
    half_width = model_width // CORES
    ff_width = mlp_src.shape[1] // 3
    low = jnp.bfloat16
    for at in range(CHIPS):
        for half in range(CORES):
            for which in range(3):
                start = which * model_width + at * head_cols + half * part_cols
                src_q[at, half, :, which * part_cols : (which + 1) * part_cols] = attn_src[:, start : start + part_cols]
    meet()
    block = rows_at(chip, tok_rows)
    mine = rows_at(core, rows)
    half_at = pl.ds(pl.multiple_of(3 * model_width + core * half_width, 128), half_width)
    other_at = pl.ds(pl.multiple_of(3 * model_width + (1 - core) * half_width, 128), half_width)
    swap_o = begin(remote(attn_src.at[:, other_at], stage_o.at[mine], q_send.at[1], q_recv.at[1], twin()))
    swap_q = begin(remote(src_q.at[:, 1 - core], stage_q.at[:, mine], q_send.at[0], q_recv.at[0], twin()))
    stage_o[mine, :] = attn_src[:, half_at]
    stage_q[:, mine, :] = src_q[:, core]
    m_swaps, m_keeps = [], []
    for part in range(3):
        for at in range(CHIPS):
            start = part * ff_width + at * CORES * half_units
            theirs = pl.ds(pl.multiple_of(start + (1 - core) * half_units, 128), half_units)
            ours = pl.ds(pl.multiple_of(start + core * half_units, 128), half_units)
            there = stage_m.at[part, at, mine]
            m_swaps.append(begin(remote(mlp_src.at[:, theirs], there, mt_send.at[part, at], mt_recv.at[part, at], twin())))
            m_keeps.append(begin(pltpu.make_async_copy(mlp_src.at[:, ours], there, local_sem.at[part * CHIPS + at])))
    my_rows = rows_at(seq * CHIPS + chip, chip_rows)
    seq_at = rows_at(seq, seq_rows)
    swap_o.wait()
    low_o[...] = stage_o[...].astype(low)
    o_line = to_line(low_o, w_out.at[core, my_rows], oz_send, oz_recv)
    w_out[core, my_rows, :] = low_o[...]
    swap_q.wait()
    low_q[...] = stage_q[...].astype(low)
    line = []
    for step in STEPS:
        device, other = chip_peer(step)
        line.append(begin(remote(low_q.at[other], w_qkv.at[core, my_rows], wz_send.at[step], wz_recv.at[step], device)))
    w_qkv[core, my_rows, :] = low_q[chip]
    states_all[block, :] = states[...]
    key_positions(places, key_pos, tok_rows)
    for copy in line:
        copy.wait_recv()
    gather_start(states, states_all, tok_rows, x_send, x_recv)

    def across(whole, send, recv):
        return spread_start(whole.at[seq_at], whole, seq_rows, send, recv)

    q_across = across(w_qkv.at[core], ws_send, ws_recv)
    for copy in m_keeps:
        copy.wait()
    for copy in m_swaps:
        copy.wait()
    low_m[...] = stage_m[:2].astype(low)
    low_down[...] = stage_m[2].astype(low)
    gather_hop(states_all, tok_rows, 1, x_send, x_recv)
    more = spread_relay(w_qkv.at[core], seq_rows, ws_send, ws_recv)
    for copy in o_line:
        copy.wait_recv()
    o_across = across(w_out.at[core], os_send, os_recv)
    for copy in more:
        copy.wait_recv()
    q_across += more
    swap = begin(remote(w_qkv.at[core], w_qkv.at[core], wt_send.at[0], wt_recv.at[0], twin()))
    gather_hop(states_all, tok_rows, 2, x_send, x_recv)
    o_more = spread_relay(w_out.at[core], seq_rows, os_send, os_recv)
    gather_hop(states_all, tok_rows, 3, x_send, x_recv)
    here = rows_at(chip, chip_rows)

    def to_chips(part, there):
        return [
            begin(remote(low_m.at[part, chip_peer(step)[1]], there, m_send.at[part, step], m_recv.at[part, step], chip_peer(step)[0]))
            for step in STEPS
        ]

    m_line = to_chips(0, w_up.at[my_rows])
    w_up[my_rows, :] = low_m[0, chip]
    w_gate[here, :] = low_m[1, chip]
    swap.wait()
    kept = []

    def keep(src, dst):
        kept.append(begin(pltpu.make_async_copy(src, dst, keep_sem.at[len(kept)])))

    keep(states_all, to_states)
    keep(w_qkv, to_qkv)
    for half in range(CORES):
        value = dot(states_all[...], w_qkv[half])
        for which in range(3):
            start = which * head_cols + half * part_cols
            raw[:, start : start + part_cols] = value[:, which * part_cols : (which + 1) * part_cols]
    for head in reversed(range(3 * heads)):
        which, head = head // heads, head % heads
        start = which * head_cols + head * HEAD_DIM
        value = raw[:, start : start + HEAD_DIM]
        if which == 2:
            both[core, 1, head] = value.astype(low)
            continue
        factor = lax.rsqrt(jnp.sum(value * value, axis=-1, keepdims=True) + EPSILON)
        scaled = (value * factor * qk_gain[head]).astype(low)
        raw_out[which, head] = value
        if which == 1:
            both[core, 0, head] = scaled
            if head == 0:
                swap = begin(remote(both.at[core], both.at[core], kv_send.at[0], kv_recv.at[0], twin()))
        else:
            query_out[head] = scaled * math.sqrt(HEAD_DIM)
    keep(raw_out, to_raw)
    keep(query_out, to_query)
    for copy in m_line + o_more:
        copy.wait_recv()
    m_line += to_chips(1, w_gate.at[here])
    swap_o = begin(remote(w_out.at[core], w_out.at[core], wt_send.at[1], wt_recv.at[1], twin()))
    up_across = across(w_up, ms_send, ms_recv)
    swap.wait()
    keep(both, to_both)

    def one_block(index, carry):
        step = lax.rem(index + 1, CHIPS)
        device, other = chip_peer(step)
        at = rows_at(other, tok_rows)
        allowed = kept_pairs(places, key_pos, other, core, tok_rows)

        def one_head(head, carry):
            query = query_out[head, at, :]
            scores = jnp.concatenate([dot_nt(query, both[half, 0, head]) for half in range(CORES)], axis=1)
            powered = jnp.exp(jnp.where(allowed, scores, NEG_LARGE))
            inverse = 1.0 / jnp.sum(powered, axis=-1, keepdims=True)
            weights = (powered * inverse).astype(low)
            att_out[head, at, :] = sum(
                dot(weights[:, half * group_rows : (half + 1) * group_rows], both[half, 1, head])
                for half in range(CORES)
            )
            inv_out[head, at, :] = inverse
            return carry

        lax.fori_loop(0, heads, one_head, 0)
        for head in range(heads):
            att_low[at, head * HEAD_DIM : (head + 1) * HEAD_DIM] = att_out[head, at, :].astype(low)
        when(step != 0, remote(att_low.at[at], attx.at[chip], a_send.at[step], a_recv.at[step], device).start)
        pltpu.make_async_copy(att_out.at[:, at], to_att.at[:, at], att_sem.at[0, step]).start()
        pltpu.make_async_copy(inv_out.at[:, at], to_inv.at[:, at], att_sem.at[1, step]).start()
        return carry

    lax.fori_loop(0, CHIPS, one_block, 0)
    attx[chip] = att_low[block, :]
    swap_o.wait()
    keep(w_out, to_out)
    up_more = spread_relay(w_up, seq_rows, ms_send, ms_recv)
    for step in STEPS:
        remote(att_low.at[block], attx.at[chip], a_send.at[step], a_recv.at[step], chip_peer(step)[0]).wait()
    for copy in m_line[3:] + up_more:
        copy.wait_recv()
    gather_drain(states_all, tok_rows, x_send, x_recv)
    for step in range(CHIPS):
        pltpu.make_async_copy(att_out.at[:, block], to_att.at[:, block], att_sem.at[0, step]).wait()
        pltpu.make_async_copy(inv_out.at[:, block], to_inv.at[:, block], att_sem.at[1, step]).wait()
    for copy in kept:
        copy.wait()
    for copy in m_line + line + o_line + q_across + o_across + o_more + up_across + up_more:
        copy.wait_send()


def in_smem():
    return pl.BlockSpec(memory_space=pltpu.SMEM)


def attend_call(states, attn_src, mlp_src, qk_gain, places):
    tok_rows, model_width = states.shape
    rows = attn_src.shape[0]
    heads = qk_gain.shape[0]
    chips, chip_rows = CHIPS, CORES * rows
    group_rows = chips * tok_rows
    half_units = mlp_src.shape[1] // 3 // chips // CORES
    half_width, half_cols = model_width // CORES, 3 * heads * HEAD_DIM // CORES
    f32, low = jnp.float32, jnp.bfloat16
    shape = jax.ShapeDtypeStruct
    return pl.pallas_call(
        attend_kernel,
        out_shape=[
            shape((group_rows, model_width), low),
            shape((CORES, model_width, half_cols), low),
            shape((CORES, model_width, half_width), low),
            shape((model_width, half_units), low),
            shape((chips * chip_rows, half_units), low),
            shape((chips, chip_rows, half_units), low),
            shape((2, heads, group_rows, HEAD_DIM), f32),
            shape((heads, group_rows, HEAD_DIM), low),
            shape((CORES, 2, heads, group_rows, HEAD_DIM), low),
            shape((heads, group_rows, HEAD_DIM), f32),
            shape((heads, group_rows, 1), f32),
            shape((chips, tok_rows, heads * HEAD_DIM), low),
        ],
        in_specs=[in_vmem(), in_vmem(), in_hbm(), in_vmem(), in_smem()],
        out_specs=[in_hbm()] * 3 + [in_vmem()] * 3 + [in_hbm()] * 5 + [in_vmem()],
        scratch_shapes=[
            VMEM((group_rows, model_width), low),
            VMEM((CORES, model_width, half_cols), low),
            VMEM((CORES, model_width, half_width), low),
            VMEM((2, heads, group_rows, HEAD_DIM), f32),
            VMEM((heads, group_rows, HEAD_DIM), low),
            VMEM((CORES, 2, heads, group_rows, HEAD_DIM), low),
            VMEM((heads, group_rows, HEAD_DIM), f32),
            VMEM((heads, group_rows, 1), f32),
            VMEM((chips, CORES, rows, half_cols), f32),
            VMEM((chips, chip_rows, half_cols), f32),
            VMEM((chips, chip_rows, half_cols), low),
            VMEM((chip_rows, half_width), f32),
            VMEM((chip_rows, half_width), low),
            VMEM((3, chips, chip_rows, half_units), f32),
            VMEM((2, chips, chip_rows, half_units), low),
            VMEM((group_rows, 3 * heads * HEAD_DIM), f32),
            VMEM((group_rows, heads * HEAD_DIM), low),
            VMEM((1, CORES * group_rows), jnp.int32),
            dma(12), dma(6), dma(2, 4), line_dma(), line_dma(), dma(2), dma(2), dma(3, 4), dma(3, 4), dma(4), dma(4),
            dma(4), dma(4), dma(2), dma(2), dma(4), dma(4), dma(4), dma(4), dma(2, 4), dma(2, 4),
            dma(4), dma(4), dma(1), dma(1), dma(4), dma(4),
        ],
        compiler_params=pltpu.CompilerParams(
            collective_id=1, has_side_effects=True, vmem_limit_bytes=LIMIT
        ),
        name="attend",
    )(states, attn_src, mlp_src, qk_gain, places)


def unit_of(value):
    factor = lax.rsqrt(jnp.sum(value * value, axis=-1, keepdims=True) + EPSILON)
    return value * factor, factor


def mlp_kernel(
    attx, states, cotangent, from_out, alpha_attn, alpha_mlp, gain_u, gain_v, w_up, w_gate, low_down,
    out, grad_attx, grad_w_out, grad_direct, small, to_half, grad_down,
    w_out, grad_half, weights, mixed_one, attn_unit, factors, mixed_low, mixed_all, up, gate, hidden, part,
    sums, via, passed, total, grad_two, branch_low, branch_all, grad_u, grad_v, wide, turned, arrived,
    w_down, down_half, down_got, dot_u, dot_v,
    local_sem, ws_send, ws_recv, wt_send, wt_recv, x_send, x_recv, r_send, r_recv,
    g_send, g_recv, b_send, b_recv, d_send, d_recv, wz_send, wz_recv, ds_send, ds_recv,
):
    seq, chip, core = place_of()
    tok_rows, model_width = states.shape
    chip_heads = attx.shape[2]
    seq_rows, half_units = w_gate.shape
    chip_rows = low_down.shape[1]
    half_width = w_out.shape[2]
    group_rows = CHIPS * tok_rows
    block = rows_at(chip, tok_rows)
    load = begin(pltpu.make_async_copy(from_out, w_out, local_sem.at[2]))
    meet()
    seq_at = rows_at(seq, seq_rows)
    here = rows_at(chip, chip_rows)
    swaps = [begin(remote(w_up, weights.at[0, core], wt_send.at[0], wt_recv.at[0], twin()))]
    to_chips = [
        begin(remote(low_down.at[chip_peer(step)[1]], w_down.at[here], wz_send.at[step], wz_recv.at[step], chip_peer(step)[0]))
        for step in STEPS
    ]

    across = spread_start(w_gate, weights.at[1, core], seq_rows, ws_send.at[1], ws_recv.at[1])
    keeps = [
        begin(pltpu.make_async_copy(w_up, weights.at[0, core], local_sem.at[0])),
        begin(pltpu.make_async_copy(w_gate, weights.at[1, core, seq_at], local_sem.at[1])),
    ]
    w_down[here, :] = low_down[chip]
    load.wait()
    part_at = [slice(at * chip_heads, (at + 1) * chip_heads) for at in range(CHIPS)]
    half_at = [slice(half * half_width, (half + 1) * half_width) for half in range(CORES)]
    branch = jnp.concatenate(
        [sum(dot(attx[at], w_out[half, part_at[at], :]) for at in range(CHIPS)) for half in range(CORES)],
        axis=1,
    )
    unit, factor = unit_of(branch)
    attn_unit[...] = unit
    factors[0] = factor
    base = states[...].astype(jnp.float32)
    value, factor = unit_of(base + alpha_attn[...] * (unit - base))
    mixed_one[...] = value
    factors[1] = factor
    mixed_low[...] = value.astype(jnp.bfloat16)
    gather_start(mixed_low, mixed_all, tok_rows, x_send, x_recv)
    mixed_all[block, :] = mixed_low[...]
    for copy in keeps:
        copy.wait()
    for copy in to_chips:
        copy.wait_recv()
    more = spread_relay(weights.at[1, core], seq_rows, ws_send.at[1], ws_recv.at[1])
    across += spread_start(w_down, weights.at[2, core], seq_rows, ws_send.at[2], ws_recv.at[2])
    weights[2, core, seq_at, :] = w_down[...]
    gather_hop(mixed_all, tok_rows, 1, x_send, x_recv)
    for copy in more:
        copy.wait_recv()
    swaps.append(begin(remote(weights.at[1, core], weights.at[1, core], wt_send.at[1], wt_recv.at[1], twin())))
    gather_hop(mixed_all, tok_rows, 2, x_send, x_recv)
    down_more = spread_relay(weights.at[2, core], seq_rows, ws_send.at[2], ws_recv.at[2])
    gather_hop(mixed_all, tok_rows, 3, x_send, x_recv)
    for copy in swaps:
        copy.wait_recv()
    for half in range(CORES):
        up[half] = dot(mixed_all[...], weights[0, half])
        gate[half] = dot(mixed_all[...], weights[1, half])
    slab = min(64, group_rows)
    slabs = group_rows // slab

    def activate(index, carry):
        half = index // slabs
        at = rows_at(lax.rem(index, slabs), slab)
        gated = gate[half, at, :] * gain_v[half]
        scaled = up[half, at, :] * gain_u[half]
        hidden[half, at, :] = (gated * jax.nn.sigmoid(gated) * scaled).astype(jnp.bfloat16)
        return carry

    lax.fori_loop(0, CORES * slabs, activate, 0)
    for copy in down_more:
        copy.wait_recv()
    swap = begin(remote(weights.at[2, core], weights.at[2, core], wt_send.at[2], wt_recv.at[2], twin()))
    swaps.append(swap)
    swap.wait_recv()
    tile = model_width // 5

    def down(index, carry):
        at = rows_at(index, tile)
        part[0, :, at] = sum(dot_nt(hidden[half], weights[2, half, at, :]) for half in range(CORES)).astype(jnp.bfloat16)
        return carry

    lax.fori_loop(0, model_width // tile, down, 0)

    reduce_start(part.at[0], tok_rows, sums.at[0], via.at[0], r_send, r_recv)
    reduce_relay(part.at[0], tok_rows, sums.at[0], via.at[0], passed.at[0], r_send, r_recv)
    reduce_wait(part.at[0], tok_rows, sums.at[0], total, r_send, r_recv)
    mlp_unit, mlp_factor = unit_of(total[...])
    value, factor = unit_of(mixed_one[...] + alpha_mlp[...] * (mlp_unit - mixed_one[...]))
    out[...] = value.astype(jnp.bfloat16)
    above = cotangent[...].astype(jnp.float32)
    grad = factor * (above - value * jnp.sum(above * value, axis=-1, keepdims=True))
    grad_two[...] = grad
    small[...] = jnp.zeros_like(small)
    small[1:2, :] = jnp.sum(grad * (mlp_unit - mixed_one[...]), axis=0, keepdims=True)
    grad = grad * alpha_mlp[...]
    grad = mlp_factor * (grad - mlp_unit * jnp.sum(grad * mlp_unit, axis=-1, keepdims=True))
    branch_low[...] = grad.astype(jnp.bfloat16)
    gather_start(branch_low, branch_all, tok_rows, g_send, g_recv)
    branch_all[block, :] = branch_low[...]
    gather_hop(branch_all, tok_rows, 1, g_send, g_recv)
    gather_hop(branch_all, tok_rows, 2, g_send, g_recv)
    turned[0] = mixed_all[...].T
    gather_hop(branch_all, tok_rows, 3, g_send, g_recv)
    for half in range(CORES):
        wide[half] = dot(branch_all[...], weights[2, half])
    dot_u[...] = jnp.zeros_like(dot_u)
    dot_v[...] = jnp.zeros_like(dot_v)

    def deactivate(index, carry):
        half = index // slabs
        at = rows_at(lax.rem(index, slabs), slab)
        gated = gate[half, at, :] * gain_v[half]
        scaled = up[half, at, :] * gain_u[half]
        upstream = wide[half, at, :]
        sig = jax.nn.sigmoid(gated)
        to_up = upstream * (gated * sig)
        to_gate = upstream * scaled * sig * (1.0 + gated * (1.0 - sig))
        dot_u[half] += jnp.sum(to_up * up[half, at, :], axis=0, keepdims=True)
        dot_v[half] += jnp.sum(to_gate * gate[half, at, :], axis=0, keepdims=True)
        grad_u[half, at, :] = (to_up * gain_u[half]).astype(jnp.bfloat16)
        grad_v[half, at, :] = (to_gate * gain_v[half]).astype(jnp.bfloat16)
        return carry

    lax.fori_loop(0, CORES * slabs, deactivate, 0)

    def back_down(index, carry):
        at = rows_at(index, tile)
        part[1, :, at] = sum(
            dot_nt(grad_u[half], weights[0, half, at, :]) + dot_nt(grad_v[half], weights[1, half, at, :])
            for half in range(CORES)
        ).astype(jnp.bfloat16)
        return carry

    lax.fori_loop(0, model_width // tile, back_down, 0)
    for copy in swaps + more + down_more:
        copy.wait_send()
    reduce_start(part.at[1], tok_rows, sums.at[1], via.at[1], b_send, b_recv)
    turned[1] = branch_all[...].T
    swaps = {}

    def weight_grads(which, left, right):
        def one(index, carry):
            half = index // 5
            at = rows_at(lax.rem(index, 5), tile)
            weights[which, half, at, :] = dot(turned[left, at, :], right[half]).astype(jnp.bfloat16)
            return carry

        lax.fori_loop(0, CORES * 5, one, 0)
        swaps[which] = begin(remote(weights.at[which, 1 - core], arrived.at[which], d_send.at[which], d_recv.at[which], twin()))

    def both_cores(which):
        swaps[which].wait_recv()
        return (weights[which, core].astype(jnp.float32) + arrived[which].astype(jnp.float32)).astype(jnp.bfloat16)

    weight_grads(2, 1, hidden)
    reduce_relay(part.at[1], tok_rows, sums.at[1], via.at[1], passed.at[1], b_send, b_recv)
    down_half[...] = both_cores(2)
    down_across = [
        begin(remote(down_half.at[rows_at(seq_peer(step)[1], seq_rows)], down_got.at[step - 1], ds_send.at[step], ds_recv.at[step], seq_peer(step)[0]))
        for step in STEPS
    ]
    weight_grads(0, 0, grad_u)
    weight_grads(1, 0, grad_v)
    kept = []
    for which in range(2):
        grad_half[which] = both_cores(which)
        kept.append(begin(pltpu.make_async_copy(grad_half.at[which], to_half.at[which], local_sem.at[which])))
    reduce_wait(part.at[1], tok_rows, sums.at[1], total, b_send, b_recv)
    grad = grad_two[...] * (1.0 - alpha_mlp[...]) + total[...]
    value = mixed_one[...]
    grad = factors[1] * (grad - value * jnp.sum(grad * value, axis=-1, keepdims=True))
    unit = attn_unit[...]
    small[0:1, :] = jnp.sum(grad * (unit - states[...].astype(jnp.float32)), axis=0, keepdims=True)
    grad_direct[...] = grad * (1.0 - alpha_attn[...])
    grad = grad * alpha_attn[...]
    grad = factors[0] * (grad - unit * jnp.sum(grad * unit, axis=-1, keepdims=True))
    low = grad.astype(jnp.bfloat16)
    for at in range(CHIPS):
        grad_attx[at] = sum(
            dot_nt(low[:, half_at[half]], w_out[half, part_at[at], :]) for half in range(CORES)
        ).astype(jnp.bfloat16)
        for half in range(CORES):
            grad_w_out[half, at] = dot_tn(attx[at], low[:, half_at[half]]).astype(jnp.bfloat16)
    for half in range(CORES):
        unit_at = slice(half * half_units, (half + 1) * half_units)
        small[2:3, unit_at] = dot_u[half]
        small[3:4, unit_at] = dot_v[half] * math.sqrt(D)
    whole = down_half[seq_at, :].astype(jnp.float32)
    for step in STEPS:
        down_across[step - 1].wait_recv()
        whole = whole + down_got[step - 1].astype(jnp.float32)
    grad_down[...] = whole.astype(jnp.bfloat16)
    for copy in kept:
        copy.wait()
    gather_drain(mixed_all, tok_rows, x_send, x_recv)
    gather_drain(branch_all, tok_rows, g_send, g_recv)
    reduce_drain(part.at[0], tok_rows, sums.at[0], r_send, r_recv)
    reduce_drain(part.at[1], tok_rows, sums.at[1], b_send, b_recv)
    for copy in across + to_chips + down_across + [swaps[which] for which in range(3)]:
        copy.wait_send()


def mlp_call(attx, states, cotangent, w_out, alpha_attn, alpha_mlp, gain_u, gain_v, w_up, w_gate, low_down):
    tok_rows, model_width = states.shape
    chips, _, chip_heads = attx.shape
    seq_rows, half_units = w_gate.shape
    group_rows = chips * tok_rows
    f32, low = jnp.float32, jnp.bfloat16
    shape = jax.ShapeDtypeStruct
    tokens, group = (tok_rows, model_width), (group_rows, model_width)
    wide = (CORES, group_rows, half_units)
    matrix = (model_width, half_units)
    return pl.pallas_call(
        mlp_kernel,
        out_shape=[
            shape(tokens, low),
            shape(attx.shape, low),
            shape((CORES, chips, chip_heads, model_width // CORES), low),
            shape(tokens, f32),
            shape((8, max(model_width, CORES * half_units)), f32),
            shape((2,) + matrix, low),
            shape((seq_rows, half_units), low),
        ],
        in_specs=[in_vmem()] * 3 + [in_hbm()] + [in_vmem()] * 4 + [in_hbm(), in_vmem(), in_vmem()],
        out_specs=[in_vmem()] * 5 + [in_hbm(), in_vmem()],
        scratch_shapes=[
            VMEM(w_out.shape, low),
            VMEM((2,) + matrix, low),
            VMEM((3, CORES) + matrix, low),
            VMEM(tokens, f32),
            VMEM(tokens, f32),
            VMEM((2, tok_rows, 1), f32),
            VMEM(tokens, low),
            VMEM(group, low),
            VMEM(wide, f32),
            VMEM(wide, f32),
            VMEM(wide, low),
            VMEM((2,) + group, low),
            VMEM((2, 3) + tokens, low),
            VMEM((2,) + tokens, low),
            VMEM((2,) + tokens, low),
            VMEM(tokens, f32),
            VMEM(tokens, f32),
            VMEM(tokens, low),
            VMEM(group, low),
            VMEM(wide, low),
            VMEM(wide, low),
            VMEM(wide, f32),
            VMEM((2, model_width, group_rows), low),
            VMEM((3,) + matrix, low),
            VMEM((seq_rows, half_units), low),
            VMEM(matrix, low),
            VMEM((3, seq_rows, half_units), low),
            VMEM((CORES, 1, half_units), f32),
            VMEM((CORES, 1, half_units), f32),
            dma(3), dma(3, 4), dma(3, 4), dma(3), dma(3), line_dma(), line_dma(), dma(4), dma(4),
            line_dma(), line_dma(), dma(4), dma(4), dma(3), dma(3), dma(4), dma(4), dma(4), dma(4),
        ],
        compiler_params=pltpu.CompilerParams(
            collective_id=2, has_side_effects=True, vmem_limit_bytes=LIMIT
        ),
        name="mlp",
    )(
        attx, states, cotangent, w_out, alpha_attn, alpha_mlp, gain_u, gain_v, w_up, w_gate, low_down
    )


def back_kernel(
    grad_attx, from_half, grad_down, from_grad_out, small_in, from_raw, from_query, from_both, from_att,
    from_inv, from_states, from_qkv, qk_gain, places, grad_direct,
    grad_states, out_mlp, out_attn, feature, unit,
    grad_half, grad_w_out, raw, query, both, att, inverse, states_all, w_qkv, att_low, heads_low, to_keys, swap_low, swap_kv, grad_heads, grad_sides, part, sums, via, passed, total, turned,
    grad_q, half_q, seq_q, line_q, wide_q, half_o, pair_o, seq_got, seq_held, seq_last, seq_low, q_got, q_held, q_last, line_got, wide,
    wide_o, small, small_pair, small_seq, dots, small_all, flat_q, sides_q, key_pos,
    local_sem, load_sem, a_send, a_recv, s_send, s_recv, o_send, o_recv, kv_send, kv_recv, r_send, r_recv,
    qt_send, qt_recv, qs_send, qs_recv, qz_send, qz_recv, z_send, z_recv, f_send, f_recv,
    p_send, p_recv, t_send, t_recv,
):
    seq, chip, core = place_of()
    tok_rows, model_width = grad_direct.shape
    heads = qk_gain.shape[0]
    head_cols = heads * HEAD_DIM
    group_rows = CHIPS * tok_rows
    half_units = grad_half.shape[2]
    seq_rows = seq_low.shape[1]
    chip_rows = seq_rows // CHIPS
    rows = chip_rows // CORES
    part_cols = head_cols // CORES
    ff_width = out_mlp.shape[1] // 3
    scale = math.sqrt(HEAD_DIM)
    block = rows_at(chip, tok_rows)
    f32, low = jnp.float32, jnp.bfloat16
    loads = [
        begin(pltpu.make_async_copy(src, dst, load_sem.at[at]))
        for at, (src, dst) in enumerate(
            (
                (from_query, query), (from_both, both), (from_inv, inverse), (from_att, att), (from_raw, raw),
                (from_grad_out, grad_w_out), (from_states, states_all), (from_half, grad_half), (from_qkv, w_qkv),
            )
        )
    ]
    meet()
    waits = []
    line = []
    for step in STEPS:
        device, other = chip_peer(step)
        line.append(begin(remote(grad_attx.at[other], att_low.at[block], a_send.at[step], a_recv.at[step], device)))
    att_low[block, :] = grad_attx[chip]
    key_positions(places, key_pos, tok_rows)
    pair = begin(remote(from_grad_out.at[1 - core], pair_o, o_send.at[0], o_recv.at[0], twin()))
    onward = {}

    def to_chips(which, src):
        onward[which] = [
            begin(remote(src.at[rows_at(chip_peer(step)[1], chip_rows)], line_got.at[which, chip], z_send.at[which, step], z_recv.at[which, step], chip_peer(step)[0]))
            for step in STEPS
        ]
        line_got[which, chip] = src[rows_at(chip, chip_rows), :]

    def cross(which, src):
        return fold_start(src, seq_got.at[which], seq_rows, s_send.at[which], s_recv.at[which])

    def cross_on(which, src, copies):
        return fold_relay(src, seq_got.at[which], seq_held.at[which], seq_last.at[which], seq_rows, copies, s_send.at[which], s_recv.at[which])

    def cross_end(which, src, copies, more):
        fold_end(src, seq_got.at[which], seq_last.at[which], seq_low.at[which], seq_rows, copies, more)

    crossing = [cross(which, from_half.at[which]) for which in range(2)]
    to_keys[...] = jnp.zeros_like(to_keys)
    dots[...] = jnp.zeros_like(dots)
    for copy in loads:
        copy.wait()
    turned[...] = states_all[...].T
    pair.wait_recv()
    for at in range(4):
        half_o[at * seq_rows : (at + 1) * seq_rows, :] = (
            grad_w_out[core, at].astype(f32) + pair_o[at].astype(f32)
        ).astype(low)
    crossing.append(cross(2, half_o))
    tile = tok_rows
    tiles = CHIPS

    def raw_back(which, head, at, upstream):
        value = raw[which, head, at, :]
        unit, factor = unit_of(value)
        dots[head] += jnp.sum(upstream * unit, axis=0, keepdims=True)
        upstream = upstream * qk_gain[head]
        upstream = factor * (upstream - unit * jnp.sum(upstream * unit, axis=-1, keepdims=True))
        grad_heads[which, head, at, :] = upstream.astype(low)

    def one_block(step, carry):
        other = lax.rem(chip + CHIPS - step, CHIPS)
        at = rows_at(other, tok_rows)
        copy = remote(grad_attx.at[0], att_low.at[at], a_send.at[step], a_recv.at[step], device_on(other))
        when(step > 0, copy.wait_recv)
        for head in range(heads):
            heads_low[head, at, :] = att_low[at, head * HEAD_DIM : (head + 1) * HEAD_DIM]
        allowed = kept_pairs(places, key_pos, other, core, tok_rows)

        def one_head(head, carry):
            rows_q = query[head, at, :]
            grad_att = heads_low[head, at, :]
            scores = jnp.concatenate([dot_nt(rows_q, both[half, 0, head]) for half in range(CORES)], axis=1)
            probs = jnp.exp(jnp.where(allowed, scores, NEG_LARGE)) * inverse[head, at, :]
            grad_prob = jnp.concatenate([dot_nt(grad_att, both[half, 1, head]) for half in range(CORES)], axis=1)
            row_dot = jnp.sum(grad_att.astype(f32) * att[head, at, :], axis=-1, keepdims=True)
            grad_scores = (probs * (grad_prob - row_dot)).astype(low)
            weights = probs.astype(low)
            to_query = jnp.zeros((tok_rows, HEAD_DIM), f32)
            for half in range(CORES):
                cols = slice(half * group_rows, (half + 1) * group_rows)
                to_query = to_query + dot(grad_scores[:, cols], both[half, 0, head])
                to_keys[half, 0, head] += dot_tn(grad_scores[:, cols], rows_q)
                to_keys[half, 1, head] += dot_tn(weights[:, cols], grad_att)
            raw_back(0, head, at, to_query * scale)
            return carry

        lax.fori_loop(0, heads, one_head, 0)
        return carry

    lax.fori_loop(0, CHIPS, one_block, 0)
    to_chips(2, grad_down)
    sources = (grad_half.at[0], grad_half.at[1], half_o)
    onwards = [cross_on(which, sources[which], crossing[which]) for which in range(2)]
    swap_low[...] = to_keys[1 - core].astype(low)
    swap = begin(remote(swap_low, swap_kv, kv_send.at[0], kv_recv.at[0], twin()))
    swap.wait()

    def one_key(index, carry):
        head = index // tiles
        at = rows_at(lax.rem(index, tiles), tile)
        mine = to_keys[core, 0, head, at, :] + swap_kv[0, head, at, :].astype(f32)
        raw_back(1, head, at, mine)
        value = to_keys[core, 1, head, at, :] + swap_kv[1, head, at, :].astype(f32)
        grad_heads[2, head, at, :] = value.astype(low)
        return carry

    lax.fori_loop(0, heads * tiles, one_key, 0)
    for which in range(3):
        full = jnp.concatenate([grad_heads[which, head] for head in range(heads)], axis=1)
        for half in range(CORES):
            grad_sides[half, :, which * part_cols : (which + 1) * part_cols] = full[:, half * part_cols : (half + 1) * part_cols]
    onwards.append(cross_on(2, half_o, crossing[2]))
    cross_end(0, sources[0], crossing[0], onwards[0])
    to_chips(0, seq_low.at[0])
    wide_tile = model_width // 5

    def down(index, carry):
        at = rows_at(index, wide_tile)
        part[:, at] = sum(dot_nt(grad_sides[half], w_qkv[half, at, :]) for half in range(CORES)).astype(low)
        return carry

    lax.fori_loop(0, 5, down, 0)
    reduce_start(part, tok_rows, sums, via, r_send, r_recv)

    def weight_grad(index, carry):
        half = index // 5
        at = rows_at(lax.rem(index, 5), wide_tile)
        grad_q[half, at, :] = dot(turned[at, :], grad_sides[half]).astype(low)
        return carry

    lax.fori_loop(0, CORES * 5, weight_grad, 0)
    swap_q = begin(remote(grad_q.at[1 - core], half_q, qt_send.at[0], qt_recv.at[0], twin()))
    cross_end(1, sources[1], crossing[1], onwards[1])
    to_chips(1, seq_low.at[1])
    reduce_relay(part, tok_rows, sums, via, passed, r_send, r_recv)
    small[...] = small_in[...]
    small[4:5, :head_cols] = jnp.concatenate([dots[head] for head in range(heads)], axis=1)
    swap_s = begin(remote(small, small_pair, t_send.at[0], t_recv.at[0], twin()))
    swap_q.wait()
    half_q[...] = (grad_q[core].astype(f32) + half_q[...].astype(f32)).astype(low)
    crossing_q = fold_start(half_q, q_got, seq_rows, qs_send, qs_recv)
    cross_end(2, half_o, crossing[2], onwards[2])
    to_chips(3, seq_low.at[2])
    swap_s.wait()
    small[...] = small[...] + small_pair[...]
    spread_s = [
        begin(remote(small, small_seq.at[step - 1], t_send.at[step], t_recv.at[step], seq_peer(step)[0]))
        for step in STEPS
    ]
    more_q = fold_relay(half_q, q_got, q_held, q_last, seq_rows, crossing_q, qs_send, qs_recv)
    fold_end(half_q, q_got, q_last, seq_q, seq_rows, crossing_q, more_q)
    onward_q = []
    for step in STEPS:
        device, other = chip_peer(step)
        onward_q.append(begin(remote(seq_q.at[rows_at(other, chip_rows)], line_q.at[chip], qz_send.at[step], qz_recv.at[step], device)))
    line_q[chip] = seq_q[rows_at(chip, chip_rows), :]
    for copy in spread_s:
        copy.wait()
    small_pair[...] = small[...] + small_seq[0] + small_seq[1] + small_seq[2]
    small_all[chip] = small_pair[...]
    ends = to_line(small_pair, small_all.at[chip], p_send, p_recv)
    reduce_wait(part, tok_rows, sums, total, r_send, r_recv)
    grad_states[...] = (total[...] + grad_direct[...]).astype(low)

    mine = rows_at(core, rows)
    theirs = rows_at(1 - core, rows)
    last, lasts = [], []
    for which in (2, 0, 1):
        for copy in onward[which]:
            copy.wait_recv()
        for at in range(CHIPS):
            wide[which, at] = line_got[which, at].astype(f32)
            start = which * ff_width + at * CORES * half_units + core * half_units
            there = out_mlp.at[:, pl.ds(pl.multiple_of(start, 128), half_units)]
            last.append(begin(remote(wide.at[which, at, theirs], there, f_send.at[which, at], f_recv.at[which, at], twin())))
            lasts.append(begin(pltpu.make_async_copy(wide.at[which, at, mine], there, local_sem.at[3 + which * CHIPS + at])))
    for copy in onward[3]:
        copy.wait_recv()
    whole = line_got[3, 0].astype(f32)
    for at in range(1, CHIPS):
        whole = whole + line_got[3, at].astype(f32)
    wide_o[...] = whole
    start = 3 * model_width + core * half_units
    there = out_attn.at[:, pl.ds(pl.multiple_of(start, 128), half_units)]
    last.append(begin(remote(wide_o.at[theirs], there, f_send.at[3, 0], f_recv.at[3, 0], twin())))
    lasts.append(begin(pltpu.make_async_copy(wide_o.at[mine], there, local_sem.at[15])))
    for copy in onward_q:
        copy.wait_recv()
    wide_q[...] = line_q[...].astype(f32)
    sides_q[core] = wide_q[:, mine, :]
    swap_q = begin(remote(wide_q.at[:, theirs], sides_q.at[core], f_send.at[3, 1], f_recv.at[3, 1], twin()))
    for copy in ends:
        copy.wait()
    alphas = small_all[0] + small_all[1] + small_all[2] + small_all[3]
    feature[1:3, :] = alphas[0:2, :]
    for at in range(CHIPS):
        feature[0:1, at * head_cols : (at + 1) * head_cols] = small_all[at, 4:5, :head_cols]
        width = CORES * half_units
        unit[:, at * width : (at + 1) * width] = small_all[at, 2:4, :width]
    swap_q.wait()
    for at in range(CHIPS):
        for half in range(CORES):
            for which in range(3):
                start = which * model_width + at * head_cols + half * part_cols
                flat_q[:, start : start + part_cols] = sides_q[half, at, :, which * part_cols : (which + 1) * part_cols]
    lasts.append(begin(pltpu.make_async_copy(flat_q, out_attn.at[:, pl.ds(0, 3 * model_width)], local_sem.at[16])))
    for copy in last + lasts:
        copy.wait()
    reduce_drain(part, tok_rows, sums, r_send, r_recv)
    for copy in line + [pair] + sum(crossing + onwards + list(onward.values()), crossing_q + more_q + onward_q):
        copy.wait_send()


def back_call(
    grad_attx, grad_half, grad_down, grad_w_out, small_in, raw, query, both, att, inverse, states_all,
    w_qkv, qk_gain, places, grad_direct, rows,
):
    tok_rows, model_width = grad_direct.shape
    chips = grad_attx.shape[0]
    heads = qk_gain.shape[0]
    head_cols = heads * HEAD_DIM
    group_rows = chips * tok_rows
    half_units = grad_half.shape[2]
    half_cols = w_qkv.shape[2]
    chip_rows = CORES * rows
    seq_rows = chips * chip_rows
    f32, low = jnp.float32, jnp.bfloat16
    shape = jax.ShapeDtypeStruct
    per_head = (heads, group_rows, HEAD_DIM)
    return pl.pallas_call(
        back_kernel,
        out_shape=[
            shape((tok_rows, model_width), low),
            shape((rows, 3 * chips * CORES * half_units), f32),
            shape((rows, 4 * model_width), f32),
            shape((3, model_width), f32),
            shape((2, chips * CORES * half_units), f32),
        ],
        in_specs=[in_vmem(), in_hbm(), in_vmem(), in_hbm(), in_vmem()] + [in_hbm()] * 7 + [in_vmem(), in_smem(), in_vmem()],
        out_specs=[in_vmem(), in_hbm(), in_hbm(), in_vmem(), in_vmem()],
        scratch_shapes=[
            *(VMEM(value.shape, value.dtype) for value in (grad_half, grad_w_out, raw, query, both, att, inverse, states_all, w_qkv)),
            VMEM((group_rows, head_cols), low),
            VMEM(per_head, low),
            VMEM((CORES, 2) + per_head, f32),
            VMEM((2,) + per_head, low),
            VMEM((2,) + per_head, low),
            VMEM((3,) + per_head, low),
            VMEM((CORES, group_rows, half_cols), low),
            VMEM((group_rows, model_width), low),
            VMEM((3, tok_rows, model_width), low),
            VMEM((tok_rows, model_width), low),
            VMEM((tok_rows, model_width), low),
            VMEM((tok_rows, model_width), f32),
            VMEM((model_width, group_rows), low),
            VMEM((CORES, model_width, half_cols), low),
            VMEM((model_width, half_cols), low),
            VMEM((seq_rows, half_cols), low),
            VMEM((chips, chip_rows, half_cols), low),
            VMEM((chips, chip_rows, half_cols), f32),
            VMEM((4 * seq_rows, half_units), low),
            VMEM((4, seq_rows, half_units), low),
            VMEM((3, 2, 2, seq_rows // 2, half_units), low),
            VMEM((3, 2, seq_rows // 2, half_units), low),
            VMEM((3, 2, seq_rows // 2, half_units), low),
            VMEM((3, seq_rows, half_units), low),
            VMEM((2, 2, seq_rows // 2, half_cols), low),
            VMEM((2, seq_rows // 2, half_cols), low),
            VMEM((2, seq_rows // 2, half_cols), low),
            VMEM((4, chips, chip_rows, half_units), low),
            VMEM((3, chips, chip_rows, half_units), f32),
            VMEM((chip_rows, half_units), f32),
            VMEM(small_in.shape, f32),
            VMEM(small_in.shape, f32),
            VMEM((3,) + small_in.shape, f32),
            VMEM((heads, 1, HEAD_DIM), f32),
            VMEM((chips,) + small_in.shape, f32),
            VMEM((rows, 3 * model_width), f32),
            VMEM((CORES, chips, rows, half_cols), f32),
            VMEM((1, CORES * group_rows), jnp.int32),
            dma(17), dma(9), dma(4), dma(4), dma(3, 3, 2), dma(3, 3, 2), dma(1), dma(1), dma(1), dma(1),
            dma(4), dma(4), dma(1), dma(1), dma(3, 2), dma(3, 2), dma(4), dma(4), dma(4, 4), dma(4, 4),
            dma(4, 4), dma(4, 4), dma(4), dma(4), dma(4), dma(4),
        ],
        compiler_params=pltpu.CompilerParams(
            collective_id=3, has_side_effects=True, vmem_limit_bytes=LIMIT
        ),
        name="back",
    )(
        grad_attx, grad_half, grad_down, grad_w_out, small_in, raw, query, both, att, inverse, states_all,
        w_qkv, qk_gain, places, grad_direct,
    )


def shards_split(states, cotangent, attn_weights, mlp_weights, feature_gains, unit_gains, block_place):
    tok_rows, model_width = states.shape
    ff_width = unit_gains.shape[0]
    n_seq, n_ctx = lax.axis_size("seq"), lax.axis_size("ctx")
    chips = n_ctx // CORES
    chip = lax.axis_index("ctx") // CORES
    heads = HEADS // chips
    head_cols = heads * HEAD_DIM
    units = ff_width // chips
    rows = attn_weights.shape[0]
    qk_gain = lax.dynamic_slice_in_dim(feature_gains[:, 0], chip * head_cols, head_cols)
    qk_gain = qk_gain.reshape(heads, 1, HEAD_DIM)
    states_all, w_qkv, w_out, w_up, w_gate, low_down, raw, query, both, att, inverse, attx = attend_call(
        states, attn_weights, mlp_weights, qk_gain, block_place
    )
    gain_u = lax.dynamic_slice_in_dim(unit_gains[:, 0], chip * units, units)
    gain_v = lax.dynamic_slice_in_dim(unit_gains[:, 1], chip * units, units) * math.sqrt(D)
    out_low, grad_attx, grad_w_out, grad_direct, small, grad_half, grad_down = mlp_call(
        attx, states, cotangent, w_out, feature_gains[:, 1].reshape(1, model_width),
        feature_gains[:, 2].reshape(1, model_width), gain_u.reshape(CORES, 1, units // CORES),
        gain_v.reshape(CORES, 1, units // CORES), w_up, w_gate, low_down,
    )
    grad_states, grad_mlp, grad_attn, feature, unit = back_call(
        grad_attx, grad_half, grad_down, grad_w_out, small, raw, query, both, att, inverse, states_all,
        w_qkv, qk_gain, block_place, grad_direct, rows,
    )
    rank = lax.axis_index(ALL)
    unit_rows_own = ff_width // (n_seq * n_ctx)
    return (
        out_low,
        grad_states,
        grad_attn,
        grad_mlp,
        lax.dynamic_slice_in_dim(feature, rank * rows, rows, axis=1).T,
        lax.dynamic_slice_in_dim(unit, rank * unit_rows_own, unit_rows_own, axis=1).T,
    )


def solution(mesh):
    in_specs = (
        P(("seq", "ctx"), None),
        P(("seq", "ctx"), None),
        P(("seq", "ctx"), None),
        P(("seq", "ctx"), None),
        P(),
        P(),
        P("seq", None),
    )
    out_specs = (
        P(("seq", "ctx"), None),
        P(("seq", "ctx"), None),
        P(("seq", "ctx"), None),
        P(("seq", "ctx"), None),
        P(("seq", "ctx"), None),
        P(("seq", "ctx"), None),
    )
    chips = mesh.shape["ctx"] // CORES
    shards = shards_split if fits(mesh.shape["seq"], chips) else shards_general
    return jax.shard_map(shards, mesh=mesh, in_specs=in_specs, out_specs=out_specs, check_vma=False)
```

```python
import functools
import math

import jax
import jax.numpy as jnp
from jax import lax
from jax.experimental import pallas as pl
from jax.experimental.pallas import tpu as pltpu
from jax.sharding import PartitionSpec as P

D = 1280
HEADS = 20
HEAD_DIM = 64


EPSILON = 1e-06
NEG_LARGE = -1e30


def unit_rows(values_in):
    factor = lax.rsqrt(jnp.sum(values_in * values_in, axis=-1, keepdims=True) + EPSILON)
    return (values_in * factor, factor)


def unit_back(normed, factor, upstream):
    return factor * (upstream - normed * jnp.sum(upstream * normed, axis=-1, keepdims=True))


def contract_rows(left_mat, right_mat):
    return lax.dot_general(
        left_mat, right_mat, (((0,), (0,)), ((), ())), preferred_element_type=jnp.float32
    )


def contract_cols(left_mat, right_mat):
    return lax.dot_general(
        left_mat, right_mat, (((1,), (1,)), ((), ())), preferred_element_type=jnp.float32
    )


def shards_general(states, cotangent, attn_weights, mlp_weights, feature_gains, unit_gains, block_place):
    tok_rows = states.shape[0]
    model_width = states.shape[1]
    ff_width = unit_gains.shape[0]
    score_scale = math.sqrt(HEAD_DIM)
    gate_factor = unit_gains[:, 1] * math.sqrt(D)
    w_attn = lax.all_gather(attn_weights.astype(jnp.bfloat16), ("seq", "ctx"), axis=0, tiled=True)
    w_mlp = lax.all_gather(mlp_weights.astype(jnp.bfloat16), ("seq", "ctx"), axis=0, tiled=True)
    states_full = states.astype(jnp.float32)
    projected = jnp.dot(states, w_attn[:, : 3 * model_width], preferred_element_type=jnp.float32)
    head_shape = (tok_rows, HEADS, HEAD_DIM)
    qk_gain = feature_gains[:, 0].reshape(HEADS, HEAD_DIM)
    query_unit, query_factor = unit_rows(projected[:, :model_width].reshape(head_shape))
    key_unit, key_factor = unit_rows(
        projected[:, model_width : 2 * model_width].reshape(head_shape)
    )
    query_low = (query_unit * qk_gain).astype(jnp.bfloat16)
    key_low = (key_unit * qk_gain).astype(jnp.bfloat16).reshape(tok_rows, model_width)
    value_low = projected[:, 2 * model_width :].astype(jnp.bfloat16)
    keys_all, values_all = (
        lax.all_gather(key_low, "ctx", axis=0, tiled=True),
        lax.all_gather(value_low, "ctx", axis=0, tiled=True),
    )
    seq_len = keys_all.shape[0]
    ctx_lanes = jnp.arange(lax.axis_size("ctx"), dtype=jnp.int32)
    places = block_place[0]
    own_block = jnp.sum(jnp.where(ctx_lanes == lax.axis_index("ctx"), places, 0))
    query_pos = own_block * tok_rows + jnp.arange(tok_rows, dtype=jnp.int32)
    key_index = jnp.arange(seq_len, dtype=jnp.int32)
    key_owner = key_index // tok_rows
    key_pos = (
        jnp.sum(jnp.where(key_owner[:, None] == ctx_lanes[None, :], places[None, :], 0), axis=1)
        * tok_rows
        + key_index % tok_rows
    )
    kblock = min(512, seq_len)
    nblocks = seq_len // kblock
    key_blocks = keys_all.reshape(nblocks, kblock, HEADS, HEAD_DIM)
    value_blocks = values_all.reshape(nblocks, kblock, HEADS, HEAD_DIM)
    pos_blocks = key_pos.reshape(nblocks, kblock)

    def block_scores(key_rows, key_places):
        raw_scores = score_scale * jnp.einsum(
            "qhd,khd->hqk", query_low, key_rows, preferred_element_type=jnp.float32
        )
        allowed = key_places[None, None, :] <= query_pos[None, :, None]
        return (raw_scores, allowed)

    def max_step(running, inputs):
        running_max, running_sum = running
        key_rows, key_places = inputs
        raw_scores, allowed = block_scores(key_rows, key_places)
        masked = jnp.where(allowed, raw_scores, NEG_LARGE)
        new_max = jnp.maximum(running_max, jnp.max(masked, axis=-1))
        powered = jnp.where(allowed, jnp.exp(masked - new_max[..., None]), 0.0)
        running_sum = running_sum * jnp.exp(running_max - new_max) + jnp.sum(powered, axis=-1)
        return ((new_max, running_sum), None)

    start_max = jnp.full((HEADS, tok_rows), NEG_LARGE, jnp.float32)
    start_sum = jnp.zeros((HEADS, tok_rows), jnp.float32)
    (final_max, final_sum), _ = lax.scan(max_step, (start_max, start_sum), (key_blocks, pos_blocks))
    log_total = final_max + jnp.log(final_sum)

    def value_step(accumulated, inputs):
        key_rows, value_rows, key_places = inputs
        raw_scores, allowed = block_scores(key_rows, key_places)
        weights_low = jnp.where(allowed, jnp.exp(raw_scores - log_total[..., None]), 0.0).astype(
            jnp.bfloat16
        )
        accumulated = accumulated + jnp.einsum(
            "hqk,khd->qhd", weights_low, value_rows, preferred_element_type=jnp.float32
        )
        return (accumulated, None)

    attended, _ = lax.scan(
        value_step, jnp.zeros(head_shape, jnp.float32), (key_blocks, value_blocks, pos_blocks)
    )
    attended_low = attended.reshape(tok_rows, model_width).astype(jnp.bfloat16)
    branch_attn = jnp.dot(
        attended_low, w_attn[:, 3 * model_width :], preferred_element_type=jnp.float32
    )
    attn_unit, attn_factor = unit_rows(branch_attn)
    alpha_attn = feature_gains[:, 1]
    mixed_one, mix_factor = unit_rows(states_full + alpha_attn * (attn_unit - states_full))
    mixed_low = mixed_one.astype(jnp.bfloat16)
    up_gate = jnp.dot(mixed_low, w_mlp[:, : 2 * ff_width], preferred_element_type=jnp.float32)
    up_scaled = up_gate[:, :ff_width] * unit_gains[:, 0]
    gate_scaled = up_gate[:, ff_width:] * gate_factor
    sigmoid_gate = jax.nn.sigmoid(gate_scaled)
    activated = gate_scaled * sigmoid_gate
    hidden = (activated * up_scaled).astype(jnp.bfloat16)
    branch_mlp = contract_cols(hidden, w_mlp[:, 2 * ff_width :])
    mlp_unit, mlp_factor = unit_rows(branch_mlp)
    alpha_mlp = feature_gains[:, 2]
    out_full, out_factor = unit_rows(mixed_one + alpha_mlp * (mlp_unit - mixed_one))
    grad_mix_two = unit_back(out_full, out_factor, cotangent.astype(jnp.float32))
    grad_alpha_m = jnp.sum(grad_mix_two * (mlp_unit - mixed_one), axis=0)
    grad_branch_mlp = unit_back(mlp_unit, mlp_factor, grad_mix_two * alpha_mlp).astype(jnp.bfloat16)
    grad_hidden = jnp.dot(
        grad_branch_mlp, w_mlp[:, 2 * ff_width :], preferred_element_type=jnp.float32
    )
    grad_up_scaled = grad_hidden * activated
    grad_gate_scaled = (
        grad_hidden * up_scaled * sigmoid_gate * (1.0 + gate_scaled * (1.0 - sigmoid_gate))
    )
    grad_s_u = jnp.sum(grad_up_scaled * up_gate[:, :ff_width], axis=0)
    grad_s_v = jnp.sum(grad_gate_scaled * up_gate[:, ff_width:], axis=0) * math.sqrt(D)
    grad_up_gate = jnp.concatenate(
        [grad_up_scaled * unit_gains[:, 0], grad_gate_scaled * gate_factor], axis=1
    ).astype(jnp.bfloat16)
    grad_mixed_one = grad_mix_two * (1.0 - alpha_mlp) + contract_cols(
        grad_up_gate, w_mlp[:, : 2 * ff_width]
    )
    grad_mix_one = unit_back(mixed_one, mix_factor, grad_mixed_one)
    grad_alpha_a = jnp.sum(grad_mix_one * (attn_unit - states_full), axis=0)
    grad_branch_attn = unit_back(attn_unit, attn_factor, grad_mix_one * alpha_attn).astype(
        jnp.bfloat16
    )
    grad_attended = (
        contract_cols(grad_branch_attn, w_attn[:, 3 * model_width :])
        .astype(jnp.bfloat16)
        .reshape(head_shape)
    )
    row_dots = jnp.einsum("qhd,qhd->hq", grad_attended.astype(jnp.float32), attended)

    def grad_step(grad_query, inputs):
        key_rows, value_rows, key_places = inputs
        raw_scores, allowed = block_scores(key_rows, key_places)
        probabilities = jnp.where(allowed, jnp.exp(raw_scores - log_total[..., None]), 0.0)
        grad_prob = jnp.einsum(
            "qhd,khd->hqk", grad_attended, value_rows, preferred_element_type=jnp.float32
        )
        grad_scores = (probabilities * (grad_prob - row_dots[..., None])).astype(jnp.bfloat16)
        grad_query = grad_query + score_scale * jnp.einsum(
            "hqk,khd->qhd", grad_scores, key_rows, preferred_element_type=jnp.float32
        )
        key_terms = score_scale * jnp.einsum(
            "hqk,qhd->khd", grad_scores, query_low, preferred_element_type=jnp.float32
        )
        value_terms = jnp.einsum(
            "hqk,qhd->khd",
            probabilities.astype(jnp.bfloat16),
            grad_attended,
            preferred_element_type=jnp.float32,
        )
        return (grad_query, (key_terms, value_terms))

    grad_query_low, (key_terms, value_terms) = lax.scan(
        grad_step, jnp.zeros(head_shape, jnp.float32), (key_blocks, value_blocks, pos_blocks)
    )
    key_terms = key_terms.reshape(seq_len, model_width)
    value_terms = value_terms.reshape(seq_len, model_width)
    own_key_grad, own_value_grad = (
        lax.psum_scatter(
            key_terms.astype(jnp.bfloat16), "ctx", scatter_dimension=0, tiled=True
        ).astype(jnp.float32),
        lax.psum_scatter(
            value_terms.astype(jnp.bfloat16), "ctx", scatter_dimension=0, tiled=True
        ).astype(jnp.float32),
    )
    grad_key_low = own_key_grad.reshape(head_shape)
    grad_s_qk = jnp.sum(grad_query_low * query_unit + grad_key_low * key_unit, axis=0).reshape(
        model_width
    )
    grad_query_raw = unit_back(query_unit, query_factor, grad_query_low * qk_gain).reshape(
        tok_rows, model_width
    )
    grad_key_raw = unit_back(key_unit, key_factor, grad_key_low * qk_gain).reshape(
        tok_rows, model_width
    )
    grad_projected = jnp.concatenate([grad_query_raw, grad_key_raw, own_value_grad], axis=1).astype(
        jnp.bfloat16
    )
    grad_states = grad_mix_one * (1.0 - alpha_attn) + contract_cols(
        grad_projected, w_attn[:, : 3 * model_width]
    )
    feature_total = jnp.stack([grad_s_qk, grad_alpha_a, grad_alpha_m], axis=1)
    unit_fold = jnp.stack([grad_s_u, grad_s_v], axis=1).reshape(
        model_width, 2 * ff_width // model_width
    )
    attn_cols = 4 * model_width
    mlp_cols = 3 * ff_width
    attn_share = lax.psum_scatter(
        jnp.concatenate(
            [
                contract_rows(states, grad_projected),
                contract_rows(attended_low, grad_branch_attn),
                feature_total,
            ],
            axis=1,
        ),
        ("seq", "ctx"),
        scatter_dimension=0,
        tiled=True,
    )
    mlp_share = lax.psum_scatter(
        jnp.concatenate(
            [
                contract_rows(mixed_low, grad_up_gate),
                contract_rows(grad_branch_mlp, hidden),
                unit_fold,
            ],
            axis=1,
        ),
        ("seq", "ctx"),
        scatter_dimension=0,
        tiled=True,
    )
    grad_attn = attn_share[:, :attn_cols]
    grad_feature = attn_share[:, attn_cols:]
    grad_mlp = mlp_share[:, :mlp_cols]
    grad_unit = mlp_share[:, mlp_cols:].reshape(
        unit_gains.shape[0] // lax.axis_size(("seq", "ctx")), 2
    )
    return (
        out_full.astype(jnp.bfloat16),
        grad_states.astype(jnp.bfloat16),
        grad_attn,
        grad_mlp,
        grad_feature,
        grad_unit,
    )


CORES = 2
ALL = ("seq", "ctx")


def fits(n_seq, chips):
    return n_seq == 4 and chips == 4 and HEADS % chips == 0


MESH = pl.DeviceIdType.MESH
VMEM = pltpu.VMEM
CHIPS = 4
STEPS = (1, 2, 3)
LIMIT = 60 * 1024 * 1024


def place_of():
    seq = lax.axis_index("seq")
    ctx = lax.axis_index("ctx")
    return seq, ctx // CORES, ctx % CORES


def chip_peer(step):
    seq, chip, core = place_of()
    other = lax.rem(chip + step, CHIPS)
    return (seq, other * CORES + core), other


def seq_peer(step):
    seq, chip, core = place_of()
    other = seq ^ step
    return (other, chip * CORES + core), other


def twin():
    seq, chip, core = place_of()
    return (seq, chip * CORES + 1 - core)


def meet():
    devices = [chip_peer(step)[0] for step in STEPS] + [seq_peer(step)[0] for step in STEPS] + [twin()]
    gate = pltpu.get_barrier_semaphore()
    for device in devices:
        pl.semaphore_signal(gate, inc=1, device_id=device, device_id_type=MESH)
    pl.semaphore_wait(gate, len(devices))


def remote(src, dst, send, recv, device):
    return pltpu.make_async_remote_copy(
        src_ref=src, dst_ref=dst, send_sem=send, recv_sem=recv, device_id=device,
        device_id_type=MESH,
    )


def begin(copy):
    copy.start()
    return copy


def rows_at(index, count):
    return pl.ds(pl.multiple_of(index * count, count), count)


def device_on(chip):
    seq, _, core = place_of()
    return (seq, chip * CORES + core)


def when(condition, action):
    pl.when(condition)(action)


PIECES = 2


def piece_at(block, piece, count):
    step = count // PIECES
    return pl.ds(pl.multiple_of(block * count + piece * step, step), step)


def gather_copy(src, everything, count, block, side, hop, piece, send, recv):
    chip = place_of()[1]
    there = everything.at[piece_at(block, piece, count)]
    near = chip + 1 if side == 0 else chip - 1
    here = there if src is None else src.at[piece_at(0, piece, count)]
    return remote(here, there, send.at[side, hop, piece], recv.at[side, hop, piece], device_on(near))


def gather_start(src, everything, count, send, recv):
    chip = place_of()[1]
    for piece in range(PIECES):
        for side in range(2):
            copy = gather_copy(src, everything, count, chip, side, 0, piece, send, recv)
            when(chip < CHIPS - 1 if side == 0 else chip > 0, copy.start)


def gather_hop(everything, count, hop, send, recv):
    chip = place_of()[1]
    for piece in range(PIECES):
        for side in range(2):
            block = chip - hop if side == 0 else chip + hop

            def pass_on(side=side, piece=piece, block=block):
                gather_copy(None, everything, count, block, side, hop - 1, piece, send, recv).wait_recv()
                if hop < CHIPS - 1:
                    copy = gather_copy(None, everything, count, block, side, hop, piece, send, recv)
                    when(chip < CHIPS - 1 if side == 0 else chip > 0, copy.start)

            when(block >= 0 if side == 0 else block < CHIPS, pass_on)


def gather_drain(everything, count, send, recv):
    chip = place_of()[1]
    for hop in range(CHIPS - 1):
        for piece in range(PIECES):
            for side in range(2):
                copy = gather_copy(None, everything, count, chip, side, hop, piece, send, recv)
                block = chip - hop if side == 0 else chip + hop
                sent = (block >= 0) & (chip < CHIPS - 1) if side == 0 else (block < CHIPS) & (chip > 0)
                when(sent, copy.wait_send)


def inside_line():
    chip = place_of()[1]
    return (chip > 0) & (chip < CHIPS - 1)


def spans_line(other):
    return abs(place_of()[1] - other) == CHIPS - 1


def reduce_start(part, count, sums, via, send, recv, ahead=True):
    chip = place_of()[1]
    near = jnp.where(chip == 0, 1, CHIPS - 2)
    first = remote(part.at[rows_at(CHIPS - 1 - chip, count)], via, send.at[0], recv.at[0], device_on(near))

    def begin_far():
        first.start()
        if ahead:
            first.wait_send()

    when(jnp.logical_not(inside_line()), begin_far)
    for step in STEPS:
        device, other = chip_peer(step)
        copy = remote(part.at[rows_at(other, count)], sums.at[step - 1], send.at[step], recv.at[step], device)
        if step == 2:
            when(jnp.logical_not(inside_line()), copy.start)
        else:
            when(jnp.logical_not(spans_line(other)), copy.start)


def reduce_relay(part, count, sums, via, mixed, send, recv):
    chip = place_of()[1]
    other = lax.rem(chip + 2, CHIPS)
    copy = remote(mixed, sums.at[1], send.at[2], recv.at[2], device_on(other))

    def pass_on():
        remote(mixed, via, send.at[0], recv.at[0], device_on(other)).wait_recv()
        mixed[...] = (
            part[rows_at(other, count), :].astype(jnp.float32) + via[...].astype(jnp.float32)
        ).astype(mixed.dtype)
        copy.start()

    when(inside_line(), pass_on)


def reduce_wait(part, count, sums, total, send, recv):
    chip = place_of()[1]
    total[...] = part[rows_at(chip, count), :].astype(jnp.float32)
    for step in (1, 3, 2):
        source = lax.rem(chip + CHIPS - step, CHIPS)

        def add(step=step, source=source):
            here = sums.at[step - 1]
            remote(here, here, send.at[step], recv.at[step], device_on(source)).wait_recv()
            total[...] += sums[step - 1].astype(jnp.float32)

        when(jnp.logical_not(spans_line(source)), add)


def reduce_drain(part, count, sums, send, recv, ahead=True):
    rows = part.at[rows_at(0, count)]
    for step in STEPS:
        device, other = chip_peer(step)
        copy = remote(rows, sums.at[step - 1], send.at[step], recv.at[step], device)
        when(jnp.logical_not(spans_line(other)), copy.wait_send)
    if not ahead:
        copy = remote(rows, sums.at[0], send.at[0], recv.at[0], device_on(place_of()[1]))
        when(jnp.logical_not(inside_line()), copy.wait_send)


def side_peer(side):
    return seq_peer(side + 1)


def seq_rows_at(block, side, count):
    half = count // 2
    return pl.ds(pl.multiple_of(block * count + side * half, half), half)


def spread_start(src, dst, count, send, recv):
    seq = place_of()[0]
    return [
        begin(remote(src, dst.at[rows_at(seq, count)], send.at[side], recv.at[side], side_peer(side)[0]))
        for side in range(2)
    ]


def spread_relay(dst, count, send, recv):
    copies = []
    for side in range(2):
        block = side_peer(side)[1]
        whole = dst.at[rows_at(block, count)]
        remote(whole, whole, send.at[side], recv.at[side], side_peer(side)[0]).wait_recv()
        part = dst.at[seq_rows_at(block, side, count)]
        copies.append(begin(remote(part, part, send.at[2 + side], recv.at[2 + side], side_peer(1 - side)[0])))
    return copies


def fold_start(src, got, count, send, recv):
    seq = place_of()[0]
    copies = []
    for side in range(2):
        device, other = side_peer(side)
        for at, block in enumerate((other, seq ^ 3)):
            here = src.at[seq_rows_at(block, side, count)]
            copies.append(begin(remote(here, got.at[side, at], send.at[side, at], recv.at[side, at], device)))
    return copies


def fold_relay(src, got, held, last, count, copies, send, recv):
    more = []
    for side in range(2):
        device, other = side_peer(1 - side)
        copies[2 * side + 1].wait_recv()
        rows = seq_rows_at(other, side, count)
        held[side] = (src[rows, :].astype(jnp.float32) + got[side, 1].astype(jnp.float32)).astype(held.dtype)
        more.append(begin(remote(held.at[side], last.at[side], send.at[2, side], recv.at[2, side], device)))
    return more


def fold_end(src, got, last, out, count, copies, more):
    seq = place_of()[0]
    half = count // 2
    for side in range(2):
        copies[2 * side].wait_recv()
        more[side].wait_recv()
        rows = seq_rows_at(seq, side, count)
        out[side * half : (side + 1) * half, :] = (
            src[rows, :].astype(jnp.float32) + got[side, 0].astype(jnp.float32) + last[side].astype(jnp.float32)
        ).astype(out.dtype)


def to_line(src, there, send, recv):
    return [
        begin(remote(src, there, send.at[step], recv.at[step], chip_peer(step)[0])) for step in STEPS
    ]


def dot(left, right):
    return jnp.dot(left, right, preferred_element_type=jnp.float32)


def dot_nt(left, right):
    return lax.dot_general(
        left, right, (((1,), (1,)), ((), ())), preferred_element_type=jnp.float32
    )


def dot_tn(left, right):
    return lax.dot_general(
        left, right, (((0,), (0,)), ((), ())), preferred_element_type=jnp.float32
    )


def dma(*shape):
    return pltpu.SemaphoreType.DMA(shape)


def line_dma():
    return dma(2, CHIPS, PIECES)


def in_vmem():
    return pl.BlockSpec(memory_space=pltpu.VMEM)


def in_hbm():
    return pl.BlockSpec(memory_space=pl.ANY)


def key_positions(places, key_pos, tok_rows):
    lanes = lax.broadcasted_iota(jnp.int32, (1, tok_rows), 1)
    for at_core in range(CORES):
        for at_chip in range(CHIPS):
            start = (at_core * CHIPS + at_chip) * tok_rows
            key_pos[:, start : start + tok_rows] = places[0, CORES * at_chip + at_core] * tok_rows + lanes


def kept_pairs(places, key_pos, block, core, tok_rows):
    down = lax.broadcasted_iota(jnp.int32, (tok_rows, 1), 0)
    return key_pos[...] <= places[0, CORES * block + core] * tok_rows + down


def attend_kernel(
    states, attn_src, mlp_src, qk_gain, places,
    to_states, to_qkv, to_out, w_up, w_gate, low_down, to_raw, to_query, to_both, to_att, to_inv, attx,
    states_all, w_qkv, w_out, raw_out, query_out, both, att_out, inv_out, src_q, stage_q, low_q, stage_o, low_o, stage_m, low_m, raw, att_low, key_pos,
    local_sem, keep_sem, att_sem, x_send, x_recv, q_send, q_recv, mt_send, mt_recv, wz_send, wz_recv,
    ws_send, ws_recv, wt_send, wt_recv, oz_send, oz_recv, os_send, os_recv, m_send, m_recv,
    ms_send, ms_recv, kv_send, kv_recv, a_send, a_recv,
):
    seq, chip, core = place_of()
    rows = attn_src.shape[0]
    tok_rows, model_width = states.shape
    heads = qk_gain.shape[0]
    head_cols = heads * HEAD_DIM
    part_cols = head_cols // CORES
    group_rows = tok_rows * CHIPS
    chip_rows = CORES * rows
    seq_rows = CHIPS * chip_rows
    half_units = w_up.shape[1]
    half_width = model_width // CORES
    ff_width = mlp_src.shape[1] // 3
    low = jnp.bfloat16
    for at in range(CHIPS):
        for half in range(CORES):
            for which in range(3):
                start = which * model_width + at * head_cols + half * part_cols
                src_q[at, half, :, which * part_cols : (which + 1) * part_cols] = attn_src[:, start : start + part_cols]
    meet()
    block = rows_at(chip, tok_rows)
    mine = rows_at(core, rows)
    half_at = pl.ds(pl.multiple_of(3 * model_width + core * half_width, 128), half_width)
    other_at = pl.ds(pl.multiple_of(3 * model_width + (1 - core) * half_width, 128), half_width)
    swap_o = begin(remote(attn_src.at[:, other_at], stage_o.at[mine], q_send.at[1], q_recv.at[1], twin()))
    swap_q = begin(remote(src_q.at[:, 1 - core], stage_q.at[:, mine], q_send.at[0], q_recv.at[0], twin()))
    stage_o[mine, :] = attn_src[:, half_at]
    stage_q[:, mine, :] = src_q[:, core]
    m_swaps, m_keeps = [], []
    for part in range(3):
        for at in range(CHIPS):
            start = part * ff_width + at * CORES * half_units
            theirs = pl.ds(pl.multiple_of(start + (1 - core) * half_units, 128), half_units)
            ours = pl.ds(pl.multiple_of(start + core * half_units, 128), half_units)
            there = stage_m.at[part, at, mine]
            m_swaps.append(begin(remote(mlp_src.at[:, theirs], there, mt_send.at[part, at], mt_recv.at[part, at], twin())))
            m_keeps.append(begin(pltpu.make_async_copy(mlp_src.at[:, ours], there, local_sem.at[part * CHIPS + at])))
    my_rows = rows_at(seq * CHIPS + chip, chip_rows)
    seq_at = rows_at(seq, seq_rows)
    swap_o.wait()
    low_o[...] = stage_o[...].astype(low)
    o_line = to_line(low_o, w_out.at[core, my_rows], oz_send, oz_recv)
    w_out[core, my_rows, :] = low_o[...]
    swap_q.wait()
    low_q[...] = stage_q[...].astype(low)
    line = []
    for step in STEPS:
        device, other = chip_peer(step)
        line.append(begin(remote(low_q.at[other], w_qkv.at[core, my_rows], wz_send.at[step], wz_recv.at[step], device)))
    w_qkv[core, my_rows, :] = low_q[chip]
    states_all[block, :] = states[...]
    key_positions(places, key_pos, tok_rows)
    gather_start(states, states_all, tok_rows, x_send, x_recv)
    for copy in line:
        copy.wait_recv()

    def across(whole, send, recv):
        return spread_start(whole.at[seq_at], whole, seq_rows, send, recv)

    q_across = across(w_qkv.at[core], ws_send, ws_recv)
    for copy in m_keeps:
        copy.wait()
    for copy in m_swaps:
        copy.wait()
    low_m[...] = stage_m[:2].astype(low)
    low_down[...] = stage_m[2].astype(low)
    gather_hop(states_all, tok_rows, 1, x_send, x_recv)
    more = spread_relay(w_qkv.at[core], seq_rows, ws_send, ws_recv)
    for copy in o_line:
        copy.wait_recv()
    o_across = across(w_out.at[core], os_send, os_recv)
    for copy in more:
        copy.wait_recv()
    q_across += more
    swap = begin(remote(w_qkv.at[core], w_qkv.at[core], wt_send.at[0], wt_recv.at[0], twin()))
    gather_hop(states_all, tok_rows, 2, x_send, x_recv)
    o_more = spread_relay(w_out.at[core], seq_rows, os_send, os_recv)
    gather_hop(states_all, tok_rows, 3, x_send, x_recv)
    here = rows_at(chip, chip_rows)

    def to_chips(part, there):
        return [
            begin(remote(low_m.at[part, chip_peer(step)[1]], there, m_send.at[part, step], m_recv.at[part, step], chip_peer(step)[0]))
            for step in STEPS
        ]

    m_line = to_chips(0, w_up.at[my_rows])
    w_up[my_rows, :] = low_m[0, chip]
    w_gate[here, :] = low_m[1, chip]
    swap.wait()
    kept = []

    def keep(src, dst):
        kept.append(begin(pltpu.make_async_copy(src, dst, keep_sem.at[len(kept)])))

    keep(states_all, to_states)
    keep(w_qkv, to_qkv)
    for half in range(CORES):
        value = dot(states_all[...], w_qkv[half])
        for which in range(3):
            start = which * head_cols + half * part_cols
            raw[:, start : start + part_cols] = value[:, which * part_cols : (which + 1) * part_cols]
    for head in reversed(range(3 * heads)):
        which, head = head // heads, head % heads
        start = which * head_cols + head * HEAD_DIM
        value = raw[:, start : start + HEAD_DIM]
        if which == 2:
            both[core, 1, head] = value.astype(low)
            continue
        factor = lax.rsqrt(jnp.sum(value * value, axis=-1, keepdims=True) + EPSILON)
        scaled = (value * factor * qk_gain[head]).astype(low)
        raw_out[which, head] = value
        if which == 1:
            both[core, 0, head] = scaled
            if head == 0:
                swap = begin(remote(both.at[core], both.at[core], kv_send.at[0], kv_recv.at[0], twin()))
        else:
            query_out[head] = scaled * math.sqrt(HEAD_DIM)
    keep(raw_out, to_raw)
    keep(query_out, to_query)
    for copy in m_line + o_more:
        copy.wait_recv()
    m_line += to_chips(1, w_gate.at[here])
    swap_o = begin(remote(w_out.at[core], w_out.at[core], wt_send.at[1], wt_recv.at[1], twin()))
    up_across = across(w_up, ms_send, ms_recv)
    swap.wait()
    keep(both, to_both)

    def one_block(index, carry):
        step = lax.rem(index + 1, CHIPS)
        device, other = chip_peer(step)
        at = rows_at(other, tok_rows)
        allowed = kept_pairs(places, key_pos, other, core, tok_rows)

        def one_head(head, carry):
            query = query_out[head, at, :]
            scores = jnp.concatenate([dot_nt(query, both[half, 0, head]) for half in range(CORES)], axis=1)
            powered = jnp.exp(jnp.where(allowed, scores, NEG_LARGE))
            inverse = 1.0 / jnp.sum(powered, axis=-1, keepdims=True)
            weights = (powered * inverse).astype(low)
            att_out[head, at, :] = sum(
                dot(weights[:, half * group_rows : (half + 1) * group_rows], both[half, 1, head])
                for half in range(CORES)
            )
            inv_out[head, at, :] = inverse
            return carry

        lax.fori_loop(0, heads, one_head, 0)
        for head in range(heads):
            att_low[at, head * HEAD_DIM : (head + 1) * HEAD_DIM] = att_out[head, at, :].astype(low)
        when(step != 0, remote(att_low.at[at], attx.at[chip], a_send.at[step], a_recv.at[step], device).start)
        pltpu.make_async_copy(att_out.at[:, at], to_att.at[:, at], att_sem.at[0, step]).start()
        pltpu.make_async_copy(inv_out.at[:, at], to_inv.at[:, at], att_sem.at[1, step]).start()
        return carry

    lax.fori_loop(0, CHIPS, one_block, 0)
    attx[chip] = att_low[block, :]
    swap_o.wait()
    keep(w_out, to_out)
    up_more = spread_relay(w_up, seq_rows, ms_send, ms_recv)
    for step in STEPS:
        remote(att_low.at[block], attx.at[chip], a_send.at[step], a_recv.at[step], chip_peer(step)[0]).wait()
    for copy in m_line[3:] + up_more:
        copy.wait_recv()
    gather_drain(states_all, tok_rows, x_send, x_recv)
    for step in range(CHIPS):
        pltpu.make_async_copy(att_out.at[:, block], to_att.at[:, block], att_sem.at[0, step]).wait()
        pltpu.make_async_copy(inv_out.at[:, block], to_inv.at[:, block], att_sem.at[1, step]).wait()
    for copy in kept:
        copy.wait()
    for copy in m_line + line + o_line + q_across + o_across + o_more + up_across + up_more:
        copy.wait_send()


def in_smem():
    return pl.BlockSpec(memory_space=pltpu.SMEM)


def attend_call(states, attn_src, mlp_src, qk_gain, places):
    tok_rows, model_width = states.shape
    rows = attn_src.shape[0]
    heads = qk_gain.shape[0]
    chips, chip_rows = CHIPS, CORES * rows
    group_rows = chips * tok_rows
    half_units = mlp_src.shape[1] // 3 // chips // CORES
    half_width, half_cols = model_width // CORES, 3 * heads * HEAD_DIM // CORES
    f32, low = jnp.float32, jnp.bfloat16
    shape = jax.ShapeDtypeStruct
    return pl.pallas_call(
        attend_kernel,
        out_shape=[
            shape((group_rows, model_width), low),
            shape((CORES, model_width, half_cols), low),
            shape((CORES, model_width, half_width), low),
            shape((model_width, half_units), low),
            shape((chips * chip_rows, half_units), low),
            shape((chips, chip_rows, half_units), low),
            shape((2, heads, group_rows, HEAD_DIM), f32),
            shape((heads, group_rows, HEAD_DIM), low),
            shape((CORES, 2, heads, group_rows, HEAD_DIM), low),
            shape((heads, group_rows, HEAD_DIM), f32),
            shape((heads, group_rows, 1), f32),
            shape((chips, tok_rows, heads * HEAD_DIM), low),
        ],
        in_specs=[in_vmem(), in_vmem(), in_hbm(), in_vmem(), in_smem()],
        out_specs=[in_hbm()] * 3 + [in_vmem()] * 3 + [in_hbm()] * 5 + [in_vmem()],
        scratch_shapes=[
            VMEM((group_rows, model_width), low),
            VMEM((CORES, model_width, half_cols), low),
            VMEM((CORES, model_width, half_width), low),
            VMEM((2, heads, group_rows, HEAD_DIM), f32),
            VMEM((heads, group_rows, HEAD_DIM), low),
            VMEM((CORES, 2, heads, group_rows, HEAD_DIM), low),
            VMEM((heads, group_rows, HEAD_DIM), f32),
            VMEM((heads, group_rows, 1), f32),
            VMEM((chips, CORES, rows, half_cols), f32),
            VMEM((chips, chip_rows, half_cols), f32),
            VMEM((chips, chip_rows, half_cols), low),
            VMEM((chip_rows, half_width), f32),
            VMEM((chip_rows, half_width), low),
            VMEM((3, chips, chip_rows, half_units), f32),
            VMEM((2, chips, chip_rows, half_units), low),
            VMEM((group_rows, 3 * heads * HEAD_DIM), f32),
            VMEM((group_rows, heads * HEAD_DIM), low),
            VMEM((1, CORES * group_rows), jnp.int32),
            dma(12), dma(6), dma(2, 4), line_dma(), line_dma(), dma(2), dma(2), dma(3, 4), dma(3, 4), dma(4), dma(4),
            dma(4), dma(4), dma(2), dma(2), dma(4), dma(4), dma(4), dma(4), dma(2, 4), dma(2, 4),
            dma(4), dma(4), dma(1), dma(1), dma(4), dma(4),
        ],
        compiler_params=pltpu.CompilerParams(
            collective_id=1, has_side_effects=True, vmem_limit_bytes=LIMIT
        ),
        name="attend",
    )(states, attn_src, mlp_src, qk_gain, places)


def unit_of(value):
    factor = lax.rsqrt(jnp.sum(value * value, axis=-1, keepdims=True) + EPSILON)
    return value * factor, factor


def mlp_kernel(
    attx, states, cotangent, from_out, alpha_attn, alpha_mlp, gain_u, gain_v, w_up, w_gate, low_down,
    out, grad_attx, grad_w_out, grad_direct, small, to_half, grad_down,
    w_out, grad_half, weights, mixed_one, attn_unit, factors, mixed_low, mixed_all, up, gate, hidden, part,
    sums, via, passed, total, grad_two, branch_low, branch_all, grad_u, grad_v, wide, turned, arrived,
    w_down, down_half, down_got, dot_u, dot_v,
    local_sem, ws_send, ws_recv, wt_send, wt_recv, x_send, x_recv, r_send, r_recv,
    g_send, g_recv, b_send, b_recv, d_send, d_recv, wz_send, wz_recv, ds_send, ds_recv,
):
    seq, chip, core = place_of()
    tok_rows, model_width = states.shape
    chip_heads = attx.shape[2]
    seq_rows, half_units = w_gate.shape
    chip_rows = low_down.shape[1]
    half_width = w_out.shape[2]
    group_rows = CHIPS * tok_rows
    block = rows_at(chip, tok_rows)
    load = begin(pltpu.make_async_copy(from_out, w_out, local_sem.at[2]))
    meet()
    seq_at = rows_at(seq, seq_rows)
    here = rows_at(chip, chip_rows)
    swaps = [begin(remote(w_up, weights.at[0, core], wt_send.at[0], wt_recv.at[0], twin()))]
    to_chips = [
        begin(remote(low_down.at[chip_peer(step)[1]], w_down.at[here], wz_send.at[step], wz_recv.at[step], chip_peer(step)[0]))
        for step in STEPS
    ]

    across = spread_start(w_gate, weights.at[1, core], seq_rows, ws_send.at[1], ws_recv.at[1])
    keeps = [
        begin(pltpu.make_async_copy(w_up, weights.at[0, core], local_sem.at[0])),
        begin(pltpu.make_async_copy(w_gate, weights.at[1, core, seq_at], local_sem.at[1])),
    ]
    w_down[here, :] = low_down[chip]
    load.wait()
    part_at = [slice(at * chip_heads, (at + 1) * chip_heads) for at in range(CHIPS)]
    half_at = [slice(half * half_width, (half + 1) * half_width) for half in range(CORES)]
    branch = jnp.concatenate(
        [sum(dot(attx[at], w_out[half, part_at[at], :]) for at in range(CHIPS)) for half in range(CORES)],
        axis=1,
    )
    unit, factor = unit_of(branch)
    attn_unit[...] = unit
    factors[0] = factor
    base = states[...].astype(jnp.float32)
    value, factor = unit_of(base + alpha_attn[...] * (unit - base))
    mixed_one[...] = value
    factors[1] = factor
    mixed_low[...] = value.astype(jnp.bfloat16)
    gather_start(mixed_low, mixed_all, tok_rows, x_send, x_recv)
    mixed_all[block, :] = mixed_low[...]
    for copy in keeps:
        copy.wait()
    for copy in to_chips:
        copy.wait_recv()
    more = spread_relay(weights.at[1, core], seq_rows, ws_send.at[1], ws_recv.at[1])
    across += spread_start(w_down, weights.at[2, core], seq_rows, ws_send.at[2], ws_recv.at[2])
    weights[2, core, seq_at, :] = w_down[...]
    gather_hop(mixed_all, tok_rows, 1, x_send, x_recv)
    for copy in more:
        copy.wait_recv()
    swaps.append(begin(remote(weights.at[1, core], weights.at[1, core], wt_send.at[1], wt_recv.at[1], twin())))
    slab = min(64, group_rows)
    slabs = group_rows // slab
    half_slabs = slabs // 2
    half_rows = group_rows // 2
    mine = chip // 2

    def forward(group):
        rows = rows_at(group, half_rows)
        for half in range(CORES):
            up[half, rows, :] = dot(mixed_all[rows, :], weights[0, half])
            gate[half, rows, :] = dot(mixed_all[rows, :], weights[1, half])

        def activate(index, carry):
            half = index // half_slabs
            at = rows_at(group * half_slabs + lax.rem(index, half_slabs), slab)
            gated = gate[half, at, :] * gain_v[half]
            scaled = up[half, at, :] * gain_u[half]
            hidden[half, at, :] = (gated * jax.nn.sigmoid(gated) * scaled).astype(jnp.bfloat16)
            return carry

        lax.fori_loop(0, CORES * half_slabs, activate, 0)

    for copy in swaps:
        copy.wait_recv()
    forward(mine)
    gather_hop(mixed_all, tok_rows, 2, x_send, x_recv)
    down_more = spread_relay(weights.at[2, core], seq_rows, ws_send.at[2], ws_recv.at[2])
    gather_hop(mixed_all, tok_rows, 3, x_send, x_recv)
    forward(1 - mine)
    for copy in down_more:
        copy.wait_recv()
    swap = begin(remote(weights.at[2, core], weights.at[2, core], wt_send.at[2], wt_recv.at[2], twin()))
    swaps.append(swap)
    swap.wait_recv()
    tile = model_width // 5

    def down(index, carry):
        at = rows_at(index, tile)
        part[0, :, at] = sum(dot_nt(hidden[half], weights[2, half, at, :]) for half in range(CORES)).astype(jnp.bfloat16)
        return carry

    lax.fori_loop(0, model_width // tile, down, 0)

    reduce_start(part.at[0], tok_rows, sums.at[0], via.at[0], r_send, r_recv)
    reduce_relay(part.at[0], tok_rows, sums.at[0], via.at[0], passed.at[0], r_send, r_recv)
    reduce_wait(part.at[0], tok_rows, sums.at[0], total, r_send, r_recv)
    mlp_unit, mlp_factor = unit_of(total[...])
    value, factor = unit_of(mixed_one[...] + alpha_mlp[...] * (mlp_unit - mixed_one[...]))
    out[...] = value.astype(jnp.bfloat16)
    above = cotangent[...].astype(jnp.float32)
    grad = factor * (above - value * jnp.sum(above * value, axis=-1, keepdims=True))
    grad_two[...] = grad
    small[...] = jnp.zeros_like(small)
    small[1:2, :] = jnp.sum(grad * (mlp_unit - mixed_one[...]), axis=0, keepdims=True)
    grad = grad * alpha_mlp[...]
    grad = mlp_factor * (grad - mlp_unit * jnp.sum(grad * mlp_unit, axis=-1, keepdims=True))
    branch_low[...] = grad.astype(jnp.bfloat16)
    gather_start(branch_low, branch_all, tok_rows, g_send, g_recv)
    branch_all[block, :] = branch_low[...]
    gather_hop(branch_all, tok_rows, 1, g_send, g_recv)
    gather_hop(branch_all, tok_rows, 2, g_send, g_recv)
    turned[0] = mixed_all[...].T
    gather_hop(branch_all, tok_rows, 3, g_send, g_recv)
    for half in range(CORES):
        wide[half] = dot(branch_all[...], weights[2, half])
    dot_u[...] = jnp.zeros_like(dot_u)
    dot_v[...] = jnp.zeros_like(dot_v)

    def deactivate(index, carry):
        half = index // slabs
        at = rows_at(lax.rem(index, slabs), slab)
        gated = gate[half, at, :] * gain_v[half]
        scaled = up[half, at, :] * gain_u[half]
        upstream = wide[half, at, :]
        sig = jax.nn.sigmoid(gated)
        to_up = upstream * (gated * sig)
        to_gate = upstream * scaled * sig * (1.0 + gated * (1.0 - sig))
        dot_u[half] += jnp.sum(to_up * up[half, at, :], axis=0, keepdims=True)
        dot_v[half] += jnp.sum(to_gate * gate[half, at, :], axis=0, keepdims=True)
        grad_u[half, at, :] = (to_up * gain_u[half]).astype(jnp.bfloat16)
        grad_v[half, at, :] = (to_gate * gain_v[half]).astype(jnp.bfloat16)
        return carry

    lax.fori_loop(0, CORES * slabs, deactivate, 0)

    def back_down(index, carry):
        at = rows_at(index, tile)
        part[1, :, at] = sum(
            dot_nt(grad_u[half], weights[0, half, at, :]) + dot_nt(grad_v[half], weights[1, half, at, :])
            for half in range(CORES)
        ).astype(jnp.bfloat16)
        return carry

    lax.fori_loop(0, model_width // tile, back_down, 0)
    for copy in swaps + more + down_more:
        copy.wait_send()
    reduce_start(part.at[1], tok_rows, sums.at[1], via.at[1], b_send, b_recv, False)
    turned[1] = branch_all[...].T
    swaps = {}

    def weight_grads(which, left, right):
        def one(index, carry):
            half = index // 5
            at = rows_at(lax.rem(index, 5), tile)
            weights[which, half, at, :] = dot(turned[left, at, :], right[half]).astype(jnp.bfloat16)
            return carry

        lax.fori_loop(0, CORES * 5, one, 0)
        swaps[which] = begin(remote(weights.at[which, 1 - core], arrived.at[which], d_send.at[which], d_recv.at[which], twin()))

    def both_cores(which):
        swaps[which].wait_recv()
        return (weights[which, core].astype(jnp.float32) + arrived[which].astype(jnp.float32)).astype(jnp.bfloat16)

    weight_grads(2, 1, hidden)
    reduce_relay(part.at[1], tok_rows, sums.at[1], via.at[1], passed.at[1], b_send, b_recv)
    weight_grads(0, 0, grad_u)
    down_half[...] = both_cores(2)
    down_across = [
        begin(remote(down_half.at[rows_at(seq_peer(step)[1], seq_rows)], down_got.at[step - 1], ds_send.at[step], ds_recv.at[step], seq_peer(step)[0]))
        for step in STEPS
    ]
    weight_grads(1, 0, grad_v)
    kept = []
    for which in range(2):
        grad_half[which] = both_cores(which)
        kept.append(begin(pltpu.make_async_copy(grad_half.at[which], to_half.at[which], local_sem.at[which])))
    reduce_wait(part.at[1], tok_rows, sums.at[1], total, b_send, b_recv)
    grad = grad_two[...] * (1.0 - alpha_mlp[...]) + total[...]
    value = mixed_one[...]
    grad = factors[1] * (grad - value * jnp.sum(grad * value, axis=-1, keepdims=True))
    unit = attn_unit[...]
    small[0:1, :] = jnp.sum(grad * (unit - states[...].astype(jnp.float32)), axis=0, keepdims=True)
    grad_direct[...] = grad * (1.0 - alpha_attn[...])
    grad = grad * alpha_attn[...]
    grad = factors[0] * (grad - unit * jnp.sum(grad * unit, axis=-1, keepdims=True))
    low = grad.astype(jnp.bfloat16)
    for at in range(CHIPS):
        grad_attx[at] = sum(
            dot_nt(low[:, half_at[half]], w_out[half, part_at[at], :]) for half in range(CORES)
        ).astype(jnp.bfloat16)
        for half in range(CORES):
            grad_w_out[half, at] = dot_tn(attx[at], low[:, half_at[half]]).astype(jnp.bfloat16)
    for half in range(CORES):
        unit_at = slice(half * half_units, (half + 1) * half_units)
        small[2:3, unit_at] = dot_u[half]
        small[3:4, unit_at] = dot_v[half] * math.sqrt(D)
    whole = down_half[seq_at, :].astype(jnp.float32)
    for step in STEPS:
        down_across[step - 1].wait_recv()
        whole = whole + down_got[step - 1].astype(jnp.float32)
    grad_down[...] = whole.astype(jnp.bfloat16)
    for copy in kept:
        copy.wait()
    gather_drain(mixed_all, tok_rows, x_send, x_recv)
    gather_drain(branch_all, tok_rows, g_send, g_recv)
    reduce_drain(part.at[0], tok_rows, sums.at[0], r_send, r_recv)
    reduce_drain(part.at[1], tok_rows, sums.at[1], b_send, b_recv, False)
    for copy in across + to_chips + down_across + [swaps[which] for which in range(3)]:
        copy.wait_send()


def mlp_call(attx, states, cotangent, w_out, alpha_attn, alpha_mlp, gain_u, gain_v, w_up, w_gate, low_down):
    tok_rows, model_width = states.shape
    chips, _, chip_heads = attx.shape
    seq_rows, half_units = w_gate.shape
    group_rows = chips * tok_rows
    f32, low = jnp.float32, jnp.bfloat16
    shape = jax.ShapeDtypeStruct
    tokens, group = (tok_rows, model_width), (group_rows, model_width)
    wide = (CORES, group_rows, half_units)
    matrix = (model_width, half_units)
    return pl.pallas_call(
        mlp_kernel,
        out_shape=[
            shape(tokens, low),
            shape(attx.shape, low),
            shape((CORES, chips, chip_heads, model_width // CORES), low),
            shape(tokens, f32),
            shape((8, max(model_width, CORES * half_units)), f32),
            shape((2,) + matrix, low),
            shape((seq_rows, half_units), low),
        ],
        in_specs=[in_vmem()] * 3 + [in_hbm()] + [in_vmem()] * 4 + [in_hbm(), in_vmem(), in_vmem()],
        out_specs=[in_vmem()] * 5 + [in_hbm(), in_vmem()],
        scratch_shapes=[
            VMEM(w_out.shape, low),
            VMEM((2,) + matrix, low),
            VMEM((3, CORES) + matrix, low),
            VMEM(tokens, f32),
            VMEM(tokens, f32),
            VMEM((2, tok_rows, 1), f32),
            VMEM(tokens, low),
            VMEM(group, low),
            VMEM(wide, f32),
            VMEM(wide, f32),
            VMEM(wide, low),
            VMEM((2,) + group, low),
            VMEM((2, 3) + tokens, low),
            VMEM((2,) + tokens, low),
            VMEM((2,) + tokens, low),
            VMEM(tokens, f32),
            VMEM(tokens, f32),
            VMEM(tokens, low),
            VMEM(group, low),
            VMEM(wide, low),
            VMEM(wide, low),
            VMEM(wide, f32),
            VMEM((2, model_width, group_rows), low),
            VMEM((3,) + matrix, low),
            VMEM((seq_rows, half_units), low),
            VMEM(matrix, low),
            VMEM((3, seq_rows, half_units), low),
            VMEM((CORES, 1, half_units), f32),
            VMEM((CORES, 1, half_units), f32),
            dma(3), dma(3, 4), dma(3, 4), dma(3), dma(3), line_dma(), line_dma(), dma(4), dma(4),
            line_dma(), line_dma(), dma(4), dma(4), dma(3), dma(3), dma(4), dma(4), dma(4), dma(4),
        ],
        compiler_params=pltpu.CompilerParams(
            collective_id=2, has_side_effects=True, vmem_limit_bytes=LIMIT
        ),
        name="mlp",
    )(
        attx, states, cotangent, w_out, alpha_attn, alpha_mlp, gain_u, gain_v, w_up, w_gate, low_down
    )


def back_kernel(
    grad_attx, from_half, grad_down, from_grad_out, small_in, from_raw, from_query, from_both, from_att,
    from_inv, from_states, from_qkv, qk_gain, places, grad_direct,
    grad_states, out_mlp, out_attn, feature, unit,
    grad_half, grad_w_out, raw, query, both, att, inverse, states_all, w_qkv, att_low, heads_low, to_keys, swap_low, swap_kv, grad_heads, grad_sides, part, sums, via, passed, total, turned,
    grad_q, half_q, seq_q, line_q, wide_q, half_o, pair_o, seq_got, seq_held, seq_last, seq_low, q_got, q_held, q_last, line_got, wide,
    wide_o, small, small_pair, small_seq, dots, small_all, flat_q, sides_q, key_pos,
    local_sem, load_sem, a_send, a_recv, s_send, s_recv, o_send, o_recv, kv_send, kv_recv, r_send, r_recv,
    qt_send, qt_recv, qs_send, qs_recv, qz_send, qz_recv, z_send, z_recv, f_send, f_recv,
    p_send, p_recv, t_send, t_recv,
):
    seq, chip, core = place_of()
    tok_rows, model_width = grad_direct.shape
    heads = qk_gain.shape[0]
    head_cols = heads * HEAD_DIM
    group_rows = CHIPS * tok_rows
    half_units = grad_half.shape[2]
    seq_rows = seq_low.shape[1]
    chip_rows = seq_rows // CHIPS
    rows = chip_rows // CORES
    part_cols = head_cols // CORES
    ff_width = out_mlp.shape[1] // 3
    scale = math.sqrt(HEAD_DIM)
    block = rows_at(chip, tok_rows)
    f32, low = jnp.float32, jnp.bfloat16
    loads = [
        begin(pltpu.make_async_copy(src, dst, load_sem.at[at]))
        for at, (src, dst) in enumerate(
            (
                (from_query, query), (from_both, both), (from_inv, inverse), (from_att, att), (from_raw, raw),
                (from_grad_out, grad_w_out), (from_states, states_all), (from_half, grad_half), (from_qkv, w_qkv),
            )
        )
    ]
    meet()
    waits = []
    line = []
    for step in STEPS:
        device, other = chip_peer(step)
        line.append(begin(remote(grad_attx.at[other], att_low.at[block], a_send.at[step], a_recv.at[step], device)))
    att_low[block, :] = grad_attx[chip]
    key_positions(places, key_pos, tok_rows)
    pair = begin(remote(from_grad_out.at[1 - core], pair_o, o_send.at[0], o_recv.at[0], twin()))
    onward = {}

    def to_chips(which, src):
        onward[which] = [
            begin(remote(src.at[rows_at(chip_peer(step)[1], chip_rows)], line_got.at[which, chip], z_send.at[which, step], z_recv.at[which, step], chip_peer(step)[0]))
            for step in STEPS
        ]
        line_got[which, chip] = src[rows_at(chip, chip_rows), :]

    def cross(which, src):
        return fold_start(src, seq_got.at[which], seq_rows, s_send.at[which], s_recv.at[which])

    def cross_on(which, src, copies):
        return fold_relay(src, seq_got.at[which], seq_held.at[which], seq_last.at[which], seq_rows, copies, s_send.at[which], s_recv.at[which])

    def cross_end(which, src, copies, more):
        fold_end(src, seq_got.at[which], seq_last.at[which], seq_low.at[which], seq_rows, copies, more)

    crossing = [cross(which, from_half.at[which]) for which in range(2)]
    to_keys[...] = jnp.zeros_like(to_keys)
    dots[...] = jnp.zeros_like(dots)
    for copy in loads:
        copy.wait()
    turned[...] = states_all[...].T
    pair.wait_recv()
    for at in range(4):
        half_o[at * seq_rows : (at + 1) * seq_rows, :] = (
            grad_w_out[core, at].astype(f32) + pair_o[at].astype(f32)
        ).astype(low)
    crossing.append(cross(2, half_o))
    tile = tok_rows
    tiles = CHIPS

    def raw_back(which, head, at, upstream):
        value = raw[which, head, at, :]
        unit, factor = unit_of(value)
        dots[head] += jnp.sum(upstream * unit, axis=0, keepdims=True)
        upstream = upstream * qk_gain[head]
        upstream = factor * (upstream - unit * jnp.sum(upstream * unit, axis=-1, keepdims=True))
        grad_heads[which, head, at, :] = upstream.astype(low)

    def one_block(step, carry):
        other = lax.rem(chip + CHIPS - step, CHIPS)
        at = rows_at(other, tok_rows)
        copy = remote(grad_attx.at[0], att_low.at[at], a_send.at[step], a_recv.at[step], device_on(other))
        when(step > 0, copy.wait_recv)
        for head in range(heads):
            heads_low[head, at, :] = att_low[at, head * HEAD_DIM : (head + 1) * HEAD_DIM]
        allowed = kept_pairs(places, key_pos, other, core, tok_rows)

        def one_head(head, carry):
            rows_q = query[head, at, :]
            grad_att = heads_low[head, at, :]
            scores = jnp.concatenate([dot_nt(rows_q, both[half, 0, head]) for half in range(CORES)], axis=1)
            probs = jnp.exp(jnp.where(allowed, scores, NEG_LARGE)) * inverse[head, at, :]
            grad_prob = jnp.concatenate([dot_nt(grad_att, both[half, 1, head]) for half in range(CORES)], axis=1)
            row_dot = jnp.sum(grad_att.astype(f32) * att[head, at, :], axis=-1, keepdims=True)
            grad_scores = (probs * (grad_prob - row_dot)).astype(low)
            weights = probs.astype(low)
            to_query = jnp.zeros((tok_rows, HEAD_DIM), f32)
            for half in range(CORES):
                cols = slice(half * group_rows, (half + 1) * group_rows)
                to_query = to_query + dot(grad_scores[:, cols], both[half, 0, head])
                to_keys[half, 0, head] += dot_tn(grad_scores[:, cols], rows_q)
                to_keys[half, 1, head] += dot_tn(weights[:, cols], grad_att)
            raw_back(0, head, at, to_query * scale)
            return carry

        lax.fori_loop(0, heads, one_head, 0)
        return carry

    lax.fori_loop(0, CHIPS, one_block, 0)
    to_chips(2, grad_down)
    sources = (grad_half.at[0], grad_half.at[1], half_o)
    onwards = [cross_on(which, sources[which], crossing[which]) for which in range(2)]
    swap_low[...] = to_keys[1 - core].astype(low)
    swap = begin(remote(swap_low, swap_kv, kv_send.at[0], kv_recv.at[0], twin()))
    swap.wait()

    def one_key(index, carry):
        head = index // tiles
        at = rows_at(lax.rem(index, tiles), tile)
        mine = to_keys[core, 0, head, at, :] + swap_kv[0, head, at, :].astype(f32)
        raw_back(1, head, at, mine)
        value = to_keys[core, 1, head, at, :] + swap_kv[1, head, at, :].astype(f32)
        grad_heads[2, head, at, :] = value.astype(low)
        return carry

    lax.fori_loop(0, heads * tiles, one_key, 0)
    for which in range(3):
        full = jnp.concatenate([grad_heads[which, head] for head in range(heads)], axis=1)
        for half in range(CORES):
            grad_sides[half, :, which * part_cols : (which + 1) * part_cols] = full[:, half * part_cols : (half + 1) * part_cols]
    wide_tile = model_width // 5
    def weight_grad(index, carry):
        half = index // 5
        at = rows_at(lax.rem(index, 5), wide_tile)
        grad_q[half, at, :] = dot(turned[at, :], grad_sides[half]).astype(low)
        return carry

    lax.fori_loop(0, CORES * 5, weight_grad, 0)
    swap_q = begin(remote(grad_q.at[1 - core], half_q, qt_send.at[0], qt_recv.at[0], twin()))
    onwards.append(cross_on(2, half_o, crossing[2]))
    cross_end(0, sources[0], crossing[0], onwards[0])
    to_chips(0, seq_low.at[0])

    def down(index, carry):
        at = rows_at(index, wide_tile)
        part[:, at] = sum(dot_nt(grad_sides[half], w_qkv[half, at, :]) for half in range(CORES)).astype(low)
        return carry

    lax.fori_loop(0, 5, down, 0)
    reduce_start(part, tok_rows, sums, via, r_send, r_recv, False)
    swap_q.wait()
    half_q[...] = (grad_q[core].astype(f32) + half_q[...].astype(f32)).astype(low)
    crossing_q = fold_start(half_q, q_got, seq_rows, qs_send, qs_recv)
    cross_end(1, sources[1], crossing[1], onwards[1])
    to_chips(1, seq_low.at[1])
    cross_end(2, half_o, crossing[2], onwards[2])
    to_chips(3, seq_low.at[2])
    small[...] = small_in[...]
    small[4:5, :head_cols] = jnp.concatenate([dots[head] for head in range(heads)], axis=1)
    swap_s = begin(remote(small, small_pair, t_send.at[0], t_recv.at[0], twin()))
    more_q = fold_relay(half_q, q_got, q_held, q_last, seq_rows, crossing_q, qs_send, qs_recv)
    reduce_relay(part, tok_rows, sums, via, passed, r_send, r_recv)
    swap_s.wait()
    small[...] = small[...] + small_pair[...]
    spread_s = [
        begin(remote(small, small_seq.at[step - 1], t_send.at[step], t_recv.at[step], seq_peer(step)[0]))
        for step in STEPS
    ]
    fold_end(half_q, q_got, q_last, seq_q, seq_rows, crossing_q, more_q)
    onward_q = []
    for step in STEPS:
        device, other = chip_peer(step)
        onward_q.append(begin(remote(seq_q.at[rows_at(other, chip_rows)], line_q.at[chip], qz_send.at[step], qz_recv.at[step], device)))
    line_q[chip] = seq_q[rows_at(chip, chip_rows), :]
    for copy in spread_s:
        copy.wait()
    small_pair[...] = small[...] + small_seq[0] + small_seq[1] + small_seq[2]
    small_all[chip] = small_pair[...]
    ends = to_line(small_pair, small_all.at[chip], p_send, p_recv)

    mine = rows_at(core, rows)
    theirs = rows_at(1 - core, rows)
    last, lasts = [], []
    for which in (2, 0, 1):
        for copy in onward[which]:
            copy.wait_recv()
        for at in range(CHIPS):
            wide[which, at] = line_got[which, at].astype(f32)
            start = which * ff_width + at * CORES * half_units + core * half_units
            there = out_mlp.at[:, pl.ds(pl.multiple_of(start, 128), half_units)]
            last.append(begin(remote(wide.at[which, at, theirs], there, f_send.at[which, at], f_recv.at[which, at], twin())))
            lasts.append(begin(pltpu.make_async_copy(wide.at[which, at, mine], there, local_sem.at[3 + which * CHIPS + at])))
    for copy in onward[3]:
        copy.wait_recv()
    whole = line_got[3, 0].astype(f32)
    for at in range(1, CHIPS):
        whole = whole + line_got[3, at].astype(f32)
    wide_o[...] = whole
    start = 3 * model_width + core * half_units
    there = out_attn.at[:, pl.ds(pl.multiple_of(start, 128), half_units)]
    last.append(begin(remote(wide_o.at[theirs], there, f_send.at[3, 0], f_recv.at[3, 0], twin())))
    lasts.append(begin(pltpu.make_async_copy(wide_o.at[mine], there, local_sem.at[15])))
    for copy in onward_q:
        copy.wait_recv()
    wide_q[...] = line_q[...].astype(f32)
    sides_q[core] = wide_q[:, mine, :]
    swap_q = begin(remote(wide_q.at[:, theirs], sides_q.at[core], f_send.at[3, 1], f_recv.at[3, 1], twin()))
    for copy in ends:
        copy.wait()
    alphas = small_all[0] + small_all[1] + small_all[2] + small_all[3]
    feature[1:3, :] = alphas[0:2, :]
    for at in range(CHIPS):
        feature[0:1, at * head_cols : (at + 1) * head_cols] = small_all[at, 4:5, :head_cols]
        width = CORES * half_units
        unit[:, at * width : (at + 1) * width] = small_all[at, 2:4, :width]
    swap_q.wait()
    for at in range(CHIPS):
        for half in range(CORES):
            for which in range(3):
                start = which * model_width + at * head_cols + half * part_cols
                flat_q[:, start : start + part_cols] = sides_q[half, at, :, which * part_cols : (which + 1) * part_cols]
    lasts.append(begin(pltpu.make_async_copy(flat_q, out_attn.at[:, pl.ds(0, 3 * model_width)], local_sem.at[16])))
    reduce_wait(part, tok_rows, sums, total, r_send, r_recv)
    grad_states[...] = (total[...] + grad_direct[...]).astype(low)
    for copy in last + lasts:
        copy.wait()
    reduce_drain(part, tok_rows, sums, r_send, r_recv, False)
    for copy in line + [pair] + sum(crossing + onwards + list(onward.values()), crossing_q + more_q + onward_q):
        copy.wait_send()


def back_call(
    grad_attx, grad_half, grad_down, grad_w_out, small_in, raw, query, both, att, inverse, states_all,
    w_qkv, qk_gain, places, grad_direct, rows,
):
    tok_rows, model_width = grad_direct.shape
    chips = grad_attx.shape[0]
    heads = qk_gain.shape[0]
    head_cols = heads * HEAD_DIM
    group_rows = chips * tok_rows
    half_units = grad_half.shape[2]
    half_cols = w_qkv.shape[2]
    chip_rows = CORES * rows
    seq_rows = chips * chip_rows
    f32, low = jnp.float32, jnp.bfloat16
    shape = jax.ShapeDtypeStruct
    per_head = (heads, group_rows, HEAD_DIM)
    return pl.pallas_call(
        back_kernel,
        out_shape=[
            shape((tok_rows, model_width), low),
            shape((rows, 3 * chips * CORES * half_units), f32),
            shape((rows, 4 * model_width), f32),
            shape((3, model_width), f32),
            shape((2, chips * CORES * half_units), f32),
        ],
        in_specs=[in_vmem(), in_hbm(), in_vmem(), in_hbm(), in_vmem()] + [in_hbm()] * 7 + [in_vmem(), in_smem(), in_vmem()],
        out_specs=[in_vmem(), in_hbm(), in_hbm(), in_vmem(), in_vmem()],
        scratch_shapes=[
            *(VMEM(value.shape, value.dtype) for value in (grad_half, grad_w_out, raw, query, both, att, inverse, states_all, w_qkv)),
            VMEM((group_rows, head_cols), low),
            VMEM(per_head, low),
            VMEM((CORES, 2) + per_head, f32),
            VMEM((2,) + per_head, low),
            VMEM((2,) + per_head, low),
            VMEM((3,) + per_head, low),
            VMEM((CORES, group_rows, half_cols), low),
            VMEM((group_rows, model_width), low),
            VMEM((3, tok_rows, model_width), low),
            VMEM((tok_rows, model_width), low),
            VMEM((tok_rows, model_width), low),
            VMEM((tok_rows, model_width), f32),
            VMEM((model_width, group_rows), low),
            VMEM((CORES, model_width, half_cols), low),
            VMEM((model_width, half_cols), low),
            VMEM((seq_rows, half_cols), low),
            VMEM((chips, chip_rows, half_cols), low),
            VMEM((chips, chip_rows, half_cols), f32),
            VMEM((4 * seq_rows, half_units), low),
            VMEM((4, seq_rows, half_units), low),
            VMEM((3, 2, 2, seq_rows // 2, half_units), low),
            VMEM((3, 2, seq_rows // 2, half_units), low),
            VMEM((3, 2, seq_rows // 2, half_units), low),
            VMEM((3, seq_rows, half_units), low),
            VMEM((2, 2, seq_rows // 2, half_cols), low),
            VMEM((2, seq_rows // 2, half_cols), low),
            VMEM((2, seq_rows // 2, half_cols), low),
            VMEM((4, chips, chip_rows, half_units), low),
            VMEM((3, chips, chip_rows, half_units), f32),
            VMEM((chip_rows, half_units), f32),
            VMEM(small_in.shape, f32),
            VMEM(small_in.shape, f32),
            VMEM((3,) + small_in.shape, f32),
            VMEM((heads, 1, HEAD_DIM), f32),
            VMEM((chips,) + small_in.shape, f32),
            VMEM((rows, 3 * model_width), f32),
            VMEM((CORES, chips, rows, half_cols), f32),
            VMEM((1, CORES * group_rows), jnp.int32),
            dma(17), dma(9), dma(4), dma(4), dma(3, 3, 2), dma(3, 3, 2), dma(1), dma(1), dma(1), dma(1),
            dma(4), dma(4), dma(1), dma(1), dma(3, 2), dma(3, 2), dma(4), dma(4), dma(4, 4), dma(4, 4),
            dma(4, 4), dma(4, 4), dma(4), dma(4), dma(4), dma(4),
        ],
        compiler_params=pltpu.CompilerParams(
            collective_id=3, has_side_effects=True, vmem_limit_bytes=LIMIT
        ),
        name="back",
    )(
        grad_attx, grad_half, grad_down, grad_w_out, small_in, raw, query, both, att, inverse, states_all,
        w_qkv, qk_gain, places, grad_direct,
    )


def shards_split(states, cotangent, attn_weights, mlp_weights, feature_gains, unit_gains, block_place):
    tok_rows, model_width = states.shape
    ff_width = unit_gains.shape[0]
    n_seq, n_ctx = lax.axis_size("seq"), lax.axis_size("ctx")
    chips = n_ctx // CORES
    chip = lax.axis_index("ctx") // CORES
    heads = HEADS // chips
    head_cols = heads * HEAD_DIM
    units = ff_width // chips
    rows = attn_weights.shape[0]
    qk_gain = lax.dynamic_slice_in_dim(feature_gains[:, 0], chip * head_cols, head_cols)
    qk_gain = qk_gain.reshape(heads, 1, HEAD_DIM)
    states_all, w_qkv, w_out, w_up, w_gate, low_down, raw, query, both, att, inverse, attx = attend_call(
        states, attn_weights, mlp_weights, qk_gain, block_place
    )
    gain_u = lax.dynamic_slice_in_dim(unit_gains[:, 0], chip * units, units)
    gain_v = lax.dynamic_slice_in_dim(unit_gains[:, 1], chip * units, units) * math.sqrt(D)
    out_low, grad_attx, grad_w_out, grad_direct, small, grad_half, grad_down = mlp_call(
        attx, states, cotangent, w_out, feature_gains[:, 1].reshape(1, model_width),
        feature_gains[:, 2].reshape(1, model_width), gain_u.reshape(CORES, 1, units // CORES),
        gain_v.reshape(CORES, 1, units // CORES), w_up, w_gate, low_down,
    )
    grad_states, grad_mlp, grad_attn, feature, unit = back_call(
        grad_attx, grad_half, grad_down, grad_w_out, small, raw, query, both, att, inverse, states_all,
        w_qkv, qk_gain, block_place, grad_direct, rows,
    )
    rank = lax.axis_index(ALL)
    unit_rows_own = ff_width // (n_seq * n_ctx)
    return (
        out_low,
        grad_states,
        grad_attn,
        grad_mlp,
        lax.dynamic_slice_in_dim(feature, rank * rows, rows, axis=1).T,
        lax.dynamic_slice_in_dim(unit, rank * unit_rows_own, unit_rows_own, axis=1).T,
    )


def solution(mesh):
    in_specs = (
        P(("seq", "ctx"), None),
        P(("seq", "ctx"), None),
        P(("seq", "ctx"), None),
        P(("seq", "ctx"), None),
        P(),
        P(),
        P("seq", None),
    )
    out_specs = (
        P(("seq", "ctx"), None),
        P(("seq", "ctx"), None),
        P(("seq", "ctx"), None),
        P(("seq", "ctx"), None),
        P(("seq", "ctx"), None),
        P(("seq", "ctx"), None),
    )
    chips = mesh.shape["ctx"] // CORES
    shards = shards_split if fits(mesh.shape["seq"], chips) else shards_general
    return jax.shard_map(shards, mesh=mesh, in_specs=in_specs, out_specs=out_specs, check_vma=False)
```

```python
import functools
import math

import jax
import jax.numpy as jnp
from jax import lax
from jax.experimental import pallas as pl
from jax.experimental.pallas import tpu as pltpu
from jax.sharding import PartitionSpec as P

D = 1280
HEADS = 20
HEAD_DIM = 64


EPSILON = 1e-06
NEG_LARGE = -1e30


def unit_rows(values_in):
    factor = lax.rsqrt(jnp.sum(values_in * values_in, axis=-1, keepdims=True) + EPSILON)
    return (values_in * factor, factor)


def unit_back(normed, factor, upstream):
    return factor * (upstream - normed * jnp.sum(upstream * normed, axis=-1, keepdims=True))


def contract_rows(left_mat, right_mat):
    return lax.dot_general(
        left_mat, right_mat, (((0,), (0,)), ((), ())), preferred_element_type=jnp.float32
    )


def contract_cols(left_mat, right_mat):
    return lax.dot_general(
        left_mat, right_mat, (((1,), (1,)), ((), ())), preferred_element_type=jnp.float32
    )


def shards_general(states, cotangent, attn_weights, mlp_weights, feature_gains, unit_gains, block_place):
    tok_rows = states.shape[0]
    model_width = states.shape[1]
    ff_width = unit_gains.shape[0]
    score_scale = math.sqrt(HEAD_DIM)
    gate_factor = unit_gains[:, 1] * math.sqrt(D)
    w_attn = lax.all_gather(attn_weights.astype(jnp.bfloat16), ("seq", "ctx"), axis=0, tiled=True)
    w_mlp = lax.all_gather(mlp_weights.astype(jnp.bfloat16), ("seq", "ctx"), axis=0, tiled=True)
    states_full = states.astype(jnp.float32)
    projected = jnp.dot(states, w_attn[:, : 3 * model_width], preferred_element_type=jnp.float32)
    head_shape = (tok_rows, HEADS, HEAD_DIM)
    qk_gain = feature_gains[:, 0].reshape(HEADS, HEAD_DIM)
    query_unit, query_factor = unit_rows(projected[:, :model_width].reshape(head_shape))
    key_unit, key_factor = unit_rows(
        projected[:, model_width : 2 * model_width].reshape(head_shape)
    )
    query_low = (query_unit * qk_gain).astype(jnp.bfloat16)
    key_low = (key_unit * qk_gain).astype(jnp.bfloat16).reshape(tok_rows, model_width)
    value_low = projected[:, 2 * model_width :].astype(jnp.bfloat16)
    keys_all, values_all = (
        lax.all_gather(key_low, "ctx", axis=0, tiled=True),
        lax.all_gather(value_low, "ctx", axis=0, tiled=True),
    )
    seq_len = keys_all.shape[0]
    ctx_lanes = jnp.arange(lax.axis_size("ctx"), dtype=jnp.int32)
    places = block_place[0]
    own_block = jnp.sum(jnp.where(ctx_lanes == lax.axis_index("ctx"), places, 0))
    query_pos = own_block * tok_rows + jnp.arange(tok_rows, dtype=jnp.int32)
    key_index = jnp.arange(seq_len, dtype=jnp.int32)
    key_owner = key_index // tok_rows
    key_pos = (
        jnp.sum(jnp.where(key_owner[:, None] == ctx_lanes[None, :], places[None, :], 0), axis=1)
        * tok_rows
        + key_index % tok_rows
    )
    kblock = min(512, seq_len)
    nblocks = seq_len // kblock
    key_blocks = keys_all.reshape(nblocks, kblock, HEADS, HEAD_DIM)
    value_blocks = values_all.reshape(nblocks, kblock, HEADS, HEAD_DIM)
    pos_blocks = key_pos.reshape(nblocks, kblock)

    def block_scores(key_rows, key_places):
        raw_scores = score_scale * jnp.einsum(
            "qhd,khd->hqk", query_low, key_rows, preferred_element_type=jnp.float32
        )
        allowed = key_places[None, None, :] <= query_pos[None, :, None]
        return (raw_scores, allowed)

    def max_step(running, inputs):
        running_max, running_sum = running
        key_rows, key_places = inputs
        raw_scores, allowed = block_scores(key_rows, key_places)
        masked = jnp.where(allowed, raw_scores, NEG_LARGE)
        new_max = jnp.maximum(running_max, jnp.max(masked, axis=-1))
        powered = jnp.where(allowed, jnp.exp(masked - new_max[..., None]), 0.0)
        running_sum = running_sum * jnp.exp(running_max - new_max) + jnp.sum(powered, axis=-1)
        return ((new_max, running_sum), None)

    start_max = jnp.full((HEADS, tok_rows), NEG_LARGE, jnp.float32)
    start_sum = jnp.zeros((HEADS, tok_rows), jnp.float32)
    (final_max, final_sum), _ = lax.scan(max_step, (start_max, start_sum), (key_blocks, pos_blocks))
    log_total = final_max + jnp.log(final_sum)

    def value_step(accumulated, inputs):
        key_rows, value_rows, key_places = inputs
        raw_scores, allowed = block_scores(key_rows, key_places)
        weights_low = jnp.where(allowed, jnp.exp(raw_scores - log_total[..., None]), 0.0).astype(
            jnp.bfloat16
        )
        accumulated = accumulated + jnp.einsum(
            "hqk,khd->qhd", weights_low, value_rows, preferred_element_type=jnp.float32
        )
        return (accumulated, None)

    attended, _ = lax.scan(
        value_step, jnp.zeros(head_shape, jnp.float32), (key_blocks, value_blocks, pos_blocks)
    )
    attended_low = attended.reshape(tok_rows, model_width).astype(jnp.bfloat16)
    branch_attn = jnp.dot(
        attended_low, w_attn[:, 3 * model_width :], preferred_element_type=jnp.float32
    )
    attn_unit, attn_factor = unit_rows(branch_attn)
    alpha_attn = feature_gains[:, 1]
    mixed_one, mix_factor = unit_rows(states_full + alpha_attn * (attn_unit - states_full))
    mixed_low = mixed_one.astype(jnp.bfloat16)
    up_gate = jnp.dot(mixed_low, w_mlp[:, : 2 * ff_width], preferred_element_type=jnp.float32)
    up_scaled = up_gate[:, :ff_width] * unit_gains[:, 0]
    gate_scaled = up_gate[:, ff_width:] * gate_factor
    sigmoid_gate = jax.nn.sigmoid(gate_scaled)
    activated = gate_scaled * sigmoid_gate
    hidden = (activated * up_scaled).astype(jnp.bfloat16)
    branch_mlp = contract_cols(hidden, w_mlp[:, 2 * ff_width :])
    mlp_unit, mlp_factor = unit_rows(branch_mlp)
    alpha_mlp = feature_gains[:, 2]
    out_full, out_factor = unit_rows(mixed_one + alpha_mlp * (mlp_unit - mixed_one))
    grad_mix_two = unit_back(out_full, out_factor, cotangent.astype(jnp.float32))
    grad_alpha_m = jnp.sum(grad_mix_two * (mlp_unit - mixed_one), axis=0)
    grad_branch_mlp = unit_back(mlp_unit, mlp_factor, grad_mix_two * alpha_mlp).astype(jnp.bfloat16)
    grad_hidden = jnp.dot(
        grad_branch_mlp, w_mlp[:, 2 * ff_width :], preferred_element_type=jnp.float32
    )
    grad_up_scaled = grad_hidden * activated
    grad_gate_scaled = (
        grad_hidden * up_scaled * sigmoid_gate * (1.0 + gate_scaled * (1.0 - sigmoid_gate))
    )
    grad_s_u = jnp.sum(grad_up_scaled * up_gate[:, :ff_width], axis=0)
    grad_s_v = jnp.sum(grad_gate_scaled * up_gate[:, ff_width:], axis=0) * math.sqrt(D)
    grad_up_gate = jnp.concatenate(
        [grad_up_scaled * unit_gains[:, 0], grad_gate_scaled * gate_factor], axis=1
    ).astype(jnp.bfloat16)
    grad_mixed_one = grad_mix_two * (1.0 - alpha_mlp) + contract_cols(
        grad_up_gate, w_mlp[:, : 2 * ff_width]
    )
    grad_mix_one = unit_back(mixed_one, mix_factor, grad_mixed_one)
    grad_alpha_a = jnp.sum(grad_mix_one * (attn_unit - states_full), axis=0)
    grad_branch_attn = unit_back(attn_unit, attn_factor, grad_mix_one * alpha_attn).astype(
        jnp.bfloat16
    )
    grad_attended = (
        contract_cols(grad_branch_attn, w_attn[:, 3 * model_width :])
        .astype(jnp.bfloat16)
        .reshape(head_shape)
    )
    row_dots = jnp.einsum("qhd,qhd->hq", grad_attended.astype(jnp.float32), attended)

    def grad_step(grad_query, inputs):
        key_rows, value_rows, key_places = inputs
        raw_scores, allowed = block_scores(key_rows, key_places)
        probabilities = jnp.where(allowed, jnp.exp(raw_scores - log_total[..., None]), 0.0)
        grad_prob = jnp.einsum(
            "qhd,khd->hqk", grad_attended, value_rows, preferred_element_type=jnp.float32
        )
        grad_scores = (probabilities * (grad_prob - row_dots[..., None])).astype(jnp.bfloat16)
        grad_query = grad_query + score_scale * jnp.einsum(
            "hqk,khd->qhd", grad_scores, key_rows, preferred_element_type=jnp.float32
        )
        key_terms = score_scale * jnp.einsum(
            "hqk,qhd->khd", grad_scores, query_low, preferred_element_type=jnp.float32
        )
        value_terms = jnp.einsum(
            "hqk,qhd->khd",
            probabilities.astype(jnp.bfloat16),
            grad_attended,
            preferred_element_type=jnp.float32,
        )
        return (grad_query, (key_terms, value_terms))

    grad_query_low, (key_terms, value_terms) = lax.scan(
        grad_step, jnp.zeros(head_shape, jnp.float32), (key_blocks, value_blocks, pos_blocks)
    )
    key_terms = key_terms.reshape(seq_len, model_width)
    value_terms = value_terms.reshape(seq_len, model_width)
    own_key_grad, own_value_grad = (
        lax.psum_scatter(
            key_terms.astype(jnp.bfloat16), "ctx", scatter_dimension=0, tiled=True
        ).astype(jnp.float32),
        lax.psum_scatter(
            value_terms.astype(jnp.bfloat16), "ctx", scatter_dimension=0, tiled=True
        ).astype(jnp.float32),
    )
    grad_key_low = own_key_grad.reshape(head_shape)
    grad_s_qk = jnp.sum(grad_query_low * query_unit + grad_key_low * key_unit, axis=0).reshape(
        model_width
    )
    grad_query_raw = unit_back(query_unit, query_factor, grad_query_low * qk_gain).reshape(
        tok_rows, model_width
    )
    grad_key_raw = unit_back(key_unit, key_factor, grad_key_low * qk_gain).reshape(
        tok_rows, model_width
    )
    grad_projected = jnp.concatenate([grad_query_raw, grad_key_raw, own_value_grad], axis=1).astype(
        jnp.bfloat16
    )
    grad_states = grad_mix_one * (1.0 - alpha_attn) + contract_cols(
        grad_projected, w_attn[:, : 3 * model_width]
    )
    feature_total = jnp.stack([grad_s_qk, grad_alpha_a, grad_alpha_m], axis=1)
    unit_fold = jnp.stack([grad_s_u, grad_s_v], axis=1).reshape(
        model_width, 2 * ff_width // model_width
    )
    attn_cols = 4 * model_width
    mlp_cols = 3 * ff_width
    attn_share = lax.psum_scatter(
        jnp.concatenate(
            [
                contract_rows(states, grad_projected),
                contract_rows(attended_low, grad_branch_attn),
                feature_total,
            ],
            axis=1,
        ),
        ("seq", "ctx"),
        scatter_dimension=0,
        tiled=True,
    )
    mlp_share = lax.psum_scatter(
        jnp.concatenate(
            [
                contract_rows(mixed_low, grad_up_gate),
                contract_rows(grad_branch_mlp, hidden),
                unit_fold,
            ],
            axis=1,
        ),
        ("seq", "ctx"),
        scatter_dimension=0,
        tiled=True,
    )
    grad_attn = attn_share[:, :attn_cols]
    grad_feature = attn_share[:, attn_cols:]
    grad_mlp = mlp_share[:, :mlp_cols]
    grad_unit = mlp_share[:, mlp_cols:].reshape(
        unit_gains.shape[0] // lax.axis_size(("seq", "ctx")), 2
    )
    return (
        out_full.astype(jnp.bfloat16),
        grad_states.astype(jnp.bfloat16),
        grad_attn,
        grad_mlp,
        grad_feature,
        grad_unit,
    )


CORES = 2
ALL = ("seq", "ctx")


def fits(n_seq, chips):
    return n_seq == 4 and chips == 4 and HEADS % chips == 0


MESH = pl.DeviceIdType.MESH
VMEM = pltpu.VMEM
CHIPS = 4
STEPS = (1, 2, 3)
LIMIT = 60 * 1024 * 1024


def place_of():
    seq = lax.axis_index("seq")
    ctx = lax.axis_index("ctx")
    return seq, ctx // CORES, ctx % CORES


def chip_peer(step):
    seq, chip, core = place_of()
    other = lax.rem(chip + step, CHIPS)
    return (seq, other * CORES + core), other


def seq_peer(step):
    seq, chip, core = place_of()
    other = seq ^ step
    return (other, chip * CORES + core), other


def twin():
    seq, chip, core = place_of()
    return (seq, chip * CORES + 1 - core)


def meet():
    devices = [chip_peer(step)[0] for step in STEPS] + [seq_peer(step)[0] for step in STEPS] + [twin()]
    gate = pltpu.get_barrier_semaphore()
    for device in devices:
        pl.semaphore_signal(gate, inc=1, device_id=device, device_id_type=MESH)
    pl.semaphore_wait(gate, len(devices))


def remote(src, dst, send, recv, device):
    return pltpu.make_async_remote_copy(
        src_ref=src, dst_ref=dst, send_sem=send, recv_sem=recv, device_id=device,
        device_id_type=MESH,
    )


def begin(copy):
    copy.start()
    return copy


def rows_at(index, count):
    return pl.ds(pl.multiple_of(index * count, count), count)


def device_on(chip):
    seq, _, core = place_of()
    return (seq, chip * CORES + core)


def when(condition, action):
    pl.when(condition)(action)


PIECES = 2


def piece_at(block, piece, count):
    step = count // PIECES
    return pl.ds(pl.multiple_of(block * count + piece * step, step), step)


def gather_copy(src, everything, count, block, side, hop, piece, send, recv):
    chip = place_of()[1]
    there = everything.at[piece_at(block, piece, count)]
    near = chip + 1 if side == 0 else chip - 1
    here = there if src is None else src.at[piece_at(0, piece, count)]
    return remote(here, there, send.at[side, hop, piece], recv.at[side, hop, piece], device_on(near))


def gather_start(src, everything, count, send, recv):
    chip = place_of()[1]
    for piece in range(PIECES):
        for side in range(2):
            copy = gather_copy(src, everything, count, chip, side, 0, piece, send, recv)
            when(chip < CHIPS - 1 if side == 0 else chip > 0, copy.start)


def gather_hop(everything, count, hop, send, recv):
    chip = place_of()[1]
    for piece in range(PIECES):
        for side in range(2):
            block = chip - hop if side == 0 else chip + hop

            def pass_on(side=side, piece=piece, block=block):
                gather_copy(None, everything, count, block, side, hop - 1, piece, send, recv).wait_recv()
                if hop < CHIPS - 1:
                    copy = gather_copy(None, everything, count, block, side, hop, piece, send, recv)
                    when(chip < CHIPS - 1 if side == 0 else chip > 0, copy.start)

            when(block >= 0 if side == 0 else block < CHIPS, pass_on)


def gather_drain(everything, count, send, recv):
    chip = place_of()[1]
    for hop in range(CHIPS - 1):
        for piece in range(PIECES):
            for side in range(2):
                copy = gather_copy(None, everything, count, chip, side, hop, piece, send, recv)
                block = chip - hop if side == 0 else chip + hop
                sent = (block >= 0) & (chip < CHIPS - 1) if side == 0 else (block < CHIPS) & (chip > 0)
                when(sent, copy.wait_send)


def inside_line():
    chip = place_of()[1]
    return (chip > 0) & (chip < CHIPS - 1)


def spans_line(other):
    return abs(place_of()[1] - other) == CHIPS - 1


def reduce_start(part, count, sums, via, send, recv, ahead=True):
    chip = place_of()[1]
    near = jnp.where(chip == 0, 1, CHIPS - 2)
    first = remote(part.at[rows_at(CHIPS - 1 - chip, count)], via, send.at[0], recv.at[0], device_on(near))

    def begin_far():
        first.start()
        if ahead:
            first.wait_send()

    when(jnp.logical_not(inside_line()), begin_far)
    for step in STEPS:
        device, other = chip_peer(step)
        copy = remote(part.at[rows_at(other, count)], sums.at[step - 1], send.at[step], recv.at[step], device)
        if step == 2:
            when(jnp.logical_not(inside_line()), copy.start)
        else:
            when(jnp.logical_not(spans_line(other)), copy.start)


def reduce_relay(part, count, sums, via, mixed, send, recv):
    chip = place_of()[1]
    other = lax.rem(chip + 2, CHIPS)
    copy = remote(mixed, sums.at[1], send.at[2], recv.at[2], device_on(other))

    def pass_on():
        remote(mixed, via, send.at[0], recv.at[0], device_on(other)).wait_recv()
        mixed[...] = (
            part[rows_at(other, count), :].astype(jnp.float32) + via[...].astype(jnp.float32)
        ).astype(mixed.dtype)
        copy.start()

    when(inside_line(), pass_on)


def reduce_wait(part, count, sums, total, send, recv):
    chip = place_of()[1]
    total[...] = part[rows_at(chip, count), :].astype(jnp.float32)
    for step in (1, 3, 2):
        source = lax.rem(chip + CHIPS - step, CHIPS)

        def add(step=step, source=source):
            here = sums.at[step - 1]
            remote(here, here, send.at[step], recv.at[step], device_on(source)).wait_recv()
            total[...] += sums[step - 1].astype(jnp.float32)

        when(jnp.logical_not(spans_line(source)), add)


def reduce_drain(part, count, sums, send, recv, ahead=True):
    rows = part.at[rows_at(0, count)]
    for step in STEPS:
        device, other = chip_peer(step)
        copy = remote(rows, sums.at[step - 1], send.at[step], recv.at[step], device)
        when(jnp.logical_not(spans_line(other)), copy.wait_send)
    if not ahead:
        copy = remote(rows, sums.at[0], send.at[0], recv.at[0], device_on(place_of()[1]))
        when(jnp.logical_not(inside_line()), copy.wait_send)


def side_peer(side):
    return seq_peer(side + 1)


def seq_rows_at(block, side, count):
    half = count // 2
    return pl.ds(pl.multiple_of(block * count + side * half, half), half)


def spread_start(src, dst, count, send, recv):
    seq = place_of()[0]
    return [
        begin(remote(src, dst.at[rows_at(seq, count)], send.at[side], recv.at[side], side_peer(side)[0]))
        for side in range(2)
    ]


def spread_relay(dst, count, send, recv):
    copies = []
    for side in range(2):
        block = side_peer(side)[1]
        whole = dst.at[rows_at(block, count)]
        remote(whole, whole, send.at[side], recv.at[side], side_peer(side)[0]).wait_recv()
        part = dst.at[seq_rows_at(block, side, count)]
        copies.append(begin(remote(part, part, send.at[2 + side], recv.at[2 + side], side_peer(1 - side)[0])))
    return copies


def fold_start(src, got, count, send, recv):
    seq = place_of()[0]
    copies = []
    for side in range(2):
        device, other = side_peer(side)
        for at, block in enumerate((other, seq ^ 3)):
            here = src.at[seq_rows_at(block, side, count)]
            copies.append(begin(remote(here, got.at[side, at], send.at[side, at], recv.at[side, at], device)))
    return copies


def fold_relay(src, got, held, last, count, copies, send, recv):
    more = []
    for side in range(2):
        device, other = side_peer(1 - side)
        copies[2 * side + 1].wait_recv()
        rows = seq_rows_at(other, side, count)
        held[side] = (src[rows, :].astype(jnp.float32) + got[side, 1].astype(jnp.float32)).astype(held.dtype)
        more.append(begin(remote(held.at[side], last.at[side], send.at[2, side], recv.at[2, side], device)))
    return more


def fold_end(src, got, last, out, count, copies, more):
    seq = place_of()[0]
    half = count // 2
    for side in range(2):
        copies[2 * side].wait_recv()
        more[side].wait_recv()
        rows = seq_rows_at(seq, side, count)
        out[side * half : (side + 1) * half, :] = (
            src[rows, :].astype(jnp.float32) + got[side, 0].astype(jnp.float32) + last[side].astype(jnp.float32)
        ).astype(out.dtype)


def to_line(src, there, send, recv):
    return [
        begin(remote(src, there, send.at[step], recv.at[step], chip_peer(step)[0])) for step in STEPS
    ]


def dot(left, right):
    return jnp.dot(left, right, preferred_element_type=jnp.float32)


def dot_nt(left, right):
    return lax.dot_general(
        left, right, (((1,), (1,)), ((), ())), preferred_element_type=jnp.float32
    )


def dot_tn(left, right):
    return lax.dot_general(
        left, right, (((0,), (0,)), ((), ())), preferred_element_type=jnp.float32
    )


def dma(*shape):
    return pltpu.SemaphoreType.DMA(shape)


def line_dma():
    return dma(2, CHIPS, PIECES)


def in_vmem():
    return pl.BlockSpec(memory_space=pltpu.VMEM)


def in_hbm():
    return pl.BlockSpec(memory_space=pl.ANY)


def key_positions(places, key_pos, tok_rows):
    lanes = lax.broadcasted_iota(jnp.int32, (1, tok_rows), 1)
    for at_core in range(CORES):
        for at_chip in range(CHIPS):
            start = (at_core * CHIPS + at_chip) * tok_rows
            key_pos[:, start : start + tok_rows] = places[0, CORES * at_chip + at_core] * tok_rows + lanes


def kept_pairs(places, key_pos, block, core, tok_rows):
    down = lax.broadcasted_iota(jnp.int32, (tok_rows, 1), 0)
    return key_pos[...] <= places[0, CORES * block + core] * tok_rows + down


def attend_kernel(
    states, attn_src, mlp_src, qk_gain, places,
    to_states, to_qkv, to_out, w_up, w_gate, low_down, to_raw, to_query, to_both, to_att, to_inv, attx,
    states_all, w_qkv, w_out, raw_out, query_out, both, att_out, inv_out, src_q, stage_q, low_q, stage_o, low_o, stage_m, low_m, raw, att_low, key_pos,
    local_sem, keep_sem, att_sem, x_send, x_recv, q_send, q_recv, mt_send, mt_recv, wz_send, wz_recv,
    ws_send, ws_recv, wt_send, wt_recv, oz_send, oz_recv, os_send, os_recv, m_send, m_recv,
    ms_send, ms_recv, kv_send, kv_recv, a_send, a_recv,
):
    seq, chip, core = place_of()
    rows = attn_src.shape[0]
    tok_rows, model_width = states.shape
    heads = qk_gain.shape[0]
    head_cols = heads * HEAD_DIM
    part_cols = head_cols // CORES
    group_rows = tok_rows * CHIPS
    chip_rows = CORES * rows
    seq_rows = CHIPS * chip_rows
    half_units = w_up.shape[1]
    half_width = model_width // CORES
    ff_width = mlp_src.shape[1] // 3
    low = jnp.bfloat16
    for at in range(CHIPS):
        for half in range(CORES):
            for which in range(3):
                start = which * model_width + at * head_cols + half * part_cols
                src_q[at, half, :, which * part_cols : (which + 1) * part_cols] = attn_src[:, start : start + part_cols]
    meet()
    block = rows_at(chip, tok_rows)
    mine = rows_at(core, rows)
    half_at = pl.ds(pl.multiple_of(3 * model_width + core * half_width, 128), half_width)
    other_at = pl.ds(pl.multiple_of(3 * model_width + (1 - core) * half_width, 128), half_width)
    swap_o = begin(remote(attn_src.at[:, other_at], stage_o.at[mine], q_send.at[1], q_recv.at[1], twin()))
    swap_q = begin(remote(src_q.at[:, 1 - core], stage_q.at[:, mine], q_send.at[0], q_recv.at[0], twin()))
    stage_o[mine, :] = attn_src[:, half_at]
    stage_q[:, mine, :] = src_q[:, core]
    m_swaps, m_keeps = [], []
    for part in range(3):
        for at in range(CHIPS):
            start = part * ff_width + at * CORES * half_units
            theirs = pl.ds(pl.multiple_of(start + (1 - core) * half_units, 128), half_units)
            ours = pl.ds(pl.multiple_of(start + core * half_units, 128), half_units)
            there = stage_m.at[part, at, mine]
            m_swaps.append(begin(remote(mlp_src.at[:, theirs], there, mt_send.at[part, at], mt_recv.at[part, at], twin())))
            m_keeps.append(begin(pltpu.make_async_copy(mlp_src.at[:, ours], there, local_sem.at[part * CHIPS + at])))
    my_rows = rows_at(seq * CHIPS + chip, chip_rows)
    seq_at = rows_at(seq, seq_rows)
    swap_o.wait()
    low_o[...] = stage_o[...].astype(low)
    o_line = to_line(low_o, w_out.at[core, my_rows], oz_send, oz_recv)
    w_out[core, my_rows, :] = low_o[...]
    swap_q.wait()
    low_q[...] = stage_q[...].astype(low)
    line = []
    for step in STEPS:
        device, other = chip_peer(step)
        line.append(begin(remote(low_q.at[other], w_qkv.at[core, my_rows], wz_send.at[step], wz_recv.at[step], device)))
    w_qkv[core, my_rows, :] = low_q[chip]
    states_all[block, :] = states[...]
    key_positions(places, key_pos, tok_rows)
    gather_start(states, states_all, tok_rows, x_send, x_recv)
    for copy in line:
        copy.wait_recv()

    def across(whole, send, recv):
        return spread_start(whole.at[seq_at], whole, seq_rows, send, recv)

    q_across = across(w_qkv.at[core], ws_send, ws_recv)
    for copy in m_keeps:
        copy.wait()
    for copy in m_swaps:
        copy.wait()
    low_m[...] = stage_m[:2].astype(low)
    low_down[...] = stage_m[2].astype(low)
    gather_hop(states_all, tok_rows, 1, x_send, x_recv)
    more = spread_relay(w_qkv.at[core], seq_rows, ws_send, ws_recv)
    for copy in o_line:
        copy.wait_recv()
    o_across = across(w_out.at[core], os_send, os_recv)
    for copy in more:
        copy.wait_recv()
    q_across += more
    swap = begin(remote(w_qkv.at[core], w_qkv.at[core], wt_send.at[0], wt_recv.at[0], twin()))
    gather_hop(states_all, tok_rows, 2, x_send, x_recv)
    o_more = spread_relay(w_out.at[core], seq_rows, os_send, os_recv)
    gather_hop(states_all, tok_rows, 3, x_send, x_recv)
    here = rows_at(chip, chip_rows)

    def to_chips(part, there):
        return [
            begin(remote(low_m.at[part, chip_peer(step)[1]], there, m_send.at[part, step], m_recv.at[part, step], chip_peer(step)[0]))
            for step in STEPS
        ]

    m_line = to_chips(0, w_up.at[my_rows])
    w_up[my_rows, :] = low_m[0, chip]
    w_gate[here, :] = low_m[1, chip]
    swap.wait()
    kept = []

    def keep(src, dst):
        kept.append(begin(pltpu.make_async_copy(src, dst, keep_sem.at[len(kept)])))

    keep(states_all, to_states)
    keep(w_qkv, to_qkv)
    for half in range(CORES):
        value = dot(states_all[...], w_qkv[half])
        for which in range(3):
            start = which * head_cols + half * part_cols
            raw[:, start : start + part_cols] = value[:, which * part_cols : (which + 1) * part_cols]
    for head in reversed(range(3 * heads)):
        which, head = head // heads, head % heads
        start = which * head_cols + head * HEAD_DIM
        value = raw[:, start : start + HEAD_DIM]
        if which == 2:
            both[core, 1, head] = value.astype(low)
            continue
        factor = lax.rsqrt(jnp.sum(value * value, axis=-1, keepdims=True) + EPSILON)
        scaled = (value * factor * qk_gain[head]).astype(low)
        raw_out[which, head] = value
        if which == 1:
            both[core, 0, head] = scaled
            if head == 0:
                swap = begin(remote(both.at[core], both.at[core], kv_send.at[0], kv_recv.at[0], twin()))
        else:
            query_out[head] = scaled * math.sqrt(HEAD_DIM)
    keep(raw_out, to_raw)
    keep(query_out, to_query)
    for copy in m_line + o_more:
        copy.wait_recv()
    m_line += to_chips(1, w_gate.at[here])
    swap_o = begin(remote(w_out.at[core], w_out.at[core], wt_send.at[1], wt_recv.at[1], twin()))
    up_across = across(w_up, ms_send, ms_recv)
    swap.wait()
    keep(both, to_both)

    def one_block(index, carry):
        step = lax.rem(index + 1, CHIPS)
        device, other = chip_peer(step)
        at = rows_at(other, tok_rows)
        allowed = kept_pairs(places, key_pos, other, core, tok_rows)

        def one_head(head, carry):
            query = query_out[head, at, :]
            scores = jnp.concatenate([dot_nt(query, both[half, 0, head]) for half in range(CORES)], axis=1)
            powered = jnp.exp(jnp.where(allowed, scores, NEG_LARGE))
            inverse = 1.0 / jnp.sum(powered, axis=-1, keepdims=True)
            weights = (powered * inverse).astype(low)
            att_out[head, at, :] = sum(
                dot(weights[:, half * group_rows : (half + 1) * group_rows], both[half, 1, head])
                for half in range(CORES)
            )
            inv_out[head, at, :] = inverse
            return carry

        lax.fori_loop(0, heads, one_head, 0)
        for head in range(heads):
            att_low[at, head * HEAD_DIM : (head + 1) * HEAD_DIM] = att_out[head, at, :].astype(low)
        when(step != 0, remote(att_low.at[at], attx.at[chip], a_send.at[step], a_recv.at[step], device).start)
        pltpu.make_async_copy(att_out.at[:, at], to_att.at[:, at], att_sem.at[0, step]).start()
        pltpu.make_async_copy(inv_out.at[:, at], to_inv.at[:, at], att_sem.at[1, step]).start()
        return carry

    lax.fori_loop(0, CHIPS, one_block, 0)
    attx[chip] = att_low[block, :]
    swap_o.wait()
    keep(w_out, to_out)
    up_more = spread_relay(w_up, seq_rows, ms_send, ms_recv)
    for step in STEPS:
        remote(att_low.at[block], attx.at[chip], a_send.at[step], a_recv.at[step], chip_peer(step)[0]).wait()
    for copy in m_line[3:] + up_more:
        copy.wait_recv()
    gather_drain(states_all, tok_rows, x_send, x_recv)
    for step in range(CHIPS):
        pltpu.make_async_copy(att_out.at[:, block], to_att.at[:, block], att_sem.at[0, step]).wait()
        pltpu.make_async_copy(inv_out.at[:, block], to_inv.at[:, block], att_sem.at[1, step]).wait()
    for copy in kept:
        copy.wait()
    for copy in m_line + line + o_line + q_across + o_across + o_more + up_across + up_more:
        copy.wait_send()


def in_smem():
    return pl.BlockSpec(memory_space=pltpu.SMEM)


def attend_call(states, attn_src, mlp_src, qk_gain, places):
    tok_rows, model_width = states.shape
    rows = attn_src.shape[0]
    heads = qk_gain.shape[0]
    chips, chip_rows = CHIPS, CORES * rows
    group_rows = chips * tok_rows
    half_units = mlp_src.shape[1] // 3 // chips // CORES
    half_width, half_cols = model_width // CORES, 3 * heads * HEAD_DIM // CORES
    f32, low = jnp.float32, jnp.bfloat16
    shape = jax.ShapeDtypeStruct
    return pl.pallas_call(
        attend_kernel,
        out_shape=[
            shape((group_rows, model_width), low),
            shape((CORES, model_width, half_cols), low),
            shape((CORES, model_width, half_width), low),
            shape((model_width, half_units), low),
            shape((chips * chip_rows, half_units), low),
            shape((chips, chip_rows, half_units), low),
            shape((2, heads, group_rows, HEAD_DIM), f32),
            shape((heads, group_rows, HEAD_DIM), low),
            shape((CORES, 2, heads, group_rows, HEAD_DIM), low),
            shape((heads, group_rows, HEAD_DIM), f32),
            shape((heads, group_rows, 1), f32),
            shape((chips, tok_rows, heads * HEAD_DIM), low),
        ],
        in_specs=[in_vmem(), in_vmem(), in_hbm(), in_vmem(), in_smem()],
        out_specs=[in_hbm()] * 3 + [in_vmem()] * 3 + [in_hbm()] * 5 + [in_vmem()],
        scratch_shapes=[
            VMEM((group_rows, model_width), low),
            VMEM((CORES, model_width, half_cols), low),
            VMEM((CORES, model_width, half_width), low),
            VMEM((2, heads, group_rows, HEAD_DIM), f32),
            VMEM((heads, group_rows, HEAD_DIM), low),
            VMEM((CORES, 2, heads, group_rows, HEAD_DIM), low),
            VMEM((heads, group_rows, HEAD_DIM), f32),
            VMEM((heads, group_rows, 1), f32),
            VMEM((chips, CORES, rows, half_cols), f32),
            VMEM((chips, chip_rows, half_cols), f32),
            VMEM((chips, chip_rows, half_cols), low),
            VMEM((chip_rows, half_width), f32),
            VMEM((chip_rows, half_width), low),
            VMEM((3, chips, chip_rows, half_units), f32),
            VMEM((2, chips, chip_rows, half_units), low),
            VMEM((group_rows, 3 * heads * HEAD_DIM), f32),
            VMEM((group_rows, heads * HEAD_DIM), low),
            VMEM((1, CORES * group_rows), jnp.int32),
            dma(12), dma(6), dma(2, 4), line_dma(), line_dma(), dma(2), dma(2), dma(3, 4), dma(3, 4), dma(4), dma(4),
            dma(4), dma(4), dma(2), dma(2), dma(4), dma(4), dma(4), dma(4), dma(2, 4), dma(2, 4),
            dma(4), dma(4), dma(1), dma(1), dma(4), dma(4),
        ],
        compiler_params=pltpu.CompilerParams(
            collective_id=1, has_side_effects=True, vmem_limit_bytes=LIMIT
        ),
        name="attend",
    )(states, attn_src, mlp_src, qk_gain, places)


def unit_of(value):
    factor = lax.rsqrt(jnp.sum(value * value, axis=-1, keepdims=True) + EPSILON)
    return value * factor, factor


def mlp_kernel(
    attx, states, cotangent, from_out, alpha_attn, alpha_mlp, gain_u, gain_v, w_up, w_gate, low_down,
    out, grad_attx, grad_w_out, grad_direct, small, to_half, grad_down,
    w_out, grad_half, weights, mixed_one, attn_unit, factors, mixed_low, mixed_all, up, gate, hidden, part,
    sums, via, passed, total, grad_two, branch_low, branch_all, grad_u, grad_v, wide, turned, arrived,
    w_down, down_half, down_got, dot_u, dot_v,
    local_sem, ws_send, ws_recv, wt_send, wt_recv, x_send, x_recv, r_send, r_recv,
    g_send, g_recv, b_send, b_recv, d_send, d_recv, wz_send, wz_recv, ds_send, ds_recv,
):
    seq, chip, core = place_of()
    tok_rows, model_width = states.shape
    chip_heads = attx.shape[2]
    seq_rows, half_units = w_gate.shape
    chip_rows = low_down.shape[1]
    half_width = w_out.shape[2]
    group_rows = CHIPS * tok_rows
    block = rows_at(chip, tok_rows)
    load = begin(pltpu.make_async_copy(from_out, w_out, local_sem.at[2]))
    meet()
    seq_at = rows_at(seq, seq_rows)
    here = rows_at(chip, chip_rows)
    swaps = [begin(remote(w_up, weights.at[0, core], wt_send.at[0], wt_recv.at[0], twin()))]
    to_chips = [
        begin(remote(low_down.at[chip_peer(step)[1]], w_down.at[here], wz_send.at[step], wz_recv.at[step], chip_peer(step)[0]))
        for step in STEPS
    ]

    across = spread_start(w_gate, weights.at[1, core], seq_rows, ws_send.at[1], ws_recv.at[1])
    keeps = [
        begin(pltpu.make_async_copy(w_up, weights.at[0, core], local_sem.at[0])),
        begin(pltpu.make_async_copy(w_gate, weights.at[1, core, seq_at], local_sem.at[1])),
    ]
    w_down[here, :] = low_down[chip]
    load.wait()
    part_at = [slice(at * chip_heads, (at + 1) * chip_heads) for at in range(CHIPS)]
    half_at = [slice(half * half_width, (half + 1) * half_width) for half in range(CORES)]
    branch = jnp.concatenate(
        [sum(dot(attx[at], w_out[half, part_at[at], :]) for at in range(CHIPS)) for half in range(CORES)],
        axis=1,
    )
    unit, factor = unit_of(branch)
    attn_unit[...] = unit
    factors[0] = factor
    base = states[...].astype(jnp.float32)
    value, factor = unit_of(base + alpha_attn[...] * (unit - base))
    mixed_one[...] = value
    factors[1] = factor
    mixed_low[...] = value.astype(jnp.bfloat16)
    gather_start(mixed_low, mixed_all, tok_rows, x_send, x_recv)
    mixed_all[block, :] = mixed_low[...]
    for copy in keeps:
        copy.wait()
    for copy in to_chips:
        copy.wait_recv()
    more = spread_relay(weights.at[1, core], seq_rows, ws_send.at[1], ws_recv.at[1])
    across += spread_start(w_down, weights.at[2, core], seq_rows, ws_send.at[2], ws_recv.at[2])
    weights[2, core, seq_at, :] = w_down[...]
    gather_hop(mixed_all, tok_rows, 1, x_send, x_recv)
    for copy in more:
        copy.wait_recv()
    swaps.append(begin(remote(weights.at[1, core], weights.at[1, core], wt_send.at[1], wt_recv.at[1], twin())))
    slab = min(64, group_rows)
    slabs = group_rows // slab
    half_slabs = slabs // 2
    half_rows = group_rows // 2
    mine = chip // 2

    def forward(group):
        rows = rows_at(group, half_rows)
        for half in range(CORES):
            up[half, rows, :] = dot(mixed_all[rows, :], weights[0, half])
            gate[half, rows, :] = dot(mixed_all[rows, :], weights[1, half])

        def activate(index, carry):
            half = index // half_slabs
            at = rows_at(group * half_slabs + lax.rem(index, half_slabs), slab)
            gated = gate[half, at, :] * gain_v[half]
            scaled = up[half, at, :] * gain_u[half]
            hidden[half, at, :] = (gated * jax.nn.sigmoid(gated) * scaled).astype(jnp.bfloat16)
            return carry

        lax.fori_loop(0, CORES * half_slabs, activate, 0)

    for copy in swaps:
        copy.wait_recv()
    forward(mine)
    gather_hop(mixed_all, tok_rows, 2, x_send, x_recv)
    down_more = spread_relay(weights.at[2, core], seq_rows, ws_send.at[2], ws_recv.at[2])
    gather_hop(mixed_all, tok_rows, 3, x_send, x_recv)
    forward(1 - mine)
    for copy in down_more:
        copy.wait_recv()
    swap = begin(remote(weights.at[2, core], weights.at[2, core], wt_send.at[2], wt_recv.at[2], twin()))
    swaps.append(swap)
    swap.wait_recv()
    tile = model_width // 5

    def down(index, carry):
        at = rows_at(index, tile)
        part[0, :, at] = sum(dot_nt(hidden[half], weights[2, half, at, :]) for half in range(CORES)).astype(jnp.bfloat16)
        return carry

    lax.fori_loop(0, model_width // tile, down, 0)

    reduce_start(part.at[0], tok_rows, sums.at[0], via.at[0], r_send, r_recv)
    reduce_relay(part.at[0], tok_rows, sums.at[0], via.at[0], passed.at[0], r_send, r_recv)
    reduce_wait(part.at[0], tok_rows, sums.at[0], total, r_send, r_recv)
    mlp_unit, mlp_factor = unit_of(total[...])
    value, factor = unit_of(mixed_one[...] + alpha_mlp[...] * (mlp_unit - mixed_one[...]))
    out[...] = value.astype(jnp.bfloat16)
    above = cotangent[...].astype(jnp.float32)
    grad = factor * (above - value * jnp.sum(above * value, axis=-1, keepdims=True))
    grad_two[...] = grad
    small[...] = jnp.zeros_like(small)
    small[1:2, :] = jnp.sum(grad * (mlp_unit - mixed_one[...]), axis=0, keepdims=True)
    grad = grad * alpha_mlp[...]
    grad = mlp_factor * (grad - mlp_unit * jnp.sum(grad * mlp_unit, axis=-1, keepdims=True))
    branch_low[...] = grad.astype(jnp.bfloat16)
    gather_start(branch_low, branch_all, tok_rows, g_send, g_recv)
    branch_all[block, :] = branch_low[...]
    gather_hop(branch_all, tok_rows, 1, g_send, g_recv)
    gather_hop(branch_all, tok_rows, 2, g_send, g_recv)
    turned[0] = mixed_all[...].T
    gather_hop(branch_all, tok_rows, 3, g_send, g_recv)
    for half in range(CORES):
        wide[half] = dot(branch_all[...], weights[2, half])
    dot_u[...] = jnp.zeros_like(dot_u)
    dot_v[...] = jnp.zeros_like(dot_v)

    def deactivate(index, carry):
        half = index // slabs
        at = rows_at(lax.rem(index, slabs), slab)
        gated = gate[half, at, :] * gain_v[half]
        scaled = up[half, at, :] * gain_u[half]
        upstream = wide[half, at, :]
        sig = jax.nn.sigmoid(gated)
        to_up = upstream * (gated * sig)
        to_gate = upstream * scaled * sig * (1.0 + gated * (1.0 - sig))
        dot_u[half] += jnp.sum(to_up * up[half, at, :], axis=0, keepdims=True)
        dot_v[half] += jnp.sum(to_gate * gate[half, at, :], axis=0, keepdims=True)
        grad_u[half, at, :] = (to_up * gain_u[half]).astype(jnp.bfloat16)
        grad_v[half, at, :] = (to_gate * gain_v[half]).astype(jnp.bfloat16)
        return carry

    lax.fori_loop(0, CORES * slabs, deactivate, 0)

    def back_down(index, carry):
        at = rows_at(index, tile)
        part[1, :, at] = sum(
            dot_nt(grad_u[half], weights[0, half, at, :]) + dot_nt(grad_v[half], weights[1, half, at, :])
            for half in range(CORES)
        ).astype(jnp.bfloat16)
        return carry

    lax.fori_loop(0, model_width // tile, back_down, 0)
    for copy in swaps + more + down_more:
        copy.wait_send()
    reduce_start(part.at[1], tok_rows, sums.at[1], via.at[1], b_send, b_recv, False)
    turned[1] = branch_all[...].T
    swaps = {}

    def weight_grads(which, left, right):
        def one(index, carry):
            half = index // 5
            at = rows_at(lax.rem(index, 5), tile)
            weights[which, half, at, :] = dot(turned[left, at, :], right[half]).astype(jnp.bfloat16)
            return carry

        lax.fori_loop(0, CORES * 5, one, 0)
        swaps[which] = begin(remote(weights.at[which, 1 - core], arrived.at[which], d_send.at[which], d_recv.at[which], twin()))

    def both_cores(which):
        swaps[which].wait_recv()
        return (weights[which, core].astype(jnp.float32) + arrived[which].astype(jnp.float32)).astype(jnp.bfloat16)

    weight_grads(2, 1, hidden)
    reduce_relay(part.at[1], tok_rows, sums.at[1], via.at[1], passed.at[1], b_send, b_recv)
    weight_grads(0, 0, grad_u)
    down_half[...] = both_cores(2)
    down_across = [
        begin(remote(down_half.at[rows_at(seq_peer(step)[1], seq_rows)], down_got.at[step - 1], ds_send.at[step], ds_recv.at[step], seq_peer(step)[0]))
        for step in STEPS
    ]
    weight_grads(1, 0, grad_v)
    kept = []
    for which in range(2):
        grad_half[which] = both_cores(which)
        kept.append(begin(pltpu.make_async_copy(grad_half.at[which], to_half.at[which], local_sem.at[which])))
    reduce_wait(part.at[1], tok_rows, sums.at[1], total, b_send, b_recv)
    grad = grad_two[...] * (1.0 - alpha_mlp[...]) + total[...]
    value = mixed_one[...]
    grad = factors[1] * (grad - value * jnp.sum(grad * value, axis=-1, keepdims=True))
    unit = attn_unit[...]
    small[0:1, :] = jnp.sum(grad * (unit - states[...].astype(jnp.float32)), axis=0, keepdims=True)
    grad_direct[...] = grad * (1.0 - alpha_attn[...])
    grad = grad * alpha_attn[...]
    grad = factors[0] * (grad - unit * jnp.sum(grad * unit, axis=-1, keepdims=True))
    low = grad.astype(jnp.bfloat16)
    for at in range(CHIPS):
        grad_attx[at] = sum(
            dot_nt(low[:, half_at[half]], w_out[half, part_at[at], :]) for half in range(CORES)
        ).astype(jnp.bfloat16)
        for half in range(CORES):
            grad_w_out[half, at] = dot_tn(attx[at], low[:, half_at[half]]).astype(jnp.bfloat16)
    for half in range(CORES):
        unit_at = slice(half * half_units, (half + 1) * half_units)
        small[2:3, unit_at] = dot_u[half]
        small[3:4, unit_at] = dot_v[half] * math.sqrt(D)
    whole = down_half[seq_at, :].astype(jnp.float32)
    for step in STEPS:
        down_across[step - 1].wait_recv()
        whole = whole + down_got[step - 1].astype(jnp.float32)
    grad_down[...] = whole.astype(jnp.bfloat16)
    for copy in kept:
        copy.wait()
    gather_drain(mixed_all, tok_rows, x_send, x_recv)
    gather_drain(branch_all, tok_rows, g_send, g_recv)
    reduce_drain(part.at[0], tok_rows, sums.at[0], r_send, r_recv)
    reduce_drain(part.at[1], tok_rows, sums.at[1], b_send, b_recv, False)
    for copy in across + to_chips + down_across + [swaps[which] for which in range(3)]:
        copy.wait_send()


def mlp_call(attx, states, cotangent, w_out, alpha_attn, alpha_mlp, gain_u, gain_v, w_up, w_gate, low_down):
    tok_rows, model_width = states.shape
    chips, _, chip_heads = attx.shape
    seq_rows, half_units = w_gate.shape
    group_rows = chips * tok_rows
    f32, low = jnp.float32, jnp.bfloat16
    shape = jax.ShapeDtypeStruct
    tokens, group = (tok_rows, model_width), (group_rows, model_width)
    wide = (CORES, group_rows, half_units)
    matrix = (model_width, half_units)
    return pl.pallas_call(
        mlp_kernel,
        out_shape=[
            shape(tokens, low),
            shape(attx.shape, low),
            shape((CORES, chips, chip_heads, model_width // CORES), low),
            shape(tokens, f32),
            shape((8, max(model_width, CORES * half_units)), f32),
            shape((2,) + matrix, low),
            shape((seq_rows, half_units), low),
        ],
        in_specs=[in_vmem()] * 3 + [in_hbm()] + [in_vmem()] * 4 + [in_hbm(), in_vmem(), in_vmem()],
        out_specs=[in_vmem()] * 5 + [in_hbm(), in_vmem()],
        scratch_shapes=[
            VMEM(w_out.shape, low),
            VMEM((2,) + matrix, low),
            VMEM((3, CORES) + matrix, low),
            VMEM(tokens, f32),
            VMEM(tokens, f32),
            VMEM((2, tok_rows, 1), f32),
            VMEM(tokens, low),
            VMEM(group, low),
            VMEM(wide, f32),
            VMEM(wide, f32),
            VMEM(wide, low),
            VMEM((2,) + group, low),
            VMEM((2, 3) + tokens, low),
            VMEM((2,) + tokens, low),
            VMEM((2,) + tokens, low),
            VMEM(tokens, f32),
            VMEM(tokens, f32),
            VMEM(tokens, low),
            VMEM(group, low),
            VMEM(wide, low),
            VMEM(wide, low),
            VMEM(wide, f32),
            VMEM((2, model_width, group_rows), low),
            VMEM((3,) + matrix, low),
            VMEM((seq_rows, half_units), low),
            VMEM(matrix, low),
            VMEM((3, seq_rows, half_units), low),
            VMEM((CORES, 1, half_units), f32),
            VMEM((CORES, 1, half_units), f32),
            dma(3), dma(3, 4), dma(3, 4), dma(3), dma(3), line_dma(), line_dma(), dma(4), dma(4),
            line_dma(), line_dma(), dma(4), dma(4), dma(3), dma(3), dma(4), dma(4), dma(4), dma(4),
        ],
        compiler_params=pltpu.CompilerParams(
            collective_id=2, has_side_effects=True, vmem_limit_bytes=LIMIT
        ),
        name="mlp",
    )(
        attx, states, cotangent, w_out, alpha_attn, alpha_mlp, gain_u, gain_v, w_up, w_gate, low_down
    )


def back_kernel(
    grad_attx, from_half, grad_down, from_grad_out, small_in, from_raw, from_query, from_both, from_att,
    from_inv, from_states, from_qkv, qk_gain, places, grad_direct,
    grad_states, out_mlp, out_attn, feature, unit,
    grad_half, grad_w_out, raw, query, both, att, inverse, states_all, w_qkv, att_low, heads_low, to_keys, swap_low, swap_kv, grad_heads, grad_sides, part, sums, via, passed, total, turned,
    grad_q, half_q, seq_q, line_q, wide_q, half_o, pair_o, seq_got, seq_held, seq_last, seq_low, q_got, q_held, q_last, line_got, wide,
    wide_o, small, small_pair, small_seq, dots, small_all, flat_q, sides_q, key_pos,
    local_sem, load_sem, a_send, a_recv, s_send, s_recv, o_send, o_recv, kv_send, kv_recv, r_send, r_recv,
    qt_send, qt_recv, qs_send, qs_recv, qz_send, qz_recv, z_send, z_recv, f_send, f_recv,
    p_send, p_recv, t_send, t_recv,
):
    seq, chip, core = place_of()
    tok_rows, model_width = grad_direct.shape
    heads = qk_gain.shape[0]
    head_cols = heads * HEAD_DIM
    group_rows = CHIPS * tok_rows
    half_units = grad_half.shape[2]
    seq_rows = seq_low.shape[1]
    chip_rows = seq_rows // CHIPS
    rows = chip_rows // CORES
    part_cols = head_cols // CORES
    ff_width = out_mlp.shape[1] // 3
    scale = math.sqrt(HEAD_DIM)
    block = rows_at(chip, tok_rows)
    f32, low = jnp.float32, jnp.bfloat16
    loads = [
        begin(pltpu.make_async_copy(src, dst, load_sem.at[at]))
        for at, (src, dst) in enumerate(
            (
                (from_query, query), (from_both, both), (from_inv, inverse), (from_att, att), (from_raw, raw),
                (from_grad_out, grad_w_out), (from_states, states_all), (from_half, grad_half), (from_qkv, w_qkv),
            )
        )
    ]
    meet()
    waits = []
    line = []
    for step in STEPS:
        device, other = chip_peer(step)
        line.append(begin(remote(grad_attx.at[other], att_low.at[block], a_send.at[step], a_recv.at[step], device)))
    att_low[block, :] = grad_attx[chip]
    key_positions(places, key_pos, tok_rows)
    pair = begin(remote(from_grad_out.at[1 - core], pair_o, o_send.at[0], o_recv.at[0], twin()))
    onward = {}

    def to_chips(which, src):
        onward[which] = [
            begin(remote(src.at[rows_at(chip_peer(step)[1], chip_rows)], line_got.at[which, chip], z_send.at[which, step], z_recv.at[which, step], chip_peer(step)[0]))
            for step in STEPS
        ]
        line_got[which, chip] = src[rows_at(chip, chip_rows), :]

    to_chips(2, grad_down)

    def cross(which, src):
        return fold_start(src, seq_got.at[which], seq_rows, s_send.at[which], s_recv.at[which])

    def cross_on(which, src, copies):
        return fold_relay(src, seq_got.at[which], seq_held.at[which], seq_last.at[which], seq_rows, copies, s_send.at[which], s_recv.at[which])

    def cross_end(which, src, copies, more):
        fold_end(src, seq_got.at[which], seq_last.at[which], seq_low.at[which], seq_rows, copies, more)

    crossing = [cross(0, from_half.at[0])]
    to_keys[...] = jnp.zeros_like(to_keys)
    dots[...] = jnp.zeros_like(dots)
    for copy in loads:
        copy.wait()
    turned[...] = states_all[...].T
    sources = (grad_half.at[0], grad_half.at[1], half_o)
    onwards = [cross_on(0, sources[0], crossing[0])]
    crossing.append(cross(1, from_half.at[1]))
    pair.wait_recv()
    for at in range(4):
        half_o[at * seq_rows : (at + 1) * seq_rows, :] = (
            grad_w_out[core, at].astype(f32) + pair_o[at].astype(f32)
        ).astype(low)
    tile = tok_rows
    tiles = CHIPS

    def raw_back(which, head, at, upstream):
        value = raw[which, head, at, :]
        unit, factor = unit_of(value)
        dots[head] += jnp.sum(upstream * unit, axis=0, keepdims=True)
        upstream = upstream * qk_gain[head]
        upstream = factor * (upstream - unit * jnp.sum(upstream * unit, axis=-1, keepdims=True))
        grad_heads[which, head, at, :] = upstream.astype(low)

    def one_block(step, carry):
        other = lax.rem(chip + CHIPS - step, CHIPS)
        at = rows_at(other, tok_rows)
        copy = remote(grad_attx.at[0], att_low.at[at], a_send.at[step], a_recv.at[step], device_on(other))
        if step > 0:
            copy.wait_recv()
        for head in range(heads):
            heads_low[head, at, :] = att_low[at, head * HEAD_DIM : (head + 1) * HEAD_DIM]
        allowed = kept_pairs(places, key_pos, other, core, tok_rows)

        def one_head(head, carry):
            rows_q = query[head, at, :]
            grad_att = heads_low[head, at, :]
            scores = jnp.concatenate([dot_nt(rows_q, both[half, 0, head]) for half in range(CORES)], axis=1)
            probs = jnp.exp(jnp.where(allowed, scores, NEG_LARGE)) * inverse[head, at, :]
            grad_prob = jnp.concatenate([dot_nt(grad_att, both[half, 1, head]) for half in range(CORES)], axis=1)
            row_dot = jnp.sum(grad_att.astype(f32) * att[head, at, :], axis=-1, keepdims=True)
            grad_scores = (probs * (grad_prob - row_dot)).astype(low)
            weights = probs.astype(low)
            to_query = jnp.zeros((tok_rows, HEAD_DIM), f32)
            for half in range(CORES):
                cols = slice(half * group_rows, (half + 1) * group_rows)
                to_query = to_query + dot(grad_scores[:, cols], both[half, 0, head])
                to_keys[half, 0, head] += dot_tn(grad_scores[:, cols], rows_q)
                to_keys[half, 1, head] += dot_tn(weights[:, cols], grad_att)
            raw_back(0, head, at, to_query * scale)
            return carry

        lax.fori_loop(0, heads, one_head, 0)
        return carry

    one_block(0, 0)
    cross_end(0, sources[0], crossing[0], onwards[0])
    to_chips(0, seq_low.at[0])
    one_block(1, 0)
    onwards.append(cross_on(1, sources[1], crossing[1]))
    crossing.append(cross(2, half_o))
    one_block(2, 0)
    one_block(3, 0)
    cross_end(1, sources[1], crossing[1], onwards[1])
    to_chips(1, seq_low.at[1])
    swap_low[...] = to_keys[1 - core].astype(low)
    swap = begin(remote(swap_low, swap_kv, kv_send.at[0], kv_recv.at[0], twin()))
    swap.wait()

    def one_key(index, carry):
        head = index // tiles
        at = rows_at(lax.rem(index, tiles), tile)
        mine = to_keys[core, 0, head, at, :] + swap_kv[0, head, at, :].astype(f32)
        raw_back(1, head, at, mine)
        value = to_keys[core, 1, head, at, :] + swap_kv[1, head, at, :].astype(f32)
        grad_heads[2, head, at, :] = value.astype(low)
        return carry

    lax.fori_loop(0, heads * tiles, one_key, 0)
    for which in range(3):
        full = jnp.concatenate([grad_heads[which, head] for head in range(heads)], axis=1)
        for half in range(CORES):
            grad_sides[half, :, which * part_cols : (which + 1) * part_cols] = full[:, half * part_cols : (half + 1) * part_cols]
    wide_tile = model_width // 5
    onwards.append(cross_on(2, half_o, crossing[2]))

    def down(index, carry):
        at = rows_at(index, wide_tile)
        part[:, at] = sum(dot_nt(grad_sides[half], w_qkv[half, at, :]) for half in range(CORES)).astype(low)
        return carry

    lax.fori_loop(0, 5, down, 0)
    reduce_start(part, tok_rows, sums, via, r_send, r_recv, False)

    def weight_grad(index, carry):
        half = index // 5
        at = rows_at(lax.rem(index, 5), wide_tile)
        grad_q[half, at, :] = dot(turned[at, :], grad_sides[half]).astype(low)
        return carry

    lax.fori_loop(0, CORES * 5, weight_grad, 0)
    swap_q = begin(remote(grad_q.at[1 - core], half_q, qt_send.at[0], qt_recv.at[0], twin()))
    swap_q.wait()
    half_q[...] = (grad_q[core].astype(f32) + half_q[...].astype(f32)).astype(low)
    crossing_q = fold_start(half_q, q_got, seq_rows, qs_send, qs_recv)
    cross_end(2, half_o, crossing[2], onwards[2])
    to_chips(3, seq_low.at[2])
    reduce_relay(part, tok_rows, sums, via, passed, r_send, r_recv)
    small[...] = small_in[...]
    small[4:5, :head_cols] = jnp.concatenate([dots[head] for head in range(heads)], axis=1)
    swap_s = begin(remote(small, small_pair, t_send.at[0], t_recv.at[0], twin()))
    more_q = fold_relay(half_q, q_got, q_held, q_last, seq_rows, crossing_q, qs_send, qs_recv)
    fold_end(half_q, q_got, q_last, seq_q, seq_rows, crossing_q, more_q)
    onward_q = []
    for step in STEPS:
        device, other = chip_peer(step)
        onward_q.append(begin(remote(seq_q.at[rows_at(other, chip_rows)], line_q.at[chip], qz_send.at[step], qz_recv.at[step], device)))
    line_q[chip] = seq_q[rows_at(chip, chip_rows), :]

    mine = rows_at(core, rows)
    theirs = rows_at(1 - core, rows)
    swap_s.wait()
    small[...] = small[...] + small_pair[...]
    spread_s = [
        begin(remote(small, small_seq.at[step - 1], t_send.at[step], t_recv.at[step], seq_peer(step)[0]))
        for step in STEPS
    ]
    last, lasts = [], []
    for which in (2, 0, 1):
        for copy in onward[which]:
            copy.wait_recv()
        for at in range(CHIPS):
            wide[which, at] = line_got[which, at].astype(f32)
            start = which * ff_width + at * CORES * half_units + core * half_units
            there = out_mlp.at[:, pl.ds(pl.multiple_of(start, 128), half_units)]
            last.append(begin(remote(wide.at[which, at, theirs], there, f_send.at[which, at], f_recv.at[which, at], twin())))
            lasts.append(begin(pltpu.make_async_copy(wide.at[which, at, mine], there, local_sem.at[3 + which * CHIPS + at])))
    for copy in spread_s:
        copy.wait()
    small_pair[...] = small[...] + small_seq[0] + small_seq[1] + small_seq[2]
    small_all[chip] = small_pair[...]
    ends = to_line(small_pair, small_all.at[chip], p_send, p_recv)
    for copy in onward[3]:
        copy.wait_recv()
    whole = line_got[3, 0].astype(f32)
    for at in range(1, CHIPS):
        whole = whole + line_got[3, at].astype(f32)
    wide_o[...] = whole
    start = 3 * model_width + core * half_units
    there = out_attn.at[:, pl.ds(pl.multiple_of(start, 128), half_units)]
    last.append(begin(remote(wide_o.at[theirs], there, f_send.at[3, 0], f_recv.at[3, 0], twin())))
    lasts.append(begin(pltpu.make_async_copy(wide_o.at[mine], there, local_sem.at[15])))
    for copy in onward_q:
        copy.wait_recv()
    wide_q[...] = line_q[...].astype(f32)
    sides_q[core] = wide_q[:, mine, :]
    swap_q = begin(remote(wide_q.at[:, theirs], sides_q.at[core], f_send.at[3, 1], f_recv.at[3, 1], twin()))
    for copy in ends:
        copy.wait()
    alphas = small_all[0] + small_all[1] + small_all[2] + small_all[3]
    feature[1:3, :] = alphas[0:2, :]
    for at in range(CHIPS):
        feature[0:1, at * head_cols : (at + 1) * head_cols] = small_all[at, 4:5, :head_cols]
        width = CORES * half_units
        unit[:, at * width : (at + 1) * width] = small_all[at, 2:4, :width]
    swap_q.wait()
    for at in range(CHIPS):
        for half in range(CORES):
            for which in range(3):
                start = which * model_width + at * head_cols + half * part_cols
                flat_q[:, start : start + part_cols] = sides_q[half, at, :, which * part_cols : (which + 1) * part_cols]
    lasts.append(begin(pltpu.make_async_copy(flat_q, out_attn.at[:, pl.ds(0, 3 * model_width)], local_sem.at[16])))
    reduce_wait(part, tok_rows, sums, total, r_send, r_recv)
    grad_states[...] = (total[...] + grad_direct[...]).astype(low)
    for copy in last + lasts:
        copy.wait()
    reduce_drain(part, tok_rows, sums, r_send, r_recv, False)
    for copy in line + [pair] + sum(crossing + onwards + list(onward.values()), crossing_q + more_q + onward_q):
        copy.wait_send()


def back_call(
    grad_attx, grad_half, grad_down, grad_w_out, small_in, raw, query, both, att, inverse, states_all,
    w_qkv, qk_gain, places, grad_direct, rows,
):
    tok_rows, model_width = grad_direct.shape
    chips = grad_attx.shape[0]
    heads = qk_gain.shape[0]
    head_cols = heads * HEAD_DIM
    group_rows = chips * tok_rows
    half_units = grad_half.shape[2]
    half_cols = w_qkv.shape[2]
    chip_rows = CORES * rows
    seq_rows = chips * chip_rows
    f32, low = jnp.float32, jnp.bfloat16
    shape = jax.ShapeDtypeStruct
    per_head = (heads, group_rows, HEAD_DIM)
    return pl.pallas_call(
        back_kernel,
        out_shape=[
            shape((tok_rows, model_width), low),
            shape((rows, 3 * chips * CORES * half_units), f32),
            shape((rows, 4 * model_width), f32),
            shape((3, model_width), f32),
            shape((2, chips * CORES * half_units), f32),
        ],
        in_specs=[in_vmem(), in_hbm(), in_vmem(), in_hbm(), in_vmem()] + [in_hbm()] * 7 + [in_vmem(), in_smem(), in_vmem()],
        out_specs=[in_vmem(), in_hbm(), in_hbm(), in_vmem(), in_vmem()],
        scratch_shapes=[
            *(VMEM(value.shape, value.dtype) for value in (grad_half, grad_w_out, raw, query, both, att, inverse, states_all, w_qkv)),
            VMEM((group_rows, head_cols), low),
            VMEM(per_head, low),
            VMEM((CORES, 2) + per_head, f32),
            VMEM((2,) + per_head, low),
            VMEM((2,) + per_head, low),
            VMEM((3,) + per_head, low),
            VMEM((CORES, group_rows, half_cols), low),
            VMEM((group_rows, model_width), low),
            VMEM((3, tok_rows, model_width), low),
            VMEM((tok_rows, model_width), low),
            VMEM((tok_rows, model_width), low),
            VMEM((tok_rows, model_width), f32),
            VMEM((model_width, group_rows), low),
            VMEM((CORES, model_width, half_cols), low),
            VMEM((model_width, half_cols), low),
            VMEM((seq_rows, half_cols), low),
            VMEM((chips, chip_rows, half_cols), low),
            VMEM((chips, chip_rows, half_cols), f32),
            VMEM((4 * seq_rows, half_units), low),
            VMEM((4, seq_rows, half_units), low),
            VMEM((3, 2, 2, seq_rows // 2, half_units), low),
            VMEM((3, 2, seq_rows // 2, half_units), low),
            VMEM((3, 2, seq_rows // 2, half_units), low),
            VMEM((3, seq_rows, half_units), low),
            VMEM((2, 2, seq_rows // 2, half_cols), low),
            VMEM((2, seq_rows // 2, half_cols), low),
            VMEM((2, seq_rows // 2, half_cols), low),
            VMEM((4, chips, chip_rows, half_units), low),
            VMEM((3, chips, chip_rows, half_units), f32),
            VMEM((chip_rows, half_units), f32),
            VMEM(small_in.shape, f32),
            VMEM(small_in.shape, f32),
            VMEM((3,) + small_in.shape, f32),
            VMEM((heads, 1, HEAD_DIM), f32),
            VMEM((chips,) + small_in.shape, f32),
            VMEM((rows, 3 * model_width), f32),
            VMEM((CORES, chips, rows, half_cols), f32),
            VMEM((1, CORES * group_rows), jnp.int32),
            dma(17), dma(9), dma(4), dma(4), dma(3, 3, 2), dma(3, 3, 2), dma(1), dma(1), dma(1), dma(1),
            dma(4), dma(4), dma(1), dma(1), dma(3, 2), dma(3, 2), dma(4), dma(4), dma(4, 4), dma(4, 4),
            dma(4, 4), dma(4, 4), dma(4), dma(4), dma(4), dma(4),
        ],
        compiler_params=pltpu.CompilerParams(
            collective_id=3, has_side_effects=True, vmem_limit_bytes=LIMIT
        ),
        name="back",
    )(
        grad_attx, grad_half, grad_down, grad_w_out, small_in, raw, query, both, att, inverse, states_all,
        w_qkv, qk_gain, places, grad_direct,
    )


def shards_split(states, cotangent, attn_weights, mlp_weights, feature_gains, unit_gains, block_place):
    tok_rows, model_width = states.shape
    ff_width = unit_gains.shape[0]
    n_seq, n_ctx = lax.axis_size("seq"), lax.axis_size("ctx")
    chips = n_ctx // CORES
    chip = lax.axis_index("ctx") // CORES
    heads = HEADS // chips
    head_cols = heads * HEAD_DIM
    units = ff_width // chips
    rows = attn_weights.shape[0]
    qk_gain = lax.dynamic_slice_in_dim(feature_gains[:, 0], chip * head_cols, head_cols)
    qk_gain = qk_gain.reshape(heads, 1, HEAD_DIM)
    states_all, w_qkv, w_out, w_up, w_gate, low_down, raw, query, both, att, inverse, attx = attend_call(
        states, attn_weights, mlp_weights, qk_gain, block_place
    )
    gain_u = lax.dynamic_slice_in_dim(unit_gains[:, 0], chip * units, units)
    gain_v = lax.dynamic_slice_in_dim(unit_gains[:, 1], chip * units, units) * math.sqrt(D)
    out_low, grad_attx, grad_w_out, grad_direct, small, grad_half, grad_down = mlp_call(
        attx, states, cotangent, w_out, feature_gains[:, 1].reshape(1, model_width),
        feature_gains[:, 2].reshape(1, model_width), gain_u.reshape(CORES, 1, units // CORES),
        gain_v.reshape(CORES, 1, units // CORES), w_up, w_gate, low_down,
    )
    grad_states, grad_mlp, grad_attn, feature, unit = back_call(
        grad_attx, grad_half, grad_down, grad_w_out, small, raw, query, both, att, inverse, states_all,
        w_qkv, qk_gain, block_place, grad_direct, rows,
    )
    rank = lax.axis_index(ALL)
    unit_rows_own = ff_width // (n_seq * n_ctx)
    return (
        out_low,
        grad_states,
        grad_attn,
        grad_mlp,
        lax.dynamic_slice_in_dim(feature, rank * rows, rows, axis=1).T,
        lax.dynamic_slice_in_dim(unit, rank * unit_rows_own, unit_rows_own, axis=1).T,
    )


def solution(mesh):
    in_specs = (
        P(("seq", "ctx"), None),
        P(("seq", "ctx"), None),
        P(("seq", "ctx"), None),
        P(("seq", "ctx"), None),
        P(),
        P(),
        P("seq", None),
    )
    out_specs = (
        P(("seq", "ctx"), None),
        P(("seq", "ctx"), None),
        P(("seq", "ctx"), None),
        P(("seq", "ctx"), None),
        P(("seq", "ctx"), None),
        P(("seq", "ctx"), None),
    )
    chips = mesh.shape["ctx"] // CORES
    shards = shards_split if fits(mesh.shape["seq"], chips) else shards_general
    return jax.shard_map(shards, mesh=mesh, in_specs=in_specs, out_specs=out_specs, check_vma=False)
```

```python
import functools
import math

import jax
import jax.numpy as jnp
from jax import lax
from jax.experimental import pallas as pl
from jax.experimental.pallas import tpu as pltpu
from jax.sharding import PartitionSpec as P

D = 1280
HEADS = 20
HEAD_DIM = 64


EPSILON = 1e-06
NEG_LARGE = -1e30


def unit_rows(values_in):
    factor = lax.rsqrt(jnp.sum(values_in * values_in, axis=-1, keepdims=True) + EPSILON)
    return (values_in * factor, factor)


def unit_back(normed, factor, upstream):
    return factor * (upstream - normed * jnp.sum(upstream * normed, axis=-1, keepdims=True))


def contract_rows(left_mat, right_mat):
    return lax.dot_general(
        left_mat, right_mat, (((0,), (0,)), ((), ())), preferred_element_type=jnp.float32
    )


def contract_cols(left_mat, right_mat):
    return lax.dot_general(
        left_mat, right_mat, (((1,), (1,)), ((), ())), preferred_element_type=jnp.float32
    )


def shards_general(states, cotangent, attn_weights, mlp_weights, feature_gains, unit_gains, block_place):
    tok_rows = states.shape[0]
    model_width = states.shape[1]
    ff_width = unit_gains.shape[0]
    score_scale = math.sqrt(HEAD_DIM)
    gate_factor = unit_gains[:, 1] * math.sqrt(D)
    w_attn = lax.all_gather(attn_weights.astype(jnp.bfloat16), ("seq", "ctx"), axis=0, tiled=True)
    w_mlp = lax.all_gather(mlp_weights.astype(jnp.bfloat16), ("seq", "ctx"), axis=0, tiled=True)
    states_full = states.astype(jnp.float32)
    projected = jnp.dot(states, w_attn[:, : 3 * model_width], preferred_element_type=jnp.float32)
    head_shape = (tok_rows, HEADS, HEAD_DIM)
    qk_gain = feature_gains[:, 0].reshape(HEADS, HEAD_DIM)
    query_unit, query_factor = unit_rows(projected[:, :model_width].reshape(head_shape))
    key_unit, key_factor = unit_rows(
        projected[:, model_width : 2 * model_width].reshape(head_shape)
    )
    query_low = (query_unit * qk_gain).astype(jnp.bfloat16)
    key_low = (key_unit * qk_gain).astype(jnp.bfloat16).reshape(tok_rows, model_width)
    value_low = projected[:, 2 * model_width :].astype(jnp.bfloat16)
    keys_all, values_all = (
        lax.all_gather(key_low, "ctx", axis=0, tiled=True),
        lax.all_gather(value_low, "ctx", axis=0, tiled=True),
    )
    seq_len = keys_all.shape[0]
    ctx_lanes = jnp.arange(lax.axis_size("ctx"), dtype=jnp.int32)
    places = block_place[0]
    own_block = jnp.sum(jnp.where(ctx_lanes == lax.axis_index("ctx"), places, 0))
    query_pos = own_block * tok_rows + jnp.arange(tok_rows, dtype=jnp.int32)
    key_index = jnp.arange(seq_len, dtype=jnp.int32)
    key_owner = key_index // tok_rows
    key_pos = (
        jnp.sum(jnp.where(key_owner[:, None] == ctx_lanes[None, :], places[None, :], 0), axis=1)
        * tok_rows
        + key_index % tok_rows
    )
    kblock = min(512, seq_len)
    nblocks = seq_len // kblock
    key_blocks = keys_all.reshape(nblocks, kblock, HEADS, HEAD_DIM)
    value_blocks = values_all.reshape(nblocks, kblock, HEADS, HEAD_DIM)
    pos_blocks = key_pos.reshape(nblocks, kblock)

    def block_scores(key_rows, key_places):
        raw_scores = score_scale * jnp.einsum(
            "qhd,khd->hqk", query_low, key_rows, preferred_element_type=jnp.float32
        )
        allowed = key_places[None, None, :] <= query_pos[None, :, None]
        return (raw_scores, allowed)

    def max_step(running, inputs):
        running_max, running_sum = running
        key_rows, key_places = inputs
        raw_scores, allowed = block_scores(key_rows, key_places)
        masked = jnp.where(allowed, raw_scores, NEG_LARGE)
        new_max = jnp.maximum(running_max, jnp.max(masked, axis=-1))
        powered = jnp.where(allowed, jnp.exp(masked - new_max[..., None]), 0.0)
        running_sum = running_sum * jnp.exp(running_max - new_max) + jnp.sum(powered, axis=-1)
        return ((new_max, running_sum), None)

    start_max = jnp.full((HEADS, tok_rows), NEG_LARGE, jnp.float32)
    start_sum = jnp.zeros((HEADS, tok_rows), jnp.float32)
    (final_max, final_sum), _ = lax.scan(max_step, (start_max, start_sum), (key_blocks, pos_blocks))
    log_total = final_max + jnp.log(final_sum)

    def value_step(accumulated, inputs):
        key_rows, value_rows, key_places = inputs
        raw_scores, allowed = block_scores(key_rows, key_places)
        weights_low = jnp.where(allowed, jnp.exp(raw_scores - log_total[..., None]), 0.0).astype(
            jnp.bfloat16
        )
        accumulated = accumulated + jnp.einsum(
            "hqk,khd->qhd", weights_low, value_rows, preferred_element_type=jnp.float32
        )
        return (accumulated, None)

    attended, _ = lax.scan(
        value_step, jnp.zeros(head_shape, jnp.float32), (key_blocks, value_blocks, pos_blocks)
    )
    attended_low = attended.reshape(tok_rows, model_width).astype(jnp.bfloat16)
    branch_attn = jnp.dot(
        attended_low, w_attn[:, 3 * model_width :], preferred_element_type=jnp.float32
    )
    attn_unit, attn_factor = unit_rows(branch_attn)
    alpha_attn = feature_gains[:, 1]
    mixed_one, mix_factor = unit_rows(states_full + alpha_attn * (attn_unit - states_full))
    mixed_low = mixed_one.astype(jnp.bfloat16)
    up_gate = jnp.dot(mixed_low, w_mlp[:, : 2 * ff_width], preferred_element_type=jnp.float32)
    up_scaled = up_gate[:, :ff_width] * unit_gains[:, 0]
    gate_scaled = up_gate[:, ff_width:] * gate_factor
    sigmoid_gate = jax.nn.sigmoid(gate_scaled)
    activated = gate_scaled * sigmoid_gate
    hidden = (activated * up_scaled).astype(jnp.bfloat16)
    branch_mlp = contract_cols(hidden, w_mlp[:, 2 * ff_width :])
    mlp_unit, mlp_factor = unit_rows(branch_mlp)
    alpha_mlp = feature_gains[:, 2]
    out_full, out_factor = unit_rows(mixed_one + alpha_mlp * (mlp_unit - mixed_one))
    grad_mix_two = unit_back(out_full, out_factor, cotangent.astype(jnp.float32))
    grad_alpha_m = jnp.sum(grad_mix_two * (mlp_unit - mixed_one), axis=0)
    grad_branch_mlp = unit_back(mlp_unit, mlp_factor, grad_mix_two * alpha_mlp).astype(jnp.bfloat16)
    grad_hidden = jnp.dot(
        grad_branch_mlp, w_mlp[:, 2 * ff_width :], preferred_element_type=jnp.float32
    )
    grad_up_scaled = grad_hidden * activated
    grad_gate_scaled = (
        grad_hidden * up_scaled * sigmoid_gate * (1.0 + gate_scaled * (1.0 - sigmoid_gate))
    )
    grad_s_u = jnp.sum(grad_up_scaled * up_gate[:, :ff_width], axis=0)
    grad_s_v = jnp.sum(grad_gate_scaled * up_gate[:, ff_width:], axis=0) * math.sqrt(D)
    grad_up_gate = jnp.concatenate(
        [grad_up_scaled * unit_gains[:, 0], grad_gate_scaled * gate_factor], axis=1
    ).astype(jnp.bfloat16)
    grad_mixed_one = grad_mix_two * (1.0 - alpha_mlp) + contract_cols(
        grad_up_gate, w_mlp[:, : 2 * ff_width]
    )
    grad_mix_one = unit_back(mixed_one, mix_factor, grad_mixed_one)
    grad_alpha_a = jnp.sum(grad_mix_one * (attn_unit - states_full), axis=0)
    grad_branch_attn = unit_back(attn_unit, attn_factor, grad_mix_one * alpha_attn).astype(
        jnp.bfloat16
    )
    grad_attended = (
        contract_cols(grad_branch_attn, w_attn[:, 3 * model_width :])
        .astype(jnp.bfloat16)
        .reshape(head_shape)
    )
    row_dots = jnp.einsum("qhd,qhd->hq", grad_attended.astype(jnp.float32), attended)

    def grad_step(grad_query, inputs):
        key_rows, value_rows, key_places = inputs
        raw_scores, allowed = block_scores(key_rows, key_places)
        probabilities = jnp.where(allowed, jnp.exp(raw_scores - log_total[..., None]), 0.0)
        grad_prob = jnp.einsum(
            "qhd,khd->hqk", grad_attended, value_rows, preferred_element_type=jnp.float32
        )
        grad_scores = (probabilities * (grad_prob - row_dots[..., None])).astype(jnp.bfloat16)
        grad_query = grad_query + score_scale * jnp.einsum(
            "hqk,khd->qhd", grad_scores, key_rows, preferred_element_type=jnp.float32
        )
        key_terms = score_scale * jnp.einsum(
            "hqk,qhd->khd", grad_scores, query_low, preferred_element_type=jnp.float32
        )
        value_terms = jnp.einsum(
            "hqk,qhd->khd",
            probabilities.astype(jnp.bfloat16),
            grad_attended,
            preferred_element_type=jnp.float32,
        )
        return (grad_query, (key_terms, value_terms))

    grad_query_low, (key_terms, value_terms) = lax.scan(
        grad_step, jnp.zeros(head_shape, jnp.float32), (key_blocks, value_blocks, pos_blocks)
    )
    key_terms = key_terms.reshape(seq_len, model_width)
    value_terms = value_terms.reshape(seq_len, model_width)
    own_key_grad, own_value_grad = (
        lax.psum_scatter(
            key_terms.astype(jnp.bfloat16), "ctx", scatter_dimension=0, tiled=True
        ).astype(jnp.float32),
        lax.psum_scatter(
            value_terms.astype(jnp.bfloat16), "ctx", scatter_dimension=0, tiled=True
        ).astype(jnp.float32),
    )
    grad_key_low = own_key_grad.reshape(head_shape)
    grad_s_qk = jnp.sum(grad_query_low * query_unit + grad_key_low * key_unit, axis=0).reshape(
        model_width
    )
    grad_query_raw = unit_back(query_unit, query_factor, grad_query_low * qk_gain).reshape(
        tok_rows, model_width
    )
    grad_key_raw = unit_back(key_unit, key_factor, grad_key_low * qk_gain).reshape(
        tok_rows, model_width
    )
    grad_projected = jnp.concatenate([grad_query_raw, grad_key_raw, own_value_grad], axis=1).astype(
        jnp.bfloat16
    )
    grad_states = grad_mix_one * (1.0 - alpha_attn) + contract_cols(
        grad_projected, w_attn[:, : 3 * model_width]
    )
    feature_total = jnp.stack([grad_s_qk, grad_alpha_a, grad_alpha_m], axis=1)
    unit_fold = jnp.stack([grad_s_u, grad_s_v], axis=1).reshape(
        model_width, 2 * ff_width // model_width
    )
    attn_cols = 4 * model_width
    mlp_cols = 3 * ff_width
    attn_share = lax.psum_scatter(
        jnp.concatenate(
            [
                contract_rows(states, grad_projected),
                contract_rows(attended_low, grad_branch_attn),
                feature_total,
            ],
            axis=1,
        ),
        ("seq", "ctx"),
        scatter_dimension=0,
        tiled=True,
    )
    mlp_share = lax.psum_scatter(
        jnp.concatenate(
            [
                contract_rows(mixed_low, grad_up_gate),
                contract_rows(grad_branch_mlp, hidden),
                unit_fold,
            ],
            axis=1,
        ),
        ("seq", "ctx"),
        scatter_dimension=0,
        tiled=True,
    )
    grad_attn = attn_share[:, :attn_cols]
    grad_feature = attn_share[:, attn_cols:]
    grad_mlp = mlp_share[:, :mlp_cols]
    grad_unit = mlp_share[:, mlp_cols:].reshape(
        unit_gains.shape[0] // lax.axis_size(("seq", "ctx")), 2
    )
    return (
        out_full.astype(jnp.bfloat16),
        grad_states.astype(jnp.bfloat16),
        grad_attn,
        grad_mlp,
        grad_feature,
        grad_unit,
    )


CORES = 2
ALL = ("seq", "ctx")


def fits(n_seq, chips):
    return n_seq == 4 and chips == 4 and HEADS % chips == 0


MESH = pl.DeviceIdType.MESH
VMEM = pltpu.VMEM
CHIPS = 4
STEPS = (1, 2, 3)
LIMIT = 60 * 1024 * 1024


def place_of():
    seq = lax.axis_index("seq")
    ctx = lax.axis_index("ctx")
    return seq, ctx // CORES, ctx % CORES


def chip_peer(step):
    seq, chip, core = place_of()
    other = lax.rem(chip + step, CHIPS)
    return (seq, other * CORES + core), other


def seq_peer(step):
    seq, chip, core = place_of()
    other = seq ^ step
    return (other, chip * CORES + core), other


def twin():
    seq, chip, core = place_of()
    return (seq, chip * CORES + 1 - core)


def meet():
    devices = [chip_peer(step)[0] for step in STEPS] + [seq_peer(step)[0] for step in STEPS] + [twin()]
    gate = pltpu.get_barrier_semaphore()
    for device in devices:
        pl.semaphore_signal(gate, inc=1, device_id=device, device_id_type=MESH)
    pl.semaphore_wait(gate, len(devices))


def remote(src, dst, send, recv, device):
    return pltpu.make_async_remote_copy(
        src_ref=src, dst_ref=dst, send_sem=send, recv_sem=recv, device_id=device,
        device_id_type=MESH,
    )


def begin(copy):
    copy.start()
    return copy


def rows_at(index, count):
    return pl.ds(pl.multiple_of(index * count, count), count)


def device_on(chip):
    seq, _, core = place_of()
    return (seq, chip * CORES + core)


def when(condition, action):
    pl.when(condition)(action)


PIECES = 2


def piece_at(block, piece, count):
    step = count // PIECES
    return pl.ds(pl.multiple_of(block * count + piece * step, step), step)


def gather_copy(src, everything, count, block, side, hop, piece, send, recv):
    chip = place_of()[1]
    there = everything.at[piece_at(block, piece, count)]
    near = chip + 1 if side == 0 else chip - 1
    here = there if src is None else src.at[piece_at(0, piece, count)]
    return remote(here, there, send.at[side, hop, piece], recv.at[side, hop, piece], device_on(near))


def gather_start(src, everything, count, send, recv):
    chip = place_of()[1]
    for piece in range(PIECES):
        for side in range(2):
            copy = gather_copy(src, everything, count, chip, side, 0, piece, send, recv)
            when(chip < CHIPS - 1 if side == 0 else chip > 0, copy.start)


def gather_hop(everything, count, hop, send, recv):
    chip = place_of()[1]
    for piece in range(PIECES):
        for side in range(2):
            block = chip - hop if side == 0 else chip + hop

            def pass_on(side=side, piece=piece, block=block):
                gather_copy(None, everything, count, block, side, hop - 1, piece, send, recv).wait_recv()
                if hop < CHIPS - 1:
                    copy = gather_copy(None, everything, count, block, side, hop, piece, send, recv)
                    when(chip < CHIPS - 1 if side == 0 else chip > 0, copy.start)

            when(block >= 0 if side == 0 else block < CHIPS, pass_on)


def gather_drain(everything, count, send, recv):
    chip = place_of()[1]
    for hop in range(CHIPS - 1):
        for piece in range(PIECES):
            for side in range(2):
                copy = gather_copy(None, everything, count, chip, side, hop, piece, send, recv)
                block = chip - hop if side == 0 else chip + hop
                sent = (block >= 0) & (chip < CHIPS - 1) if side == 0 else (block < CHIPS) & (chip > 0)
                when(sent, copy.wait_send)


def inside_line():
    chip = place_of()[1]
    return (chip > 0) & (chip < CHIPS - 1)


def spans_line(other):
    return abs(place_of()[1] - other) == CHIPS - 1


def reduce_start(part, count, sums, via, send, recv, ahead=True):
    chip = place_of()[1]
    near = jnp.where(chip == 0, 1, CHIPS - 2)
    first = remote(part.at[rows_at(CHIPS - 1 - chip, count)], via, send.at[0], recv.at[0], device_on(near))

    def begin_far():
        first.start()
        if ahead:
            first.wait_send()

    when(jnp.logical_not(inside_line()), begin_far)
    for step in STEPS:
        device, other = chip_peer(step)
        copy = remote(part.at[rows_at(other, count)], sums.at[step - 1], send.at[step], recv.at[step], device)
        if step == 2:
            when(jnp.logical_not(inside_line()), copy.start)
        else:
            when(jnp.logical_not(spans_line(other)), copy.start)


def reduce_relay(part, count, sums, via, mixed, send, recv):
    chip = place_of()[1]
    other = lax.rem(chip + 2, CHIPS)
    copy = remote(mixed, sums.at[1], send.at[2], recv.at[2], device_on(other))

    def pass_on():
        remote(mixed, via, send.at[0], recv.at[0], device_on(other)).wait_recv()
        mixed[...] = (
            part[rows_at(other, count), :].astype(jnp.float32) + via[...].astype(jnp.float32)
        ).astype(mixed.dtype)
        copy.start()

    when(inside_line(), pass_on)


def reduce_wait(part, count, sums, total, send, recv):
    chip = place_of()[1]
    total[...] = part[rows_at(chip, count), :].astype(jnp.float32)
    for step in (1, 3, 2):
        source = lax.rem(chip + CHIPS - step, CHIPS)

        def add(step=step, source=source):
            here = sums.at[step - 1]
            remote(here, here, send.at[step], recv.at[step], device_on(source)).wait_recv()
            total[...] += sums[step - 1].astype(jnp.float32)

        when(jnp.logical_not(spans_line(source)), add)


def reduce_drain(part, count, sums, send, recv, ahead=True):
    rows = part.at[rows_at(0, count)]
    for step in STEPS:
        device, other = chip_peer(step)
        copy = remote(rows, sums.at[step - 1], send.at[step], recv.at[step], device)
        when(jnp.logical_not(spans_line(other)), copy.wait_send)
    if not ahead:
        copy = remote(rows, sums.at[0], send.at[0], recv.at[0], device_on(place_of()[1]))
        when(jnp.logical_not(inside_line()), copy.wait_send)


def side_peer(side):
    return seq_peer(side + 1)


def seq_rows_at(block, side, count):
    half = count // 2
    return pl.ds(pl.multiple_of(block * count + side * half, half), half)


def spread_start(src, dst, count, send, recv):
    seq = place_of()[0]
    return [
        begin(remote(src, dst.at[rows_at(seq, count)], send.at[side], recv.at[side], side_peer(side)[0]))
        for side in range(2)
    ]


def spread_relay(dst, count, send, recv):
    copies = []
    for side in range(2):
        block = side_peer(side)[1]
        whole = dst.at[rows_at(block, count)]
        remote(whole, whole, send.at[side], recv.at[side], side_peer(side)[0]).wait_recv()
        part = dst.at[seq_rows_at(block, side, count)]
        copies.append(begin(remote(part, part, send.at[2 + side], recv.at[2 + side], side_peer(1 - side)[0])))
    return copies


def fold_start(src, got, count, send, recv):
    seq = place_of()[0]
    copies = []
    for side in range(2):
        device, other = side_peer(side)
        for at, block in enumerate((other, seq ^ 3)):
            here = src.at[seq_rows_at(block, side, count)]
            copies.append(begin(remote(here, got.at[side, at], send.at[side, at], recv.at[side, at], device)))
    return copies


def fold_relay(src, got, held, last, count, copies, send, recv):
    more = []
    for side in range(2):
        device, other = side_peer(1 - side)
        copies[2 * side + 1].wait_recv()
        rows = seq_rows_at(other, side, count)
        held[side] = (src[rows, :].astype(jnp.float32) + got[side, 1].astype(jnp.float32)).astype(held.dtype)
        more.append(begin(remote(held.at[side], last.at[side], send.at[2, side], recv.at[2, side], device)))
    return more


def fold_end(src, got, last, out, count, copies, more):
    seq = place_of()[0]
    half = count // 2
    for side in range(2):
        copies[2 * side].wait_recv()
        more[side].wait_recv()
        rows = seq_rows_at(seq, side, count)
        out[side * half : (side + 1) * half, :] = (
            src[rows, :].astype(jnp.float32) + got[side, 0].astype(jnp.float32) + last[side].astype(jnp.float32)
        ).astype(out.dtype)


def to_line(src, there, send, recv):
    return [
        begin(remote(src, there, send.at[step], recv.at[step], chip_peer(step)[0])) for step in STEPS
    ]


def dot(left, right):
    return jnp.dot(left, right, preferred_element_type=jnp.float32)


def dot_nt(left, right):
    return lax.dot_general(
        left, right, (((1,), (1,)), ((), ())), preferred_element_type=jnp.float32
    )


def dot_tn(left, right):
    return lax.dot_general(
        left, right, (((0,), (0,)), ((), ())), preferred_element_type=jnp.float32
    )


def dma(*shape):
    return pltpu.SemaphoreType.DMA(shape)


def line_dma():
    return dma(2, CHIPS, PIECES)


def in_vmem():
    return pl.BlockSpec(memory_space=pltpu.VMEM)


def in_hbm():
    return pl.BlockSpec(memory_space=pl.ANY)


def key_positions(places, key_pos, tok_rows):
    lanes = lax.broadcasted_iota(jnp.int32, (1, tok_rows), 1)
    for at_core in range(CORES):
        for at_chip in range(CHIPS):
            start = (at_core * CHIPS + at_chip) * tok_rows
            key_pos[:, start : start + tok_rows] = places[0, CORES * at_chip + at_core] * tok_rows + lanes


def kept_pairs(places, key_pos, block, core, tok_rows):
    down = lax.broadcasted_iota(jnp.int32, (tok_rows, 1), 0)
    return key_pos[...] <= places[0, CORES * block + core] * tok_rows + down


def attend_kernel(
    states, attn_src, mlp_src, qk_gain, places,
    to_states, to_qkv, to_out, w_up, w_gate, low_down, to_raw, to_query, to_both, to_att, to_inv, attx,
    states_all, w_qkv, w_out, raw_out, query_out, both, att_out, inv_out, src_q, stage_q, low_q, stage_o, low_o, stage_m, low_m, raw, att_low, key_pos,
    local_sem, keep_sem, att_sem, x_send, x_recv, q_send, q_recv, mt_send, mt_recv, wz_send, wz_recv,
    ws_send, ws_recv, wt_send, wt_recv, oz_send, oz_recv, os_send, os_recv, m_send, m_recv,
    ms_send, ms_recv, kv_send, kv_recv, a_send, a_recv,
):
    seq, chip, core = place_of()
    rows = attn_src.shape[0]
    tok_rows, model_width = states.shape
    heads = qk_gain.shape[0]
    head_cols = heads * HEAD_DIM
    part_cols = head_cols // CORES
    group_rows = tok_rows * CHIPS
    chip_rows = CORES * rows
    seq_rows = CHIPS * chip_rows
    half_units = w_up.shape[1]
    half_width = model_width // CORES
    ff_width = mlp_src.shape[1] // 3
    low = jnp.bfloat16
    for at in range(CHIPS):
        for half in range(CORES):
            for which in range(3):
                start = which * model_width + at * head_cols + half * part_cols
                src_q[at, half, :, which * part_cols : (which + 1) * part_cols] = attn_src[:, start : start + part_cols]
    meet()
    block = rows_at(chip, tok_rows)
    mine = rows_at(core, rows)
    half_at = pl.ds(pl.multiple_of(3 * model_width + core * half_width, 128), half_width)
    other_at = pl.ds(pl.multiple_of(3 * model_width + (1 - core) * half_width, 128), half_width)
    swap_o = begin(remote(attn_src.at[:, other_at], stage_o.at[mine], q_send.at[1], q_recv.at[1], twin()))
    swap_q = begin(remote(src_q.at[:, 1 - core], stage_q.at[:, mine], q_send.at[0], q_recv.at[0], twin()))
    stage_o[mine, :] = attn_src[:, half_at]
    stage_q[:, mine, :] = src_q[:, core]
    m_swaps, m_keeps = [], []
    for part in range(3):
        for at in range(CHIPS):
            start = part * ff_width + at * CORES * half_units
            theirs = pl.ds(pl.multiple_of(start + (1 - core) * half_units, 128), half_units)
            ours = pl.ds(pl.multiple_of(start + core * half_units, 128), half_units)
            there = stage_m.at[part, at, mine]
            m_swaps.append(begin(remote(mlp_src.at[:, theirs], there, mt_send.at[part, at], mt_recv.at[part, at], twin())))
            m_keeps.append(begin(pltpu.make_async_copy(mlp_src.at[:, ours], there, local_sem.at[part * CHIPS + at])))
    my_rows = rows_at(seq * CHIPS + chip, chip_rows)
    seq_at = rows_at(seq, seq_rows)
    swap_o.wait()
    low_o[...] = stage_o[...].astype(low)
    o_line = to_line(low_o, w_out.at[core, my_rows], oz_send, oz_recv)
    w_out[core, my_rows, :] = low_o[...]
    swap_q.wait()
    low_q[...] = stage_q[...].astype(low)
    line = []
    for step in STEPS:
        device, other = chip_peer(step)
        line.append(begin(remote(low_q.at[other], w_qkv.at[core, my_rows], wz_send.at[step], wz_recv.at[step], device)))
    w_qkv[core, my_rows, :] = low_q[chip]
    states_all[block, :] = states[...]
    key_positions(places, key_pos, tok_rows)
    gather_start(states, states_all, tok_rows, x_send, x_recv)
    for copy in line:
        copy.wait_recv()

    def across(whole, send, recv):
        return spread_start(whole.at[seq_at], whole, seq_rows, send, recv)

    q_across = across(w_qkv.at[core], ws_send, ws_recv)
    for copy in m_keeps:
        copy.wait()
    for copy in m_swaps:
        copy.wait()
    low_m[...] = stage_m[:2].astype(low)
    low_down[...] = stage_m[2].astype(low)
    gather_hop(states_all, tok_rows, 1, x_send, x_recv)
    more = spread_relay(w_qkv.at[core], seq_rows, ws_send, ws_recv)
    for copy in o_line:
        copy.wait_recv()
    o_across = across(w_out.at[core], os_send, os_recv)
    for copy in more:
        copy.wait_recv()
    q_across += more
    swap = begin(remote(w_qkv.at[core], w_qkv.at[core], wt_send.at[0], wt_recv.at[0], twin()))
    gather_hop(states_all, tok_rows, 2, x_send, x_recv)
    o_more = spread_relay(w_out.at[core], seq_rows, os_send, os_recv)
    gather_hop(states_all, tok_rows, 3, x_send, x_recv)
    here = rows_at(chip, chip_rows)

    def to_chips(part, there):
        return [
            begin(remote(low_m.at[part, chip_peer(step)[1]], there, m_send.at[part, step], m_recv.at[part, step], chip_peer(step)[0]))
            for step in STEPS
        ]

    m_line = to_chips(0, w_up.at[my_rows])
    w_up[my_rows, :] = low_m[0, chip]
    w_gate[here, :] = low_m[1, chip]
    swap.wait()
    kept = []

    def keep(src, dst):
        kept.append(begin(pltpu.make_async_copy(src, dst, keep_sem.at[len(kept)])))

    keep(states_all, to_states)
    keep(w_qkv, to_qkv)
    for half in range(CORES):
        value = dot(states_all[...], w_qkv[half])
        for which in range(3):
            start = which * head_cols + half * part_cols
            raw[:, start : start + part_cols] = value[:, which * part_cols : (which + 1) * part_cols]
    for head in reversed(range(3 * heads)):
        which, head = head // heads, head % heads
        start = which * head_cols + head * HEAD_DIM
        value = raw[:, start : start + HEAD_DIM]
        if which == 2:
            both[core, 1, head] = value.astype(low)
            continue
        factor = lax.rsqrt(jnp.sum(value * value, axis=-1, keepdims=True) + EPSILON)
        scaled = (value * factor * qk_gain[head]).astype(low)
        raw_out[which, head] = value
        if which == 1:
            both[core, 0, head] = scaled
            if head == 0:
                swap = begin(remote(both.at[core], both.at[core], kv_send.at[0], kv_recv.at[0], twin()))
        else:
            query_out[head] = scaled * math.sqrt(HEAD_DIM)
    keep(raw_out, to_raw)
    keep(query_out, to_query)
    for copy in m_line + o_more:
        copy.wait_recv()
    m_line += to_chips(1, w_gate.at[here])
    swap_o = begin(remote(w_out.at[core], w_out.at[core], wt_send.at[1], wt_recv.at[1], twin()))
    up_across = across(w_up, ms_send, ms_recv)
    swap.wait()
    keep(both, to_both)

    def one_block(index, carry):
        step = lax.rem(index + 1, CHIPS)
        device, other = chip_peer(step)
        at = rows_at(other, tok_rows)
        allowed = kept_pairs(places, key_pos, other, core, tok_rows)

        def one_head(head, carry):
            query = query_out[head, at, :]
            scores = jnp.concatenate([dot_nt(query, both[half, 0, head]) for half in range(CORES)], axis=1)
            powered = jnp.exp(jnp.where(allowed, scores, NEG_LARGE))
            inverse = 1.0 / jnp.sum(powered, axis=-1, keepdims=True)
            weights = (powered * inverse).astype(low)
            att_out[head, at, :] = sum(
                dot(weights[:, half * group_rows : (half + 1) * group_rows], both[half, 1, head])
                for half in range(CORES)
            )
            inv_out[head, at, :] = inverse
            return carry

        lax.fori_loop(0, heads, one_head, 0)
        for head in range(heads):
            att_low[at, head * HEAD_DIM : (head + 1) * HEAD_DIM] = att_out[head, at, :].astype(low)
        when(step != 0, remote(att_low.at[at], attx.at[chip], a_send.at[step], a_recv.at[step], device).start)
        pltpu.make_async_copy(att_out.at[:, at], to_att.at[:, at], att_sem.at[0, step]).start()
        pltpu.make_async_copy(inv_out.at[:, at], to_inv.at[:, at], att_sem.at[1, step]).start()
        return carry

    lax.fori_loop(0, CHIPS, one_block, 0)
    attx[chip] = att_low[block, :]
    swap_o.wait()
    keep(w_out, to_out)
    up_more = spread_relay(w_up, seq_rows, ms_send, ms_recv)
    for step in STEPS:
        remote(att_low.at[block], attx.at[chip], a_send.at[step], a_recv.at[step], chip_peer(step)[0]).wait()
    for copy in m_line[3:] + up_more:
        copy.wait_recv()
    gather_drain(states_all, tok_rows, x_send, x_recv)
    for step in range(CHIPS):
        pltpu.make_async_copy(att_out.at[:, block], to_att.at[:, block], att_sem.at[0, step]).wait()
        pltpu.make_async_copy(inv_out.at[:, block], to_inv.at[:, block], att_sem.at[1, step]).wait()
    for copy in kept:
        copy.wait()
    for copy in m_line + line + o_line + q_across + o_across + o_more + up_across + up_more:
        copy.wait_send()


def in_smem():
    return pl.BlockSpec(memory_space=pltpu.SMEM)


def attend_call(states, attn_src, mlp_src, qk_gain, places):
    tok_rows, model_width = states.shape
    rows = attn_src.shape[0]
    heads = qk_gain.shape[0]
    chips, chip_rows = CHIPS, CORES * rows
    group_rows = chips * tok_rows
    half_units = mlp_src.shape[1] // 3 // chips // CORES
    half_width, half_cols = model_width // CORES, 3 * heads * HEAD_DIM // CORES
    f32, low = jnp.float32, jnp.bfloat16
    shape = jax.ShapeDtypeStruct
    return pl.pallas_call(
        attend_kernel,
        out_shape=[
            shape((group_rows, model_width), low),
            shape((CORES, model_width, half_cols), low),
            shape((CORES, model_width, half_width), low),
            shape((model_width, half_units), low),
            shape((chips * chip_rows, half_units), low),
            shape((chips, chip_rows, half_units), low),
            shape((2, heads, group_rows, HEAD_DIM), f32),
            shape((heads, group_rows, HEAD_DIM), low),
            shape((CORES, 2, heads, group_rows, HEAD_DIM), low),
            shape((heads, group_rows, HEAD_DIM), f32),
            shape((heads, group_rows, 1), f32),
            shape((chips, tok_rows, heads * HEAD_DIM), low),
        ],
        in_specs=[in_vmem(), in_vmem(), in_hbm(), in_vmem(), in_smem()],
        out_specs=[in_hbm()] * 3 + [in_vmem()] * 3 + [in_hbm()] * 5 + [in_vmem()],
        scratch_shapes=[
            VMEM((group_rows, model_width), low),
            VMEM((CORES, model_width, half_cols), low),
            VMEM((CORES, model_width, half_width), low),
            VMEM((2, heads, group_rows, HEAD_DIM), f32),
            VMEM((heads, group_rows, HEAD_DIM), low),
            VMEM((CORES, 2, heads, group_rows, HEAD_DIM), low),
            VMEM((heads, group_rows, HEAD_DIM), f32),
            VMEM((heads, group_rows, 1), f32),
            VMEM((chips, CORES, rows, half_cols), f32),
            VMEM((chips, chip_rows, half_cols), f32),
            VMEM((chips, chip_rows, half_cols), low),
            VMEM((chip_rows, half_width), f32),
            VMEM((chip_rows, half_width), low),
            VMEM((3, chips, chip_rows, half_units), f32),
            VMEM((2, chips, chip_rows, half_units), low),
            VMEM((group_rows, 3 * heads * HEAD_DIM), f32),
            VMEM((group_rows, heads * HEAD_DIM), low),
            VMEM((1, CORES * group_rows), jnp.int32),
            dma(12), dma(6), dma(2, 4), line_dma(), line_dma(), dma(2), dma(2), dma(3, 4), dma(3, 4), dma(4), dma(4),
            dma(4), dma(4), dma(2), dma(2), dma(4), dma(4), dma(4), dma(4), dma(2, 4), dma(2, 4),
            dma(4), dma(4), dma(1), dma(1), dma(4), dma(4),
        ],
        compiler_params=pltpu.CompilerParams(
            collective_id=1, has_side_effects=True, vmem_limit_bytes=LIMIT
        ),
        name="attend",
    )(states, attn_src, mlp_src, qk_gain, places)


def unit_of(value):
    factor = lax.rsqrt(jnp.sum(value * value, axis=-1, keepdims=True) + EPSILON)
    return value * factor, factor


def mlp_kernel(
    attx, states, cotangent, from_out, alpha_attn, alpha_mlp, gain_u, gain_v, w_up, w_gate, low_down,
    out, grad_attx, grad_w_out, grad_direct, small, to_half, grad_down,
    w_out, grad_half, weights, mixed_one, attn_unit, factors, mixed_low, mixed_all, up, gate, hidden, part,
    sums, via, passed, total, grad_two, branch_low, branch_all, grad_u, grad_v, wide, turned, arrived,
    w_down, down_half, down_got, dot_u, dot_v,
    local_sem, ws_send, ws_recv, wt_send, wt_recv, x_send, x_recv, r_send, r_recv,
    g_send, g_recv, b_send, b_recv, d_send, d_recv, wz_send, wz_recv, ds_send, ds_recv,
):
    seq, chip, core = place_of()
    tok_rows, model_width = states.shape
    chip_heads = attx.shape[2]
    seq_rows, half_units = w_gate.shape
    chip_rows = low_down.shape[1]
    half_width = w_out.shape[2]
    group_rows = CHIPS * tok_rows
    block = rows_at(chip, tok_rows)
    load = begin(pltpu.make_async_copy(from_out, w_out, local_sem.at[2]))
    meet()
    seq_at = rows_at(seq, seq_rows)
    here = rows_at(chip, chip_rows)
    swaps = [begin(remote(w_up, weights.at[0, core], wt_send.at[0], wt_recv.at[0], twin()))]
    to_chips = [
        begin(remote(low_down.at[chip_peer(step)[1]], w_down.at[here], wz_send.at[step], wz_recv.at[step], chip_peer(step)[0]))
        for step in STEPS
    ]

    across = spread_start(w_gate, weights.at[1, core], seq_rows, ws_send.at[1], ws_recv.at[1])
    keeps = [
        begin(pltpu.make_async_copy(w_up, weights.at[0, core], local_sem.at[0])),
        begin(pltpu.make_async_copy(w_gate, weights.at[1, core, seq_at], local_sem.at[1])),
    ]
    w_down[here, :] = low_down[chip]
    load.wait()
    part_at = [slice(at * chip_heads, (at + 1) * chip_heads) for at in range(CHIPS)]
    half_at = [slice(half * half_width, (half + 1) * half_width) for half in range(CORES)]
    branch = jnp.concatenate(
        [sum(dot(attx[at], w_out[half, part_at[at], :]) for at in range(CHIPS)) for half in range(CORES)],
        axis=1,
    )
    unit, factor = unit_of(branch)
    attn_unit[...] = unit
    factors[0] = factor
    base = states[...].astype(jnp.float32)
    value, factor = unit_of(base + alpha_attn[...] * (unit - base))
    mixed_one[...] = value
    factors[1] = factor
    mixed_low[...] = value.astype(jnp.bfloat16)
    gather_start(mixed_low, mixed_all, tok_rows, x_send, x_recv)
    mixed_all[block, :] = mixed_low[...]
    for copy in keeps:
        copy.wait()
    for copy in to_chips:
        copy.wait_recv()
    more = spread_relay(weights.at[1, core], seq_rows, ws_send.at[1], ws_recv.at[1])
    across += spread_start(w_down, weights.at[2, core], seq_rows, ws_send.at[2], ws_recv.at[2])
    weights[2, core, seq_at, :] = w_down[...]
    gather_hop(mixed_all, tok_rows, 1, x_send, x_recv)
    for copy in more:
        copy.wait_recv()
    swaps.append(begin(remote(weights.at[1, core], weights.at[1, core], wt_send.at[1], wt_recv.at[1], twin())))
    slab = min(64, group_rows)
    slabs = group_rows // slab
    half_slabs = slabs // 2
    half_rows = group_rows // 2
    mine = chip // 2

    def forward(group):
        rows = rows_at(group, half_rows)
        for half in range(CORES):
            up[half, rows, :] = dot(mixed_all[rows, :], weights[0, half])
            gate[half, rows, :] = dot(mixed_all[rows, :], weights[1, half])

        def activate(index, carry):
            half = index // half_slabs
            at = rows_at(group * half_slabs + lax.rem(index, half_slabs), slab)
            gated = gate[half, at, :] * gain_v[half]
            scaled = up[half, at, :] * gain_u[half]
            hidden[half, at, :] = (gated * jax.nn.sigmoid(gated) * scaled).astype(jnp.bfloat16)
            return carry

        lax.fori_loop(0, CORES * half_slabs, activate, 0)

    for copy in swaps:
        copy.wait_recv()
    forward(mine)
    gather_hop(mixed_all, tok_rows, 2, x_send, x_recv)
    down_more = spread_relay(weights.at[2, core], seq_rows, ws_send.at[2], ws_recv.at[2])
    gather_hop(mixed_all, tok_rows, 3, x_send, x_recv)
    forward(1 - mine)
    for copy in down_more:
        copy.wait_recv()
    swap = begin(remote(weights.at[2, core], weights.at[2, core], wt_send.at[2], wt_recv.at[2], twin()))
    swaps.append(swap)
    swap.wait_recv()
    tile = model_width // 5

    def down(index, carry):
        at = rows_at(index, tile)
        part[0, :, at] = sum(dot_nt(hidden[half], weights[2, half, at, :]) for half in range(CORES)).astype(jnp.bfloat16)
        return carry

    lax.fori_loop(0, model_width // tile, down, 0)

    reduce_start(part.at[0], tok_rows, sums.at[0], via.at[0], r_send, r_recv)
    reduce_relay(part.at[0], tok_rows, sums.at[0], via.at[0], passed.at[0], r_send, r_recv)
    reduce_wait(part.at[0], tok_rows, sums.at[0], total, r_send, r_recv)
    mlp_unit, mlp_factor = unit_of(total[...])
    value, factor = unit_of(mixed_one[...] + alpha_mlp[...] * (mlp_unit - mixed_one[...]))
    out[...] = value.astype(jnp.bfloat16)
    above = cotangent[...].astype(jnp.float32)
    grad = factor * (above - value * jnp.sum(above * value, axis=-1, keepdims=True))
    grad_two[...] = grad
    small[...] = jnp.zeros_like(small)
    small[1:2, :] = jnp.sum(grad * (mlp_unit - mixed_one[...]), axis=0, keepdims=True)
    grad = grad * alpha_mlp[...]
    grad = mlp_factor * (grad - mlp_unit * jnp.sum(grad * mlp_unit, axis=-1, keepdims=True))
    branch_low[...] = grad.astype(jnp.bfloat16)
    gather_start(branch_low, branch_all, tok_rows, g_send, g_recv)
    branch_all[block, :] = branch_low[...]
    gather_hop(branch_all, tok_rows, 1, g_send, g_recv)
    gather_hop(branch_all, tok_rows, 2, g_send, g_recv)
    turned[0] = mixed_all[...].T
    gather_hop(branch_all, tok_rows, 3, g_send, g_recv)
    for half in range(CORES):
        wide[half] = dot(branch_all[...], weights[2, half])
    dot_u[...] = jnp.zeros_like(dot_u)
    dot_v[...] = jnp.zeros_like(dot_v)

    def deactivate(index, carry):
        half = index // slabs
        at = rows_at(lax.rem(index, slabs), slab)
        gated = gate[half, at, :] * gain_v[half]
        scaled = up[half, at, :] * gain_u[half]
        upstream = wide[half, at, :]
        sig = jax.nn.sigmoid(gated)
        to_up = upstream * (gated * sig)
        to_gate = upstream * scaled * sig * (1.0 + gated * (1.0 - sig))
        dot_u[half] += jnp.sum(to_up * up[half, at, :], axis=0, keepdims=True)
        dot_v[half] += jnp.sum(to_gate * gate[half, at, :], axis=0, keepdims=True)
        grad_u[half, at, :] = (to_up * gain_u[half]).astype(jnp.bfloat16)
        grad_v[half, at, :] = (to_gate * gain_v[half]).astype(jnp.bfloat16)
        return carry

    lax.fori_loop(0, CORES * slabs, deactivate, 0)

    def back_down(index, carry):
        at = rows_at(index, tile)
        part[1, :, at] = sum(
            dot_nt(grad_u[half], weights[0, half, at, :]) + dot_nt(grad_v[half], weights[1, half, at, :])
            for half in range(CORES)
        ).astype(jnp.bfloat16)
        return carry

    lax.fori_loop(0, model_width // tile, back_down, 0)
    for copy in swaps + more + down_more:
        copy.wait_send()
    reduce_start(part.at[1], tok_rows, sums.at[1], via.at[1], b_send, b_recv, False)
    turned[1] = branch_all[...].T
    swaps = {}

    def weight_grads(which, left, right):
        def one(index, carry):
            half = index // 5
            at = rows_at(lax.rem(index, 5), tile)
            weights[which, half, at, :] = dot(turned[left, at, :], right[half]).astype(jnp.bfloat16)
            return carry

        lax.fori_loop(0, CORES * 5, one, 0)
        swaps[which] = begin(remote(weights.at[which, 1 - core], arrived.at[which], d_send.at[which], d_recv.at[which], twin()))

    def both_cores(which):
        swaps[which].wait_recv()
        return (weights[which, core].astype(jnp.float32) + arrived[which].astype(jnp.float32)).astype(jnp.bfloat16)

    weight_grads(2, 1, hidden)
    reduce_relay(part.at[1], tok_rows, sums.at[1], via.at[1], passed.at[1], b_send, b_recv)
    weight_grads(0, 0, grad_u)
    down_half[...] = both_cores(2)
    down_across = [
        begin(remote(down_half.at[rows_at(seq_peer(step)[1], seq_rows)], down_got.at[step - 1], ds_send.at[step], ds_recv.at[step], seq_peer(step)[0]))
        for step in STEPS
    ]
    weight_grads(1, 0, grad_v)
    kept = []
    for which in range(2):
        grad_half[which] = both_cores(which)
        kept.append(begin(pltpu.make_async_copy(grad_half.at[which], to_half.at[which], local_sem.at[which])))
    reduce_wait(part.at[1], tok_rows, sums.at[1], total, b_send, b_recv)
    grad = grad_two[...] * (1.0 - alpha_mlp[...]) + total[...]
    value = mixed_one[...]
    grad = factors[1] * (grad - value * jnp.sum(grad * value, axis=-1, keepdims=True))
    unit = attn_unit[...]
    small[0:1, :] = jnp.sum(grad * (unit - states[...].astype(jnp.float32)), axis=0, keepdims=True)
    grad_direct[...] = grad * (1.0 - alpha_attn[...])
    grad = grad * alpha_attn[...]
    grad = factors[0] * (grad - unit * jnp.sum(grad * unit, axis=-1, keepdims=True))
    low = grad.astype(jnp.bfloat16)
    for at in range(CHIPS):
        grad_attx[at] = sum(
            dot_nt(low[:, half_at[half]], w_out[half, part_at[at], :]) for half in range(CORES)
        ).astype(jnp.bfloat16)
        for half in range(CORES):
            grad_w_out[half, at] = dot_tn(attx[at], low[:, half_at[half]]).astype(jnp.bfloat16)
    for half in range(CORES):
        unit_at = slice(half * half_units, (half + 1) * half_units)
        small[2:3, unit_at] = dot_u[half]
        small[3:4, unit_at] = dot_v[half] * math.sqrt(D)
    whole = down_half[seq_at, :].astype(jnp.float32)
    for step in STEPS:
        down_across[step - 1].wait_recv()
        whole = whole + down_got[step - 1].astype(jnp.float32)
    grad_down[...] = whole.astype(jnp.bfloat16)
    for copy in kept:
        copy.wait()
    gather_drain(mixed_all, tok_rows, x_send, x_recv)
    gather_drain(branch_all, tok_rows, g_send, g_recv)
    reduce_drain(part.at[0], tok_rows, sums.at[0], r_send, r_recv)
    reduce_drain(part.at[1], tok_rows, sums.at[1], b_send, b_recv, False)
    for copy in across + to_chips + down_across + [swaps[which] for which in range(3)]:
        copy.wait_send()


def mlp_call(attx, states, cotangent, w_out, alpha_attn, alpha_mlp, gain_u, gain_v, w_up, w_gate, low_down):
    tok_rows, model_width = states.shape
    chips, _, chip_heads = attx.shape
    seq_rows, half_units = w_gate.shape
    group_rows = chips * tok_rows
    f32, low = jnp.float32, jnp.bfloat16
    shape = jax.ShapeDtypeStruct
    tokens, group = (tok_rows, model_width), (group_rows, model_width)
    wide = (CORES, group_rows, half_units)
    matrix = (model_width, half_units)
    return pl.pallas_call(
        mlp_kernel,
        out_shape=[
            shape(tokens, low),
            shape(attx.shape, low),
            shape((CORES, chips, chip_heads, model_width // CORES), low),
            shape(tokens, f32),
            shape((8, max(model_width, CORES * half_units)), f32),
            shape((2,) + matrix, low),
            shape((seq_rows, half_units), low),
        ],
        in_specs=[in_vmem()] * 3 + [in_hbm()] + [in_vmem()] * 4 + [in_hbm(), in_vmem(), in_vmem()],
        out_specs=[in_vmem()] * 5 + [in_hbm(), in_vmem()],
        scratch_shapes=[
            VMEM(w_out.shape, low),
            VMEM((2,) + matrix, low),
            VMEM((3, CORES) + matrix, low),
            VMEM(tokens, f32),
            VMEM(tokens, f32),
            VMEM((2, tok_rows, 1), f32),
            VMEM(tokens, low),
            VMEM(group, low),
            VMEM(wide, f32),
            VMEM(wide, f32),
            VMEM(wide, low),
            VMEM((2,) + group, low),
            VMEM((2, 3) + tokens, low),
            VMEM((2,) + tokens, low),
            VMEM((2,) + tokens, low),
            VMEM(tokens, f32),
            VMEM(tokens, f32),
            VMEM(tokens, low),
            VMEM(group, low),
            VMEM(wide, low),
            VMEM(wide, low),
            VMEM(wide, f32),
            VMEM((2, model_width, group_rows), low),
            VMEM((3,) + matrix, low),
            VMEM((seq_rows, half_units), low),
            VMEM(matrix, low),
            VMEM((3, seq_rows, half_units), low),
            VMEM((CORES, 1, half_units), f32),
            VMEM((CORES, 1, half_units), f32),
            dma(3), dma(3, 4), dma(3, 4), dma(3), dma(3), line_dma(), line_dma(), dma(4), dma(4),
            line_dma(), line_dma(), dma(4), dma(4), dma(3), dma(3), dma(4), dma(4), dma(4), dma(4),
        ],
        compiler_params=pltpu.CompilerParams(
            collective_id=2, has_side_effects=True, vmem_limit_bytes=LIMIT
        ),
        name="mlp",
    )(
        attx, states, cotangent, w_out, alpha_attn, alpha_mlp, gain_u, gain_v, w_up, w_gate, low_down
    )


def back_kernel(
    grad_attx, from_half, grad_down, from_grad_out, small_in, from_raw, from_query, from_both, from_att,
    from_inv, from_states, from_qkv, qk_gain, places, grad_direct,
    grad_states, out_mlp, out_attn, feature, unit,
    grad_half, grad_w_out, raw, query, both, att, inverse, states_all, w_qkv, att_low, heads_low, to_keys, swap_low, swap_kv, grad_heads, grad_sides, part, sums, via, passed, total, turned,
    grad_q, half_q, seq_q, line_q, wide_q, half_o, pair_o, seq_got, seq_held, seq_last, seq_low, q_got, q_held, q_last, line_got, wide,
    wide_o, small, small_pair, small_seq, dots, small_all, flat_q, sides_q, key_pos,
    local_sem, load_sem, a_send, a_recv, s_send, s_recv, o_send, o_recv, kv_send, kv_recv, r_send, r_recv,
    qt_send, qt_recv, qs_send, qs_recv, qz_send, qz_recv, z_send, z_recv, f_send, f_recv,
    p_send, p_recv, t_send, t_recv,
):
    seq, chip, core = place_of()
    tok_rows, model_width = grad_direct.shape
    heads = qk_gain.shape[0]
    head_cols = heads * HEAD_DIM
    group_rows = CHIPS * tok_rows
    half_units = grad_half.shape[2]
    seq_rows = seq_low.shape[1]
    chip_rows = seq_rows // CHIPS
    rows = chip_rows // CORES
    part_cols = head_cols // CORES
    ff_width = out_mlp.shape[1] // 3
    scale = math.sqrt(HEAD_DIM)
    block = rows_at(chip, tok_rows)
    f32, low = jnp.float32, jnp.bfloat16
    loads = [
        begin(pltpu.make_async_copy(src, dst, load_sem.at[at]))
        for at, (src, dst) in enumerate(
            (
                (from_query, query), (from_both, both), (from_inv, inverse), (from_att, att), (from_raw, raw),
                (from_grad_out, grad_w_out), (from_states, states_all), (from_half, grad_half), (from_qkv, w_qkv),
            )
        )
    ]
    meet()
    waits = []
    line = []
    for step in STEPS:
        device, other = chip_peer(step)
        line.append(begin(remote(grad_attx.at[other], att_low.at[block], a_send.at[step], a_recv.at[step], device)))
    att_low[block, :] = grad_attx[chip]
    key_positions(places, key_pos, tok_rows)
    pair = begin(remote(from_grad_out.at[1 - core], pair_o, o_send.at[0], o_recv.at[0], twin()))
    onward = {}

    def to_chips(which, src):
        onward[which] = [
            begin(remote(src.at[rows_at(chip_peer(step)[1], chip_rows)], line_got.at[which, chip], z_send.at[which, step], z_recv.at[which, step], chip_peer(step)[0]))
            for step in STEPS
        ]
        line_got[which, chip] = src[rows_at(chip, chip_rows), :]

    to_chips(2, grad_down)

    def cross(which, src):
        return fold_start(src, seq_got.at[which], seq_rows, s_send.at[which], s_recv.at[which])

    def cross_on(which, src, copies):
        return fold_relay(src, seq_got.at[which], seq_held.at[which], seq_last.at[which], seq_rows, copies, s_send.at[which], s_recv.at[which])

    def cross_end(which, src, copies, more):
        fold_end(src, seq_got.at[which], seq_last.at[which], seq_low.at[which], seq_rows, copies, more)

    crossing = [cross(0, from_half.at[0])]
    to_keys[...] = jnp.zeros_like(to_keys)
    dots[...] = jnp.zeros_like(dots)
    for copy in loads:
        copy.wait()
    turned[...] = states_all[...].T
    sources = (grad_half.at[0], grad_half.at[1], half_o)
    onwards = [cross_on(0, sources[0], crossing[0])]
    crossing.append(cross(1, from_half.at[1]))
    pair.wait_recv()
    for at in range(4):
        half_o[at * seq_rows : (at + 1) * seq_rows, :] = (
            grad_w_out[core, at].astype(f32) + pair_o[at].astype(f32)
        ).astype(low)
    tile = tok_rows
    tiles = CHIPS

    def raw_back(which, head, at, upstream):
        value = raw[which, head, at, :]
        unit, factor = unit_of(value)
        dots[head] += jnp.sum(upstream * unit, axis=0, keepdims=True)
        upstream = upstream * qk_gain[head]
        upstream = factor * (upstream - unit * jnp.sum(upstream * unit, axis=-1, keepdims=True))
        grad_heads[which, head, at, :] = upstream.astype(low)

    def one_block(step, carry):
        other = lax.rem(chip + CHIPS - step, CHIPS)
        at = rows_at(other, tok_rows)
        copy = remote(grad_attx.at[0], att_low.at[at], a_send.at[step], a_recv.at[step], device_on(other))
        if step > 0:
            copy.wait_recv()
        for head in range(heads):
            heads_low[head, at, :] = att_low[at, head * HEAD_DIM : (head + 1) * HEAD_DIM]
        allowed = kept_pairs(places, key_pos, other, core, tok_rows)

        def one_head(head, carry):
            rows_q = query[head, at, :]
            grad_att = heads_low[head, at, :]
            scores = jnp.concatenate([dot_nt(rows_q, both[half, 0, head]) for half in range(CORES)], axis=1)
            probs = jnp.exp(jnp.where(allowed, scores, NEG_LARGE)) * inverse[head, at, :]
            grad_prob = jnp.concatenate([dot_nt(grad_att, both[half, 1, head]) for half in range(CORES)], axis=1)
            row_dot = jnp.sum(grad_att.astype(f32) * att[head, at, :], axis=-1, keepdims=True)
            grad_scores = (probs * (grad_prob - row_dot)).astype(low)
            weights = probs.astype(low)
            to_query = jnp.zeros((tok_rows, HEAD_DIM), f32)
            for half in range(CORES):
                cols = slice(half * group_rows, (half + 1) * group_rows)
                to_query = to_query + dot(grad_scores[:, cols], both[half, 0, head])
                to_keys[half, 0, head] += dot_tn(grad_scores[:, cols], rows_q)
                to_keys[half, 1, head] += dot_tn(weights[:, cols], grad_att)
            raw_back(0, head, at, to_query * scale)
            return carry

        lax.fori_loop(0, heads, one_head, 0)
        return carry

    one_block(0, 0)
    cross_end(0, sources[0], crossing[0], onwards[0])
    to_chips(0, seq_low.at[0])
    one_block(1, 0)
    onwards.append(cross_on(1, sources[1], crossing[1]))
    crossing.append(cross(2, half_o))
    one_block(2, 0)
    one_block(3, 0)
    cross_end(1, sources[1], crossing[1], onwards[1])
    to_chips(1, seq_low.at[1])
    swap_low[...] = to_keys[1 - core].astype(low)
    swap = begin(remote(swap_low, swap_kv, kv_send.at[0], kv_recv.at[0], twin()))
    swap.wait()

    def one_key(index, carry):
        head = index // tiles
        at = rows_at(lax.rem(index, tiles), tile)
        mine = to_keys[core, 0, head, at, :] + swap_kv[0, head, at, :].astype(f32)
        raw_back(1, head, at, mine)
        value = to_keys[core, 1, head, at, :] + swap_kv[1, head, at, :].astype(f32)
        grad_heads[2, head, at, :] = value.astype(low)
        return carry

    lax.fori_loop(0, heads * tiles, one_key, 0)
    for which in range(3):
        full = jnp.concatenate([grad_heads[which, head] for head in range(heads)], axis=1)
        for half in range(CORES):
            grad_sides[half, :, which * part_cols : (which + 1) * part_cols] = full[:, half * part_cols : (half + 1) * part_cols]
    wide_tile = model_width // 5
    onwards.append(cross_on(2, half_o, crossing[2]))

    def down(index, carry):
        at = rows_at(index, wide_tile)
        part[:, at] = sum(dot_nt(grad_sides[half], w_qkv[half, at, :]) for half in range(CORES)).astype(low)
        return carry

    lax.fori_loop(0, 5, down, 0)
    reduce_start(part, tok_rows, sums, via, r_send, r_recv, False)

    def weight_grad(index, carry):
        half = index // 5
        at = rows_at(lax.rem(index, 5), wide_tile)
        grad_q[half, at, :] = dot(turned[at, :], grad_sides[half]).astype(low)
        return carry

    lax.fori_loop(0, CORES * 5, weight_grad, 0)
    swap_q = begin(remote(grad_q.at[1 - core], half_q, qt_send.at[0], qt_recv.at[0], twin()))
    swap_q.wait()
    half_q[...] = (grad_q[core].astype(f32) + half_q[...].astype(f32)).astype(low)
    crossing_q = fold_start(half_q, q_got, seq_rows, qs_send, qs_recv)
    cross_end(2, half_o, crossing[2], onwards[2])
    to_chips(3, seq_low.at[2])
    reduce_relay(part, tok_rows, sums, via, passed, r_send, r_recv)
    small[...] = small_in[...]
    small[4:5, :head_cols] = jnp.concatenate([dots[head] for head in range(heads)], axis=1)
    swap_s = begin(remote(small, small_pair, t_send.at[0], t_recv.at[0], twin()))
    more_q = fold_relay(half_q, q_got, q_held, q_last, seq_rows, crossing_q, qs_send, qs_recv)
    fold_end(half_q, q_got, q_last, seq_q, seq_rows, crossing_q, more_q)
    onward_q = []
    for step in STEPS:
        device, other = chip_peer(step)
        onward_q.append(begin(remote(seq_q.at[rows_at(other, chip_rows)], line_q.at[chip], qz_send.at[step], qz_recv.at[step], device)))
    line_q[chip] = seq_q[rows_at(chip, chip_rows), :]

    mine = rows_at(core, rows)
    theirs = rows_at(1 - core, rows)
    swap_s.wait()
    small[...] = small[...] + small_pair[...]
    spread_s = [
        begin(remote(small, small_seq.at[step - 1], t_send.at[step], t_recv.at[step], seq_peer(step)[0]))
        for step in STEPS
    ]
    last, lasts = [], []
    for which in (2, 0, 1):
        for copy in onward[which]:
            copy.wait_recv()
        for at in range(CHIPS):
            wide[which, at] = line_got[which, at].astype(f32)
            start = which * ff_width + at * CORES * half_units + core * half_units
            there = out_mlp.at[:, pl.ds(pl.multiple_of(start, 128), half_units)]
            last.append(begin(remote(wide.at[which, at, theirs], there, f_send.at[which, at], f_recv.at[which, at], twin())))
            lasts.append(begin(pltpu.make_async_copy(wide.at[which, at, mine], there, local_sem.at[3 + which * CHIPS + at])))
    for copy in spread_s:
        copy.wait()
    small_pair[...] = small[...] + small_seq[0] + small_seq[1] + small_seq[2]
    small_all[chip] = small_pair[...]
    ends = to_line(small_pair, small_all.at[chip], p_send, p_recv)
    for copy in onward[3]:
        copy.wait_recv()
    whole = line_got[3, 0].astype(f32)
    for at in range(1, CHIPS):
        whole = whole + line_got[3, at].astype(f32)
    wide_o[...] = whole
    start = 3 * model_width + core * half_units
    there = out_attn.at[:, pl.ds(pl.multiple_of(start, 128), half_units)]
    last.append(begin(remote(wide_o.at[theirs], there, f_send.at[3, 0], f_recv.at[3, 0], twin())))
    lasts.append(begin(pltpu.make_async_copy(wide_o.at[mine], there, local_sem.at[15])))
    for copy in onward_q:
        copy.wait_recv()
    wide_q[...] = line_q[...].astype(f32)
    sides_q[core] = wide_q[:, mine, :]
    swap_q = begin(remote(wide_q.at[:, theirs], sides_q.at[core], f_send.at[3, 1], f_recv.at[3, 1], twin()))
    for copy in ends:
        copy.wait()
    alphas = small_all[0] + small_all[1] + small_all[2] + small_all[3]
    feature[1:3, :] = alphas[0:2, :]
    for at in range(CHIPS):
        feature[0:1, at * head_cols : (at + 1) * head_cols] = small_all[at, 4:5, :head_cols]
        width = CORES * half_units
        unit[:, at * width : (at + 1) * width] = small_all[at, 2:4, :width]
    swap_q.wait()
    for at in range(CHIPS):
        for half in range(CORES):
            for which in range(3):
                start = which * model_width + at * head_cols + half * part_cols
                flat_q[:, start : start + part_cols] = sides_q[half, at, :, which * part_cols : (which + 1) * part_cols]
    lasts.append(begin(pltpu.make_async_copy(flat_q, out_attn.at[:, pl.ds(0, 3 * model_width)], local_sem.at[16])))
    reduce_wait(part, tok_rows, sums, total, r_send, r_recv)
    grad_states[...] = (total[...] + grad_direct[...]).astype(low)
    for copy in last + lasts:
        copy.wait()
    reduce_drain(part, tok_rows, sums, r_send, r_recv, False)
    for copy in line + [pair] + sum(crossing + onwards + list(onward.values()), crossing_q + more_q + onward_q):
        copy.wait_send()


def back_call(
    grad_attx, grad_half, grad_down, grad_w_out, small_in, raw, query, both, att, inverse, states_all,
    w_qkv, qk_gain, places, grad_direct, rows,
):
    tok_rows, model_width = grad_direct.shape
    chips = grad_attx.shape[0]
    heads = qk_gain.shape[0]
    head_cols = heads * HEAD_DIM
    group_rows = chips * tok_rows
    half_units = grad_half.shape[2]
    half_cols = w_qkv.shape[2]
    chip_rows = CORES * rows
    seq_rows = chips * chip_rows
    f32, low = jnp.float32, jnp.bfloat16
    shape = jax.ShapeDtypeStruct
    per_head = (heads, group_rows, HEAD_DIM)
    return pl.pallas_call(
        back_kernel,
        out_shape=[
            shape((tok_rows, model_width), low),
            shape((rows, 3 * chips * CORES * half_units), f32),
            shape((rows, 4 * model_width), f32),
            shape((3, model_width), f32),
            shape((2, chips * CORES * half_units), f32),
        ],
        in_specs=[in_vmem(), in_hbm(), in_vmem(), in_hbm(), in_vmem()] + [in_hbm()] * 7 + [in_vmem(), in_smem(), in_vmem()],
        out_specs=[in_vmem(), in_hbm(), in_hbm(), in_vmem(), in_vmem()],
        scratch_shapes=[
            *(VMEM(value.shape, value.dtype) for value in (grad_half, grad_w_out, raw, query, both, att, inverse, states_all, w_qkv)),
            VMEM((group_rows, head_cols), low),
            VMEM(per_head, low),
            VMEM((CORES, 2) + per_head, f32),
            VMEM((2,) + per_head, low),
            VMEM((2,) + per_head, low),
            VMEM((3,) + per_head, low),
            VMEM((CORES, group_rows, half_cols), low),
            VMEM((group_rows, model_width), low),
            VMEM((3, tok_rows, model_width), low),
            VMEM((tok_rows, model_width), low),
            VMEM((tok_rows, model_width), low),
            VMEM((tok_rows, model_width), f32),
            VMEM((model_width, group_rows), low),
            VMEM((CORES, model_width, half_cols), low),
            VMEM((model_width, half_cols), low),
            VMEM((seq_rows, half_cols), low),
            VMEM((chips, chip_rows, half_cols), low),
            VMEM((chips, chip_rows, half_cols), f32),
            VMEM((4 * seq_rows, half_units), low),
            VMEM((4, seq_rows, half_units), low),
            VMEM((3, 2, 2, seq_rows // 2, half_units), low),
            VMEM((3, 2, seq_rows // 2, half_units), low),
            VMEM((3, 2, seq_rows // 2, half_units), low),
            VMEM((3, seq_rows, half_units), low),
            VMEM((2, 2, seq_rows // 2, half_cols), low),
            VMEM((2, seq_rows // 2, half_cols), low),
            VMEM((2, seq_rows // 2, half_cols), low),
            VMEM((4, chips, chip_rows, half_units), low),
            VMEM((3, chips, chip_rows, half_units), f32),
            VMEM((chip_rows, half_units), f32),
            VMEM(small_in.shape, f32),
            VMEM(small_in.shape, f32),
            VMEM((3,) + small_in.shape, f32),
            VMEM((heads, 1, HEAD_DIM), f32),
            VMEM((chips,) + small_in.shape, f32),
            VMEM((rows, 3 * model_width), f32),
            VMEM((CORES, chips, rows, half_cols), f32),
            VMEM((1, CORES * group_rows), jnp.int32),
            dma(17), dma(9), dma(4), dma(4), dma(3, 3, 2), dma(3, 3, 2), dma(1), dma(1), dma(1), dma(1),
            dma(4), dma(4), dma(1), dma(1), dma(3, 2), dma(3, 2), dma(4), dma(4), dma(4, 4), dma(4, 4),
            dma(4, 4), dma(4, 4), dma(4), dma(4), dma(4), dma(4),
        ],
        compiler_params=pltpu.CompilerParams(
            collective_id=3, has_side_effects=True, vmem_limit_bytes=LIMIT
        ),
        name="back",
    )(
        grad_attx, grad_half, grad_down, grad_w_out, small_in, raw, query, both, att, inverse, states_all,
        w_qkv, qk_gain, places, grad_direct,
    )


def finish_kernel(*refs):
    count = len(refs) // 3
    sources, results, held = refs[:count], refs[count : 2 * count], refs[2 * count : 3 * count]
    sem = refs[-1]
    copies = [begin(pltpu.make_async_copy(sources[at], held[at], sem.at[0, at])) for at in range(count)]
    leaving = []
    for at in range(count):
        copies[at].wait()
        leaving.append(begin(pltpu.make_async_copy(held[at], results[at], sem.at[1, at])))
    for copy in leaving:
        copy.wait()


def finish_call(*arrays):
    return pl.pallas_call(
        finish_kernel,
        out_shape=[jax.ShapeDtypeStruct(array.shape, array.dtype) for array in arrays],
        in_specs=[in_hbm()] * len(arrays),
        out_specs=[in_hbm()] * len(arrays),
        scratch_shapes=[VMEM(array.shape, array.dtype) for array in arrays] + [dma(2, len(arrays))],
        compiler_params=pltpu.CompilerParams(vmem_limit_bytes=LIMIT),
        name="finish",
    )(*arrays)


def shards_split(states, cotangent, attn_weights, mlp_weights, feature_gains, unit_gains, block_place):
    tok_rows, model_width = states.shape
    ff_width = unit_gains.shape[0]
    n_seq, n_ctx = lax.axis_size("seq"), lax.axis_size("ctx")
    chips = n_ctx // CORES
    chip = lax.axis_index("ctx") // CORES
    heads = HEADS // chips
    head_cols = heads * HEAD_DIM
    units = ff_width // chips
    rows = attn_weights.shape[0]
    qk_gain = lax.dynamic_slice_in_dim(feature_gains[:, 0], chip * head_cols, head_cols)
    qk_gain = qk_gain.reshape(heads, 1, HEAD_DIM)
    states_all, w_qkv, w_out, w_up, w_gate, low_down, raw, query, both, att, inverse, attx = attend_call(
        states, attn_weights, mlp_weights, qk_gain, block_place
    )
    gain_u = lax.dynamic_slice_in_dim(unit_gains[:, 0], chip * units, units)
    gain_v = lax.dynamic_slice_in_dim(unit_gains[:, 1], chip * units, units) * math.sqrt(D)
    out_low, grad_attx, grad_w_out, grad_direct, small, grad_half, grad_down = mlp_call(
        attx, states, cotangent, w_out, feature_gains[:, 1].reshape(1, model_width),
        feature_gains[:, 2].reshape(1, model_width), gain_u.reshape(CORES, 1, units // CORES),
        gain_v.reshape(CORES, 1, units // CORES), w_up, w_gate, low_down,
    )
    grad_states, grad_mlp, grad_attn, feature, unit = back_call(
        grad_attx, grad_half, grad_down, grad_w_out, small, raw, query, both, att, inverse, states_all,
        w_qkv, qk_gain, block_place, grad_direct, rows,
    )
    out_low, grad_states, grad_mlp, grad_attn = finish_call(out_low, grad_states, grad_mlp, grad_attn)
    rank = lax.axis_index(ALL)
    unit_rows_own = ff_width // (n_seq * n_ctx)
    return (
        out_low,
        grad_states,
        grad_attn,
        grad_mlp,
        lax.dynamic_slice_in_dim(feature, rank * rows, rows, axis=1).T,
        lax.dynamic_slice_in_dim(unit, rank * unit_rows_own, unit_rows_own, axis=1).T,
    )


def solution(mesh):
    in_specs = (
        P(("seq", "ctx"), None),
        P(("seq", "ctx"), None),
        P(("seq", "ctx"), None),
        P(("seq", "ctx"), None),
        P(),
        P(),
        P("seq", None),
    )
    out_specs = (
        P(("seq", "ctx"), None),
        P(("seq", "ctx"), None),
        P(("seq", "ctx"), None),
        P(("seq", "ctx"), None),
        P(("seq", "ctx"), None),
        P(("seq", "ctx"), None),
    )
    chips = mesh.shape["ctx"] // CORES
    shards = shards_split if fits(mesh.shape["seq"], chips) else shards_general
    return jax.shard_map(shards, mesh=mesh, in_specs=in_specs, out_specs=out_specs, check_vma=False)
```

```python
import functools
import math

import jax
import jax.numpy as jnp
from jax import lax
from jax.experimental import pallas as pl
from jax.experimental.pallas import tpu as pltpu
from jax.sharding import PartitionSpec as P

D = 1280
HEADS = 20
HEAD_DIM = 64


EPSILON = 1e-06
NEG_LARGE = -1e30


def unit_rows(values_in):
    factor = lax.rsqrt(jnp.sum(values_in * values_in, axis=-1, keepdims=True) + EPSILON)
    return (values_in * factor, factor)


def unit_back(normed, factor, upstream):
    return factor * (upstream - normed * jnp.sum(upstream * normed, axis=-1, keepdims=True))


def contract_rows(left_mat, right_mat):
    return lax.dot_general(
        left_mat, right_mat, (((0,), (0,)), ((), ())), preferred_element_type=jnp.float32
    )


def contract_cols(left_mat, right_mat):
    return lax.dot_general(
        left_mat, right_mat, (((1,), (1,)), ((), ())), preferred_element_type=jnp.float32
    )


def shards_general(states, cotangent, attn_weights, mlp_weights, feature_gains, unit_gains, block_place):
    tok_rows = states.shape[0]
    model_width = states.shape[1]
    ff_width = unit_gains.shape[0]
    score_scale = math.sqrt(HEAD_DIM)
    gate_factor = unit_gains[:, 1] * math.sqrt(D)
    w_attn = lax.all_gather(attn_weights.astype(jnp.bfloat16), ("seq", "ctx"), axis=0, tiled=True)
    w_mlp = lax.all_gather(mlp_weights.astype(jnp.bfloat16), ("seq", "ctx"), axis=0, tiled=True)
    states_full = states.astype(jnp.float32)
    projected = jnp.dot(states, w_attn[:, : 3 * model_width], preferred_element_type=jnp.float32)
    head_shape = (tok_rows, HEADS, HEAD_DIM)
    qk_gain = feature_gains[:, 0].reshape(HEADS, HEAD_DIM)
    query_unit, query_factor = unit_rows(projected[:, :model_width].reshape(head_shape))
    key_unit, key_factor = unit_rows(
        projected[:, model_width : 2 * model_width].reshape(head_shape)
    )
    query_low = (query_unit * qk_gain).astype(jnp.bfloat16)
    key_low = (key_unit * qk_gain).astype(jnp.bfloat16).reshape(tok_rows, model_width)
    value_low = projected[:, 2 * model_width :].astype(jnp.bfloat16)
    keys_all, values_all = (
        lax.all_gather(key_low, "ctx", axis=0, tiled=True),
        lax.all_gather(value_low, "ctx", axis=0, tiled=True),
    )
    seq_len = keys_all.shape[0]
    ctx_lanes = jnp.arange(lax.axis_size("ctx"), dtype=jnp.int32)
    places = block_place[0]
    own_block = jnp.sum(jnp.where(ctx_lanes == lax.axis_index("ctx"), places, 0))
    query_pos = own_block * tok_rows + jnp.arange(tok_rows, dtype=jnp.int32)
    key_index = jnp.arange(seq_len, dtype=jnp.int32)
    key_owner = key_index // tok_rows
    key_pos = (
        jnp.sum(jnp.where(key_owner[:, None] == ctx_lanes[None, :], places[None, :], 0), axis=1)
        * tok_rows
        + key_index % tok_rows
    )
    kblock = min(512, seq_len)
    nblocks = seq_len // kblock
    key_blocks = keys_all.reshape(nblocks, kblock, HEADS, HEAD_DIM)
    value_blocks = values_all.reshape(nblocks, kblock, HEADS, HEAD_DIM)
    pos_blocks = key_pos.reshape(nblocks, kblock)

    def block_scores(key_rows, key_places):
        raw_scores = score_scale * jnp.einsum(
            "qhd,khd->hqk", query_low, key_rows, preferred_element_type=jnp.float32
        )
        allowed = key_places[None, None, :] <= query_pos[None, :, None]
        return (raw_scores, allowed)

    def max_step(running, inputs):
        running_max, running_sum = running
        key_rows, key_places = inputs
        raw_scores, allowed = block_scores(key_rows, key_places)
        masked = jnp.where(allowed, raw_scores, NEG_LARGE)
        new_max = jnp.maximum(running_max, jnp.max(masked, axis=-1))
        powered = jnp.where(allowed, jnp.exp(masked - new_max[..., None]), 0.0)
        running_sum = running_sum * jnp.exp(running_max - new_max) + jnp.sum(powered, axis=-1)
        return ((new_max, running_sum), None)

    start_max = jnp.full((HEADS, tok_rows), NEG_LARGE, jnp.float32)
    start_sum = jnp.zeros((HEADS, tok_rows), jnp.float32)
    (final_max, final_sum), _ = lax.scan(max_step, (start_max, start_sum), (key_blocks, pos_blocks))
    log_total = final_max + jnp.log(final_sum)

    def value_step(accumulated, inputs):
        key_rows, value_rows, key_places = inputs
        raw_scores, allowed = block_scores(key_rows, key_places)
        weights_low = jnp.where(allowed, jnp.exp(raw_scores - log_total[..., None]), 0.0).astype(
            jnp.bfloat16
        )
        accumulated = accumulated + jnp.einsum(
            "hqk,khd->qhd", weights_low, value_rows, preferred_element_type=jnp.float32
        )
        return (accumulated, None)

    attended, _ = lax.scan(
        value_step, jnp.zeros(head_shape, jnp.float32), (key_blocks, value_blocks, pos_blocks)
    )
    attended_low = attended.reshape(tok_rows, model_width).astype(jnp.bfloat16)
    branch_attn = jnp.dot(
        attended_low, w_attn[:, 3 * model_width :], preferred_element_type=jnp.float32
    )
    attn_unit, attn_factor = unit_rows(branch_attn)
    alpha_attn = feature_gains[:, 1]
    mixed_one, mix_factor = unit_rows(states_full + alpha_attn * (attn_unit - states_full))
    mixed_low = mixed_one.astype(jnp.bfloat16)
    up_gate = jnp.dot(mixed_low, w_mlp[:, : 2 * ff_width], preferred_element_type=jnp.float32)
    up_scaled = up_gate[:, :ff_width] * unit_gains[:, 0]
    gate_scaled = up_gate[:, ff_width:] * gate_factor
    sigmoid_gate = jax.nn.sigmoid(gate_scaled)
    activated = gate_scaled * sigmoid_gate
    hidden = (activated * up_scaled).astype(jnp.bfloat16)
    branch_mlp = contract_cols(hidden, w_mlp[:, 2 * ff_width :])
    mlp_unit, mlp_factor = unit_rows(branch_mlp)
    alpha_mlp = feature_gains[:, 2]
    out_full, out_factor = unit_rows(mixed_one + alpha_mlp * (mlp_unit - mixed_one))
    grad_mix_two = unit_back(out_full, out_factor, cotangent.astype(jnp.float32))
    grad_alpha_m = jnp.sum(grad_mix_two * (mlp_unit - mixed_one), axis=0)
    grad_branch_mlp = unit_back(mlp_unit, mlp_factor, grad_mix_two * alpha_mlp).astype(jnp.bfloat16)
    grad_hidden = jnp.dot(
        grad_branch_mlp, w_mlp[:, 2 * ff_width :], preferred_element_type=jnp.float32
    )
    grad_up_scaled = grad_hidden * activated
    grad_gate_scaled = (
        grad_hidden * up_scaled * sigmoid_gate * (1.0 + gate_scaled * (1.0 - sigmoid_gate))
    )
    grad_s_u = jnp.sum(grad_up_scaled * up_gate[:, :ff_width], axis=0)
    grad_s_v = jnp.sum(grad_gate_scaled * up_gate[:, ff_width:], axis=0) * math.sqrt(D)
    grad_up_gate = jnp.concatenate(
        [grad_up_scaled * unit_gains[:, 0], grad_gate_scaled * gate_factor], axis=1
    ).astype(jnp.bfloat16)
    grad_mixed_one = grad_mix_two * (1.0 - alpha_mlp) + contract_cols(
        grad_up_gate, w_mlp[:, : 2 * ff_width]
    )
    grad_mix_one = unit_back(mixed_one, mix_factor, grad_mixed_one)
    grad_alpha_a = jnp.sum(grad_mix_one * (attn_unit - states_full), axis=0)
    grad_branch_attn = unit_back(attn_unit, attn_factor, grad_mix_one * alpha_attn).astype(
        jnp.bfloat16
    )
    grad_attended = (
        contract_cols(grad_branch_attn, w_attn[:, 3 * model_width :])
        .astype(jnp.bfloat16)
        .reshape(head_shape)
    )
    row_dots = jnp.einsum("qhd,qhd->hq", grad_attended.astype(jnp.float32), attended)

    def grad_step(grad_query, inputs):
        key_rows, value_rows, key_places = inputs
        raw_scores, allowed = block_scores(key_rows, key_places)
        probabilities = jnp.where(allowed, jnp.exp(raw_scores - log_total[..., None]), 0.0)
        grad_prob = jnp.einsum(
            "qhd,khd->hqk", grad_attended, value_rows, preferred_element_type=jnp.float32
        )
        grad_scores = (probabilities * (grad_prob - row_dots[..., None])).astype(jnp.bfloat16)
        grad_query = grad_query + score_scale * jnp.einsum(
            "hqk,khd->qhd", grad_scores, key_rows, preferred_element_type=jnp.float32
        )
        key_terms = score_scale * jnp.einsum(
            "hqk,qhd->khd", grad_scores, query_low, preferred_element_type=jnp.float32
        )
        value_terms = jnp.einsum(
            "hqk,qhd->khd",
            probabilities.astype(jnp.bfloat16),
            grad_attended,
            preferred_element_type=jnp.float32,
        )
        return (grad_query, (key_terms, value_terms))

    grad_query_low, (key_terms, value_terms) = lax.scan(
        grad_step, jnp.zeros(head_shape, jnp.float32), (key_blocks, value_blocks, pos_blocks)
    )
    key_terms = key_terms.reshape(seq_len, model_width)
    value_terms = value_terms.reshape(seq_len, model_width)
    own_key_grad, own_value_grad = (
        lax.psum_scatter(
            key_terms.astype(jnp.bfloat16), "ctx", scatter_dimension=0, tiled=True
        ).astype(jnp.float32),
        lax.psum_scatter(
            value_terms.astype(jnp.bfloat16), "ctx", scatter_dimension=0, tiled=True
        ).astype(jnp.float32),
    )
    grad_key_low = own_key_grad.reshape(head_shape)
    grad_s_qk = jnp.sum(grad_query_low * query_unit + grad_key_low * key_unit, axis=0).reshape(
        model_width
    )
    grad_query_raw = unit_back(query_unit, query_factor, grad_query_low * qk_gain).reshape(
        tok_rows, model_width
    )
    grad_key_raw = unit_back(key_unit, key_factor, grad_key_low * qk_gain).reshape(
        tok_rows, model_width
    )
    grad_projected = jnp.concatenate([grad_query_raw, grad_key_raw, own_value_grad], axis=1).astype(
        jnp.bfloat16
    )
    grad_states = grad_mix_one * (1.0 - alpha_attn) + contract_cols(
        grad_projected, w_attn[:, : 3 * model_width]
    )
    feature_total = jnp.stack([grad_s_qk, grad_alpha_a, grad_alpha_m], axis=1)
    unit_fold = jnp.stack([grad_s_u, grad_s_v], axis=1).reshape(
        model_width, 2 * ff_width // model_width
    )
    attn_cols = 4 * model_width
    mlp_cols = 3 * ff_width
    attn_share = lax.psum_scatter(
        jnp.concatenate(
            [
                contract_rows(states, grad_projected),
                contract_rows(attended_low, grad_branch_attn),
                feature_total,
            ],
            axis=1,
        ),
        ("seq", "ctx"),
        scatter_dimension=0,
        tiled=True,
    )
    mlp_share = lax.psum_scatter(
        jnp.concatenate(
            [
                contract_rows(mixed_low, grad_up_gate),
                contract_rows(grad_branch_mlp, hidden),
                unit_fold,
            ],
            axis=1,
        ),
        ("seq", "ctx"),
        scatter_dimension=0,
        tiled=True,
    )
    grad_attn = attn_share[:, :attn_cols]
    grad_feature = attn_share[:, attn_cols:]
    grad_mlp = mlp_share[:, :mlp_cols]
    grad_unit = mlp_share[:, mlp_cols:].reshape(
        unit_gains.shape[0] // lax.axis_size(("seq", "ctx")), 2
    )
    return (
        out_full.astype(jnp.bfloat16),
        grad_states.astype(jnp.bfloat16),
        grad_attn,
        grad_mlp,
        grad_feature,
        grad_unit,
    )


CORES = 2
ALL = ("seq", "ctx")


def fits(n_seq, chips):
    return n_seq == 4 and chips == 4 and HEADS % chips == 0


MESH = pl.DeviceIdType.MESH
VMEM = pltpu.VMEM
CHIPS = 4
STEPS = (1, 2, 3)
LIMIT = 60 * 1024 * 1024


def place_of():
    seq = lax.axis_index("seq")
    ctx = lax.axis_index("ctx")
    return seq, ctx // CORES, ctx % CORES


def chip_peer(step):
    seq, chip, core = place_of()
    other = lax.rem(chip + step, CHIPS)
    return (seq, other * CORES + core), other


def seq_peer(step):
    seq, chip, core = place_of()
    other = seq ^ step
    return (other, chip * CORES + core), other


def twin():
    seq, chip, core = place_of()
    return (seq, chip * CORES + 1 - core)


def meet():
    devices = [chip_peer(step)[0] for step in STEPS] + [seq_peer(step)[0] for step in STEPS] + [twin()]
    gate = pltpu.get_barrier_semaphore()
    for device in devices:
        pl.semaphore_signal(gate, inc=1, device_id=device, device_id_type=MESH)
    pl.semaphore_wait(gate, len(devices))


def remote(src, dst, send, recv, device):
    return pltpu.make_async_remote_copy(
        src_ref=src, dst_ref=dst, send_sem=send, recv_sem=recv, device_id=device,
        device_id_type=MESH,
    )


def begin(copy):
    copy.start()
    return copy


def rows_at(index, count):
    return pl.ds(pl.multiple_of(index * count, count), count)


def device_on(chip):
    seq, _, core = place_of()
    return (seq, chip * CORES + core)


def when(condition, action):
    pl.when(condition)(action)


PIECES = 2


def piece_at(block, piece, count):
    step = count // PIECES
    return pl.ds(pl.multiple_of(block * count + piece * step, step), step)


def gather_copy(src, everything, count, block, side, hop, piece, send, recv):
    chip = place_of()[1]
    there = everything.at[piece_at(block, piece, count)]
    near = chip + 1 if side == 0 else chip - 1
    here = there if src is None else src.at[piece_at(0, piece, count)]
    return remote(here, there, send.at[side, hop, piece], recv.at[side, hop, piece], device_on(near))


def gather_start(src, everything, count, send, recv):
    chip = place_of()[1]
    for piece in range(PIECES):
        for side in range(2):
            copy = gather_copy(src, everything, count, chip, side, 0, piece, send, recv)
            when(chip < CHIPS - 1 if side == 0 else chip > 0, copy.start)


def gather_hop(everything, count, hop, send, recv):
    chip = place_of()[1]
    for piece in range(PIECES):
        for side in range(2):
            block = chip - hop if side == 0 else chip + hop

            def pass_on(side=side, piece=piece, block=block):
                gather_copy(None, everything, count, block, side, hop - 1, piece, send, recv).wait_recv()
                if hop < CHIPS - 1:
                    copy = gather_copy(None, everything, count, block, side, hop, piece, send, recv)
                    when(chip < CHIPS - 1 if side == 0 else chip > 0, copy.start)

            when(block >= 0 if side == 0 else block < CHIPS, pass_on)


def gather_drain(everything, count, send, recv):
    chip = place_of()[1]
    for hop in range(CHIPS - 1):
        for piece in range(PIECES):
            for side in range(2):
                copy = gather_copy(None, everything, count, chip, side, hop, piece, send, recv)
                block = chip - hop if side == 0 else chip + hop
                sent = (block >= 0) & (chip < CHIPS - 1) if side == 0 else (block < CHIPS) & (chip > 0)
                when(sent, copy.wait_send)


def inside_line():
    chip = place_of()[1]
    return (chip > 0) & (chip < CHIPS - 1)


def spans_line(other):
    return abs(place_of()[1] - other) == CHIPS - 1


def reduce_start(part, count, sums, via, send, recv, ahead=True):
    chip = place_of()[1]
    near = jnp.where(chip == 0, 1, CHIPS - 2)
    first = remote(part.at[rows_at(CHIPS - 1 - chip, count)], via, send.at[0], recv.at[0], device_on(near))

    def begin_far():
        first.start()
        if ahead:
            first.wait_send()

    when(jnp.logical_not(inside_line()), begin_far)
    for step in STEPS:
        device, other = chip_peer(step)
        copy = remote(part.at[rows_at(other, count)], sums.at[step - 1], send.at[step], recv.at[step], device)
        if step == 2:
            when(jnp.logical_not(inside_line()), copy.start)
        else:
            when(jnp.logical_not(spans_line(other)), copy.start)


def reduce_relay(part, count, sums, via, mixed, send, recv):
    chip = place_of()[1]
    other = lax.rem(chip + 2, CHIPS)
    copy = remote(mixed, sums.at[1], send.at[2], recv.at[2], device_on(other))

    def pass_on():
        remote(mixed, via, send.at[0], recv.at[0], device_on(other)).wait_recv()
        mixed[...] = (
            part[rows_at(other, count), :].astype(jnp.float32) + via[...].astype(jnp.float32)
        ).astype(mixed.dtype)
        copy.start()

    when(inside_line(), pass_on)


def reduce_wait(part, count, sums, total, send, recv):
    chip = place_of()[1]
    total[...] = part[rows_at(chip, count), :].astype(jnp.float32)
    for step in (1, 3, 2):
        source = lax.rem(chip + CHIPS - step, CHIPS)

        def add(step=step, source=source):
            here = sums.at[step - 1]
            remote(here, here, send.at[step], recv.at[step], device_on(source)).wait_recv()
            total[...] += sums[step - 1].astype(jnp.float32)

        when(jnp.logical_not(spans_line(source)), add)


def reduce_drain(part, count, sums, send, recv, ahead=True):
    rows = part.at[rows_at(0, count)]
    for step in STEPS:
        device, other = chip_peer(step)
        copy = remote(rows, sums.at[step - 1], send.at[step], recv.at[step], device)
        when(jnp.logical_not(spans_line(other)), copy.wait_send)
    if not ahead:
        copy = remote(rows, sums.at[0], send.at[0], recv.at[0], device_on(place_of()[1]))
        when(jnp.logical_not(inside_line()), copy.wait_send)


def side_peer(side):
    return seq_peer(side + 1)


def seq_rows_at(block, side, count):
    half = count // 2
    return pl.ds(pl.multiple_of(block * count + side * half, half), half)


def spread_start(src, dst, count, send, recv):
    seq = place_of()[0]
    return [
        begin(remote(src, dst.at[rows_at(seq, count)], send.at[side], recv.at[side], side_peer(side)[0]))
        for side in range(2)
    ]


def spread_relay(dst, count, send, recv):
    copies = []
    for side in range(2):
        block = side_peer(side)[1]
        whole = dst.at[rows_at(block, count)]
        remote(whole, whole, send.at[side], recv.at[side], side_peer(side)[0]).wait_recv()
        part = dst.at[seq_rows_at(block, side, count)]
        copies.append(begin(remote(part, part, send.at[2 + side], recv.at[2 + side], side_peer(1 - side)[0])))
    return copies


def fold_start(src, got, count, send, recv):
    seq = place_of()[0]
    copies = []
    for side in range(2):
        device, other = side_peer(side)
        for at, block in enumerate((other, seq ^ 3)):
            here = src.at[seq_rows_at(block, side, count)]
            copies.append(begin(remote(here, got.at[side, at], send.at[side, at], recv.at[side, at], device)))
    return copies


def fold_relay(src, got, held, last, count, copies, send, recv):
    more = []
    for side in range(2):
        device, other = side_peer(1 - side)
        copies[2 * side + 1].wait_recv()
        rows = seq_rows_at(other, side, count)
        held[side] = (src[rows, :].astype(jnp.float32) + got[side, 1].astype(jnp.float32)).astype(held.dtype)
        more.append(begin(remote(held.at[side], last.at[side], send.at[2, side], recv.at[2, side], device)))
    return more


def fold_end(src, got, last, out, count, copies, more):
    seq = place_of()[0]
    half = count // 2
    for side in range(2):
        copies[2 * side].wait_recv()
        more[side].wait_recv()
        rows = seq_rows_at(seq, side, count)
        out[side * half : (side + 1) * half, :] = (
            src[rows, :].astype(jnp.float32) + got[side, 0].astype(jnp.float32) + last[side].astype(jnp.float32)
        ).astype(out.dtype)


def to_line(src, there, send, recv):
    return [
        begin(remote(src, there, send.at[step], recv.at[step], chip_peer(step)[0])) for step in STEPS
    ]


def dot(left, right):
    return jnp.dot(left, right, preferred_element_type=jnp.float32)


def dot_nt(left, right):
    return lax.dot_general(
        left, right, (((1,), (1,)), ((), ())), preferred_element_type=jnp.float32
    )


def dot_tn(left, right):
    return lax.dot_general(
        left, right, (((0,), (0,)), ((), ())), preferred_element_type=jnp.float32
    )


def dma(*shape):
    return pltpu.SemaphoreType.DMA(shape)


def line_dma():
    return dma(2, CHIPS, PIECES)


def in_vmem():
    return pl.BlockSpec(memory_space=pltpu.VMEM)


def in_hbm():
    return pl.BlockSpec(memory_space=pl.ANY)


def key_positions(places, key_pos, tok_rows):
    lanes = lax.broadcasted_iota(jnp.int32, (1, tok_rows), 1)
    for at_core in range(CORES):
        for at_chip in range(CHIPS):
            start = (at_core * CHIPS + at_chip) * tok_rows
            key_pos[:, start : start + tok_rows] = places[0, CORES * at_chip + at_core] * tok_rows + lanes


def kept_pairs(places, key_pos, block, core, tok_rows):
    down = lax.broadcasted_iota(jnp.int32, (tok_rows, 1), 0)
    return key_pos[...] <= places[0, CORES * block + core] * tok_rows + down


def attend_kernel(
    states, attn_src, mlp_src, qk_gain, places,
    to_states, to_qkv, to_out, w_up, w_gate, low_down, to_raw, to_query, to_both, to_att, to_inv, attx,
    states_all, w_qkv, w_out, raw_out, query_out, both, att_out, inv_out, src_q, stage_q, low_q, stage_o, low_o, stage_m, low_m, raw, att_low, key_pos,
    local_sem, keep_sem, att_sem, x_send, x_recv, q_send, q_recv, mt_send, mt_recv, wz_send, wz_recv,
    ws_send, ws_recv, wt_send, wt_recv, oz_send, oz_recv, os_send, os_recv, m_send, m_recv,
    ms_send, ms_recv, kv_send, kv_recv, a_send, a_recv,
):
    seq, chip, core = place_of()
    rows = attn_src.shape[0]
    tok_rows, model_width = states.shape
    heads = qk_gain.shape[0]
    head_cols = heads * HEAD_DIM
    part_cols = head_cols // CORES
    group_rows = tok_rows * CHIPS
    chip_rows = CORES * rows
    seq_rows = CHIPS * chip_rows
    half_units = w_up.shape[1]
    half_width = model_width // CORES
    ff_width = mlp_src.shape[1] // 3
    low = jnp.bfloat16
    for at in range(CHIPS):
        for half in range(CORES):
            for which in range(3):
                start = which * model_width + at * head_cols + half * part_cols
                src_q[at, half, :, which * part_cols : (which + 1) * part_cols] = attn_src[:, start : start + part_cols]
    meet()
    block = rows_at(chip, tok_rows)
    mine = rows_at(core, rows)
    half_at = pl.ds(pl.multiple_of(3 * model_width + core * half_width, 128), half_width)
    other_at = pl.ds(pl.multiple_of(3 * model_width + (1 - core) * half_width, 128), half_width)
    swap_o = begin(remote(attn_src.at[:, other_at], stage_o.at[mine], q_send.at[1], q_recv.at[1], twin()))
    swap_q = begin(remote(src_q.at[:, 1 - core], stage_q.at[:, mine], q_send.at[0], q_recv.at[0], twin()))
    stage_o[mine, :] = attn_src[:, half_at]
    stage_q[:, mine, :] = src_q[:, core]
    m_swaps, m_keeps = [], []
    for part in range(3):
        for at in range(CHIPS):
            start = part * ff_width + at * CORES * half_units
            theirs = pl.ds(pl.multiple_of(start + (1 - core) * half_units, 128), half_units)
            ours = pl.ds(pl.multiple_of(start + core * half_units, 128), half_units)
            there = stage_m.at[part, at, mine]
            m_swaps.append(begin(remote(mlp_src.at[:, theirs], there, mt_send.at[part, at], mt_recv.at[part, at], twin())))
            m_keeps.append(begin(pltpu.make_async_copy(mlp_src.at[:, ours], there, local_sem.at[part * CHIPS + at])))
    my_rows = rows_at(seq * CHIPS + chip, chip_rows)
    seq_at = rows_at(seq, seq_rows)
    swap_o.wait()
    low_o[...] = stage_o[...].astype(low)
    o_line = to_line(low_o, w_out.at[core, my_rows], oz_send, oz_recv)
    w_out[core, my_rows, :] = low_o[...]
    swap_q.wait()
    low_q[...] = stage_q[...].astype(low)
    line = []
    for step in STEPS:
        device, other = chip_peer(step)
        line.append(begin(remote(low_q.at[other], w_qkv.at[core, my_rows], wz_send.at[step], wz_recv.at[step], device)))
    w_qkv[core, my_rows, :] = low_q[chip]
    states_all[block, :] = states[...]
    key_positions(places, key_pos, tok_rows)
    gather_start(states, states_all, tok_rows, x_send, x_recv)
    for copy in line:
        copy.wait_recv()

    def across(whole, send, recv):
        return spread_start(whole.at[seq_at], whole, seq_rows, send, recv)

    q_across = across(w_qkv.at[core], ws_send, ws_recv)
    for copy in m_keeps:
        copy.wait()
    for copy in m_swaps:
        copy.wait()
    low_m[...] = stage_m[:2].astype(low)
    low_down[...] = stage_m[2].astype(low)
    gather_hop(states_all, tok_rows, 1, x_send, x_recv)
    more = spread_relay(w_qkv.at[core], seq_rows, ws_send, ws_recv)
    for copy in o_line:
        copy.wait_recv()
    o_across = across(w_out.at[core], os_send, os_recv)
    for copy in more:
        copy.wait_recv()
    q_across += more
    swap = begin(remote(w_qkv.at[core], w_qkv.at[core], wt_send.at[0], wt_recv.at[0], twin()))
    gather_hop(states_all, tok_rows, 2, x_send, x_recv)
    o_more = spread_relay(w_out.at[core], seq_rows, os_send, os_recv)
    gather_hop(states_all, tok_rows, 3, x_send, x_recv)
    here = rows_at(chip, chip_rows)

    def to_chips(part, there):
        return [
            begin(remote(low_m.at[part, chip_peer(step)[1]], there, m_send.at[part, step], m_recv.at[part, step], chip_peer(step)[0]))
            for step in STEPS
        ]

    m_line = to_chips(0, w_up.at[my_rows])
    w_up[my_rows, :] = low_m[0, chip]
    w_gate[here, :] = low_m[1, chip]
    swap.wait()
    kept = []

    def keep(src, dst):
        kept.append(begin(pltpu.make_async_copy(src, dst, keep_sem.at[len(kept)])))

    keep(states_all, to_states)
    keep(w_qkv, to_qkv)
    for half in range(CORES):
        value = dot(states_all[...], w_qkv[half])
        for which in range(3):
            start = which * head_cols + half * part_cols
            raw[:, start : start + part_cols] = value[:, which * part_cols : (which + 1) * part_cols]
    for head in reversed(range(3 * heads)):
        which, head = head // heads, head % heads
        start = which * head_cols + head * HEAD_DIM
        value = raw[:, start : start + HEAD_DIM]
        if which == 2:
            both[core, 1, head] = value.astype(low)
            continue
        factor = lax.rsqrt(jnp.sum(value * value, axis=-1, keepdims=True) + EPSILON)
        scaled = (value * factor * qk_gain[head]).astype(low)
        raw_out[which, head] = value
        if which == 1:
            both[core, 0, head] = scaled
            if head == 0:
                swap = begin(remote(both.at[core], both.at[core], kv_send.at[0], kv_recv.at[0], twin()))
        else:
            query_out[head] = scaled * math.sqrt(HEAD_DIM)
    keep(raw_out, to_raw)
    keep(query_out, to_query)
    for copy in m_line + o_more:
        copy.wait_recv()
    m_line += to_chips(1, w_gate.at[here])
    swap_o = begin(remote(w_out.at[core], w_out.at[core], wt_send.at[1], wt_recv.at[1], twin()))
    up_across = across(w_up, ms_send, ms_recv)
    swap.wait()
    keep(both, to_both)

    def one_block(index, carry):
        step = lax.rem(index + 1, CHIPS)
        device, other = chip_peer(step)
        at = rows_at(other, tok_rows)
        allowed = kept_pairs(places, key_pos, other, core, tok_rows)

        def one_head(head, carry):
            query = query_out[head, at, :]
            scores = jnp.concatenate([dot_nt(query, both[half, 0, head]) for half in range(CORES)], axis=1)
            powered = jnp.exp(jnp.where(allowed, scores, NEG_LARGE))
            inverse = 1.0 / jnp.sum(powered, axis=-1, keepdims=True)
            weights = (powered * inverse).astype(low)
            att_out[head, at, :] = sum(
                dot(weights[:, half * group_rows : (half + 1) * group_rows], both[half, 1, head])
                for half in range(CORES)
            )
            inv_out[head, at, :] = inverse
            return carry

        lax.fori_loop(0, heads, one_head, 0)
        for head in range(heads):
            att_low[at, head * HEAD_DIM : (head + 1) * HEAD_DIM] = att_out[head, at, :].astype(low)
        when(step != 0, remote(att_low.at[at], attx.at[chip], a_send.at[step], a_recv.at[step], device).start)
        pltpu.make_async_copy(att_out.at[:, at], to_att.at[:, at], att_sem.at[0, step]).start()
        pltpu.make_async_copy(inv_out.at[:, at], to_inv.at[:, at], att_sem.at[1, step]).start()
        return carry

    lax.fori_loop(0, CHIPS, one_block, 0)
    attx[chip] = att_low[block, :]
    swap_o.wait()
    keep(w_out, to_out)
    up_more = spread_relay(w_up, seq_rows, ms_send, ms_recv)
    for step in STEPS:
        remote(att_low.at[block], attx.at[chip], a_send.at[step], a_recv.at[step], chip_peer(step)[0]).wait()
    for copy in m_line[3:] + up_more:
        copy.wait_recv()
    gather_drain(states_all, tok_rows, x_send, x_recv)
    for step in range(CHIPS):
        pltpu.make_async_copy(att_out.at[:, block], to_att.at[:, block], att_sem.at[0, step]).wait()
        pltpu.make_async_copy(inv_out.at[:, block], to_inv.at[:, block], att_sem.at[1, step]).wait()
    for copy in kept:
        copy.wait()
    for copy in m_line + line + o_line + q_across + o_across + o_more + up_across + up_more:
        copy.wait_send()


def in_smem():
    return pl.BlockSpec(memory_space=pltpu.SMEM)


def attend_call(states, attn_src, mlp_src, qk_gain, places):
    tok_rows, model_width = states.shape
    rows = attn_src.shape[0]
    heads = qk_gain.shape[0]
    chips, chip_rows = CHIPS, CORES * rows
    group_rows = chips * tok_rows
    half_units = mlp_src.shape[1] // 3 // chips // CORES
    half_width, half_cols = model_width // CORES, 3 * heads * HEAD_DIM // CORES
    f32, low = jnp.float32, jnp.bfloat16
    shape = jax.ShapeDtypeStruct
    return pl.pallas_call(
        attend_kernel,
        out_shape=[
            shape((group_rows, model_width), low),
            shape((CORES, model_width, half_cols), low),
            shape((CORES, model_width, half_width), low),
            shape((model_width, half_units), low),
            shape((chips * chip_rows, half_units), low),
            shape((chips, chip_rows, half_units), low),
            shape((2, heads, group_rows, HEAD_DIM), f32),
            shape((heads, group_rows, HEAD_DIM), low),
            shape((CORES, 2, heads, group_rows, HEAD_DIM), low),
            shape((heads, group_rows, HEAD_DIM), f32),
            shape((heads, group_rows, 1), f32),
            shape((chips, tok_rows, heads * HEAD_DIM), low),
        ],
        in_specs=[in_vmem(), in_vmem(), in_hbm(), in_vmem(), in_smem()],
        out_specs=[in_hbm()] * 3 + [in_vmem()] * 3 + [in_hbm()] * 5 + [in_vmem()],
        scratch_shapes=[
            VMEM((group_rows, model_width), low),
            VMEM((CORES, model_width, half_cols), low),
            VMEM((CORES, model_width, half_width), low),
            VMEM((2, heads, group_rows, HEAD_DIM), f32),
            VMEM((heads, group_rows, HEAD_DIM), low),
            VMEM((CORES, 2, heads, group_rows, HEAD_DIM), low),
            VMEM((heads, group_rows, HEAD_DIM), f32),
            VMEM((heads, group_rows, 1), f32),
            VMEM((chips, CORES, rows, half_cols), f32),
            VMEM((chips, chip_rows, half_cols), f32),
            VMEM((chips, chip_rows, half_cols), low),
            VMEM((chip_rows, half_width), f32),
            VMEM((chip_rows, half_width), low),
            VMEM((3, chips, chip_rows, half_units), f32),
            VMEM((2, chips, chip_rows, half_units), low),
            VMEM((group_rows, 3 * heads * HEAD_DIM), f32),
            VMEM((group_rows, heads * HEAD_DIM), low),
            VMEM((1, CORES * group_rows), jnp.int32),
            dma(12), dma(6), dma(2, 4), line_dma(), line_dma(), dma(2), dma(2), dma(3, 4), dma(3, 4), dma(4), dma(4),
            dma(4), dma(4), dma(2), dma(2), dma(4), dma(4), dma(4), dma(4), dma(2, 4), dma(2, 4),
            dma(4), dma(4), dma(1), dma(1), dma(4), dma(4),
        ],
        compiler_params=pltpu.CompilerParams(
            collective_id=1, has_side_effects=True, vmem_limit_bytes=LIMIT
        ),
        name="attend",
    )(states, attn_src, mlp_src, qk_gain, places)


def unit_of(value):
    factor = lax.rsqrt(jnp.sum(value * value, axis=-1, keepdims=True) + EPSILON)
    return value * factor, factor


def mlp_kernel(
    attx, states, cotangent, from_out, alpha_attn, alpha_mlp, gain_u, gain_v, w_up, w_gate, low_down,
    out, grad_attx, grad_w_out, grad_direct, small, to_half, grad_down,
    w_out, grad_half, weights, mixed_one, attn_unit, factors, mixed_low, mixed_all, up, gate, hidden, part,
    sums, via, passed, total, grad_two, branch_low, branch_all, grad_u, grad_v, wide, turned, arrived,
    w_down, down_half, down_got, dot_u, dot_v,
    local_sem, ws_send, ws_recv, wt_send, wt_recv, x_send, x_recv, r_send, r_recv,
    g_send, g_recv, b_send, b_recv, d_send, d_recv, wz_send, wz_recv, ds_send, ds_recv,
):
    seq, chip, core = place_of()
    tok_rows, model_width = states.shape
    chip_heads = attx.shape[2]
    seq_rows, half_units = w_gate.shape
    chip_rows = low_down.shape[1]
    half_width = w_out.shape[2]
    group_rows = CHIPS * tok_rows
    block = rows_at(chip, tok_rows)
    load = begin(pltpu.make_async_copy(from_out, w_out, local_sem.at[2]))
    meet()
    seq_at = rows_at(seq, seq_rows)
    here = rows_at(chip, chip_rows)
    swaps = [begin(remote(w_up, weights.at[0, core], wt_send.at[0], wt_recv.at[0], twin()))]
    to_chips = [
        begin(remote(low_down.at[chip_peer(step)[1]], w_down.at[here], wz_send.at[step], wz_recv.at[step], chip_peer(step)[0]))
        for step in STEPS
    ]

    across = spread_start(w_gate, weights.at[1, core], seq_rows, ws_send.at[1], ws_recv.at[1])
    keeps = [
        begin(pltpu.make_async_copy(w_up, weights.at[0, core], local_sem.at[0])),
        begin(pltpu.make_async_copy(w_gate, weights.at[1, core, seq_at], local_sem.at[1])),
    ]
    w_down[here, :] = low_down[chip]
    load.wait()
    part_at = [slice(at * chip_heads, (at + 1) * chip_heads) for at in range(CHIPS)]
    half_at = [slice(half * half_width, (half + 1) * half_width) for half in range(CORES)]
    branch = jnp.concatenate(
        [sum(dot(attx[at], w_out[half, part_at[at], :]) for at in range(CHIPS)) for half in range(CORES)],
        axis=1,
    )
    unit, factor = unit_of(branch)
    attn_unit[...] = unit
    factors[0] = factor
    base = states[...].astype(jnp.float32)
    value, factor = unit_of(base + alpha_attn[...] * (unit - base))
    mixed_one[...] = value
    factors[1] = factor
    mixed_low[...] = value.astype(jnp.bfloat16)
    gather_start(mixed_low, mixed_all, tok_rows, x_send, x_recv)
    mixed_all[block, :] = mixed_low[...]
    for copy in keeps:
        copy.wait()
    for copy in to_chips:
        copy.wait_recv()
    more = spread_relay(weights.at[1, core], seq_rows, ws_send.at[1], ws_recv.at[1])
    across += spread_start(w_down, weights.at[2, core], seq_rows, ws_send.at[2], ws_recv.at[2])
    weights[2, core, seq_at, :] = w_down[...]
    gather_hop(mixed_all, tok_rows, 1, x_send, x_recv)
    for copy in more:
        copy.wait_recv()
    swaps.append(begin(remote(weights.at[1, core], weights.at[1, core], wt_send.at[1], wt_recv.at[1], twin())))
    slab = min(64, group_rows)
    slabs = group_rows // slab
    half_slabs = slabs // 2
    half_rows = group_rows // 2
    mine = chip // 2

    def forward(group):
        rows = rows_at(group, half_rows)
        for half in range(CORES):
            up[half, rows, :] = dot(mixed_all[rows, :], weights[0, half])
            gate[half, rows, :] = dot(mixed_all[rows, :], weights[1, half])

        def activate(index, carry):
            half = index // half_slabs
            at = rows_at(group * half_slabs + lax.rem(index, half_slabs), slab)
            gated = gate[half, at, :] * gain_v[half]
            scaled = up[half, at, :] * gain_u[half]
            hidden[half, at, :] = (gated * jax.nn.sigmoid(gated) * scaled).astype(jnp.bfloat16)
            return carry

        lax.fori_loop(0, CORES * half_slabs, activate, 0)

    for copy in swaps:
        copy.wait_recv()
    forward(mine)
    gather_hop(mixed_all, tok_rows, 2, x_send, x_recv)
    down_more = spread_relay(weights.at[2, core], seq_rows, ws_send.at[2], ws_recv.at[2])
    gather_hop(mixed_all, tok_rows, 3, x_send, x_recv)
    forward(1 - mine)
    for copy in down_more:
        copy.wait_recv()
    swap = begin(remote(weights.at[2, core], weights.at[2, core], wt_send.at[2], wt_recv.at[2], twin()))
    swaps.append(swap)
    swap.wait_recv()
    tile = model_width // 5

    def down(index, carry):
        at = rows_at(index, tile)
        part[0, :, at] = sum(dot_nt(hidden[half], weights[2, half, at, :]) for half in range(CORES)).astype(jnp.bfloat16)
        return carry

    lax.fori_loop(0, model_width // tile, down, 0)

    reduce_start(part.at[0], tok_rows, sums.at[0], via.at[0], r_send, r_recv)
    reduce_relay(part.at[0], tok_rows, sums.at[0], via.at[0], passed.at[0], r_send, r_recv)
    reduce_wait(part.at[0], tok_rows, sums.at[0], total, r_send, r_recv)
    mlp_unit, mlp_factor = unit_of(total[...])
    value, factor = unit_of(mixed_one[...] + alpha_mlp[...] * (mlp_unit - mixed_one[...]))
    out[...] = value.astype(jnp.bfloat16)
    above = cotangent[...].astype(jnp.float32)
    grad = factor * (above - value * jnp.sum(above * value, axis=-1, keepdims=True))
    grad_two[...] = grad
    small[...] = jnp.zeros_like(small)
    small[1:2, :] = jnp.sum(grad * (mlp_unit - mixed_one[...]), axis=0, keepdims=True)
    grad = grad * alpha_mlp[...]
    grad = mlp_factor * (grad - mlp_unit * jnp.sum(grad * mlp_unit, axis=-1, keepdims=True))
    branch_low[...] = grad.astype(jnp.bfloat16)
    gather_start(branch_low, branch_all, tok_rows, g_send, g_recv)
    branch_all[block, :] = branch_low[...]
    gather_hop(branch_all, tok_rows, 1, g_send, g_recv)
    gather_hop(branch_all, tok_rows, 2, g_send, g_recv)
    turned[0] = mixed_all[...].T
    gather_hop(branch_all, tok_rows, 3, g_send, g_recv)
    for half in range(CORES):
        wide[half] = dot(branch_all[...], weights[2, half])
    dot_u[...] = jnp.zeros_like(dot_u)
    dot_v[...] = jnp.zeros_like(dot_v)

    def deactivate(index, carry):
        half = index // slabs
        at = rows_at(lax.rem(index, slabs), slab)
        gated = gate[half, at, :] * gain_v[half]
        scaled = up[half, at, :] * gain_u[half]
        upstream = wide[half, at, :]
        sig = jax.nn.sigmoid(gated)
        to_up = upstream * (gated * sig)
        to_gate = upstream * scaled * sig * (1.0 + gated * (1.0 - sig))
        dot_u[half] += jnp.sum(to_up * up[half, at, :], axis=0, keepdims=True)
        dot_v[half] += jnp.sum(to_gate * gate[half, at, :], axis=0, keepdims=True)
        grad_u[half, at, :] = (to_up * gain_u[half]).astype(jnp.bfloat16)
        grad_v[half, at, :] = (to_gate * gain_v[half]).astype(jnp.bfloat16)
        return carry

    lax.fori_loop(0, CORES * slabs, deactivate, 0)

    def back_down(index, carry):
        at = rows_at(index, tile)
        part[1, :, at] = sum(
            dot_nt(grad_u[half], weights[0, half, at, :]) + dot_nt(grad_v[half], weights[1, half, at, :])
            for half in range(CORES)
        ).astype(jnp.bfloat16)
        return carry

    lax.fori_loop(0, model_width // tile, back_down, 0)
    for copy in swaps + more + down_more:
        copy.wait_send()
    reduce_start(part.at[1], tok_rows, sums.at[1], via.at[1], b_send, b_recv, False)
    turned[1] = branch_all[...].T
    swaps = {}

    def weight_grads(which, left, right):
        def one(index, carry):
            half = index // 5
            at = rows_at(lax.rem(index, 5), tile)
            weights[which, half, at, :] = dot(turned[left, at, :], right[half]).astype(jnp.bfloat16)
            return carry

        lax.fori_loop(0, CORES * 5, one, 0)
        swaps[which] = begin(remote(weights.at[which, 1 - core], arrived.at[which], d_send.at[which], d_recv.at[which], twin()))

    def both_cores(which):
        swaps[which].wait_recv()
        return (weights[which, core].astype(jnp.float32) + arrived[which].astype(jnp.float32)).astype(jnp.bfloat16)

    weight_grads(2, 1, hidden)
    weight_grads(0, 0, grad_u)
    reduce_relay(part.at[1], tok_rows, sums.at[1], via.at[1], passed.at[1], b_send, b_recv)
    down_half[...] = both_cores(2)
    down_across = [
        begin(remote(down_half.at[rows_at(seq_peer(step)[1], seq_rows)], down_got.at[step - 1], ds_send.at[step], ds_recv.at[step], seq_peer(step)[0]))
        for step in STEPS
    ]
    weight_grads(1, 0, grad_v)
    kept = []
    for which in range(2):
        grad_half[which] = both_cores(which)
        kept.append(begin(pltpu.make_async_copy(grad_half.at[which], to_half.at[which], local_sem.at[which])))
    reduce_wait(part.at[1], tok_rows, sums.at[1], total, b_send, b_recv)
    grad = grad_two[...] * (1.0 - alpha_mlp[...]) + total[...]
    value = mixed_one[...]
    grad = factors[1] * (grad - value * jnp.sum(grad * value, axis=-1, keepdims=True))
    unit = attn_unit[...]
    small[0:1, :] = jnp.sum(grad * (unit - states[...].astype(jnp.float32)), axis=0, keepdims=True)
    grad_direct[...] = grad * (1.0 - alpha_attn[...])
    grad = grad * alpha_attn[...]
    grad = factors[0] * (grad - unit * jnp.sum(grad * unit, axis=-1, keepdims=True))
    low = grad.astype(jnp.bfloat16)
    for at in range(CHIPS):
        grad_attx[at] = sum(
            dot_nt(low[:, half_at[half]], w_out[half, part_at[at], :]) for half in range(CORES)
        ).astype(jnp.bfloat16)
        for half in range(CORES):
            grad_w_out[half, at] = dot_tn(attx[at], low[:, half_at[half]]).astype(jnp.bfloat16)
    for half in range(CORES):
        unit_at = slice(half * half_units, (half + 1) * half_units)
        small[2:3, unit_at] = dot_u[half]
        small[3:4, unit_at] = dot_v[half] * math.sqrt(D)
    whole = down_half[seq_at, :].astype(jnp.float32)
    for step in STEPS:
        down_across[step - 1].wait_recv()
        whole = whole + down_got[step - 1].astype(jnp.float32)
    grad_down[...] = whole.astype(jnp.bfloat16)
    for copy in kept:
        copy.wait()
    gather_drain(mixed_all, tok_rows, x_send, x_recv)
    gather_drain(branch_all, tok_rows, g_send, g_recv)
    reduce_drain(part.at[0], tok_rows, sums.at[0], r_send, r_recv)
    reduce_drain(part.at[1], tok_rows, sums.at[1], b_send, b_recv, False)
    for copy in across + to_chips + down_across + [swaps[which] for which in range(3)]:
        copy.wait_send()


def mlp_call(attx, states, cotangent, w_out, alpha_attn, alpha_mlp, gain_u, gain_v, w_up, w_gate, low_down):
    tok_rows, model_width = states.shape
    chips, _, chip_heads = attx.shape
    seq_rows, half_units = w_gate.shape
    group_rows = chips * tok_rows
    f32, low = jnp.float32, jnp.bfloat16
    shape = jax.ShapeDtypeStruct
    tokens, group = (tok_rows, model_width), (group_rows, model_width)
    wide = (CORES, group_rows, half_units)
    matrix = (model_width, half_units)
    return pl.pallas_call(
        mlp_kernel,
        out_shape=[
            shape(tokens, low),
            shape(attx.shape, low),
            shape((CORES, chips, chip_heads, model_width // CORES), low),
            shape(tokens, f32),
            shape((8, max(model_width, CORES * half_units)), f32),
            shape((2,) + matrix, low),
            shape((seq_rows, half_units), low),
        ],
        in_specs=[in_vmem()] * 3 + [in_hbm()] + [in_vmem()] * 4 + [in_hbm(), in_vmem(), in_vmem()],
        out_specs=[in_vmem()] * 5 + [in_hbm(), in_vmem()],
        scratch_shapes=[
            VMEM(w_out.shape, low),
            VMEM((2,) + matrix, low),
            VMEM((3, CORES) + matrix, low),
            VMEM(tokens, f32),
            VMEM(tokens, f32),
            VMEM((2, tok_rows, 1), f32),
            VMEM(tokens, low),
            VMEM(group, low),
            VMEM(wide, f32),
            VMEM(wide, f32),
            VMEM(wide, low),
            VMEM((2,) + group, low),
            VMEM((2, 3) + tokens, low),
            VMEM((2,) + tokens, low),
            VMEM((2,) + tokens, low),
            VMEM(tokens, f32),
            VMEM(tokens, f32),
            VMEM(tokens, low),
            VMEM(group, low),
            VMEM(wide, low),
            VMEM(wide, low),
            VMEM(wide, f32),
            VMEM((2, model_width, group_rows), low),
            VMEM((3,) + matrix, low),
            VMEM((seq_rows, half_units), low),
            VMEM(matrix, low),
            VMEM((3, seq_rows, half_units), low),
            VMEM((CORES, 1, half_units), f32),
            VMEM((CORES, 1, half_units), f32),
            dma(3), dma(3, 4), dma(3, 4), dma(3), dma(3), line_dma(), line_dma(), dma(4), dma(4),
            line_dma(), line_dma(), dma(4), dma(4), dma(3), dma(3), dma(4), dma(4), dma(4), dma(4),
        ],
        compiler_params=pltpu.CompilerParams(
            collective_id=2, has_side_effects=True, vmem_limit_bytes=LIMIT
        ),
        name="mlp",
    )(
        attx, states, cotangent, w_out, alpha_attn, alpha_mlp, gain_u, gain_v, w_up, w_gate, low_down
    )


def back_kernel(
    grad_attx, from_half, grad_down, from_grad_out, small_in, from_raw, from_query, from_both, from_att,
    from_inv, from_states, from_qkv, qk_gain, places, grad_direct,
    grad_states, out_mlp, out_attn, feature, unit,
    grad_half, grad_w_out, raw, query, both, att, inverse, states_all, w_qkv, att_low, heads_low, to_keys, swap_low, swap_kv, grad_heads, grad_sides, part, sums, via, passed, total, turned,
    grad_q, half_q, seq_q, line_q, wide_q, half_o, pair_o, seq_got, seq_held, seq_last, seq_low, q_got, q_held, q_last, line_got, wide,
    wide_o, small, small_pair, small_seq, dots, small_all, flat_q, sides_q, key_pos,
    local_sem, load_sem, a_send, a_recv, s_send, s_recv, o_send, o_recv, kv_send, kv_recv, r_send, r_recv,
    qt_send, qt_recv, qs_send, qs_recv, qz_send, qz_recv, z_send, z_recv, f_send, f_recv,
    p_send, p_recv, t_send, t_recv,
):
    seq, chip, core = place_of()
    tok_rows, model_width = grad_direct.shape
    heads = qk_gain.shape[0]
    head_cols = heads * HEAD_DIM
    group_rows = CHIPS * tok_rows
    half_units = grad_half.shape[2]
    seq_rows = seq_low.shape[1]
    chip_rows = seq_rows // CHIPS
    rows = chip_rows // CORES
    part_cols = head_cols // CORES
    ff_width = out_mlp.shape[1] // 3
    scale = math.sqrt(HEAD_DIM)
    block = rows_at(chip, tok_rows)
    f32, low = jnp.float32, jnp.bfloat16
    loads = [
        begin(pltpu.make_async_copy(src, dst, load_sem.at[at]))
        for at, (src, dst) in enumerate(
            (
                (from_query, query), (from_both, both), (from_inv, inverse), (from_att, att), (from_raw, raw),
                (from_grad_out, grad_w_out), (from_states, states_all), (from_half, grad_half), (from_qkv, w_qkv),
            )
        )
    ]
    meet()
    waits = []
    line = []
    for step in STEPS:
        device, other = chip_peer(step)
        line.append(begin(remote(grad_attx.at[other], att_low.at[block], a_send.at[step], a_recv.at[step], device)))
    att_low[block, :] = grad_attx[chip]
    key_positions(places, key_pos, tok_rows)
    pair = begin(remote(from_grad_out.at[1 - core], pair_o, o_send.at[0], o_recv.at[0], twin()))
    onward = {}

    def to_chips(which, src):
        onward[which] = [
            begin(remote(src.at[rows_at(chip_peer(step)[1], chip_rows)], line_got.at[which, chip], z_send.at[which, step], z_recv.at[which, step], chip_peer(step)[0]))
            for step in STEPS
        ]
        line_got[which, chip] = src[rows_at(chip, chip_rows), :]

    to_chips(2, grad_down)

    def cross(which, src):
        return fold_start(src, seq_got.at[which], seq_rows, s_send.at[which], s_recv.at[which])

    def cross_on(which, src, copies):
        return fold_relay(src, seq_got.at[which], seq_held.at[which], seq_last.at[which], seq_rows, copies, s_send.at[which], s_recv.at[which])

    def cross_end(which, src, copies, more):
        fold_end(src, seq_got.at[which], seq_last.at[which], seq_low.at[which], seq_rows, copies, more)

    crossing = [cross(0, from_half.at[0])]
    to_keys[...] = jnp.zeros_like(to_keys)
    dots[...] = jnp.zeros_like(dots)
    for copy in loads:
        copy.wait()
    turned[...] = states_all[...].T
    sources = (grad_half.at[0], grad_half.at[1], half_o)
    onwards = [cross_on(0, sources[0], crossing[0])]
    crossing.append(cross(1, from_half.at[1]))
    pair.wait_recv()
    for at in range(4):
        half_o[at * seq_rows : (at + 1) * seq_rows, :] = (
            grad_w_out[core, at].astype(f32) + pair_o[at].astype(f32)
        ).astype(low)
    tile = tok_rows
    tiles = CHIPS

    def raw_back(which, head, at, upstream):
        value = raw[which, head, at, :]
        unit, factor = unit_of(value)
        dots[head] += jnp.sum(upstream * unit, axis=0, keepdims=True)
        upstream = upstream * qk_gain[head]
        upstream = factor * (upstream - unit * jnp.sum(upstream * unit, axis=-1, keepdims=True))
        grad_heads[which, head, at, :] = upstream.astype(low)

    def one_block(step, carry):
        other = lax.rem(chip + CHIPS - step, CHIPS)
        at = rows_at(other, tok_rows)
        copy = remote(grad_attx.at[0], att_low.at[at], a_send.at[step], a_recv.at[step], device_on(other))
        if step > 0:
            copy.wait_recv()
        for head in range(heads):
            heads_low[head, at, :] = att_low[at, head * HEAD_DIM : (head + 1) * HEAD_DIM]
        allowed = kept_pairs(places, key_pos, other, core, tok_rows)

        def one_head(head, carry):
            rows_q = query[head, at, :]
            grad_att = heads_low[head, at, :]
            scores = jnp.concatenate([dot_nt(rows_q, both[half, 0, head]) for half in range(CORES)], axis=1)
            probs = jnp.exp(jnp.where(allowed, scores, NEG_LARGE)) * inverse[head, at, :]
            grad_prob = jnp.concatenate([dot_nt(grad_att, both[half, 1, head]) for half in range(CORES)], axis=1)
            row_dot = jnp.sum(grad_att.astype(f32) * att[head, at, :], axis=-1, keepdims=True)
            grad_scores = (probs * (grad_prob - row_dot)).astype(low)
            weights = probs.astype(low)
            to_query = jnp.zeros((tok_rows, HEAD_DIM), f32)
            for half in range(CORES):
                cols = slice(half * group_rows, (half + 1) * group_rows)
                to_query = to_query + dot(grad_scores[:, cols], both[half, 0, head])
                to_keys[half, 0, head] += dot_tn(grad_scores[:, cols], rows_q)
                to_keys[half, 1, head] += dot_tn(weights[:, cols], grad_att)
            raw_back(0, head, at, to_query * scale)
            return carry

        lax.fori_loop(0, heads, one_head, 0)
        return carry

    one_block(0, 0)
    cross_end(0, sources[0], crossing[0], onwards[0])
    to_chips(0, seq_low.at[0])
    one_block(1, 0)
    onwards.append(cross_on(1, sources[1], crossing[1]))
    crossing.append(cross(2, half_o))
    one_block(2, 0)
    one_block(3, 0)
    cross_end(1, sources[1], crossing[1], onwards[1])
    to_chips(1, seq_low.at[1])
    swap_low[...] = to_keys[1 - core].astype(low)
    swap = begin(remote(swap_low, swap_kv, kv_send.at[0], kv_recv.at[0], twin()))
    swap.wait()

    def one_key(index, carry):
        head = index // tiles
        at = rows_at(lax.rem(index, tiles), tile)
        mine = to_keys[core, 0, head, at, :] + swap_kv[0, head, at, :].astype(f32)
        raw_back(1, head, at, mine)
        value = to_keys[core, 1, head, at, :] + swap_kv[1, head, at, :].astype(f32)
        grad_heads[2, head, at, :] = value.astype(low)
        return carry

    onwards.append(cross_on(2, half_o, crossing[2]))
    lax.fori_loop(0, heads * tiles, one_key, 0)
    for which in range(3):
        full = jnp.concatenate([grad_heads[which, head] for head in range(heads)], axis=1)
        for half in range(CORES):
            grad_sides[half, :, which * part_cols : (which + 1) * part_cols] = full[:, half * part_cols : (half + 1) * part_cols]
    wide_tile = model_width // 5

    def down(index, carry):
        at = rows_at(index, wide_tile)
        part[:, at] = sum(dot_nt(grad_sides[half], w_qkv[half, at, :]) for half in range(CORES)).astype(low)
        return carry

    lax.fori_loop(0, 5, down, 0)
    reduce_start(part, tok_rows, sums, via, r_send, r_recv, False)

    def weight_grad(index, carry):
        half = index // 5
        at = rows_at(lax.rem(index, 5), wide_tile)
        grad_q[half, at, :] = dot(turned[at, :], grad_sides[half]).astype(low)
        return carry

    lax.fori_loop(0, CORES * 5, weight_grad, 0)
    swap_q = begin(remote(grad_q.at[1 - core], half_q, qt_send.at[0], qt_recv.at[0], twin()))
    swap_q.wait()
    half_q[...] = (grad_q[core].astype(f32) + half_q[...].astype(f32)).astype(low)
    crossing_q = fold_start(half_q, q_got, seq_rows, qs_send, qs_recv)
    cross_end(2, half_o, crossing[2], onwards[2])
    to_chips(3, seq_low.at[2])
    reduce_relay(part, tok_rows, sums, via, passed, r_send, r_recv)
    small[...] = small_in[...]
    small[4:5, :head_cols] = jnp.concatenate([dots[head] for head in range(heads)], axis=1)
    swap_s = begin(remote(small, small_pair, t_send.at[0], t_recv.at[0], twin()))
    more_q = fold_relay(half_q, q_got, q_held, q_last, seq_rows, crossing_q, qs_send, qs_recv)
    fold_end(half_q, q_got, q_last, seq_q, seq_rows, crossing_q, more_q)
    onward_q = []
    for step in STEPS:
        device, other = chip_peer(step)
        onward_q.append(begin(remote(seq_q.at[rows_at(other, chip_rows)], line_q.at[chip], qz_send.at[step], qz_recv.at[step], device)))
    line_q[chip] = seq_q[rows_at(chip, chip_rows), :]

    mine = rows_at(core, rows)
    theirs = rows_at(1 - core, rows)
    swap_s.wait()
    small[...] = small[...] + small_pair[...]
    spread_s = [
        begin(remote(small, small_seq.at[step - 1], t_send.at[step], t_recv.at[step], seq_peer(step)[0]))
        for step in STEPS
    ]
    last, lasts = [], []
    for which in (2, 0, 1):
        for copy in onward[which]:
            copy.wait_recv()
        for at in range(CHIPS):
            wide[which, at] = line_got[which, at].astype(f32)
            start = which * ff_width + at * CORES * half_units + core * half_units
            there = out_mlp.at[:, pl.ds(pl.multiple_of(start, 128), half_units)]
            last.append(begin(remote(wide.at[which, at, theirs], there, f_send.at[which, at], f_recv.at[which, at], twin())))
            lasts.append(begin(pltpu.make_async_copy(wide.at[which, at, mine], there, local_sem.at[3 + which * CHIPS + at])))
    for copy in spread_s:
        copy.wait()
    small_pair[...] = small[...] + small_seq[0] + small_seq[1] + small_seq[2]
    small_all[chip] = small_pair[...]
    ends = to_line(small_pair, small_all.at[chip], p_send, p_recv)
    for copy in onward[3]:
        copy.wait_recv()
    whole = line_got[3, 0].astype(f32)
    for at in range(1, CHIPS):
        whole = whole + line_got[3, at].astype(f32)
    wide_o[...] = whole
    start = 3 * model_width + core * half_units
    there = out_attn.at[:, pl.ds(pl.multiple_of(start, 128), half_units)]
    last.append(begin(remote(wide_o.at[theirs], there, f_send.at[3, 0], f_recv.at[3, 0], twin())))
    lasts.append(begin(pltpu.make_async_copy(wide_o.at[mine], there, local_sem.at[15])))
    for copy in onward_q:
        copy.wait_recv()
    wide_q[...] = line_q[...].astype(f32)
    sides_q[core] = wide_q[:, mine, :]
    swap_q = begin(remote(wide_q.at[:, theirs], sides_q.at[core], f_send.at[3, 1], f_recv.at[3, 1], twin()))
    for copy in ends:
        copy.wait()
    alphas = small_all[0] + small_all[1] + small_all[2] + small_all[3]
    feature[1:3, :] = alphas[0:2, :]
    for at in range(CHIPS):
        feature[0:1, at * head_cols : (at + 1) * head_cols] = small_all[at, 4:5, :head_cols]
        width = CORES * half_units
        unit[:, at * width : (at + 1) * width] = small_all[at, 2:4, :width]
    swap_q.wait()
    for at in range(CHIPS):
        for half in range(CORES):
            for which in range(3):
                start = which * model_width + at * head_cols + half * part_cols
                flat_q[:, start : start + part_cols] = sides_q[half, at, :, which * part_cols : (which + 1) * part_cols]
    lasts.append(begin(pltpu.make_async_copy(flat_q, out_attn.at[:, pl.ds(0, 3 * model_width)], local_sem.at[16])))
    reduce_wait(part, tok_rows, sums, total, r_send, r_recv)
    grad_states[...] = (total[...] + grad_direct[...]).astype(low)
    for copy in last + lasts:
        copy.wait()
    reduce_drain(part, tok_rows, sums, r_send, r_recv, False)
    for copy in line + [pair] + sum(crossing + onwards + list(onward.values()), crossing_q + more_q + onward_q):
        copy.wait_send()


def back_call(
    grad_attx, grad_half, grad_down, grad_w_out, small_in, raw, query, both, att, inverse, states_all,
    w_qkv, qk_gain, places, grad_direct, rows,
):
    tok_rows, model_width = grad_direct.shape
    chips = grad_attx.shape[0]
    heads = qk_gain.shape[0]
    head_cols = heads * HEAD_DIM
    group_rows = chips * tok_rows
    half_units = grad_half.shape[2]
    half_cols = w_qkv.shape[2]
    chip_rows = CORES * rows
    seq_rows = chips * chip_rows
    f32, low = jnp.float32, jnp.bfloat16
    shape = jax.ShapeDtypeStruct
    per_head = (heads, group_rows, HEAD_DIM)
    return pl.pallas_call(
        back_kernel,
        out_shape=[
            shape((tok_rows, model_width), low),
            shape((rows, 3 * chips * CORES * half_units), f32),
            shape((rows, 4 * model_width), f32),
            shape((3, model_width), f32),
            shape((2, chips * CORES * half_units), f32),
        ],
        in_specs=[in_vmem(), in_hbm(), in_vmem(), in_hbm(), in_vmem()] + [in_hbm()] * 7 + [in_vmem(), in_smem(), in_vmem()],
        out_specs=[in_vmem(), in_hbm(), in_hbm(), in_vmem(), in_vmem()],
        scratch_shapes=[
            *(VMEM(value.shape, value.dtype) for value in (grad_half, grad_w_out, raw, query, both, att, inverse, states_all, w_qkv)),
            VMEM((group_rows, head_cols), low),
            VMEM(per_head, low),
            VMEM((CORES, 2) + per_head, f32),
            VMEM((2,) + per_head, low),
            VMEM((2,) + per_head, low),
            VMEM((3,) + per_head, low),
            VMEM((CORES, group_rows, half_cols), low),
            VMEM((group_rows, model_width), low),
            VMEM((3, tok_rows, model_width), low),
            VMEM((tok_rows, model_width), low),
            VMEM((tok_rows, model_width), low),
            VMEM((tok_rows, model_width), f32),
            VMEM((model_width, group_rows), low),
            VMEM((CORES, model_width, half_cols), low),
            VMEM((model_width, half_cols), low),
            VMEM((seq_rows, half_cols), low),
            VMEM((chips, chip_rows, half_cols), low),
            VMEM((chips, chip_rows, half_cols), f32),
            VMEM((4 * seq_rows, half_units), low),
            VMEM((4, seq_rows, half_units), low),
            VMEM((3, 2, 2, seq_rows // 2, half_units), low),
            VMEM((3, 2, seq_rows // 2, half_units), low),
            VMEM((3, 2, seq_rows // 2, half_units), low),
            VMEM((3, seq_rows, half_units), low),
            VMEM((2, 2, seq_rows // 2, half_cols), low),
            VMEM((2, seq_rows // 2, half_cols), low),
            VMEM((2, seq_rows // 2, half_cols), low),
            VMEM((4, chips, chip_rows, half_units), low),
            VMEM((3, chips, chip_rows, half_units), f32),
            VMEM((chip_rows, half_units), f32),
            VMEM(small_in.shape, f32),
            VMEM(small_in.shape, f32),
            VMEM((3,) + small_in.shape, f32),
            VMEM((heads, 1, HEAD_DIM), f32),
            VMEM((chips,) + small_in.shape, f32),
            VMEM((rows, 3 * model_width), f32),
            VMEM((CORES, chips, rows, half_cols), f32),
            VMEM((1, CORES * group_rows), jnp.int32),
            dma(17), dma(9), dma(4), dma(4), dma(3, 3, 2), dma(3, 3, 2), dma(1), dma(1), dma(1), dma(1),
            dma(4), dma(4), dma(1), dma(1), dma(3, 2), dma(3, 2), dma(4), dma(4), dma(4, 4), dma(4, 4),
            dma(4, 4), dma(4, 4), dma(4), dma(4), dma(4), dma(4),
        ],
        compiler_params=pltpu.CompilerParams(
            collective_id=3, has_side_effects=True, vmem_limit_bytes=LIMIT
        ),
        name="back",
    )(
        grad_attx, grad_half, grad_down, grad_w_out, small_in, raw, query, both, att, inverse, states_all,
        w_qkv, qk_gain, places, grad_direct,
    )


def finish_kernel(*refs):
    count = len(refs) // 3
    sources, results, held = refs[:count], refs[count : 2 * count], refs[2 * count : 3 * count]
    sem = refs[-1]
    copies = [begin(pltpu.make_async_copy(sources[at], held[at], sem.at[0, at])) for at in range(count)]
    leaving = []
    for at in range(count):
        copies[at].wait()
        leaving.append(begin(pltpu.make_async_copy(held[at], results[at], sem.at[1, at])))
    for copy in leaving:
        copy.wait()


def finish_call(*arrays):
    return pl.pallas_call(
        finish_kernel,
        out_shape=[jax.ShapeDtypeStruct(array.shape, array.dtype) for array in arrays],
        in_specs=[in_hbm()] * len(arrays),
        out_specs=[in_hbm()] * len(arrays),
        scratch_shapes=[VMEM(array.shape, array.dtype) for array in arrays] + [dma(2, len(arrays))],
        compiler_params=pltpu.CompilerParams(vmem_limit_bytes=LIMIT),
        name="finish",
    )(*arrays)


def shards_split(states, cotangent, attn_weights, mlp_weights, feature_gains, unit_gains, block_place):
    tok_rows, model_width = states.shape
    ff_width = unit_gains.shape[0]
    n_seq, n_ctx = lax.axis_size("seq"), lax.axis_size("ctx")
    chips = n_ctx // CORES
    chip = lax.axis_index("ctx") // CORES
    heads = HEADS // chips
    head_cols = heads * HEAD_DIM
    units = ff_width // chips
    rows = attn_weights.shape[0]
    qk_gain = lax.dynamic_slice_in_dim(feature_gains[:, 0], chip * head_cols, head_cols)
    qk_gain = qk_gain.reshape(heads, 1, HEAD_DIM)
    states_all, w_qkv, w_out, w_up, w_gate, low_down, raw, query, both, att, inverse, attx = attend_call(
        states, attn_weights, mlp_weights, qk_gain, block_place
    )
    gain_u = lax.dynamic_slice_in_dim(unit_gains[:, 0], chip * units, units)
    gain_v = lax.dynamic_slice_in_dim(unit_gains[:, 1], chip * units, units) * math.sqrt(D)
    out_low, grad_attx, grad_w_out, grad_direct, small, grad_half, grad_down = mlp_call(
        attx, states, cotangent, w_out, feature_gains[:, 1].reshape(1, model_width),
        feature_gains[:, 2].reshape(1, model_width), gain_u.reshape(CORES, 1, units // CORES),
        gain_v.reshape(CORES, 1, units // CORES), w_up, w_gate, low_down,
    )
    grad_states, grad_mlp, grad_attn, feature, unit = back_call(
        grad_attx, grad_half, grad_down, grad_w_out, small, raw, query, both, att, inverse, states_all,
        w_qkv, qk_gain, block_place, grad_direct, rows,
    )
    out_low, grad_states, grad_mlp, grad_attn = finish_call(out_low, grad_states, grad_mlp, grad_attn)
    rank = lax.axis_index(ALL)
    unit_rows_own = ff_width // (n_seq * n_ctx)
    return (
        out_low,
        grad_states,
        grad_attn,
        grad_mlp,
        lax.dynamic_slice_in_dim(feature, rank * rows, rows, axis=1).T,
        lax.dynamic_slice_in_dim(unit, rank * unit_rows_own, unit_rows_own, axis=1).T,
    )


def solution(mesh):
    in_specs = (
        P(("seq", "ctx"), None),
        P(("seq", "ctx"), None),
        P(("seq", "ctx"), None),
        P(("seq", "ctx"), None),
        P(),
        P(),
        P("seq", None),
    )
    out_specs = (
        P(("seq", "ctx"), None),
        P(("seq", "ctx"), None),
        P(("seq", "ctx"), None),
        P(("seq", "ctx"), None),
        P(("seq", "ctx"), None),
        P(("seq", "ctx"), None),
    )
    chips = mesh.shape["ctx"] // CORES
    shards = shards_split if fits(mesh.shape["seq"], chips) else shards_general
    return jax.shard_map(shards, mesh=mesh, in_specs=in_specs, out_specs=out_specs, check_vma=False)
```
